32 devices in a mesh: rep: 2 (over x), fsdp: 16 (over z, y, core).
Axes of the slice: x: 2, y: 2, z: 4, core: 2. Of those that a mesh axis runs over, the one named last changes fastest.
Arguments:
- tokens: bfloat16 [4096, 1536], P(('rep', 'fsdp')), may hold values from -6 to 6
- cotangent: bfloat16 [4096, 1536], P(('rep', 'fsdp')), may hold values from -6 to 6
- positions: int32 [4096], P(('rep', 'fsdp')), may hold values from 0 to 2047
- segments: int32 [2, 2048], P('rep'), may hold values from 0 to 7, never falling along the last dimension, each value on 1 to 1536 neighbouring positions
- routes: int32 [2, 4096, 8], P(None, ('rep', 'fsdp')), may hold values from 0 to 15, all different within a row; in each aligned block of 128 rows (0 to 127, 128 to 255, ..., all dimensions but the last counted through in order) at most 96 rows name the same one
- attn_gain: bfloat16 [2, 1536], P(None, 'fsdp'), may hold values from 0.5 to 1.5
- w_query: bfloat16 [2, 1536, 1536], P(None, 'fsdp'), may hold values from -0.15625 to 0.15625
- w_key: bfloat16 [2, 1536, 512], P(None, 'fsdp'), may hold values from -0.15625 to 0.15625
- w_value: bfloat16 [2, 1536, 512], P(None, 'fsdp'), may hold values from -0.15625 to 0.15625
- w_out: bfloat16 [2, 1536, 1536], P(None, 'fsdp'), may hold values from -0.875 to 0.875
- ffn_gain: bfloat16 [2, 1536], P(None, 'fsdp'), may hold values from 0.5 to 1.5
- router: bfloat16 [2, 1536, 16], P(None, 'fsdp'), may hold values from -0.078125 to 0.078125
- w_gate: bfloat16 [2, 16, 1536, 512], P(None, 'fsdp'), may hold values from -0.15625 to 0.15625
- w_up: bfloat16 [2, 16, 1536, 512], P(None, 'fsdp'), may hold values from -0.15625 to 0.15625
- w_down: bfloat16 [2, 16, 512, 1536], P(None, 'fsdp'), may hold values from -1 to 1
Outputs:
- activations: bfloat16 [4096, 1536], P(('rep', 'fsdp'))
- grad_tokens: float32 [4096, 1536], P(('rep', 'fsdp'))
- grad_attn_gain: float32 [2, 1536], P(None, 'fsdp')
- grad_w_query: float32 [2, 1536, 1536], P(None, 'fsdp')
- grad_w_key: float32 [2, 1536, 512], P(None, 'fsdp')
- grad_w_value: float32 [2, 1536, 512], P(None, 'fsdp')
- grad_w_out: float32 [2, 1536, 1536], P(None, 'fsdp')
- grad_ffn_gain: float32 [2, 1536], P(None, 'fsdp')
- grad_router: float32 [2, 1536, 16], P(None, 'fsdp')
- grad_w_gate: float32 [2, 16, 1536, 512], P(None, 'fsdp')
- grad_w_up: float32 [2, 16, 1536, 512], P(None, 'fsdp')
- grad_w_down: float32 [2, 16, 512, 1536], P(None, 'fsdp')
The draws below stay inside these ranges and needn't reach their ends.
Inputs may be any that keep to these rules, and one draw needn't show every extreme that they name: `routes`: in each block of 128 rows of one layer (the rows of one device) no expert is named by more than 96 rows, and this most is reached. `segments`: within a sequence segment ids never fall; a document has at most 1536 tokens, and some document of every sequence has exactly that many.
All inputs are finite; a program needn't handle non-finite values.
Results may differ from the reference program's by a relative error of at most 0.03.
Values may be sent and summed in bfloat16 or wider, within the bound.
A program may use at most 256 MiB of HBM per device.

```python
import math
import jax
import jax.numpy as jnp
import numpy as np
from jax import lax

D = 1536
HEADS = 24
KV_HEADS = 8
HD = 64
FF = 512
K = 8
LAYERS = 2
DOCS = 8
TOK_DEV = 128
E = 16
KV = 512
SEQ_LEN = 2048
TOKENS = 4096
NSEQ = 2
CAP = 96


def place_ends(result, stream_key, least, top_value):
    dims = result.shape
    index_at = [jax.random.randint(jax.random.fold_in(stream_key, axis), (), 0, dims[axis]) for axis in range(len(dims))]
    result = result.at[tuple(index_at)].set(least)
    longest = dims.index(max(dims))
    index_at[longest] = (index_at[longest] + 1) % dims[longest]
    return result.at[tuple(index_at)].set(top_value)


def block_levels(own_key, dims, split, smallest, high):
    def one(dim, shards_of):
        steps = jax.random.uniform(jax.random.fold_in(jax.random.fold_in(own_key, 6), dim), (shards_of,), jnp.float32, smallest / len(split), high / len(split))
        return jnp.repeat(jnp.exp(steps), dims[dim] // shards_of).reshape((-1,) + (1,) * (len(dims) - dim - 1))

    factor_of = one(*split[0])
    for cut in split[1:]:
        factor_of = factor_of * one(*cut)
    return factor_of


def profile(amount, total, bound, lean):
    portions = [(1 << 20) // math.isqrt(standing ** lean) + 1 for standing in range(2, amount + 1)]
    rest, holding = total - bound - (amount - 1), [1] * (amount - 1)
    while rest > 0:
        movable = [i for i in range(amount - 1) if holding[i] < bound]
        mass, left = sum([portions[i] for i in movable]), rest
        for i in movable:
            addition = min(bound - holding[i], max(1, left * portions[i] // mass), rest)
            holding[i] = holding[i] + addition
            rest = rest - addition
    return np.array([bound] + holding)


def uneven_parts(stream_key, amount, total, most, slope):
    if amount == 2:
        one = jax.random.randint(stream_key, (), max(1, total - most), min(most, total - 1) + 1)
        return jnp.stack([one, total - one])
    lengths = jnp.asarray(profile(amount, total, most, slope), jnp.int32)
    twos = (amount - 1) // 2
    giver, taker = lengths[1:1 + 2 * twos:2], lengths[2:2 + 2 * twos:2]
    slack = jnp.minimum(giver - 1, most - taker)
    passed = jax.random.randint(jax.random.fold_in(stream_key, 1), (twos,), 0, 1 << 20) % (slack + 1)
    lengths = lengths.at[1:1 + 2 * twos:2].set(giver - passed).at[2:2 + 2 * twos:2].set(taker + passed)
    return lengths[jax.random.permutation(jax.random.fold_in(stream_key, 2), amount)]


def assign_block(stream_key, own, number, rows, number_of, top, bound, lean):
    ranking = jax.random.permutation(stream_key, number_of)
    packed, usual = load_shares(number_of, rows * top, bound, lean, True), load_shares(number_of, rows * top, bound, lean, False)
    places = jnp.arange(number_of)

    def named(sizes, offset_by):
        used = int((sizes > 0).sum())
        fixed = max(1, used // 4)
        moved = fixed + (places - fixed + offset_by * (used - fixed)) % max(1, number_of - fixed)
        return jnp.zeros((number_of,), jnp.int32).at[ranking[jnp.where(places < fixed, places, moved)]].set(jnp.asarray(sizes, jnp.int32))

    sizes = jnp.where(number % 4 == 0, named(packed, number // 4), named(usual, number - number // 4 - 1))
    mixed = jax.random.permutation(jax.random.fold_in(own, 3), number_of)
    source_of, sink = mixed[0:number_of // 2 * 2:2], mixed[1:number_of // 2 * 2:2]
    margin = jnp.minimum(sizes[source_of] - 1, bound - sizes[sink]) // 2
    margin = jnp.where((source_of == ranking[0]) | (sink == ranking[0]) | (sizes[sink] == 0), 0, jnp.maximum(margin, 0))
    moved = jax.random.randint(jax.random.fold_in(own, 4), (number_of // 2,), 0, 1 << 20) % (margin + 1)
    sizes = sizes.at[source_of].add(-moved).at[sink].add(moved)
    labels = jnp.searchsorted(jnp.cumsum(sizes), jnp.arange(rows * top), side="right").astype(jnp.int32)
    grid = labels.reshape(top, rows).T
    grid = grid[jax.random.permutation(jax.random.fold_in(own, 1), rows)]
    offset_by = jax.random.randint(jax.random.fold_in(own, 2), (rows, 1), 0, top)
    return jnp.take_along_axis(grid, (jnp.arange(top)[None, :] + offset_by) % top, axis=1)


def load_shares(number_of, total, reach, lean, full):
    portions = [(1 << 20) // math.isqrt(grade ** lean) + 1 for grade in range(1, number_of + 1)]
    largest = reach if full else min(reach, max(-(-total // number_of), total * portions[0] // sum(portions)))
    least = 1 if total - largest >= number_of - 1 else 0
    given, spare = [largest] + [least] * (number_of - 1), total - largest - least * (number_of - 1)
    while spare > 0:
        movable = [i for i in range(1, number_of) if given[i] < largest] or [i for i in range(1, number_of) if given[i] < reach]
        pool, left = sum([portions[i] for i in movable]), spare
        for i in movable:
            addition = min(reach - given[i], max(1, left * portions[i] // pool), spare)
            given[i] = given[i] + addition
            spare = spare - addition
    return np.array(given)


def gaussian(own_key, dims, width, bound, split=(), kind=jnp.bfloat16):
    drawn = jax.random.normal(own_key, dims, jnp.float32) * width
    if len(split) > 0:
        drawn = block_levels(own_key, dims, split, -0.22, 0.18) * drawn
    return jnp.clip(drawn, min=-bound, max=bound).astype(kind)


def setup_inputs(seed: int = 0) -> dict:
    seeds = jax.random.split(jax.random.key(seed), 16)
    tokens = gaussian(seeds[0], (TOKENS, D), 1.0, 6.0, ((0, 32),))
    cotangent = gaussian(seeds[1], (TOKENS, D), 1.0, 6.0, ((0, 32),))
    positions = place_ends(jax.random.randint(seeds[2], (TOKENS,), 0, SEQ_LEN), jax.random.fold_in(seeds[2], 1), 0, SEQ_LEN - 1).astype(jnp.int32)
    segments = jax.vmap(lambda own: jnp.searchsorted(jnp.cumsum(uneven_parts(own, DOCS, SEQ_LEN, (3 * SEQ_LEN) // 4, 2)), jnp.arange(SEQ_LEN), side="right"))(jax.random.split(seeds[3], NSEQ)).reshape((NSEQ, SEQ_LEN)).astype(jnp.int32)
    routes_keys = jax.random.split(jax.random.fold_in(seeds[4], 1), LAYERS * TOKENS // TOK_DEV)
    routes_turns = jax.random.permutation(jax.random.fold_in(seeds[4], 3), LAYERS * TOKENS // TOK_DEV)
    routes = jax.vmap(lambda own, number: assign_block(jax.random.fold_in(seeds[4], 2), own, number, TOK_DEV, E, K, CAP, 2))(routes_keys, routes_turns).reshape((LAYERS, TOKENS, K))
    attn_gain = jnp.clip(1.0 + 0.1 * jax.random.normal(seeds[5], (LAYERS, D), jnp.float32), 0.5, 1.5).astype(jnp.bfloat16)
    w_query = gaussian(seeds[6], (LAYERS, D, D), D ** -0.5, 0.15625, ((1, 16),))
    w_key = gaussian(seeds[7], (LAYERS, D, KV), D ** -0.5, 0.15625, ((1, 16),))
    w_value = gaussian(seeds[8], (LAYERS, D, KV), D ** -0.5, 0.15625, ((1, 16),))
    w_out = gaussian(seeds[9], (LAYERS, D, D), (D // 32) ** -0.5, 0.875, ((1, 16),))
    ffn_gain = jnp.clip(1.0 + 0.1 * jax.random.normal(seeds[10], (LAYERS, D), jnp.float32), 0.5, 1.5).astype(jnp.bfloat16)
    router = gaussian(seeds[11], (LAYERS, D, E), (4 * D) ** -0.5, 0.078125, ((1, 16),))
    w_gate = gaussian(seeds[12], (LAYERS, E, D, FF), D ** -0.5, 0.15625, ((1, 16),))
    w_up = gaussian(seeds[13], (LAYERS, E, D, FF), D ** -0.5, 0.15625, ((1, 16),))
    w_down = gaussian(seeds[14], (LAYERS, E, FF, D), (FF // 16) ** -0.5, 1.0, ((1, 16),))
    return dict(tokens=tokens, cotangent=cotangent, positions=positions, segments=segments, routes=routes, attn_gain=attn_gain, w_query=w_query, w_key=w_key, w_value=w_value, w_out=w_out, ffn_gain=ffn_gain, router=router, w_gate=w_gate, w_up=w_up, w_down=w_down)


epsilon = 1e-06
masked_value = -1e+30
highest = lax.Precision.HIGHEST

@jax.custom_vjp
def low(v):
    return lax.optimization_barrier(v.astype(jnp.bfloat16)).astype(jnp.float32)

@jax.custom_vjp
def low_back(v):
    return v

def low_keep(v):
    return (low(v), None)

def low_pass(kept, grad):
    return (grad,)

def back_keep(v):
    return (v, None)

def back_low(kept, grad):
    return (low(grad),)
low.defvjp(low_keep, low_pass)
low_back.defvjp(back_keep, back_low)

def rope_tables(positions, half_width):
    frequency = jnp.exp(-jnp.log(10000.0) * jnp.arange(half_width, dtype=jnp.float32) / half_width)
    angles = positions.astype(jnp.float32)[:, None] * frequency[None, :]
    return (jnp.cos(angles), jnp.sin(angles))

def rotate(field, cosine, sine_table, direction):
    half_width = field.shape[-1] // 2
    first_half = field[..., :half_width]
    second_half = field[..., half_width:]
    cos_rows = cosine[:, None, :]
    sin_rows = direction * sine_table[:, None, :]
    return jnp.concatenate([first_half * cos_rows - second_half * sin_rows, second_half * cos_rows + first_half * sin_rows], -1)

def matmul(left, right):
    return jnp.dot(left, right, precision=highest)

def normalize(values, gain):
    return values * lax.rsqrt(lax.optimization_barrier(jnp.mean(values * values, -1, keepdims=True)) + epsilon) * gain

def sequence_attention(pieces):
    query_seq, key_seq, value_seq, segment_seq = pieces
    length = query_seq.shape[0]
    repeat_count = HEADS // KV_HEADS
    key_wide = jnp.repeat(key_seq, repeat_count, axis=1)
    value_wide = jnp.repeat(value_seq, repeat_count, axis=1)
    scores = low_back(jnp.einsum('qhd,khd->hqk', query_seq, key_wide, precision=highest) / math.sqrt(HD))
    position = jnp.arange(length, dtype=jnp.int32)
    allowed = (segment_seq[:, None] == segment_seq[None, :]) & (position[None, :] <= position[:, None])
    probabilities = low(jax.nn.softmax(jnp.where(allowed[None], scores, masked_value), axis=-1))
    return jnp.einsum('hqk,khd->qhd', probabilities, value_wide, precision=highest)

def layer_block(residual, layer_weights, cosine, sine_table, segments, route_rows):
    attn_gain, w_query, w_key, w_value, w_out, ffn_gain, router, w_gate, w_up, w_down = layer_weights
    total_rows = residual.shape[0]
    seq_count, seq_width = segments.shape
    x_attn = low(normalize(residual, attn_gain))
    query_pre = low_back(matmul(x_attn, w_query)).reshape(total_rows, HEADS, HD)
    query_rot = low(rotate(query_pre, cosine, sine_table, 1.0))
    key_pre = low_back(matmul(x_attn, w_key)).reshape(total_rows, KV_HEADS, HD)
    key_rot = low(rotate(key_pre, cosine, sine_table, 1.0))
    value_rows = low(low_back(matmul(x_attn, w_value))).reshape(total_rows, KV_HEADS, HD)
    attended = lax.map(jax.checkpoint(sequence_attention), (query_rot.reshape(seq_count, seq_width, HEADS, HD), key_rot.reshape(seq_count, seq_width, KV_HEADS, HD), value_rows.reshape(seq_count, seq_width, KV_HEADS, HD), segments))
    attended_rows = low(low_back(attended.reshape(total_rows, HEADS * HD)))
    middle = residual + low_back(matmul(attended_rows, w_out))
    x_moe = low(normalize(middle, ffn_gain))
    logits = matmul(x_moe, router)
    onehot = (route_rows[:, :, None] == jnp.arange(E, dtype=jnp.int32)[None, None, :]).astype(jnp.float32)
    chosen = lax.optimization_barrier(jnp.sum(onehot * logits[:, None, :], -1))
    gate_values = jax.nn.softmax(chosen, axis=-1)
    combine = lax.optimization_barrier(jnp.sum(gate_values[:, :, None] * onehot, 1))

    def expert_step(running, pieces):
        gate_matrix, up_matrix, down_matrix, column = pieces
        act_gate = low_back(matmul(x_moe, gate_matrix))
        act_up = low_back(matmul(x_moe, up_matrix))
        hidden = low(jax.nn.silu(act_gate) * act_up)
        expert_out = low(low_back(matmul(hidden, down_matrix)))
        return (running + column[:, None] * expert_out, None)
    mixed, _ = lax.scan(jax.checkpoint(expert_step), jnp.zeros_like(middle), (w_gate, w_up, w_down, combine.T))
    return middle + low_back(mixed)

def reference(tokens, cotangent, positions, segments, routes, attn_gain, w_query, w_key, w_value, w_out, ffn_gain, router, w_gate, w_up, w_down):
    cosine, sine_table = rope_tables(positions, HD // 2)
    weights = (attn_gain.astype(jnp.float32), w_query.astype(jnp.float32), w_key.astype(jnp.float32), w_value.astype(jnp.float32), w_out.astype(jnp.float32), ffn_gain.astype(jnp.float32), router.astype(jnp.float32), w_gate.astype(jnp.float32), w_up.astype(jnp.float32), w_down.astype(jnp.float32))

    def forward(residual, weight_set):
        for layer_index in range(LAYERS):
            layer_weights = tuple((weight[layer_index] for weight in weight_set))
            residual = layer_block(residual, layer_weights, cosine, sine_table, segments, routes[layer_index])
        return residual
    final, pullback = jax.vjp(forward, tokens.astype(jnp.float32), weights)
    grad_input, grad_weights = pullback(cotangent.astype(jnp.float32))
    return (final.astype(jnp.bfloat16), grad_input, grad_weights[0], grad_weights[1], grad_weights[2], grad_weights[3], grad_weights[4], grad_weights[5], grad_weights[6], grad_weights[7], grad_weights[8], grad_weights[9])
```

```python
import functools

import jax
import jax.numpy as jnp
from jax import lax
from jax.experimental import pallas as pl
from jax.experimental.pallas import tpu as pltpu
from jax.sharding import PartitionSpec as P

HEADS = 24
KV_HEADS = 8
HD = 64
LAYERS = 2
GROUP = HEADS // KV_HEADS
LANES = 128
CHUNK = 256
EPS = 1e-06
MASKED = -1e30
MESH = pl.DeviceIdType.MESH
F32 = jnp.float32
BF16 = jnp.bfloat16


def ring_place(chip, count):
    return lax.select(lax.rem(chip, 2) == 0, chip // 2, count - 1 - chip // 2)


def ring_chip(place, count):
    return lax.select(place < count // 2, 2 * place, 2 * (count - 1 - place) + 1)


def ring_setup(count):
    me = lax.axis_index("fsdp")
    chip, core = me // 2, lax.rem(me, 2)
    place = ring_place(chip, count)

    def at(offset):
        return ring_chip(lax.rem(place + offset + 2 * count, count), count)

    return chip, at, (at(1) * 2 + core, at(-1) * 2 + core)


def meet(neighbours):
    barrier = pltpu.get_barrier_semaphore()
    for other in neighbours:
        pl.semaphore_signal(barrier, inc=1, device_id={"fsdp": other}, device_id_type=MESH)
    pl.semaphore_wait(barrier, len(neighbours))


def ring_hops(count):
    half = count // 2
    return {(0, 0): half, (1, 1): half, (0, 1): half - 1, (1, 0): half - 1}


def gather_kernel(count, x_ref, side_ref, o_ref, all_ref, own_sem, send_sem, recv_sem, side_send, side_recv):
    chip, at, (right, left) = ring_setup(count)
    half_rows = x_ref.shape[0] // 2
    hops = ring_hops(count)
    steps = count // 2
    meet((right, left))
    own = pltpu.make_async_copy(x_ref, o_ref.at[chip], own_sem.at[0])
    own.start()
    own_side = pltpu.make_async_copy(side_ref, all_ref.at[chip], own_sem.at[1])
    own_side.start()

    def piece(direction, part, step):
        block = at(-step if direction == 0 else step)
        rows = pl.ds(part * half_rows, half_rows)
        target = o_ref.at[block, rows]
        return pltpu.make_async_remote_copy(
            src_ref=x_ref.at[rows] if step == 0 else target,
            dst_ref=target,
            send_sem=send_sem.at[direction, part, step],
            recv_sem=recv_sem.at[direction, part, step],
            device_id={"fsdp": right if direction == 0 else left},
            device_id_type=MESH,
        )

    def arrival(direction, part, step):
        block = at(-step - 1 if direction == 0 else step + 1)
        target = o_ref.at[block, pl.ds(part * half_rows, half_rows)]
        return pltpu.make_async_remote_copy(
            src_ref=target,
            dst_ref=target,
            send_sem=send_sem.at[direction, part, step],
            recv_sem=recv_sem.at[direction, part, step],
            device_id={"fsdp": right if direction == 0 else left},
            device_id_type=MESH,
        )

    def side_piece(direction, step, arrived):
        moved = step + 1 if arrived else step
        block = at(-moved if direction == 0 else moved)
        target = all_ref.at[block]
        return pltpu.make_async_remote_copy(
            src_ref=side_ref if step == 0 and not arrived else target,
            dst_ref=target,
            send_sem=side_send.at[direction, step],
            recv_sem=side_recv.at[direction, step],
            device_id={"fsdp": right if direction == 0 else left},
            device_id_type=MESH,
        )

    side_hops = (steps, steps - 1)
    for step in range(steps + 1):
        for direction in range(2):
            if 0 < step <= side_hops[direction]:
                side_piece(direction, step - 1, True).wait_recv()
            if step < side_hops[direction]:
                side_piece(direction, step, False).start()
        for key in hops:
            if 0 < step <= hops[key]:
                arrival(*key, step - 1).wait_recv()
            if step < hops[key]:
                piece(*key, step).start()
    for step in range(steps):
        for direction in range(2):
            if step < side_hops[direction]:
                side_piece(direction, step, False).wait_send()
        for key in hops:
            if step < hops[key]:
                piece(*key, step).wait_send()
    own.wait()
    own_side.wait()


def ring_gather(x, side, count):
    steps = count // 2
    return pl.pallas_call(
        functools.partial(gather_kernel, count),
        out_shape=(
            jax.ShapeDtypeStruct((count,) + x.shape, x.dtype),
            jax.ShapeDtypeStruct((count,) + side.shape, side.dtype),
        ),
        in_specs=[pl.BlockSpec(memory_space=pl.ANY)] * 2,
        out_specs=[pl.BlockSpec(memory_space=pl.ANY)] * 2,
        scratch_shapes=[
            pltpu.SemaphoreType.DMA((2,)),
            pltpu.SemaphoreType.DMA((2, 2, steps)),
            pltpu.SemaphoreType.DMA((2, 2, steps)),
            pltpu.SemaphoreType.DMA((2, steps)),
            pltpu.SemaphoreType.DMA((2, steps)),
        ],
        compiler_params=pltpu.CompilerParams(collective_id=0, has_side_effects=True),
        name="ring_gather",
    )(x, side)


def scatter_kernel(count, p_ref, o_ref, land, send_sem, recv_sem):
    chip, at, (right, left) = ring_setup(count)
    half_rows = o_ref.shape[0] // 2
    hops = ring_hops(count)
    steps = count // 2
    meet((right, left))

    def ahead(key, step):
        places = hops[key] - step
        return at(places if key[0] == 0 else -places)

    def piece(key, step):
        direction, part = key
        rows = pl.ds(part * half_rows, half_rows)
        first = p_ref.at[ahead(key, step), rows]
        return pltpu.make_async_remote_copy(
            src_ref=first if step == 0 else land.at[direction, part, step - 1],
            dst_ref=land.at[direction, part, step],
            send_sem=send_sem.at[direction, part, step],
            recv_sem=recv_sem.at[direction, part, step],
            device_id={"fsdp": right if direction == 0 else left},
            device_id_type=MESH,
        )

    for step in range(steps + 1):
        for key in hops:
            direction, part = key
            rows = pl.ds(part * half_rows, half_rows)
            if 0 < step <= hops[key]:
                piece(key, step - 1).wait_recv()
                if step < hops[key]:
                    slot = land.at[direction, part, step - 1]
                    total = slot[...].astype(F32) + p_ref[ahead(key, step), rows].astype(F32)
                    slot[...] = total.astype(BF16)
            if step < hops[key]:
                piece(key, step).start()
    for part in range(2):
        rows = pl.ds(part * half_rows, half_rows)
        total = p_ref[chip, rows].astype(F32)
        for direction in range(2):
            total = total + land[direction, part, hops[direction, part] - 1].astype(F32)
        o_ref[rows, :] = total
    for step in range(steps):
        for key in hops:
            if step < hops[key]:
                piece(key, step).wait_send()


def ring_scatter(partial, count):
    _, rows, width = partial.shape
    steps = count // 2
    return pl.pallas_call(
        functools.partial(scatter_kernel, count),
        out_shape=jax.ShapeDtypeStruct((rows, width), F32),
        in_specs=[pl.BlockSpec(memory_space=pltpu.VMEM)],
        out_specs=pl.BlockSpec(memory_space=pltpu.VMEM),
        scratch_shapes=[
            pltpu.VMEM((2, 2, steps, rows // 2, width), partial.dtype),
            pltpu.SemaphoreType.DMA((2, 2, steps)),
            pltpu.SemaphoreType.DMA((2, 2, steps)),
        ],
        compiler_params=pltpu.CompilerParams(
            collective_id=1, has_side_effects=True, vmem_limit_bytes=40 << 20
        ),
        name="ring_scatter",
    )(partial)


def dot(left, right, contract=((1,), (0,))):
    return lax.dot_general(left, right, (contract, ((), ())), preferred_element_type=F32)


NT = ((1,), (1,))
TN = ((0,), (0,))


def spin(field, cosine, sine):
    lane = lax.broadcasted_iota(jnp.int32, field.shape, 1)
    swapped = jnp.where(
        lane < HD // 2,
        -pltpu.roll(field, LANES - HD // 2, 1),
        pltpu.roll(field, HD // 2, 1),
    )
    return field * cosine + swapped * sine


def project_kernel(x_ref, w_ref, cos_ref, sin_ref, q_ref, kv_ref):
    rows = dot(x_ref[...], w_ref[...])
    cosine, sine = cos_ref[...], sin_ref[...]
    for head in range(GROUP):
        turned = spin(rows[:, head * LANES : (head + 1) * LANES], cosine, sine).astype(BF16)
        turned = (turned.astype(F32) * (HD**-0.5)).astype(BF16)
        for block in range(2):
            q_ref[block, head] = turned[block * LANES : (block + 1) * LANES]
    pair = rows[:, GROUP * LANES :]
    kv_ref[...] = spin(pair, cosine, sine).astype(BF16)


def project(x, w, cosine, sine):
    tokens, width = x.shape
    tile = 2 * LANES
    return pl.pallas_call(
        project_kernel,
        grid=(tokens // tile,),
        out_shape=(
            jax.ShapeDtypeStruct((tokens // LANES, GROUP, LANES, LANES), BF16),
            jax.ShapeDtypeStruct((tokens, LANES), BF16),
        ),
        in_specs=[
            pl.BlockSpec((tile, width), lambda i: (i, 0)),
            pl.BlockSpec(w.shape, lambda i: (0, 0)),
            pl.BlockSpec((tile, LANES), lambda i: (i, 0)),
            pl.BlockSpec((tile, LANES), lambda i: (i, 0)),
        ],
        out_specs=[
            pl.BlockSpec((2, GROUP, LANES, LANES), lambda i: (i, 0, 0, 0)),
            pl.BlockSpec((tile, LANES), lambda i: (i, 0)),
        ],
        name="project",
    )(x, w, cosine, sine)


def allowed_keys(begin, block, chunk):
    shape = (GROUP * LANES, CHUNK)
    key = chunk * CHUNK + lax.broadcasted_iota(jnp.int32, shape, 1)
    query = block * LANES + lax.rem(lax.broadcasted_iota(jnp.int32, shape, 0), LANES)
    return (key >= begin) & (key <= query)


def attend_kernel(info_ref, q_ref, kv_ref, begin_ref, w_ref, att_ref, lse_ref, out_ref):
    step = pl.program_id(0)
    block = 2 * step + info_ref[0]
    first = info_ref[1 + step] // CHUNK
    last = block * LANES // CHUNK
    q = q_ref[0].reshape(GROUP * LANES, LANES)
    begin = jnp.concatenate([begin_ref[0]] * GROUP, 0)

    def one(chunk, state):
        top, total, acc = state
        keys = kv_ref[pl.ds(pl.multiple_of(chunk * CHUNK, CHUNK), CHUNK), :]
        allowed = allowed_keys(begin, block, chunk)
        scores = jnp.where(allowed, dot(q, keys, NT), MASKED)
        new_top = jnp.maximum(top, jnp.max(scores, -1, keepdims=True))
        weights = jnp.where(allowed, jnp.exp(scores - new_top), 0.0)
        shrink = jnp.exp(top - new_top)
        total = total * shrink + jnp.sum(weights, -1, keepdims=True)
        return new_top, total, acc * shrink + dot(weights.astype(BF16), keys)

    rows = GROUP * LANES
    top, total, acc = lax.fori_loop(
        first,
        last + 1,
        one,
        (jnp.full((rows, 1), MASKED, F32), jnp.zeros((rows, 1), F32), jnp.zeros((rows, LANES), F32)),
    )
    lse_ref[0] = top + jnp.log(total)
    att = (acc / total).astype(BF16)
    wide = jnp.concatenate([att[h * LANES : (h + 1) * LANES] for h in range(GROUP)], 1)
    att_ref[0] = wide
    out_ref[0] = dot(wide, w_ref[...]).astype(BF16)


def attend(info, q, kv, begin, w):
    blocks = q.shape[0]
    wide = GROUP * LANES
    width = w.shape[1]
    return pl.pallas_call(
        attend_kernel,
        grid_spec=pltpu.PrefetchScalarGridSpec(
            num_scalar_prefetch=1,
            grid=(blocks,),
            in_specs=[
                pl.BlockSpec((1, GROUP, LANES, LANES), lambda i, s: (i, 0, 0, 0)),
                pl.BlockSpec(kv.shape, lambda i, s: (0, 0)),
                pl.BlockSpec((1, LANES, 1), lambda i, s: (i, 0, 0)),
                pl.BlockSpec(w.shape, lambda i, s: (0, 0)),
            ],
            out_specs=[
                pl.BlockSpec((1, LANES, wide), lambda i, s: (i, 0, 0)),
                pl.BlockSpec((1, wide, 1), lambda i, s: (i, 0, 0)),
                pl.BlockSpec((1, LANES, width), lambda i, s: (i, 0, 0)),
            ],
        ),
        out_shape=(
            jax.ShapeDtypeStruct((blocks, LANES, wide), BF16),
            jax.ShapeDtypeStruct((blocks, wide, 1), F32),
            jax.ShapeDtypeStruct((blocks, LANES, width), BF16),
        ),
        name="attend",
    )(info, q, kv, begin, w)


def attend_back_kernel(info_ref, q_ref, kv_ref, begin_ref, w_ref, att_ref, lse_ref, db_ref, cos_ref, sin_ref, dq_ref, dkv_ref):
    step = pl.program_id(0)
    block = 2 * step + info_ref[0]
    first = info_ref[1 + step] // CHUNK
    last = block * LANES // CHUNK

    @pl.when(step == 0)
    def _():
        dkv_ref[...] = jnp.zeros_like(dkv_ref)

    q = q_ref[0].reshape(GROUP * LANES, LANES)
    begin = jnp.concatenate([begin_ref[0]] * GROUP, 0)
    wide = dot(db_ref[0], w_ref[...], NT).astype(BF16)
    datt = jnp.concatenate([wide[:, h * LANES : (h + 1) * LANES] for h in range(GROUP)], 0)
    att = jnp.concatenate([att_ref[0, :, h * LANES : (h + 1) * LANES] for h in range(GROUP)], 0)
    delta = jnp.sum(datt.astype(F32) * att.astype(F32), -1, keepdims=True)
    lse = lse_ref[0]
    both = jnp.concatenate([q, datt], 0)

    def one(chunk, acc):
        place = pl.ds(pl.multiple_of(chunk * CHUNK, CHUNK), CHUNK)
        keys = kv_ref[place, :]
        allowed = allowed_keys(begin, block, chunk)
        weights = jnp.where(allowed, jnp.exp(dot(q, keys, NT) - lse), 0.0)
        slope = (weights * (dot(datt, keys, NT) - delta)).astype(BF16)
        dkv_ref[place, :] += dot(jnp.concatenate([slope, weights.astype(BF16)], 0), both, TN)
        return acc + dot(slope, keys)

    acc = lax.fori_loop(first, last + 1, one, jnp.zeros((GROUP * LANES, LANES), F32))
    cosine, sine = cos_ref[0], sin_ref[0]
    for head in range(GROUP):
        part = acc[head * LANES : (head + 1) * LANES] * (HD**-0.5)
        dq_ref[0, :, head * LANES : (head + 1) * LANES] = spin(part, cosine, -sine).astype(BF16)


def attend_back(info, q, kv, begin, w, att, lse, db, cosine, sine):
    blocks = q.shape[0]
    wide = GROUP * LANES
    width = w.shape[1]
    return pl.pallas_call(
        attend_back_kernel,
        grid_spec=pltpu.PrefetchScalarGridSpec(
            num_scalar_prefetch=1,
            grid=(blocks,),
            in_specs=[
                pl.BlockSpec((1, GROUP, LANES, LANES), lambda i, s: (i, 0, 0, 0)),
                pl.BlockSpec(kv.shape, lambda i, s: (0, 0)),
                pl.BlockSpec((1, LANES, 1), lambda i, s: (i, 0, 0)),
                pl.BlockSpec(w.shape, lambda i, s: (0, 0)),
                pl.BlockSpec((1, LANES, wide), lambda i, s: (i, 0, 0)),
                pl.BlockSpec((1, wide, 1), lambda i, s: (i, 0, 0)),
                pl.BlockSpec((1, LANES, width), lambda i, s: (i, 0, 0)),
                pl.BlockSpec((1, LANES, LANES), lambda i, s: (i, 0, 0)),
                pl.BlockSpec((1, LANES, LANES), lambda i, s: (i, 0, 0)),
            ],
            out_specs=[
                pl.BlockSpec((1, LANES, wide), lambda i, s: (i, 0, 0)),
                pl.BlockSpec(kv.shape, lambda i, s: (0, 0)),
            ],
        ),
        out_shape=(
            jax.ShapeDtypeStruct((blocks, LANES, wide), BF16),
            jax.ShapeDtypeStruct(kv.shape, F32),
        ),
        name="attend_back",
    )(info, q, kv, begin, w, att, lse, db, cosine, sine)


def on_device(
    tokens,
    cotangent,
    positions,
    segments,
    routes,
    attn_gain,
    w_query,
    w_key,
    w_value,
    w_out,
    ffn_gain,
    router,
    w_gate,
    w_up,
    w_down,
):
    rows, width = tokens.shape
    devices = lax.axis_size("fsdp")
    replicas = lax.axis_size("rep")
    count = devices // 2
    me = lax.axis_index("fsdp")
    chip, core = me // 2, lax.rem(me, 2)
    shard = w_query.shape[1]
    experts = w_gate.shape[1] * devices
    ff = w_gate.shape[3]
    pairs = [(index, index ^ 1) for index in range(devices)]

    def swap(array):
        return lax.ppermute(array, "fsdp", pairs)

    def by_core(own, other, axis):
        return jnp.where(
            core == 0, jnp.stack([own, other], axis), jnp.stack([other, own], axis)
        )

    def own_and_other(array):
        return (
            lax.dynamic_index_in_dim(array, core, 0, False),
            lax.dynamic_index_in_dim(array, 1 - core, 0, False),
        )

    def over_replicas(arrays):
        if replicas == 2:
            other = [lax.ppermute(a, "rep", [(0, 1), (1, 0)]) for a in arrays]
            return [a.astype(F32) + b.astype(F32) for a, b in zip(arrays, other)]
        return [lax.psum(a, "rep").astype(F32) for a in arrays]

    small = jnp.concatenate(
        [
            attn_gain.reshape(LAYERS, shard, 1),
            ffn_gain.reshape(LAYERS, shard, 1),
            router,
        ],
        -1,
    )
    small = lax.all_gather(small, "fsdp", axis=1, tiled=True)
    gains_one = small[:, :, 0].astype(F32)
    gains_two = small[:, :, 1].astype(F32)
    routers = small[:, :, 2:]
    by_chip = jnp.concatenate(
        [
            w_query.reshape(LAYERS, shard, count, GROUP * HD),
            w_key.reshape(LAYERS, shard, count, HD),
            w_value.reshape(LAYERS, shard, count, HD),
        ],
        -1,
    ).transpose(2, 0, 1, 3)
    head_width = by_chip.shape[-1]
    by_device = jnp.repeat(by_chip, 2, axis=0)
    mine = lax.all_to_all(by_device, "fsdp", split_axis=0, concat_axis=0, tiled=True)
    mine = mine.transpose(1, 0, 2, 3).reshape(LAYERS, width, head_width)
    hole = jnp.zeros((LAYERS, width, HD), BF16)
    w_heads = jnp.concatenate(
        [piece for h in range(GROUP) for piece in (mine[:, :, h * HD : (h + 1) * HD], hole)]
        + [mine[:, :, GROUP * HD :]],
        -1,
    )
    out_rows = by_core(w_out, swap(w_out), 1).reshape(LAYERS, GROUP, HD, width)
    w_outs = jnp.concatenate([jnp.zeros_like(out_rows), out_rows], 2).reshape(
        LAYERS, GROUP * LANES, width
    )
    gate_pair = by_core(w_gate[:, 0], swap(w_gate[:, 0]), 2).reshape(LAYERS, width, 2 * ff)
    up_pair = by_core(w_up[:, 0], swap(w_up[:, 0]), 2).reshape(LAYERS, width, 2 * ff)
    down_pair = by_core(w_down[:, 0], swap(w_down[:, 0]), 1).reshape(LAYERS, 2 * ff, width)

    flat = segments.reshape(-1)
    starts = jnp.sum(
        (flat[None, :] < jnp.arange(8, dtype=jnp.int32)[:, None]).astype(jnp.int32), 1
    )
    begin = jnp.sum(
        jnp.where(flat[:, None] == jnp.arange(8, dtype=jnp.int32)[None, :], starts[None, :], 0), 1
    )
    begin = begin.reshape(count, 2, rows)
    begin = lax.dynamic_index_in_dim(begin, core, 1, False)
    info = jnp.concatenate([core[None], begin[:, 0]]).astype(jnp.int32)
    begin = begin[:, :, None]

    side = jnp.concatenate(
        [positions.astype(F32)[None, :], jnp.zeros((experts - 1, rows), F32)], 0
    )
    cosine = sine = None
    hidden = tokens.astype(F32)
    saved = []

    def normal(values):
        inverse = lax.rsqrt(jnp.mean(values * values, -1, keepdims=True) + EPS)
        return inverse, values * inverse

    for layer in range(LAYERS):
        inverse_one, normed_one = normal(hidden)
        x_attn = (normed_one * gains_one[layer][None, :]).astype(BF16)
        x_all, side_all = ring_gather(x_attn, side, count)
        if layer == 0:
            place = side_all[:, 0, :].reshape(-1)
            lane = jnp.arange(LANES, dtype=jnp.int32)
            rate = jnp.exp(-jnp.log(10000.0) * (lane % (HD // 2)).astype(F32) / (HD // 2))
            angle = place[:, None] * jnp.where(lane < HD, rate, 0.0)[None, :]
            cosine, sine = jnp.cos(angle), jnp.sin(angle)
        x_all = x_all.reshape(count * rows, width)
        query, kv_own = project(x_all, w_heads[layer], cosine, sine)
        kv_own = kv_own.reshape(count, rows, LANES)
        kv = by_core(kv_own, swap(kv_own), 1).reshape(count * 2 * rows, LANES)
        att, lse, partial = attend(info, query, kv, begin, w_outs[layer])
        middle = hidden + ring_scatter(partial, count)
        inverse_two, normed_two = normal(middle)
        x_moe = (normed_two * gains_two[layer][None, :]).astype(BF16)
        logits = dot(x_moe, routers[layer])
        named = jnp.any(
            routes[layer][:, :, None] == jnp.arange(experts, dtype=jnp.int32)[None, None, :], 1
        )
        share = jax.nn.softmax(jnp.where(named, logits, -jnp.inf), axis=-1)
        m_all, share_all = ring_gather(x_moe, share.T, count)
        m_all = m_all.reshape(count * rows, width)
        share_mine = lax.dynamic_slice_in_dim(share_all, 2 * chip, 2, 1)
        share_mine = share_mine.transpose(0, 2, 1).reshape(count * rows, 2)
        share_wide = jnp.repeat(share_mine, ff, axis=1)
        act_gate = dot(m_all, gate_pair[layer])
        act_up = dot(m_all, up_pair[layer])
        weighted = (jax.nn.silu(act_gate) * act_up * share_wide).astype(BF16)
        partial = dot(weighted, down_pair[layer]).astype(BF16)
        mixed = ring_scatter(partial.reshape(count, rows, width), count)
        saved.append(
            (inverse_one, normed_one, x_all, query, kv, att, lse, inverse_two, normed_two)
            + (m_all, share_mine, share_wide, act_gate, act_up, weighted, mixed)
        )
        hidden = middle + mixed
    activations = hidden.astype(BF16)
    grad = cotangent.astype(F32)
    grads = [None] * LAYERS
    for layer in reversed(range(LAYERS)):
        (inverse_one, normed_one, x_all, query, kv, att, lse, inverse_two, normed_two) = saved[layer][:9]
        (m_all, share_mine, share_wide, act_gate, act_up, weighted, mixed) = saved[layer][9:]
        d_mix = grad.astype(BF16)
        balance = jnp.sum(mixed * d_mix.astype(F32), -1)
        side = jnp.concatenate([balance[None, :], jnp.zeros((experts - 1, rows), F32)], 0)
        d_all, balance_all = ring_gather(d_mix, side, count)
        d_all = d_all.reshape(count * rows, width)
        balance_all = balance_all[:, 0, :].reshape(-1, 1)
        raw = dot(d_all, down_pair[layer], NT)
        gate_sig = jax.nn.sigmoid(act_gate)
        swish = act_gate * gate_sig
        d_share = jnp.sum((swish * act_up * raw).reshape(-1, 2, ff), -1)
        d_logit = share_mine * (d_share - balance_all)
        d_hidden = raw * share_wide
        d_gate = (d_hidden * act_up * gate_sig * (1.0 + act_gate * (1.0 - gate_sig))).astype(BF16)
        d_up = (d_hidden * swish).astype(BF16)
        g_down = dot(weighted, d_all, TN)
        g_gate = dot(m_all, d_gate, TN)
        g_up = dot(m_all, d_up, TN)
        router_mine = lax.dynamic_slice_in_dim(routers[layer], 2 * chip, 2, 1).astype(F32)
        g_router = jnp.dot(d_logit.T, m_all.astype(F32), precision=lax.Precision.HIGHEST)
        partial = (
            dot(d_gate, gate_pair[layer], NT)
            + dot(d_up, up_pair[layer], NT)
            + d_logit[:, 0:1] * router_mine[:, 0][None, :]
            + d_logit[:, 1:2] * router_mine[:, 1][None, :]
        ).astype(BF16)
        d_x = ring_scatter(partial.reshape(count, rows, width), count)
        gain = gains_two[layer][None, :]
        d_norm = d_x * gain
        d_gain_two = jnp.sum(d_x * normed_two, 0)
        grad_mid = grad + inverse_two * (
            d_norm - normed_two * jnp.mean(d_norm * normed_two, -1, keepdims=True)
        )
        side = jnp.zeros((experts, rows), F32)
        b_all, _ = ring_gather(grad_mid.astype(BF16), side, count)
        d_query, d_kv = attend_back(
            info, query, kv, begin, w_outs[layer], att, lse, b_all,
            cosine.reshape(count, rows, LANES), sine.reshape(count, rows, LANES),
        )
        b_all = b_all.reshape(count * rows, width)
        g_out = dot(att.reshape(count * rows, GROUP * LANES), b_all, TN)
        halves = d_kv.astype(BF16).reshape(count, 2, rows, LANES).transpose(1, 0, 2, 3)
        own, other = own_and_other(halves)
        d_kv = (own.astype(F32) + swap(other).astype(F32)).reshape(count * rows, LANES)
        d_key, d_value = d_kv[:, :HD], d_kv[:, HD:]
        cos_half, sin_half = cosine[:, : HD // 2], sine[:, : HD // 2]
        low, high = d_key[:, : HD // 2], d_key[:, HD // 2 :]
        d_key = jnp.concatenate(
            [low * cos_half + high * sin_half, high * cos_half - low * sin_half], 1
        )
        d_heads = jnp.concatenate(
            [
                d_query.reshape(count * rows, GROUP * LANES),
                jnp.concatenate([d_key, d_value], 1).astype(BF16),
            ],
            1,
        )
        partial = dot(d_heads, w_heads[layer], NT).astype(BF16)
        d_x = ring_scatter(partial.reshape(count, rows, width), count)
        g_heads = dot(x_all, d_heads, TN)
        gain = gains_one[layer][None, :]
        d_norm = d_x * gain
        d_gain_one = jnp.sum(d_x * normed_one, 0)
        grad = grad_mid + inverse_one * (
            d_norm - normed_one * jnp.mean(d_norm * normed_one, -1, keepdims=True)
        )
        g_down = g_down.astype(BF16).reshape(2, ff, width)
        g_gate = g_gate.astype(BF16).reshape(width, 2, ff).transpose(1, 0, 2)
        g_up = g_up.astype(BF16).reshape(width, 2, ff).transpose(1, 0, 2)
        g_out = g_out.reshape(GROUP, LANES, width)[:, HD:].reshape(2, shard, width).astype(BF16)
        g_router = g_router.astype(BF16)
        sums = []
        for pair in (g_gate, g_up, g_down, g_out, g_router):
            own, other = own_and_other(pair)
            sums.append((own.astype(F32) + swap(other).astype(F32)).astype(BF16))
        g_heads = jnp.concatenate(
            [g_heads[:, h * LANES : h * LANES + HD] for h in range(GROUP)]
            + [g_heads[:, GROUP * LANES :]],
            1,
        )
        spread = jnp.concatenate(
            [
                g_heads.reshape(devices, shard, head_width),
                d_gain_one.reshape(devices, shard, 1),
                d_gain_two.reshape(devices, shard, 1),
            ],
            2,
        ).astype(BF16)
        sent_router = lax.all_to_all(
            sums[4].reshape(devices, shard), "fsdp", split_axis=0, concat_axis=0, tiled=True
        )
        spread = lax.all_to_all(spread, "fsdp", split_axis=0, concat_axis=0, tiled=True).astype(F32)
        gains = jnp.sum(spread[:, :, head_width:], 0)
        heads = jnp.sum(spread[:, :, :head_width].reshape(count, 2, shard, head_width), 1)
        heads = heads.transpose(1, 0, 2)
        q_part = heads[:, :, : GROUP * HD].reshape(shard, width)
        k_part = heads[:, :, GROUP * HD : (GROUP + 1) * HD].reshape(shard, KV_HEADS * HD)
        v_part = heads[:, :, (GROUP + 1) * HD :].reshape(shard, KV_HEADS * HD)
        packed = jnp.concatenate([q_part, k_part, v_part, sent_router.T.astype(F32), gains], 1)
        g_gate, g_up, g_down, g_out, packed = over_replicas(sums[:4] + [packed.astype(BF16)])
        edge_key = width + KV_HEADS * HD
        edge_value = edge_key + KV_HEADS * HD
        edge_router = edge_value + experts
        grads[layer] = (
            packed[:, edge_router],
            packed[:, :width],
            packed[:, width:edge_key],
            packed[:, edge_key:edge_value],
            g_out,
            packed[:, edge_router + 1],
            packed[:, edge_value:edge_router],
            g_gate[None],
            g_up[None],
            g_down[None],
        )
    return (activations, grad) + tuple(
        jnp.stack([grads[layer][index] for layer in range(LAYERS)]) for index in range(10)
    )


def solution(mesh):
    placed = (
        P(("rep", "fsdp"), None),
        P(("rep", "fsdp"), None),
        P(("rep", "fsdp")),
        P("rep", None),
        P(None, ("rep", "fsdp"), None),
        P(None, "fsdp"),
        P(None, "fsdp", None),
        P(None, "fsdp", None),
        P(None, "fsdp", None),
        P(None, "fsdp", None),
        P(None, "fsdp"),
        P(None, "fsdp", None),
        P(None, "fsdp", None, None),
        P(None, "fsdp", None, None),
        P(None, "fsdp", None, None),
    )
    return jax.shard_map(
        on_device,
        mesh=mesh,
        in_specs=placed,
        out_specs=(
            P(("rep", "fsdp"), None),
            P(("rep", "fsdp"), None),
            P(None, "fsdp"),
            P(None, "fsdp", None),
            P(None, "fsdp", None),
            P(None, "fsdp", None),
            P(None, "fsdp", None),
            P(None, "fsdp"),
            P(None, "fsdp", None),
            P(None, "fsdp", None, None),
            P(None, "fsdp", None, None),
            P(None, "fsdp", None, None),
        ),
        check_vma=False,
    )
```

```python
import functools

import jax
import jax.numpy as jnp
from jax import lax
from jax.experimental import pallas as pl
from jax.experimental.pallas import tpu as pltpu
from jax.sharding import PartitionSpec as P

HEADS = 24
KV_HEADS = 8
HD = 64
LAYERS = 2
GROUP = HEADS // KV_HEADS
LANES = 128
EPS = 1e-06
MASKED = -1e30
MESH = pl.DeviceIdType.MESH
F32 = jnp.float32
BF16 = jnp.bfloat16


def ring_place(chip, count):
    return lax.select(lax.rem(chip, 2) == 0, chip // 2, count - 1 - chip // 2)


def ring_chip(place, count):
    return lax.select(place < count // 2, 2 * place, 2 * (count - 1 - place) + 1)


def ring_setup(count):
    me = lax.axis_index("fsdp")
    chip, core = me // 2, lax.rem(me, 2)
    place = ring_place(chip, count)

    def at(offset):
        return ring_chip(lax.rem(place + offset + 2 * count, count), count)

    near = [{"fsdp": at(1) * 2 + core}, {"fsdp": at(-1) * 2 + core}]
    return chip, at, near


def partner_of(axis):
    if axis == "rep":
        return {"rep": 1 - lax.axis_index("rep")}
    me = lax.axis_index("fsdp")
    return {"fsdp": me + 1 - 2 * lax.rem(me, 2)}


def meet(others):
    barrier = pltpu.get_barrier_semaphore()
    for other in others:
        pl.semaphore_signal(barrier, inc=1, device_id=other, device_id_type=MESH)
    pl.semaphore_wait(barrier, len(others))


def remote(src, dst, send_sem, recv_sem, device):
    return pltpu.make_async_remote_copy(
        src_ref=src,
        dst_ref=dst,
        send_sem=send_sem,
        recv_sem=recv_sem,
        device_id=device,
        device_id_type=MESH,
    )


def ring_hops(count):
    half = count // 2
    return {(0, 0): half, (1, 1): half, (0, 1): half - 1, (1, 0): half - 1}


def gather_kernel(count, axes, sided, *refs):
    riders = len(axes)
    sources = refs[: 1 + sided]
    ride_in = refs[1 + sided : 1 + sided + riders]
    rest = refs[1 + sided + riders :]
    targets, rest = rest[: 1 + sided], rest[1 + sided :]
    ride_out, rest = rest[:riders], rest[riders:]
    own_sem, send_sem, recv_sem, side_send, side_recv, ride_send, ride_recv = rest
    chip, at, near = ring_setup(count)
    x_ref, o_ref = sources[0], targets[0]
    half_rows = x_ref.shape[0] // 2
    hops = ring_hops(count)
    steps = count // 2
    meet(near + [partner_of(axis) for axis in sorted(set(axes))])
    rides = [
        remote(ride_in[i], ride_out[i], ride_send.at[i], ride_recv.at[i], partner_of(axes[i]))
        for i in range(riders)
    ]
    for ride in rides:
        ride.start()
    own = [
        pltpu.make_async_copy(sources[i], targets[i].at[chip], own_sem.at[i])
        for i in range(1 + sided)
    ]
    for copy in own:
        copy.start()

    def piece(key, step, arrived):
        direction, part = key
        moved = step + 1 if arrived else step
        block = at(-moved if direction == 0 else moved)
        rows = pl.ds(part * half_rows, half_rows)
        target = o_ref.at[block, rows]
        return remote(
            x_ref.at[rows] if step == 0 and not arrived else target,
            target,
            send_sem.at[direction, part, step],
            recv_sem.at[direction, part, step],
            near[direction],
        )

    def side_piece(direction, step, arrived):
        moved = step + 1 if arrived else step
        target = targets[1].at[at(-moved if direction == 0 else moved)]
        return remote(
            sources[1] if step == 0 and not arrived else target,
            target,
            side_send.at[direction, step],
            side_recv.at[direction, step],
            near[direction],
        )

    side_hops = (steps, steps - 1) if sided else (0, 0)
    for step in range(steps + 1):
        for direction in range(2):
            if 0 < step <= side_hops[direction]:
                side_piece(direction, step - 1, True).wait_recv()
            if step < side_hops[direction]:
                side_piece(direction, step, False).start()
        for key in hops:
            if 0 < step <= hops[key]:
                piece(key, step - 1, True).wait_recv()
            if step < hops[key]:
                piece(key, step, False).start()
    for step in range(steps):
        for direction in range(2):
            if step < side_hops[direction]:
                side_piece(direction, step, False).wait_send()
        for key in hops:
            if step < hops[key]:
                piece(key, step, False).wait_send()
    for copy in own:
        copy.wait()
    for ride in rides:
        ride.wait()


IDENTITIES = {}


def identity(*key):
    return IDENTITIES.setdefault(key, len(IDENTITIES))


def shape_of(array):
    return jax.ShapeDtypeStruct(array.shape, array.dtype)


def ring_gather(count, arrays, rides=()):
    steps = count // 2
    sided = len(arrays) - 1
    axes = tuple(axis for _, axis in rides)
    passengers = [array for array, _ in rides]
    dma = pltpu.SemaphoreType.DMA
    return pl.pallas_call(
        functools.partial(gather_kernel, count, axes, sided),
        out_shape=tuple(
            jax.ShapeDtypeStruct((count,) + a.shape, a.dtype) for a in arrays
        ) + tuple(shape_of(a) for a in passengers),
        in_specs=[pl.BlockSpec(memory_space=pl.ANY)] * (len(arrays) + len(rides)),
        out_specs=[pl.BlockSpec(memory_space=pl.ANY)] * (len(arrays) + len(rides)),
        scratch_shapes=[
            dma((2,)),
            dma((2, 2, steps)),
            dma((2, 2, steps)),
            dma((2, steps)),
            dma((2, steps)),
            dma((max(len(rides), 1),)),
            dma((max(len(rides), 1),)),
        ],
        compiler_params=pltpu.CompilerParams(
            collective_id=identity("gather", sided, axes, *(a.shape for a in passengers)),
            has_side_effects=True,
        ),
        name="ring_gather",
    )(*arrays, *passengers)


def scatter_kernel(count, axes, *refs):
    riders = len(axes)
    p_ref, ride_in, o_ref, ride_out = refs[0], refs[1 : 1 + riders], refs[1 + riders], refs[2 + riders : 2 + 2 * riders]
    land, send_sem, recv_sem, ride_send, ride_recv = refs[2 + 2 * riders :]
    chip, at, near = ring_setup(count)
    half_rows = o_ref.shape[0] // 2
    hops = ring_hops(count)
    steps = count // 2
    meet(near + [partner_of(axis) for axis in sorted(set(axes))])
    rides = [
        remote(ride_in[i], ride_out[i], ride_send.at[i], ride_recv.at[i], partner_of(axes[i]))
        for i in range(riders)
    ]
    for ride in rides:
        ride.start()

    def ahead(key, step):
        places = hops[key] - step
        return at(places if key[0] == 0 else -places)

    def piece(key, step):
        direction, part = key
        rows = pl.ds(part * half_rows, half_rows)
        return remote(
            p_ref.at[ahead(key, step), rows] if step == 0 else land.at[direction, part, step - 1],
            land.at[direction, part, step],
            send_sem.at[direction, part, step],
            recv_sem.at[direction, part, step],
            near[direction],
        )

    for step in range(steps + 1):
        for key in hops:
            direction, part = key
            rows = pl.ds(part * half_rows, half_rows)
            if 0 < step <= hops[key]:
                piece(key, step - 1).wait_recv()
                if step < hops[key]:
                    slot = land.at[direction, part, step - 1]
                    total = slot[...].astype(F32) + p_ref[ahead(key, step), rows].astype(F32)
                    slot[...] = total.astype(BF16)
            if step < hops[key]:
                piece(key, step).start()
    for part in range(2):
        rows = pl.ds(part * half_rows, half_rows)
        total = p_ref[chip, rows].astype(F32)
        for direction in range(2):
            total = total + land[direction, part, hops[direction, part] - 1].astype(F32)
        o_ref[rows, :] = total
    for step in range(steps):
        for key in hops:
            if step < hops[key]:
                piece(key, step).wait_send()
    for ride in rides:
        ride.wait()


def ring_scatter(count, partial, rides=()):
    _, rows, width = partial.shape
    steps = count // 2
    axes = tuple(axis for _, axis in rides)
    passengers = [array for array, _ in rides]
    away = [pl.BlockSpec(memory_space=pl.ANY)] * len(rides)
    here = [pl.BlockSpec(memory_space=pltpu.VMEM)]
    dma = pltpu.SemaphoreType.DMA
    return pl.pallas_call(
        functools.partial(scatter_kernel, count, axes),
        out_shape=(jax.ShapeDtypeStruct((rows, width), F32),)
        + tuple(shape_of(a) for a in passengers),
        in_specs=here + away,
        out_specs=here + away,
        scratch_shapes=[
            pltpu.VMEM((2, 2, steps, rows // 2, width), partial.dtype),
            dma((2, 2, steps)),
            dma((2, 2, steps)),
            dma((max(len(rides), 1),)),
            dma((max(len(rides), 1),)),
        ],
        compiler_params=pltpu.CompilerParams(
            collective_id=identity("scatter", axes, *(a.shape for a in passengers)),
            has_side_effects=True,
            vmem_limit_bytes=24 << 20,
        ),
        name="ring_scatter",
    )(partial, *passengers)


def setup_kernel(
    count, slab_ref, out_w_ref, small_ref, table_ref,
    heads_ref, outs_ref, smalls_ref, tables_ref,
    own_sem, slab_send, slab_recv, pass_send, pass_recv,
    small_send, small_recv, table_send, table_recv, out_send, out_recv,
):
    devices = 2 * count
    me = lax.axis_index("fsdp")
    chip, core = me // 2, lax.rem(me, 2)
    layers = slab_ref.shape[1]

    def device(offset):
        return {"fsdp": lax.rem(me + offset, devices)}

    def chip_at(offset):
        return lax.rem(chip + offset + count, count)

    partner = partner_of("fsdp")
    meet([device(offset) for offset in range(1, devices)])
    copies = [
        pltpu.make_async_copy(slab_ref.at[chip, layer], heads_ref.at[layer, me], own_sem.at[layer])
        for layer in range(layers)
    ] + [
        pltpu.make_async_copy(small_ref, smalls_ref.at[me], own_sem.at[layers]),
        pltpu.make_async_copy(table_ref, tables_ref.at[chip], own_sem.at[layers + 1]),
        pltpu.make_async_copy(out_w_ref, outs_ref.at[core], own_sem.at[layers + 2]),
    ]
    sends = [
        remote(small_ref, smalls_ref.at[me], small_send.at[offset], small_recv.at[offset], device(offset))
        for offset in range(1, devices)
    ]
    for offset in range(1, count):
        there = {"fsdp": chip_at(offset) * 2 + core}
        sends.append(
            remote(table_ref, tables_ref.at[chip], table_send.at[offset], table_recv.at[offset], there)
        )
        for layer in range(layers):
            sends.append(
                remote(
                    slab_ref.at[chip_at(offset), layer], heads_ref.at[layer, me],
                    slab_send.at[offset, layer], slab_recv.at[offset, layer], there,
                )
            )
    for layer in range(layers):
        sends.append(
            remote(
                slab_ref.at[chip, layer], heads_ref.at[layer, me],
                pass_send.at[0, layer], pass_recv.at[0, layer], partner,
            )
        )
    sends.append(remote(out_w_ref, outs_ref.at[core], out_send.at[0], out_recv.at[0], partner))
    for copy in copies + sends:
        copy.start()
    for offset in range(1, count):
        origin = chip_at(-offset) * 2 + core
        for layer in range(layers):
            slot = heads_ref.at[layer, origin]
            remote(slot, slot, slab_send.at[offset, layer], slab_recv.at[offset, layer], partner).wait_recv()
            forward = remote(slot, slot, pass_send.at[offset, layer], pass_recv.at[offset, layer], partner)
            forward.start()
    for offset in range(1, count):
        origin = chip_at(-offset)
        table = tables_ref.at[origin]
        remote(table, table, table_send.at[offset], table_recv.at[offset], partner).wait_recv()
    for offset in range(count):
        origin = chip_at(-offset) * 2 + 1 - core
        mine = chip_at(-offset) * 2 + core
        for layer in range(layers):
            slot, sent = heads_ref.at[layer, origin], heads_ref.at[layer, mine]
            if offset > 0:
                remote(sent, sent, pass_send.at[offset, layer], pass_recv.at[offset, layer], partner).wait_send()
            remote(slot, slot, pass_send.at[offset, layer], pass_recv.at[offset, layer], partner).wait_recv()
    for offset in range(1, devices):
        slot = smalls_ref.at[lax.rem(me - offset + devices, devices)]
        remote(slot, slot, small_send.at[offset], small_recv.at[offset], partner).wait_recv()
    other = outs_ref.at[1 - core]
    remote(other, other, out_send.at[0], out_recv.at[0], partner).wait_recv()
    for copy in copies:
        copy.wait()
    for send in sends:
        send.wait_send()


def exchange_weights(count, slabs, out_w, small, table):
    layers = slabs.shape[1]
    devices = 2 * count
    dma = pltpu.SemaphoreType.DMA
    anywhere = pl.BlockSpec(memory_space=pl.ANY)
    return pl.pallas_call(
        functools.partial(setup_kernel, count),
        out_shape=(
            jax.ShapeDtypeStruct((layers, devices) + slabs.shape[2:], slabs.dtype),
            jax.ShapeDtypeStruct((2,) + out_w.shape, out_w.dtype),
            jax.ShapeDtypeStruct((devices,) + small.shape, small.dtype),
            jax.ShapeDtypeStruct((count,) + table.shape, table.dtype),
        ),
        in_specs=[anywhere] * 4,
        out_specs=[anywhere] * 4,
        scratch_shapes=[
            dma((layers + 3,)),
            dma((count, layers)),
            dma((count, layers)),
            dma((count, layers)),
            dma((count, layers)),
            dma((devices,)),
            dma((devices,)),
            dma((count,)),
            dma((count,)),
            dma((1,)),
            dma((1,)),
        ],
        compiler_params=pltpu.CompilerParams(
            collective_id=identity("setup"), has_side_effects=True
        ),
        name="exchange_weights",
    )(slabs, out_w, small, table)


def finish_kernel(
    count, replicas, g_ref, o_ref, land, total, mine, peer,
    pair_send, pair_recv, part_send, part_recv, rep_send, rep_recv,
):
    me = lax.axis_index("fsdp")
    chip, core = me // 2, lax.rem(me, 2)
    partner = partner_of("fsdp")

    def chip_at(offset):
        return lax.rem(chip + offset + count, count)

    def device(offset):
        return {"fsdp": chip_at(offset) * 2 + core}

    across = [partner_of("rep")] if replicas == 2 else []
    meet([device(offset) for offset in range(1, count)] + [partner] + across)
    swap = remote(g_ref.at[1 - core], land, pair_send.at[0], pair_recv.at[0], partner)
    swap.start()
    swap.wait()
    for block in range(count):
        total[block] = (g_ref[core, block].astype(F32) + land[block].astype(F32)).astype(BF16)
    sends = [
        remote(
            total.at[chip_at(offset)], mine.at[chip],
            part_send.at[offset], part_recv.at[offset], device(offset),
        )
        for offset in range(1, count)
    ]
    for send in sends:
        send.start()
    mine[chip] = total[chip]

    def to_peer(offset):
        slot = chip_at(-offset)
        return remote(mine.at[slot], peer.at[slot], rep_send.at[offset], rep_recv.at[offset], across[0])

    for offset in range(count):
        if offset > 0:
            slot = mine.at[chip_at(-offset)]
            remote(slot, slot, part_send.at[offset], part_recv.at[offset], partner).wait_recv()
        if replicas == 2:
            to_peer(offset).start()
    for offset in range(count):
        slot = chip_at(-offset)
        if replicas == 2:
            to_peer(offset).wait()
            o_ref[slot] = mine[slot].astype(F32) + peer[slot].astype(F32)
        else:
            o_ref[slot] = mine[slot].astype(F32)
    for send in sends:
        send.wait_send()


def finish_heads(count, replicas, g):
    part = g.shape[1:]
    dma = pltpu.SemaphoreType.DMA
    here = pl.BlockSpec(memory_space=pltpu.VMEM)
    buffer = pltpu.VMEM(part, BF16)
    return pl.pallas_call(
        functools.partial(finish_kernel, count, replicas),
        out_shape=jax.ShapeDtypeStruct(part, F32),
        in_specs=[here],
        out_specs=here,
        scratch_shapes=[
            buffer, buffer, buffer, buffer,
            dma((1,)), dma((1,)), dma((count,)), dma((count,)), dma((count,)), dma((count,)),
        ],
        compiler_params=pltpu.CompilerParams(
            collective_id=identity("finish"), has_side_effects=True, vmem_limit_bytes=24 << 20
        ),
        name="finish_heads",
    )(g)


def dot(left, right, contract=((1,), (0,))):
    return lax.dot_general(left, right, (contract, ((), ())), preferred_element_type=F32)


NT = ((1,), (1,))
TN = ((0,), (0,))


def lanes_of(field):
    return lax.broadcasted_iota(jnp.int32, field.shape, 1)


def turn(field):
    return pltpu.roll(field, HD, 1)


def spin(field, cosine, sine):
    swapped = jnp.where(
        lax.rem(lanes_of(field), HD) < HD // 2,
        -pltpu.roll(field, LANES - HD // 2, 1),
        pltpu.roll(field, HD // 2, 1),
    )
    return field * cosine + swapped * sine


def project_kernel(x_ref, w_ref, cos_ref, sin_ref, q_ref, kv_ref):
    rows = dot(x_ref[...], w_ref[...])
    cosine, sine = cos_ref[...], sin_ref[...]
    first = spin(rows[:, :LANES], cosine, sine)
    second = spin(rows[:, LANES : 2 * LANES], cosine, sine)
    third = rows[:, 2 * LANES :]
    low = lanes_of(first) < HD
    kv_ref[...] = jnp.where(low, turn(second), turn(third)).astype(BF16)
    for head, field in enumerate((first, turn(first), second)):
        rounded = jnp.where(low, field, 0.0).astype(BF16).astype(F32)
        scaled = (rounded * (HD**-0.5)).astype(BF16)
        for block in range(2):
            q_ref[block, head] = scaled[block * LANES : (block + 1) * LANES]


def project(x, w, cosine, sine):
    tokens, width = x.shape
    tile = 2 * LANES
    return pl.pallas_call(
        project_kernel,
        grid=(tokens // tile,),
        out_shape=(
            jax.ShapeDtypeStruct((tokens // LANES, GROUP, LANES, LANES), BF16),
            jax.ShapeDtypeStruct((tokens, LANES), BF16),
        ),
        in_specs=[
            pl.BlockSpec((tile, width), lambda i: (i, 0)),
            pl.BlockSpec(w.shape, lambda i: (0, 0)),
            pl.BlockSpec((tile, LANES), lambda i: (i, 0)),
            pl.BlockSpec((tile, LANES), lambda i: (i, 0)),
        ],
        out_specs=[
            pl.BlockSpec((2, GROUP, LANES, LANES), lambda i: (i, 0, 0, 0)),
            pl.BlockSpec((tile, LANES), lambda i: (i, 0)),
        ],
        name="project",
    )(x, w, cosine, sine)


def allowed_keys(begin, block, chunk, core):
    shape = (GROUP * LANES, 2 * LANES)
    place = lax.broadcasted_iota(jnp.int32, shape, 1)
    shift = jnp.where(place < LANES, core, -core)
    key = chunk * 2 * LANES + place + shift * LANES
    query = block * LANES + lax.rem(lax.broadcasted_iota(jnp.int32, shape, 0), LANES)
    return (key >= begin) & (key <= query)


def fill_out_weights(w_ref, wide_ref):
    rows = w_ref.shape[0]
    wide_ref[:rows] = w_ref[...]
    wide_ref[rows:] = jnp.zeros((wide_ref.shape[0] - rows, wide_ref.shape[1]), BF16)


def attend_kernel(info_ref, q_ref, own_ref, other_ref, begin_ref, w_ref, att_ref, lse_ref, out_ref, wide_ref):
    step = pl.program_id(0)
    core = info_ref[0]
    block = 2 * step + core
    first = info_ref[1 + step] // (2 * LANES)

    @pl.when(step == 0)
    def _():
        fill_out_weights(w_ref, wide_ref)

    q = q_ref[0].reshape(GROUP * LANES, LANES)
    begin = jnp.concatenate([begin_ref[0]] * GROUP, 0)

    def one(chunk, state):
        top, total, acc = state
        keys = jnp.concatenate([own_ref[chunk], other_ref[chunk]], 0)
        allowed = allowed_keys(begin, block, chunk, core)
        scores = jnp.where(allowed, dot(q, keys, NT), MASKED)
        new_top = jnp.maximum(top, jnp.max(scores, -1, keepdims=True))
        weights = jnp.where(allowed, jnp.exp(scores - new_top), 0.0)
        shrink = jnp.exp(top - new_top)
        total = total * shrink + jnp.sum(weights, -1, keepdims=True)
        return new_top, total, acc * shrink + dot(weights.astype(BF16), keys)

    rows = GROUP * LANES
    top, total, acc = lax.fori_loop(
        first,
        step + 1,
        one,
        (jnp.full((rows, 1), MASKED, F32), jnp.zeros((rows, 1), F32), jnp.zeros((rows, LANES), F32)),
    )
    lse_ref[0] = top + jnp.log(total)
    att = acc / total
    heads = [att[h * LANES : (h + 1) * LANES] for h in range(GROUP)]
    low = lanes_of(heads[0]) < HD
    wide = jnp.concatenate(
        [jnp.where(low, turn(heads[0]), heads[1]), jnp.where(low, turn(heads[2]), 0.0)], 1
    ).astype(BF16)
    att_ref[0] = wide
    out_ref[0] = dot(wide, wide_ref[...]).astype(BF16)


def attend(info, q, own, other, begin, w):
    blocks = q.shape[0]
    width = w.shape[1]
    wide = 2 * LANES
    return pl.pallas_call(
        attend_kernel,
        grid_spec=pltpu.PrefetchScalarGridSpec(
            num_scalar_prefetch=1,
            grid=(blocks,),
            in_specs=[
                pl.BlockSpec((1, GROUP, LANES, LANES), lambda i, s: (i, 0, 0, 0)),
                pl.BlockSpec(own.shape, lambda i, s: (0, 0, 0)),
                pl.BlockSpec(own.shape, lambda i, s: (0, 0, 0)),
                pl.BlockSpec((1, LANES, 1), lambda i, s: (i, 0, 0)),
                pl.BlockSpec(w.shape, lambda i, s: (0, 0)),
            ],
            out_specs=[
                pl.BlockSpec((1, LANES, wide), lambda i, s: (i, 0, 0)),
                pl.BlockSpec((1, GROUP * LANES, 1), lambda i, s: (i, 0, 0)),
                pl.BlockSpec((1, LANES, width), lambda i, s: (i, 0, 0)),
            ],
            scratch_shapes=[pltpu.VMEM((wide, width), BF16)],
        ),
        out_shape=(
            jax.ShapeDtypeStruct((blocks, LANES, wide), BF16),
            jax.ShapeDtypeStruct((blocks, GROUP * LANES, 1), F32),
            jax.ShapeDtypeStruct((blocks, LANES, width), BF16),
        ),
        name="attend",
    )(info, q, own, other, begin, w)


def attend_back_kernel(
    info_ref, q_ref, own_ref, other_ref, begin_ref, w_ref, att_ref, lse_ref, db_ref, cos_ref, sin_ref,
    dq_ref, d_own_ref, d_other_ref, wide_ref,
):
    step = pl.program_id(0)
    core = info_ref[0]
    block = 2 * step + core
    first = info_ref[1 + step] // (2 * LANES)

    @pl.when(step == 0)
    def _():
        fill_out_weights(w_ref, wide_ref)
        d_own_ref[...] = jnp.zeros_like(d_own_ref)
        d_other_ref[...] = jnp.zeros_like(d_other_ref)

    q = q_ref[0].reshape(GROUP * LANES, LANES)
    begin = jnp.concatenate([begin_ref[0]] * GROUP, 0)

    def spread(wide):
        front, back = wide[:, :LANES], wide[:, LANES:]
        low = lanes_of(front) < HD
        parts = [jnp.where(low, 0.0, part) for part in (turn(front), front, turn(back))]
        return jnp.concatenate(parts, 0)

    datt = spread(dot(db_ref[0], wide_ref[...], NT)).astype(BF16)
    att = spread(att_ref[0].astype(F32))
    delta = jnp.sum(datt.astype(F32) * att, -1, keepdims=True)
    lse = lse_ref[0]
    both = jnp.concatenate([q, datt], 0)

    def one(chunk, acc):
        keys = jnp.concatenate([own_ref[chunk], other_ref[chunk]], 0)
        allowed = allowed_keys(begin, block, chunk, core)
        weights = jnp.where(allowed, jnp.exp(dot(q, keys, NT) - lse), 0.0)
        slope = (weights * (dot(datt, keys, NT) - delta)).astype(BF16)
        d_keys = dot(jnp.concatenate([slope, weights.astype(BF16)], 0), both, TN)
        d_own_ref[chunk] += d_keys[:LANES]
        d_other_ref[chunk] += d_keys[LANES:]
        return acc + dot(slope, keys)

    acc = lax.fori_loop(first, step + 1, one, jnp.zeros((GROUP * LANES, LANES), F32))
    heads = [acc[h * LANES : (h + 1) * LANES] * (HD**-0.5) for h in range(GROUP)]
    low = lanes_of(heads[0]) < HD
    cosine, sine = cos_ref[0], -sin_ref[0]
    front = spin(jnp.where(low, heads[0], turn(heads[1])), cosine, sine)
    back = spin(jnp.where(low, heads[2], 0.0), cosine, sine)
    dq_ref[0] = jnp.concatenate([front, back], 1).astype(BF16)


def attend_back(info, q, own, other, begin, w, att, lse, db, cosine, sine):
    blocks = q.shape[0]
    width = w.shape[1]
    wide = 2 * LANES
    return pl.pallas_call(
        attend_back_kernel,
        grid_spec=pltpu.PrefetchScalarGridSpec(
            num_scalar_prefetch=1,
            grid=(blocks,),
            in_specs=[
                pl.BlockSpec((1, GROUP, LANES, LANES), lambda i, s: (i, 0, 0, 0)),
                pl.BlockSpec(own.shape, lambda i, s: (0, 0, 0)),
                pl.BlockSpec(own.shape, lambda i, s: (0, 0, 0)),
                pl.BlockSpec((1, LANES, 1), lambda i, s: (i, 0, 0)),
                pl.BlockSpec(w.shape, lambda i, s: (0, 0)),
                pl.BlockSpec((1, LANES, wide), lambda i, s: (i, 0, 0)),
                pl.BlockSpec((1, GROUP * LANES, 1), lambda i, s: (i, 0, 0)),
                pl.BlockSpec((1, LANES, width), lambda i, s: (i, 0, 0)),
                pl.BlockSpec((1, LANES, LANES), lambda i, s: (i, 0, 0)),
                pl.BlockSpec((1, LANES, LANES), lambda i, s: (i, 0, 0)),
            ],
            out_specs=[
                pl.BlockSpec((1, LANES, wide), lambda i, s: (i, 0, 0)),
                pl.BlockSpec(own.shape, lambda i, s: (0, 0, 0)),
                pl.BlockSpec(own.shape, lambda i, s: (0, 0, 0)),
            ],
            scratch_shapes=[pltpu.VMEM((wide, width), BF16)],
        ),
        out_shape=(
            jax.ShapeDtypeStruct((blocks, LANES, wide), BF16),
            jax.ShapeDtypeStruct(own.shape, F32),
            jax.ShapeDtypeStruct(own.shape, F32),
        ),
        name="attend_back",
    )(info, q, own, other, begin, w, att, lse, db, cosine, sine)


def join_kernel(dq_ref, own_ref, got_ref, cos_ref, sin_ref, w_ref, x_ref, out_ref, g_ref):
    pair = own_ref[...] + got_ref[...].astype(F32)
    front = spin(pair, cos_ref[...], -sin_ref[...])
    low = lanes_of(pair) < HD
    middle = jnp.where(low, dq_ref[:, LANES:].astype(F32), turn(front))
    last = jnp.where(low, turn(pair), 0.0)
    rows = jnp.concatenate([dq_ref[:, :LANES], middle.astype(BF16), last.astype(BF16)], 1)
    out_ref[...] = dot(rows, w_ref[...], NT).astype(BF16)
    part = dot(x_ref[...], rows, TN)

    @pl.when(pl.program_id(0) == 0)
    def _():
        g_ref[...] = part

    @pl.when(pl.program_id(0) > 0)
    def _():
        g_ref[...] += part


def join(dq, own, got, cosine, sine, w, x):
    tokens, width = x.shape
    tile = 2 * LANES

    def rows(columns):
        return pl.BlockSpec((tile, columns), lambda i: (i, 0))

    return pl.pallas_call(
        join_kernel,
        grid=(tokens // tile,),
        out_shape=(
            jax.ShapeDtypeStruct((tokens, width), BF16),
            jax.ShapeDtypeStruct(w.shape, F32),
        ),
        in_specs=[rows(2 * LANES), rows(LANES), rows(LANES), rows(LANES), rows(LANES),
                  pl.BlockSpec(w.shape, lambda i: (0, 0)), rows(width)],
        out_specs=[rows(width), pl.BlockSpec(w.shape, lambda i: (0, 0))],
        compiler_params=pltpu.CompilerParams(vmem_limit_bytes=40 << 20),
        name="join",
    )(dq, own, got, cosine, sine, w, x)


def mix_kernel(x_ref, share_ref, *refs):
    weights, out_ref = refs[:6], refs[6]
    x = x_ref[...]
    out = None
    for e in range(2):
        gate_w, up_w, down_w = weights[3 * e : 3 * e + 3]
        act_gate, act_up = dot(x, gate_w[...]), dot(x, up_w[...])
        hidden = jax.nn.silu(act_gate) * act_up * share_ref[:, e : e + 1]
        part = dot(hidden.astype(BF16), down_w[...])
        out = part if out is None else out + part
    out_ref[...] = out.astype(BF16)


def mix(x, share, weights):
    tokens, width = x.shape
    tile = 2 * LANES

    def rows(columns):
        return pl.BlockSpec((tile, columns), lambda i: (i, 0))

    return pl.pallas_call(
        mix_kernel,
        grid=(tokens // tile,),
        out_shape=jax.ShapeDtypeStruct((tokens, width), BF16),
        in_specs=[rows(width), rows(2)]
        + [pl.BlockSpec(w.shape, lambda i: (0, 0)) for w in weights],
        out_specs=rows(width),
        compiler_params=pltpu.CompilerParams(vmem_limit_bytes=50 << 20),
        name="mix",
    )(x, share, *weights)


def mix_back_kernel(x_ref, d_ref, share_ref, balance_ref, router_ref, *refs):
    weights = refs[:6]
    out_ref, logit_ref = refs[6:8]
    grads = refs[8:]
    x, d = x_ref[...], d_ref[...]
    out = None
    for e in range(2):
        gate_w, up_w, down_w = weights[3 * e : 3 * e + 3]
        share = share_ref[:, e : e + 1]
        act_gate, act_up = dot(x, gate_w[...]), dot(x, up_w[...])
        sig = jax.nn.sigmoid(act_gate)
        swish = act_gate * sig
        hidden = swish * act_up
        raw = dot(d, down_w[...], NT)
        d_logit = share * (jnp.sum(hidden * raw, -1, keepdims=True) - balance_ref[...])
        d_hidden = raw * share
        d_gate = (d_hidden * act_up * sig * (1.0 + act_gate * (1.0 - sig))).astype(BF16)
        d_up = (d_hidden * swish).astype(BF16)
        grads[3 * e][...] = d_gate
        grads[3 * e + 1][...] = d_up
        grads[3 * e + 2][...] = (hidden * share).astype(BF16)
        logit_ref[:, e : e + 1] = d_logit
        part = dot(d_gate, gate_w[...], NT) + dot(d_up, up_w[...], NT)
        part = part + d_logit * router_ref[e : e + 1, :]
        out = part if out is None else out + part
    out_ref[...] = out.astype(BF16)


def mix_back(x, d, share, balance, router, weights):
    tokens, width = x.shape
    ff = weights[0].shape[1]
    tile = 2 * LANES

    def rows(columns):
        return pl.BlockSpec((tile, columns), lambda i: (i, 0))

    return pl.pallas_call(
        mix_back_kernel,
        grid=(tokens // tile,),
        out_shape=(
            jax.ShapeDtypeStruct((tokens, width), BF16),
            jax.ShapeDtypeStruct((tokens, 2), F32),
        ) + (jax.ShapeDtypeStruct((tokens, ff), BF16),) * 6,
        in_specs=[rows(width), rows(width), rows(2), rows(1), pl.BlockSpec(router.shape, lambda i: (0, 0))]
        + [pl.BlockSpec(w.shape, lambda i: (0, 0)) for w in weights],
        out_specs=[rows(width), rows(2)] + [rows(ff)] * 6,
        compiler_params=pltpu.CompilerParams(vmem_limit_bytes=56 << 20),
        name="mix_back",
    )(x, d, share, balance, router, *weights)


def add_kernel(layers, *refs):
    o_ref = refs[-1]
    for layer in range(layers):
        own, got = refs[2 * layer], refs[2 * layer + 1]
        o_ref[layer, 0] = own[...].astype(F32) + got[...].astype(F32)


def add_layers(pairs):
    layers = len(pairs)
    rows, columns = pairs[0][0].shape
    tile = rows // 4
    flat = [array for pair in pairs for array in pair]
    return pl.pallas_call(
        functools.partial(add_kernel, layers),
        grid=(4,),
        out_shape=jax.ShapeDtypeStruct((layers, 1, rows, columns), F32),
        in_specs=[pl.BlockSpec((tile, columns), lambda i: (i, 0))] * len(flat),
        out_specs=pl.BlockSpec((layers, 1, tile, columns), lambda i: (0, 0, i, 0)),
        name="add_layers",
    )(*flat)


def on_device(
    tokens,
    cotangent,
    positions,
    segments,
    routes,
    attn_gain,
    w_query,
    w_key,
    w_value,
    w_out,
    ffn_gain,
    router,
    w_gate,
    w_up,
    w_down,
):
    rows, width = tokens.shape
    devices = lax.axis_size("fsdp")
    replicas = lax.axis_size("rep")
    count = devices // 2
    me = lax.axis_index("fsdp")
    chip, core = me // 2, lax.rem(me, 2)
    shard = w_query.shape[1]
    experts = devices
    columns = 3 * LANES
    used = (GROUP + 2) * HD
    pairs = [(index, index ^ 1) for index in range(devices)]

    def swap(array):
        return lax.ppermute(array, "fsdp", pairs)

    small = jnp.concatenate(
        [attn_gain, ffn_gain, router.transpose(0, 2, 1).reshape(LAYERS * experts, shard)], 0
    )
    small = jnp.pad(small, ((0, 48 - small.shape[0]), (0, LANES - shard)))
    rate = jnp.exp(-jnp.log(10000.0) * jnp.arange(HD // 2, dtype=F32) / (HD // 2))
    angle = rate[:, None] * positions.astype(F32)[None, :]
    table = jnp.concatenate([jnp.cos(angle), jnp.sin(angle)], 0)
    slabs = jnp.concatenate(
        [
            w_query.reshape(LAYERS, shard, count, GROUP * HD),
            w_key.reshape(LAYERS, shard, count, HD),
            w_value.reshape(LAYERS, shard, count, HD),
            jnp.zeros((LAYERS, shard, count, columns - used), BF16),
        ],
        -1,
    ).transpose(2, 0, 1, 3)
    heads_w, outs_w, smalls, tables = exchange_weights(count, slabs, w_out, small, table)
    heads_w = heads_w.reshape(LAYERS, width, columns)
    w_heads = [heads_w[layer] for layer in range(LAYERS)]
    w_outs = [outs_w[:, layer].reshape(2 * shard, width) for layer in range(LAYERS)]
    smalls = smalls[:, : (2 + experts) * LAYERS, :shard].transpose(1, 0, 2).reshape(-1, width)
    smalls = smalls.astype(F32)
    gains_one, gains_two = smalls[:LAYERS], smalls[LAYERS : 2 * LAYERS]
    routers = smalls[2 * LAYERS :].reshape(LAYERS, experts, width)
    tables = tables.transpose(0, 2, 1).reshape(count * rows, HD)
    cosine = jnp.concatenate([tables[:, : HD // 2]] * 4, 1)
    sine = jnp.concatenate([tables[:, HD // 2 :]] * 4, 1)
    experts_w = []
    for layer in range(LAYERS):
        own = [w_gate[layer, 0], w_up[layer, 0], w_down[layer, 0]]
        experts_w.append(own + [swap(w) for w in own])
    mine = [2 * chip + core, 2 * chip + 1 - core]

    flat = segments.reshape(1, -1)
    kinds = jnp.arange(8, dtype=jnp.int32)[:, None]
    starts = jnp.sum((flat < kinds).astype(jnp.int32), 1, keepdims=True)
    begin = jnp.sum(jnp.where(flat == kinds, starts, 0), 0).reshape(count, 2, rows)
    begin = lax.dynamic_index_in_dim(begin, core, 1, False)
    info = jnp.concatenate([core[None], begin[:, 0]]).astype(jnp.int32)
    begin = begin[:, :, None]

    hidden = tokens.astype(F32)
    saved = []

    def normal(values):
        inverse = lax.rsqrt(jnp.mean(values * values, -1, keepdims=True) + EPS)
        return inverse, values * inverse

    for layer in range(LAYERS):
        inverse_one, normed_one = normal(hidden)
        x_attn = (normed_one * gains_one[layer][None, :]).astype(BF16)
        (x_all,) = ring_gather(count, [x_attn])
        x_all = x_all.reshape(count * rows, width)
        query, kv = project(x_all, w_heads[layer], cosine, sine)
        kv = kv.reshape(count, rows, LANES)
        kv_other = swap(kv)
        att, lse, partial = attend(info, query, kv, kv_other, begin, w_outs[layer])
        (added,) = ring_scatter(count, partial)
        middle = hidden + added
        inverse_two, normed_two = normal(middle)
        x_moe = (normed_two * gains_two[layer][None, :]).astype(BF16)
        logits = dot(routers[layer].astype(BF16), x_moe, NT)
        named = jnp.any(
            jnp.arange(experts, dtype=jnp.int32)[:, None, None] == routes[layer].T[None, :, :], 1
        )
        share = jax.nn.softmax(jnp.where(named, logits, -jnp.inf), axis=0)
        m_all, share_all = ring_gather(count, [x_moe, share])
        m_all = m_all.reshape(count * rows, width)
        share = jnp.stack(
            [lax.dynamic_index_in_dim(share_all, e, 1, False).reshape(-1) for e in mine], 1
        )
        partial = mix(m_all, share, experts_w[layer])
        (mixed,) = ring_scatter(count, partial.reshape(count, rows, width))
        saved.append(
            (inverse_one, normed_one, x_all, query, kv, kv_other, att, lse)
            + (inverse_two, normed_two, m_all, share, mixed)
        )
        hidden = middle + mixed
    activations = hidden.astype(BF16)

    grad = cotangent.astype(F32)
    waiting = []
    own_sums = [[None] * 4 for _ in range(LAYERS)]
    peer_sums = [[None] * 4 for _ in range(LAYERS)]
    heads_sums = [None] * LAYERS

    def send(kernel, argument, rides=()):
        taken = []
        while replicas == 2 and waiting and (not taken or taken[-1][1] == 3):
            taken.append(waiting.pop(0))
        rides = list(rides)
        more = [(own_sums[layer][index], "rep") for layer, index in taken]
        results = kernel(count, argument, rides + more)
        for place, (layer, index) in enumerate(taken):
            peer_sums[layer][index] = results[len(results) - len(taken) + place]
        return results[: len(results) - len(taken)]

    def core_sum(own, got):
        return (own + got.astype(F32)).astype(BF16)

    for layer in reversed(range(LAYERS)):
        (inverse_one, normed_one, x_all, query, kv, kv_other, att, lse) = saved[layer][:8]
        (inverse_two, normed_two, m_all, share, mixed) = saved[layer][8:]
        d_mix = grad.astype(BF16)
        balance = jnp.sum(mixed * d_mix.astype(F32), -1)
        side = jnp.broadcast_to(balance[None, :], (experts, rows))
        d_all, balance = send(ring_gather, [d_mix, side])
        d_all = d_all.reshape(count * rows, width)
        balance = balance[:, 0, :].reshape(-1, 1)
        router_mine = jnp.concatenate(
            [lax.dynamic_slice_in_dim(routers[layer], e, 1, 0) for e in mine], 0
        )
        partial, d_logit, *d_acts = mix_back(
            m_all, d_all, share, balance, router_mine, experts_w[layer]
        )
        expert_grads = [
            [
                dot(m_all, d_acts[3 * e], TN),
                dot(m_all, d_acts[3 * e + 1], TN),
                dot(d_acts[3 * e + 2], d_all, TN),
            ]
            for e in range(2)
        ]
        g_router = jnp.dot(d_logit.T, m_all.astype(F32), precision=lax.Precision.HIGHEST)
        theirs = [g.astype(BF16) for g in expert_grads[1]]
        d_x, *got = send(
            ring_scatter, partial.reshape(count, rows, width), [(g, "fsdp") for g in theirs]
        )
        for index in range(3):
            own_sums[layer][index] = core_sum(expert_grads[0][index], got[index])
            waiting.append((layer, index))
        gain = gains_two[layer][None, :]
        d_norm = d_x * gain
        d_gain_two = jnp.sum(d_x * normed_two, 0)
        grad_mid = grad + inverse_two * (
            d_norm - normed_two * jnp.mean(d_norm * normed_two, -1, keepdims=True)
        )
        (b_all,) = send(ring_gather, [grad_mid.astype(BF16)])
        d_query, d_own, d_other = attend_back(
            info, query, kv, kv_other, begin, w_outs[layer], att, lse, b_all,
            cosine.reshape(count, rows, LANES), sine.reshape(count, rows, LANES),
        )
        g_out = dot(att.reshape(count * rows, 2 * LANES), b_all.reshape(count * rows, width), TN)
        g_out = g_out[: 2 * shard].reshape(2, shard, width)
        g_out_own = lax.dynamic_index_in_dim(g_out, core, 0, False)
        g_out_other = lax.dynamic_index_in_dim(g_out, 1 - core, 0, False)
        d_got = swap(d_other.astype(BF16))
        partial, g_heads = join(
            d_query.reshape(count * rows, 2 * LANES),
            d_own.reshape(count * rows, LANES),
            d_got.reshape(count * rows, LANES),
            cosine, sine, w_heads[layer], x_all,
        )
        own_sums[layer][3] = core_sum(g_out_own, swap(g_out_other.astype(BF16)))
        waiting.append((layer, 3))
        (d_x,) = send(ring_scatter, partial.reshape(count, rows, width))
        gain = gains_one[layer][None, :]
        d_norm = d_x * gain
        d_gain_one = jnp.sum(d_x * normed_one, 0)
        grad = grad_mid + inverse_one * (
            d_norm - normed_one * jnp.mean(d_norm * normed_one, -1, keepdims=True)
        )
        g_router = jnp.where(core == 0, g_router, g_router[::-1])
        extra = jnp.concatenate(
            [g_router, d_gain_one[None, :], d_gain_two[None, :]], 0
        ).T
        heads_sums[layer] = jnp.concatenate(
            [g_heads[:, :used], extra, jnp.zeros((width, columns - used - 4), F32)], 1
        ).astype(BF16).reshape(count, 2, shard, columns)
    heads_sums = jnp.stack(heads_sums, 2).transpose(1, 0, 2, 3, 4)
    total = finish_heads(count, replicas, heads_sums)
    for layer, index in waiting:
        if replicas == 2:
            peer_sums[layer][index] = lax.ppermute(own_sums[layer][index], "rep", [(0, 1), (1, 0)])
    if replicas == 2:
        g_gate, g_up, g_down, g_out = [
            add_layers([(own_sums[layer][index], peer_sums[layer][index]) for layer in range(LAYERS)])
            for index in range(4)
        ]
    else:
        total = lax.psum(total.astype(BF16), "rep").astype(F32)
        g_gate, g_up, g_down, g_out = [
            jnp.stack(
                [lax.psum(own_sums[layer][index], "rep").astype(F32) for layer in range(LAYERS)]
            )[:, None]
            for index in range(4)
        ]
    total = total.transpose(1, 2, 0, 3)

    def part(first, last):
        return total[..., first:last].reshape(LAYERS, shard, -1)

    key_edge = GROUP * HD
    gains = jnp.sum(total[..., used + 2 : used + 4], 2)
    return (
        activations,
        grad,
        gains[..., 0],
        part(0, key_edge),
        part(key_edge, key_edge + HD),
        part(key_edge + HD, used),
        g_out[:, 0],
        gains[..., 1],
        part(used, used + 2),
        g_gate,
        g_up,
        g_down,
    )


def solution(mesh):
    placed = (
        P(("rep", "fsdp"), None),
        P(("rep", "fsdp"), None),
        P(("rep", "fsdp")),
        P("rep", None),
        P(None, ("rep", "fsdp"), None),
        P(None, "fsdp"),
        P(None, "fsdp", None),
        P(None, "fsdp", None),
        P(None, "fsdp", None),
        P(None, "fsdp", None),
        P(None, "fsdp"),
        P(None, "fsdp", None),
        P(None, "fsdp", None, None),
        P(None, "fsdp", None, None),
        P(None, "fsdp", None, None),
    )
    return jax.shard_map(
        on_device,
        mesh=mesh,
        in_specs=placed,
        out_specs=(
            P(("rep", "fsdp"), None),
            P(("rep", "fsdp"), None),
            P(None, "fsdp"),
            P(None, "fsdp", None),
            P(None, "fsdp", None),
            P(None, "fsdp", None),
            P(None, "fsdp", None),
            P(None, "fsdp"),
            P(None, "fsdp", None),
            P(None, "fsdp", None, None),
            P(None, "fsdp", None, None),
            P(None, "fsdp", None, None),
        ),
        check_vma=False,
    )
```

```python
import functools

import jax
import jax.numpy as jnp
from jax import lax
from jax.experimental import pallas as pl
from jax.experimental.pallas import tpu as pltpu
from jax.sharding import PartitionSpec as P

HEADS = 24
KV_HEADS = 8
HD = 64
LAYERS = 2
GROUP = HEADS // KV_HEADS
LANES = 128
EPS = 1e-06
MASKED = -1e30
MESH = pl.DeviceIdType.MESH
F32 = jnp.float32
BF16 = jnp.bfloat16


def ring_place(chip, count):
    return lax.select(lax.rem(chip, 2) == 0, chip // 2, count - 1 - chip // 2)


def ring_chip(place, count):
    return lax.select(place < count // 2, 2 * place, 2 * (count - 1 - place) + 1)


def ring_setup(count):
    me = lax.axis_index("fsdp")
    chip, core = me // 2, lax.rem(me, 2)
    place = ring_place(chip, count)

    def at(offset):
        return ring_chip(lax.rem(place + offset + 2 * count, count), count)

    near = [{"fsdp": at(1) * 2 + core}, {"fsdp": at(-1) * 2 + core}]
    return chip, at, near


def partner_of(axis):
    if axis == "rep":
        return {"rep": 1 - lax.axis_index("rep")}
    me = lax.axis_index("fsdp")
    return {"fsdp": me + 1 - 2 * lax.rem(me, 2)}


def meet(others):
    barrier = pltpu.get_barrier_semaphore()
    for other in others:
        pl.semaphore_signal(barrier, inc=1, device_id=other, device_id_type=MESH)
    pl.semaphore_wait(barrier, len(others))


def remote(src, dst, send_sem, recv_sem, device):
    return pltpu.make_async_remote_copy(
        src_ref=src,
        dst_ref=dst,
        send_sem=send_sem,
        recv_sem=recv_sem,
        device_id=device,
        device_id_type=MESH,
    )


def ring_hops(count):
    half = count // 2
    return {(0, 0): half, (1, 1): half, (0, 1): half - 1, (1, 0): half - 1}


IDENTITIES = {}


def identity(*key):
    return IDENTITIES.setdefault(key, len(IDENTITIES))


def shape_of(array):
    return jax.ShapeDtypeStruct(array.shape, array.dtype)


class Ring:
    def __init__(self, count, rides=()):
        self.count = count
        self.steps = count // 2
        self.chip, self.at, self.near = ring_setup(count)
        self.rides = rides

    def meet(self, axes):
        meet(self.near + [partner_of(axis) for axis in sorted(set(axes))])

    def gather(self, x_ref, buf, sems, side=None, first=None, second=None):
        own_sem, send_sem, recv_sem = sems[:3]
        half_rows = x_ref.shape[0] // 2
        steps = self.steps
        own = [pltpu.make_async_copy(x_ref, buf.at[self.chip], own_sem.at[0])]
        if side is not None:
            side_ref, side_buf = side
            side_send, side_recv = sems[3:]
            own.append(pltpu.make_async_copy(side_ref, side_buf.at[self.chip], own_sem.at[1]))
        for copy in own:
            copy.start()

        def piece(key, step, block, source=None):
            direction, part = key
            rows = pl.ds(part * half_rows, half_rows)
            target = buf.at[block, rows]
            return remote(
                target if source is None else source.at[rows],
                target,
                send_sem.at[direction, part, step],
                recv_sem.at[direction, part, step],
                self.near[direction],
            )

        def side_piece(direction, step, block, source=None):
            target = side_buf.at[block]
            return remote(
                target if source is None else source,
                target,
                side_send.at[direction, step],
                side_recv.at[direction, step],
                self.near[direction],
            )

        def toward(key, places):
            return self.at(-places if key[0] == 0 else places)

        early, late = [(0, 0), (1, 1)], [(0, 1), (1, 0)]
        if side is not None:
            for direction in range(2):
                side_piece(direction, 0, self.chip, side_ref).start()
        for key in early + late:
            piece(key, 0, self.chip, x_ref).start()

        def step(s, carry):
            if side is not None:
                for direction in range(2):

                    @pl.when(s <= steps - direction)
                    def _():
                        block = toward((direction, 0), s)
                        side_piece(direction, s - 1, block).wait_recv()

                        @pl.when(s < steps - direction)
                        def _():
                            side_piece(direction, s, block).start()

            for key in early:
                block = toward(key, s)
                piece(key, s - 1, block).wait_recv()

                @pl.when(s < steps)
                def _():
                    piece(key, s, block).start()

            if first is not None:
                first(s)

            @pl.when(s < steps)
            def _():
                for key in late:
                    block = toward(key, s)
                    piece(key, s - 1, block).wait_recv()

                    @pl.when(s < steps - 1)
                    def _():
                        piece(key, s, block).start()

            if second is not None:
                second(s)
            return carry

        for copy in own:
            copy.wait()
        lax.fori_loop(1, steps + 1, step, 0)

        def drain():
            for s in range(steps):
                for key in early + (late if s < steps - 1 else []):
                    piece(key, s, toward(key, s)).wait_send()
                if side is not None:
                    for direction in range(2):
                        if s < steps - direction:
                            side_piece(direction, s, toward((direction, 0), s)).wait_send()

        return drain

    def pair(self, s):
        return self.at(s), self.at(lax.select(s < self.steps, -s, 0))

    def scatter(self, partial, land, out_ref, sems, work=None):
        send_sem, recv_sem = sems
        half_rows = out_ref.shape[0] // 2
        steps = self.steps
        hops = ring_hops(self.count)

        def ahead(key, s):
            places = hops[key] - s
            return self.at(places if key[0] == 0 else -places)

        def piece(key, s, source):
            direction, part = key
            return remote(
                source,
                land.at[direction, part, s],
                send_sem.at[direction, part, s],
                recv_sem.at[direction, part, s],
                self.near[direction],
            )

        def rows_of(key):
            return pl.ds(key[1] * half_rows, half_rows)

        for key in hops:
            piece(key, 0, partial.at[ahead(key, 0), rows_of(key)]).start()

        def step(s, carry):
            for place, key in enumerate(hops):
                if work is not None:
                    work(s - 1, place)

                @pl.when(s < hops[key])
                def _():
                    slot = land.at[key[0], key[1], s - 1]
                    piece(key, s - 1, slot).wait_recv()
                    mine = partial[ahead(key, s), rows_of(key)]
                    slot[...] = (slot[...].astype(F32) + mine.astype(F32)).astype(BF16)
                    piece(key, s, slot).start()

            return carry

        lax.fori_loop(1, steps + 1, step, 0)
        for key in hops:
            slot = land.at[key[0], key[1], hops[key] - 1]
            piece(key, hops[key] - 1, slot).wait_recv()
        for part in range(2):
            rows = pl.ds(part * half_rows, half_rows)
            total = partial[self.chip, rows].astype(F32)
            for direction in range(2):
                total = total + land[direction, part, hops[direction, part] - 1].astype(F32)
            out_ref[rows, :] = total

        def drain():
            for key in hops:
                for s in range(hops[key]):
                    piece(key, s, land.at[key[0], key[1], s]).wait_send()

        return drain


def start_rides(axes, sources, targets, sems):
    send_sem, recv_sem = sems
    rides = [
        remote(sources[i], targets[i], send_sem.at[i], recv_sem.at[i], partner_of(axis))
        for i, axis in enumerate(axes)
    ]
    for ride in rides:
        ride.start()
    return rides


def dmas(*shapes):
    return [pltpu.SemaphoreType.DMA(shape) for shape in shapes]


def gather_sems(count, sided=False):
    steps = count // 2
    shapes = [(2,), (2, 2, steps), (2, 2, steps)]
    return dmas(*(shapes + ([(2, steps), (2, steps)] if sided else [])))


def scatter_sems(count):
    return dmas((2, 2, count // 2), (2, 2, count // 2))


def ride_sems(rides):
    return dmas((max(len(rides), 1),), (max(len(rides), 1),))


ANYWHERE = pl.BlockSpec(memory_space=pl.ANY)
HERE = pl.BlockSpec(memory_space=pltpu.VMEM)


def ring_call(body, name, here, inputs, outputs, scratch, rides, megabytes):
    axes = tuple(axis for _, axis in rides)
    passengers = [array for array, _ in rides]
    arrays = [array for array, _ in inputs]
    return pl.pallas_call(
        functools.partial(body, axes),
        out_shape=tuple(shape for shape, _ in outputs) + tuple(shape_of(a) for a in passengers),
        in_specs=[spec for _, spec in inputs] + [ANYWHERE] * len(rides),
        out_specs=[spec for _, spec in outputs] + [ANYWHERE] * len(rides),
        scratch_shapes=list(scratch) + ride_sems(rides),
        compiler_params=pltpu.CompilerParams(
            collective_id=identity(name, here, axes, *(a.shape for a in passengers)),
            has_side_effects=True,
            vmem_limit_bytes=megabytes << 20,
        ),
        name=name,
    )(*arrays, *passengers)


def split(refs, *sizes):
    parts, place = [], 0
    for size in sizes:
        parts.append(refs[place : place + size])
        place += size
    return parts + [refs[place:]]


def cells(shape, dtype):
    return jax.ShapeDtypeStruct(shape, dtype)


def scatter_kernel(count, axes, *refs):
    riders = len(axes)
    p_ref, ride_in, o_ref, ride_out = refs[0], refs[1 : 1 + riders], refs[1 + riders], refs[2 + riders : 2 + 2 * riders]
    land, send_sem, recv_sem, ride_send, ride_recv = refs[2 + 2 * riders :]
    chip, at, near = ring_setup(count)
    half_rows = o_ref.shape[0] // 2
    hops = ring_hops(count)
    steps = count // 2
    meet(near + [partner_of(axis) for axis in sorted(set(axes))])
    rides = [
        remote(ride_in[i], ride_out[i], ride_send.at[i], ride_recv.at[i], partner_of(axes[i]))
        for i in range(riders)
    ]
    for ride in rides:
        ride.start()

    def ahead(key, step):
        places = hops[key] - step
        return at(places if key[0] == 0 else -places)

    def piece(key, step):
        direction, part = key
        rows = pl.ds(part * half_rows, half_rows)
        return remote(
            p_ref.at[ahead(key, step), rows] if step == 0 else land.at[direction, part, step - 1],
            land.at[direction, part, step],
            send_sem.at[direction, part, step],
            recv_sem.at[direction, part, step],
            near[direction],
        )

    for step in range(steps + 1):
        for key in hops:
            direction, part = key
            rows = pl.ds(part * half_rows, half_rows)
            if 0 < step <= hops[key]:
                piece(key, step - 1).wait_recv()
                if step < hops[key]:
                    slot = land.at[direction, part, step - 1]
                    total = slot[...].astype(F32) + p_ref[ahead(key, step), rows].astype(F32)
                    slot[...] = total.astype(BF16)
            if step < hops[key]:
                piece(key, step).start()
    for part in range(2):
        rows = pl.ds(part * half_rows, half_rows)
        total = p_ref[chip, rows].astype(F32)
        for direction in range(2):
            total = total + land[direction, part, hops[direction, part] - 1].astype(F32)
        o_ref[rows, :] = total
    for step in range(steps):
        for key in hops:
            if step < hops[key]:
                piece(key, step).wait_send()
    for ride in rides:
        ride.wait()


def ring_scatter(count, partial, rides=()):
    _, rows, width = partial.shape
    steps = count // 2
    axes = tuple(axis for _, axis in rides)
    passengers = [array for array, _ in rides]
    away = [pl.BlockSpec(memory_space=pl.ANY)] * len(rides)
    here = [pl.BlockSpec(memory_space=pltpu.VMEM)]
    dma = pltpu.SemaphoreType.DMA
    return pl.pallas_call(
        functools.partial(scatter_kernel, count, axes),
        out_shape=(jax.ShapeDtypeStruct((rows, width), F32),)
        + tuple(shape_of(a) for a in passengers),
        in_specs=here + away,
        out_specs=here + away,
        scratch_shapes=[
            pltpu.VMEM((2, 2, steps, rows // 2, width), partial.dtype),
            dma((2, 2, steps)),
            dma((2, 2, steps)),
            dma((max(len(rides), 1),)),
            dma((max(len(rides), 1),)),
        ],
        compiler_params=pltpu.CompilerParams(
            collective_id=identity("scatter", axes, *(a.shape for a in passengers)),
            has_side_effects=True,
            vmem_limit_bytes=24 << 20,
        ),
        name="ring_scatter",
    )(partial, *passengers)


def setup_kernel(
    count, slab_ref, out_w_ref, small_ref, table_ref,
    heads_ref, outs_ref, smalls_ref, tables_ref,
    own_sem, slab_send, slab_recv, pass_send, pass_recv,
    small_send, small_recv, table_send, table_recv, out_send, out_recv,
):
    devices = 2 * count
    me = lax.axis_index("fsdp")
    chip, core = me // 2, lax.rem(me, 2)
    layers = slab_ref.shape[1]

    def device(offset):
        return {"fsdp": lax.rem(me + offset, devices)}

    def chip_at(offset):
        return lax.rem(chip + offset + count, count)

    partner = partner_of("fsdp")
    meet([device(offset) for offset in range(1, devices)])
    copies = [
        pltpu.make_async_copy(slab_ref.at[chip, layer], heads_ref.at[layer, me], own_sem.at[layer])
        for layer in range(layers)
    ] + [
        pltpu.make_async_copy(small_ref, smalls_ref.at[me], own_sem.at[layers]),
        pltpu.make_async_copy(table_ref, tables_ref.at[chip], own_sem.at[layers + 1]),
        pltpu.make_async_copy(out_w_ref, outs_ref.at[core], own_sem.at[layers + 2]),
    ]
    sends = [
        remote(small_ref, smalls_ref.at[me], small_send.at[offset], small_recv.at[offset], device(offset))
        for offset in range(1, devices)
    ]
    for offset in range(1, count):
        there = {"fsdp": chip_at(offset) * 2 + core}
        sends.append(
            remote(table_ref, tables_ref.at[chip], table_send.at[offset], table_recv.at[offset], there)
        )
        for layer in range(layers):
            sends.append(
                remote(
                    slab_ref.at[chip_at(offset), layer], heads_ref.at[layer, me],
                    slab_send.at[offset, layer], slab_recv.at[offset, layer], there,
                )
            )
    for layer in range(layers):
        sends.append(
            remote(
                slab_ref.at[chip, layer], heads_ref.at[layer, me],
                pass_send.at[0, layer], pass_recv.at[0, layer], partner,
            )
        )
    sends.append(remote(out_w_ref, outs_ref.at[core], out_send.at[0], out_recv.at[0], partner))
    for copy in copies + sends:
        copy.start()
    for offset in range(1, count):
        origin = chip_at(-offset) * 2 + core
        for layer in range(layers):
            slot = heads_ref.at[layer, origin]
            remote(slot, slot, slab_send.at[offset, layer], slab_recv.at[offset, layer], partner).wait_recv()
            forward = remote(slot, slot, pass_send.at[offset, layer], pass_recv.at[offset, layer], partner)
            forward.start()
    for offset in range(1, count):
        origin = chip_at(-offset)
        table = tables_ref.at[origin]
        remote(table, table, table_send.at[offset], table_recv.at[offset], partner).wait_recv()
    for offset in range(count):
        origin = chip_at(-offset) * 2 + 1 - core
        mine = chip_at(-offset) * 2 + core
        for layer in range(layers):
            slot, sent = heads_ref.at[layer, origin], heads_ref.at[layer, mine]
            if offset > 0:
                remote(sent, sent, pass_send.at[offset, layer], pass_recv.at[offset, layer], partner).wait_send()
            remote(slot, slot, pass_send.at[offset, layer], pass_recv.at[offset, layer], partner).wait_recv()
    for offset in range(1, devices):
        slot = smalls_ref.at[lax.rem(me - offset + devices, devices)]
        remote(slot, slot, small_send.at[offset], small_recv.at[offset], partner).wait_recv()
    other = outs_ref.at[1 - core]
    remote(other, other, out_send.at[0], out_recv.at[0], partner).wait_recv()
    for copy in copies:
        copy.wait()
    for send in sends:
        send.wait_send()


def exchange_weights(count, slabs, out_w, small, table):
    layers = slabs.shape[1]
    devices = 2 * count
    dma = pltpu.SemaphoreType.DMA
    anywhere = pl.BlockSpec(memory_space=pl.ANY)
    return pl.pallas_call(
        functools.partial(setup_kernel, count),
        out_shape=(
            jax.ShapeDtypeStruct((layers, devices) + slabs.shape[2:], slabs.dtype),
            jax.ShapeDtypeStruct((2,) + out_w.shape, out_w.dtype),
            jax.ShapeDtypeStruct((devices,) + small.shape, small.dtype),
            jax.ShapeDtypeStruct((count,) + table.shape, table.dtype),
        ),
        in_specs=[anywhere] * 4,
        out_specs=[anywhere] * 4,
        scratch_shapes=[
            dma((layers + 3,)),
            dma((count, layers)),
            dma((count, layers)),
            dma((count, layers)),
            dma((count, layers)),
            dma((devices,)),
            dma((devices,)),
            dma((count,)),
            dma((count,)),
            dma((1,)),
            dma((1,)),
        ],
        compiler_params=pltpu.CompilerParams(
            collective_id=identity("setup"), has_side_effects=True
        ),
        name="exchange_weights",
    )(slabs, out_w, small, table)


def finish_kernel(
    count, replicas, g_ref, o_ref, land, total, mine, peer,
    pair_send, pair_recv, part_send, part_recv, rep_send, rep_recv,
):
    me = lax.axis_index("fsdp")
    chip, core = me // 2, lax.rem(me, 2)
    partner = partner_of("fsdp")

    def chip_at(offset):
        return lax.rem(chip + offset + count, count)

    def device(offset):
        return {"fsdp": chip_at(offset) * 2 + core}

    across = [partner_of("rep")] if replicas == 2 else []
    meet([device(offset) for offset in range(1, count)] + [partner] + across)
    swap = remote(g_ref.at[1 - core], land, pair_send.at[0], pair_recv.at[0], partner)
    swap.start()
    swap.wait()
    for block in range(count):
        total[block] = (g_ref[core, block].astype(F32) + land[block].astype(F32)).astype(BF16)
    sends = [
        remote(
            total.at[chip_at(offset)], mine.at[chip],
            part_send.at[offset], part_recv.at[offset], device(offset),
        )
        for offset in range(1, count)
    ]
    for send in sends:
        send.start()
    mine[chip] = total[chip]

    def to_peer(offset):
        slot = chip_at(-offset)
        return remote(mine.at[slot], peer.at[slot], rep_send.at[offset], rep_recv.at[offset], across[0])

    for offset in range(count):
        if offset > 0:
            slot = mine.at[chip_at(-offset)]
            remote(slot, slot, part_send.at[offset], part_recv.at[offset], partner).wait_recv()
        if replicas == 2:
            to_peer(offset).start()
    for offset in range(count):
        slot = chip_at(-offset)
        if replicas == 2:
            to_peer(offset).wait()
            o_ref[slot] = mine[slot].astype(F32) + peer[slot].astype(F32)
        else:
            o_ref[slot] = mine[slot].astype(F32)
    for send in sends:
        send.wait_send()


def finish_heads(count, replicas, g):
    part = g.shape[1:]
    dma = pltpu.SemaphoreType.DMA
    here = pl.BlockSpec(memory_space=pltpu.VMEM)
    buffer = pltpu.VMEM(part, BF16)
    return pl.pallas_call(
        functools.partial(finish_kernel, count, replicas),
        out_shape=jax.ShapeDtypeStruct(part, F32),
        in_specs=[here],
        out_specs=here,
        scratch_shapes=[
            buffer, buffer, buffer, buffer,
            dma((1,)), dma((1,)), dma((count,)), dma((count,)), dma((count,)), dma((count,)),
        ],
        compiler_params=pltpu.CompilerParams(
            collective_id=identity("finish"), has_side_effects=True, vmem_limit_bytes=24 << 20
        ),
        name="finish_heads",
    )(g)


def dot(left, right, contract=((1,), (0,))):
    return lax.dot_general(left, right, (contract, ((), ())), preferred_element_type=F32)


NT = ((1,), (1,))
TN = ((0,), (0,))


def lanes_of(field):
    return lax.broadcasted_iota(jnp.int32, field.shape, 1)


def turn(field):
    return pltpu.roll(field, HD, 1)


def spin(field, cosine, sine):
    swapped = jnp.where(
        lax.rem(lanes_of(field), HD) < HD // 2,
        -pltpu.roll(field, LANES - HD // 2, 1),
        pltpu.roll(field, HD // 2, 1),
    )
    return field * cosine + swapped * sine


def project_rows(rows, cosine, sine):
    first = spin(rows[:, :LANES], cosine, sine)
    second = spin(rows[:, LANES : 2 * LANES], cosine, sine)
    third = rows[:, 2 * LANES :]
    low = lanes_of(first) < HD
    heads = []
    for field in (first, turn(first), second):
        rounded = jnp.where(low, field, 0.0).astype(BF16).astype(F32)
        heads.append((rounded * (HD**-0.5)).astype(BF16))
    return heads, jnp.where(low, turn(second), turn(third)).astype(BF16)


def project_kernel(count, axes, *refs):
    inputs, ride_in, outputs, ride_out, scratch = split(refs, 4, len(axes), 4, len(axes))
    x_ref, w_ref, cos_ref, sin_ref = inputs
    q_ref, own_ref, other_ref, all_ref = outputs
    buf, sems, pair_sems, out_sem, ride_sem = scratch[0], scratch[1:4], scratch[4:6], scratch[6], scratch[7:]
    ring = Ring(count)
    ring.meet(axes + ("fsdp",))
    rides = start_rides(axes, ride_in, ride_out, ride_sem)
    partner = partner_of("fsdp")

    def pass_on(block):
        return remote(
            own_ref.at[block], other_ref.at[block], pair_sems[0].at[block], pair_sems[1].at[block], partner
        )

    def compute(s):
        blocks = ring.pair(s)
        rows = dot(jnp.concatenate([buf[b] for b in blocks], 0), w_ref[...])
        cosine = jnp.concatenate([cos_ref[b] for b in blocks], 0)
        sine = jnp.concatenate([sin_ref[b] for b in blocks], 0)
        heads, pair = project_rows(rows, cosine, sine)
        for place, block in enumerate(blocks):
            here = slice(place * LANES, (place + 1) * LANES)
            for head in range(GROUP):
                q_ref[block, head] = heads[head][here]
            own_ref[block] = pair[here]
            pass_on(block).start()

    def second(s):
        @pl.when(s >= 2)
        def _():
            compute(s - 1)

    drain = ring.gather(x_ref, buf, sems, None, None, second)
    keep = pltpu.make_async_copy(buf, all_ref, out_sem.at[0])
    keep.start()
    compute(ring.steps)
    drain()
    for block in range(count):
        pass_on(block).wait()
    keep.wait()
    for ride in rides:
        ride.wait()


def gather_project(count, x, w, cosine, sine, rides=()):
    rows, width = x.shape
    block = cells((count, rows, LANES), BF16)
    return ring_call(
        functools.partial(project_kernel, count),
        "project",
        0,
        [(x, ANYWHERE), (w, HERE), (cosine, HERE), (sine, HERE)],
        [
            (cells((count, GROUP, rows, LANES), BF16), HERE),
            (block, HERE),
            (block, HERE),
            (cells((count, rows, width), BF16), ANYWHERE),
        ],
        [pltpu.VMEM((count, rows, width), BF16)] + gather_sems(count) + dmas((count,), (count,), (1,)),
        rides,
        40,
    )


def column(table, block, row):
    line = table[block, pl.ds(row, 1), :]
    shape = (LANES, LANES)
    same = lax.broadcasted_iota(jnp.int32, shape, 0) == lax.broadcasted_iota(jnp.int32, shape, 1)
    return jnp.sum(jnp.where(same, jnp.broadcast_to(line, shape), 0.0), 1, keepdims=True)


def load_experts(refs, gates, ups, downs, sem):
    copies = []
    for e in range(2):
        for place, buf in enumerate((gates, ups, downs)):
            copies.append(pltpu.make_async_copy(refs[3 * e + place], buf.at[e], sem.at[3 * e + place]))
    for copy in copies:
        copy.start()
    return copies


def expert_rows(e):
    me = lax.axis_index("fsdp")
    return me if e == 0 else me + 1 - 2 * lax.rem(me, 2)


def mix_kernel(count, axes, *refs):
    inputs, ride_in, outputs, ride_out, scratch = split(refs, 8, len(axes), 3, len(axes))
    x_ref, side_ref = inputs[:2]
    out_ref, all_ref, share_ref = outputs
    buf, partial, land, acc, gates, ups, downs = scratch[:7]
    sems, scatter_sem, load_sem, out_sem, ride_sem = split(scratch[7:], 5, 2, 1, 1)
    ring = Ring(count)
    ring.meet(axes)
    rides = start_rides(axes, ride_in, ride_out, ride_sem)
    loads = load_experts(inputs[2:], gates, ups, downs, load_sem[0])

    def compute(e, s):
        blocks = ring.pair(s)
        x = jnp.concatenate([buf[b] for b in blocks], 0)
        act_gate, act_up = dot(x, gates[e]), dot(x, ups[e])
        share = jnp.concatenate([column(share_ref, b, expert_rows(e)) for b in blocks], 0)
        hidden = jax.nn.silu(act_gate) * act_up * share
        part = dot(hidden.astype(BF16), downs[e])
        if e == 0:
            acc[...] = part
        else:
            total = (acc[...] + part).astype(BF16)
            for place, block in enumerate(blocks):
                partial[block] = total[place * LANES : (place + 1) * LANES]

    def at_step(e):
        def run(s):
            @pl.when(s >= 2)
            def _():
                compute(e, s - 1)

        return run

    for load in loads:
        load.wait()
    drain = ring.gather(x_ref, buf, sems, (side_ref, share_ref), at_step(0), at_step(1))
    keep = pltpu.make_async_copy(buf, all_ref, out_sem[0].at[0])
    keep.start()
    compute(0, ring.steps)
    compute(1, ring.steps)
    finish = ring.scatter(partial, land, out_ref, scatter_sem)
    drain()
    finish()
    keep.wait()
    for ride in rides:
        ride.wait()


def expert_scratch(weights):
    return [pltpu.VMEM((2,) + w.shape, BF16) for w in weights[:3]]


def land_scratch(count, rows, width):
    return pltpu.VMEM((2, 2, count // 2, rows // 2, width), BF16)


def gather_mix_scatter(count, x, share, weights, rides=()):
    rows, width = x.shape
    everyone = pltpu.VMEM((count, rows, width), BF16)
    return ring_call(
        functools.partial(mix_kernel, count),
        "mix",
        0,
        [(x, ANYWHERE), (share, ANYWHERE)] + [(w, ANYWHERE) for w in weights],
        [
            (cells((rows, width), F32), HERE),
            (cells((count, rows, width), BF16), ANYWHERE),
            (cells((count,) + share.shape, F32), HERE),
        ],
        [everyone, everyone, land_scratch(count, rows, width), pltpu.VMEM((2 * rows, width), F32)]
        + expert_scratch(weights)
        + gather_sems(count, True)
        + scatter_sems(count)
        + dmas((6,), (1,)),
        rides,
        56,
    )


def mix_back_kernel(count, axes, *refs):
    inputs, ride_in, outputs, ride_out, scratch = split(refs, 11, len(axes), 5, len(axes))
    d_ref, side_ref, m_ref, share_ref, router_ref = inputs[:5]
    out_ref, upper_ref, lower_ref, down_ref, g_router_ref = outputs
    buf, partial, land, acc, gates, ups, downs = scratch[:7]
    tokens, acts, hiddens, balance_ref, wide_sum, down_sum, wide_got, down_got = scratch[7:15]
    sems, scatter_sem, load_sem, pair_sem, out_sem, ride_sem = split(scratch[15:], 5, 2, 1, 2, 1)
    ring = Ring(count)
    ring.meet(axes + ("fsdp",))
    rides = start_rides(axes, ride_in, ride_out, ride_sem)
    loads = load_experts(inputs[5:], gates, ups, downs, load_sem[0])
    loads.append(pltpu.make_async_copy(m_ref, tokens, load_sem[0].at[6]))
    loads[-1].start()
    ff = gates.shape[2]
    g_router_ref[...] = jnp.zeros_like(g_router_ref)

    def compute(e, s):
        blocks = ring.pair(s)
        d = jnp.concatenate([buf[b] for b in blocks], 0)
        x = jnp.concatenate([tokens[b] for b in blocks], 0)
        share = jnp.concatenate([column(share_ref, b, expert_rows(e)) for b in blocks], 0)
        balance = jnp.concatenate([column(balance_ref, b, 0) for b in blocks], 0)
        act_gate, act_up = dot(x, gates[e]), dot(x, ups[e])
        sig = jax.nn.sigmoid(act_gate)
        swish = act_gate * sig
        hidden = swish * act_up
        raw = dot(d, downs[e], NT)
        d_logit = share * (jnp.sum(hidden * raw, -1, keepdims=True) - balance)
        d_hidden = raw * share
        d_gate = (d_hidden * act_up * sig * (1.0 + act_gate * (1.0 - sig))).astype(BF16)
        d_up = (d_hidden * swish).astype(BF16)
        weighted = (hidden * share).astype(BF16)
        part = dot(d_gate, gates[e], NT) + dot(d_up, ups[e], NT)
        part = part + d_logit * router_ref[e : e + 1, :]
        g_router_ref[e : e + 1, :] += jnp.sum(d_logit * x.astype(F32), 0, keepdims=True)
        for place, block in enumerate(blocks):
            here = slice(place * LANES, (place + 1) * LANES)
            acts[e, block, :, :ff] = d_gate[here]
            acts[e, block, :, ff:] = d_up[here]
            hiddens[e, block] = weighted[here]
        if e == 0:
            acc[...] = part
        else:
            total = (acc[...] + part).astype(BF16)
            for place, block in enumerate(blocks):
                partial[block] = total[place * LANES : (place + 1) * LANES]

    def at_step(e):
        def run(s):
            @pl.when(s >= 2)
            def _():
                compute(e, s - 1)

        return run

    for load in loads:
        load.wait()
    drain = ring.gather(d_ref, buf, sems, (side_ref, balance_ref), at_step(0), at_step(1))
    compute(0, ring.steps)
    compute(1, ring.steps)

    width = buf.shape[2]
    steps = ring.steps
    partner = partner_of("fsdp")
    strip = 2 * LANES
    strips = width // (2 * strip)

    def half_of(half):
        wide_rows = pl.ds(pl.multiple_of(half * (width // 2), strip), width // 2)
        down_rows = pl.ds(pl.multiple_of(half * (ff // 2), strip), ff // 2)
        return wide_rows, down_rows

    def swap(half):
        wide_rows, down_rows = half_of(half)
        return [
            remote(wide_sum.at[1, wide_rows], wide_got.at[wide_rows], pair_sem[0].at[0, half], pair_sem[1].at[0, half], partner),
            remote(down_sum.at[1, down_rows], down_got.at[down_rows], pair_sem[0].at[1, half], pair_sem[1].at[1, half], partner),
        ]

    def store(half):
        out = [upper_ref, lower_ref][half]
        wide_rows, down_rows = half_of(half)
        return [
            pltpu.make_async_copy(wide_sum.at[0, wide_rows], out, out_sem[0].at[2 * half]),
            pltpu.make_async_copy(down_sum.at[0, down_rows], down_ref.at[down_rows], out_sem[0].at[2 * half + 1]),
        ]

    def flat(value):
        return value.reshape(value.shape[0] * value.shape[1], value.shape[2])

    def work(s, place):
        e = 1 - s // 2
        half = lax.rem(s, 2)

        def put(target, got, rows, value):
            @pl.when(s < 2)
            def _():
                target[1, rows] = value.astype(BF16)

            @pl.when(s >= 2)
            def _():
                target[0, rows] = (value + got[rows].astype(F32)).astype(BF16)

        if place == 0:
            for h in range(2):

                @pl.when(s == 2 + h)
                def _():
                    for copy in swap(h):
                        copy.wait_recv()

        if place < strips:
            rows = pl.ds(pl.multiple_of((half * strips + place) * strip, strip), strip)
            value = dot(flat(tokens[:, :, rows]), flat(acts[e]), TN)
            put(wide_sum, wide_got, rows, value)
        if place == 3:
            rows = pl.ds(pl.multiple_of(half * strip, strip), strip)
            value = dot(flat(hiddens[e, :, :, rows]), flat(buf[...]), TN)
            put(down_sum, down_got, rows, value)
            for h in range(2):

                @pl.when(s == h)
                def _():
                    for copy in swap(h):
                        copy.start()

                @pl.when(s == 2 + h)
                def _():
                    for copy in store(h):
                        copy.start()

    finish = ring.scatter(partial, land, out_ref, scatter_sem, work)
    drain()
    finish()
    for half in range(2):
        for copy in swap(half):
            copy.wait_send()
        for copy in store(half):
            copy.wait()
    for ride in rides:
        ride.wait()


def gather_mix_back_scatter(count, d, side, m_all, share, router, weights, rides=()):
    rows, width = d.shape
    ff = weights[0].shape[1]
    everyone = pltpu.VMEM((count, rows, width), BF16)
    return ring_call(
        functools.partial(mix_back_kernel, count),
        "mix_back",
        0,
        [(d, ANYWHERE), (side, ANYWHERE), (m_all, ANYWHERE), (share, HERE), (router, HERE)]
        + [(w, ANYWHERE) for w in weights],
        [
            (cells((rows, width), F32), HERE),
            (cells((width // 2, 2 * ff), BF16), ANYWHERE),
            (cells((width // 2, 2 * ff), BF16), ANYWHERE),
            (cells((ff, width), BF16), ANYWHERE),
            (cells((2, width), F32), HERE),
        ],
        [everyone, everyone, land_scratch(count, rows, width), pltpu.VMEM((2 * rows, width), F32)]
        + expert_scratch(weights)
        + [
            everyone,
            pltpu.VMEM((2, count, rows, 2 * ff), BF16),
            pltpu.VMEM((2, count, rows, ff), BF16),
            pltpu.VMEM((count,) + side.shape, F32),
            pltpu.VMEM((2, width, 2 * ff), BF16),
            pltpu.VMEM((2, ff, width), BF16),
            pltpu.VMEM((width, 2 * ff), BF16),
            pltpu.VMEM((ff, width), BF16),
        ]
        + gather_sems(count, True)
        + scatter_sems(count)
        + dmas((7,), (2, 2), (2, 2), (4,)),
        rides,
        60,
    )


def branch_back_kernel(count, axes, *refs):
    inputs, ride_in, outputs, ride_out, scratch = split(refs, 3, len(axes), 2, len(axes))
    d_ref, w_ref, att_ref = inputs
    datt_ref, g_ref = outputs
    buf, wide_w, acc, mail, got = scratch[:5]
    sems, pair_sem, ride_sem = split(scratch[5:], 3, 2)
    ring = Ring(count)
    ring.meet(axes + ("fsdp",))
    rides = start_rides(axes, ride_in, ride_out, ride_sem)
    fill_out_weights(w_ref, wide_w)
    acc[...] = jnp.zeros_like(acc)

    def compute(s):
        blocks = ring.pair(s)
        d = jnp.concatenate([buf[b] for b in blocks], 0)
        att = jnp.concatenate([att_ref[b] for b in blocks], 0)
        datt = dot(d, wide_w[...], NT).astype(BF16)
        for place, block in enumerate(blocks):
            datt_ref[block] = datt[place * LANES : (place + 1) * LANES]
        acc[...] += dot(att, d, TN)

    def second(s):
        @pl.when(s >= 2)
        def _():
            compute(s - 1)

    drain = ring.gather(d_ref, buf, sems, None, None, second)
    compute(ring.steps)
    shard = g_ref.shape[0]
    core = lax.rem(lax.axis_index("fsdp"), 2)
    mail[...] = acc[pl.ds(pl.multiple_of((1 - core) * shard, 8), shard), :].astype(BF16)
    swap = remote(mail, got, pair_sem[0].at[0], pair_sem[1].at[0], partner_of("fsdp"))
    swap.start()
    drain()
    swap.wait()
    own = acc[pl.ds(pl.multiple_of(core * shard, 8), shard), :]
    g_ref[...] = (own + got[...].astype(F32)).astype(BF16)
    for ride in rides:
        ride.wait()


def gather_branch_back(count, d, w, att, rides=()):
    rows, width = d.shape
    shard = w.shape[0] // 2
    return ring_call(
        functools.partial(branch_back_kernel, count),
        "branch_back",
        0,
        [(d, ANYWHERE), (w, HERE), (att, HERE)],
        [
            (cells((count, rows, 2 * LANES), BF16), HERE),
            (cells((shard, width), BF16), HERE),
        ],
        [
            pltpu.VMEM((count, rows, width), BF16),
            pltpu.VMEM((2 * LANES, width), BF16),
            pltpu.VMEM((2 * LANES, width), F32),
            pltpu.VMEM((shard, width), BF16),
            pltpu.VMEM((shard, width), BF16),
        ]
        + gather_sems(count)
        + dmas((1,), (1,)),
        rides,
        32,
    )


def join_kernel(count, axes, *refs):
    inputs, ride_in, outputs, ride_out, scratch = split(refs, 7, len(axes), 2, len(axes))
    dq_ref, own_ref, other_ref, cos_ref, sin_ref, w_ref, x_ref = inputs
    out_ref, g_ref = outputs
    partial, land, rows_ref, tokens, got = scratch[:5]
    scatter_sem, pair_sem, load_sem, ride_sem = split(scratch[5:], 2, 2, 1)
    ring = Ring(count)
    ring.meet(axes + ("fsdp",))
    swap = remote(other_ref, got, pair_sem[0].at[0], pair_sem[1].at[0], partner_of("fsdp"))
    swap.start()
    rides = start_rides(axes, ride_in, ride_out, ride_sem)
    load = pltpu.make_async_copy(x_ref, tokens, load_sem[0].at[0])
    load.start()
    swap.wait()

    def compute(index, carry):
        blocks = 2 * index, 2 * index + 1
        rows = []
        for b in blocks:
            pair = own_ref[b] + got[b].astype(F32)
            keys = spin(pair, cos_ref[b], -sin_ref[b])
            low = lanes_of(pair) < HD
            middle = jnp.where(low, dq_ref[b, :, LANES:].astype(F32), turn(keys))
            last = jnp.where(low, turn(pair), 0.0)
            rows.append(
                jnp.concatenate([dq_ref[b, :, :LANES], middle.astype(BF16), last.astype(BF16)], 1)
            )
            rows_ref[b] = rows[-1]
        total = dot(jnp.concatenate(rows, 0), w_ref[...], NT).astype(BF16)
        for place, block in enumerate(blocks):
            partial[block] = total[place * LANES : (place + 1) * LANES]
        return carry

    lax.fori_loop(0, count // 2, compute, 0)
    load.wait()
    strip = g_ref.shape[0] // ring.steps

    def flat(value):
        return value.reshape(value.shape[0] * value.shape[1], value.shape[2])

    def work(s, place):
        if place == 0:
            rows = pl.ds(pl.multiple_of(s * strip, LANES), strip)
            g_ref[rows] = dot(flat(tokens[:, :, rows]), flat(rows_ref[...]), TN)

    finish = ring.scatter(partial, land, out_ref, scatter_sem, work)
    finish()
    for ride in rides:
        ride.wait()


def join_scatter(count, dq, own, other, cosine, sine, w, x_all, rides=()):
    _, rows, width = x_all.shape
    everyone = pltpu.VMEM((count, rows, width), BF16)
    return ring_call(
        functools.partial(join_kernel, count),
        "join",
        0,
        [(dq, HERE), (own, HERE), (other, HERE), (cosine, HERE), (sine, HERE), (w, HERE), (x_all, ANYWHERE)],
        [(cells((rows, width), F32), HERE), (cells(w.shape, F32), HERE)],
        [
            everyone,
            land_scratch(count, rows, width),
            pltpu.VMEM((count, rows, w.shape[1]), BF16),
            everyone,
            pltpu.VMEM(other.shape, BF16),
        ]
        + scatter_sems(count)
        + dmas((1,), (1,), (1,)),
        rides,
        48,
    )


def add_wide_kernel(layers, *refs):
    gate_ref, up_ref = refs[-2:]
    ff = gate_ref.shape[-1]
    for layer in range(layers):
        for half in range(2):
            own, got = refs[4 * layer + 2 * half : 4 * layer + 2 * half + 2]
            total = own[...].astype(F32) + got[...].astype(F32)
            gate_ref[layer, 0, half] = total[:, :ff]
            up_ref[layer, 0, half] = total[:, ff:]


def add_wide(pairs):
    layers = len(pairs) // 2
    rows, columns = pairs[0][0].shape
    tile = rows // 4
    flat = [array for pair in pairs for array in pair]
    out = jax.ShapeDtypeStruct((layers, 1, 2, rows, columns // 2), F32)
    gate, up = pl.pallas_call(
        functools.partial(add_wide_kernel, layers),
        grid=(4,),
        out_shape=(out, out),
        in_specs=[pl.BlockSpec((tile, columns), lambda i: (i, 0))] * len(flat),
        out_specs=[pl.BlockSpec((layers, 1, 2, tile, columns // 2), lambda i: (0, 0, 0, i, 0))] * 2,
        name="add_wide",
    )(*flat)
    shape = (layers, 1, 2 * rows, columns // 2)
    return gate.reshape(shape), up.reshape(shape)


def allowed_keys(begin, block, chunk, core):
    shape = (GROUP * LANES, 2 * LANES)
    place = lax.broadcasted_iota(jnp.int32, shape, 1)
    shift = jnp.where(place < LANES, core, -core)
    key = chunk * 2 * LANES + place + shift * LANES
    query = block * LANES + lax.rem(lax.broadcasted_iota(jnp.int32, shape, 0), LANES)
    return (key >= begin) & (key <= query)


def fill_out_weights(w_ref, wide_ref):
    rows = w_ref.shape[0]
    wide_ref[:rows] = w_ref[...]
    wide_ref[rows:] = jnp.zeros((wide_ref.shape[0] - rows, wide_ref.shape[1]), BF16)


def attend_kernel(info_ref, q_ref, own_ref, other_ref, begin_ref, w_ref, att_ref, lse_ref, out_ref, wide_ref):
    step = pl.program_id(0)
    core = info_ref[0]
    block = 2 * step + core
    first = info_ref[1 + step] // (2 * LANES)

    @pl.when(step == 0)
    def _():
        fill_out_weights(w_ref, wide_ref)

    q = q_ref[0].reshape(GROUP * LANES, LANES)
    begin = jnp.concatenate([begin_ref[0]] * GROUP, 0)

    def one(chunk, state):
        top, total, acc = state
        keys = jnp.concatenate([own_ref[chunk], other_ref[chunk]], 0)
        allowed = allowed_keys(begin, block, chunk, core)
        scores = jnp.where(allowed, dot(q, keys, NT), MASKED)
        new_top = jnp.maximum(top, jnp.max(scores, -1, keepdims=True))
        weights = jnp.where(allowed, jnp.exp(scores - new_top), 0.0)
        shrink = jnp.exp(top - new_top)
        total = total * shrink + jnp.sum(weights, -1, keepdims=True)
        return new_top, total, acc * shrink + dot(weights.astype(BF16), keys)

    rows = GROUP * LANES
    top, total, acc = lax.fori_loop(
        first,
        step + 1,
        one,
        (jnp.full((rows, 1), MASKED, F32), jnp.zeros((rows, 1), F32), jnp.zeros((rows, LANES), F32)),
    )
    lse_ref[0] = top + jnp.log(total)
    att = acc / total
    heads = [att[h * LANES : (h + 1) * LANES] for h in range(GROUP)]
    low = lanes_of(heads[0]) < HD
    wide = jnp.concatenate(
        [jnp.where(low, turn(heads[0]), heads[1]), jnp.where(low, turn(heads[2]), 0.0)], 1
    ).astype(BF16)
    att_ref[0] = wide
    out_ref[0] = dot(wide, wide_ref[...]).astype(BF16)


def attend(info, q, own, other, begin, w):
    blocks = q.shape[0]
    width = w.shape[1]
    wide = 2 * LANES
    return pl.pallas_call(
        attend_kernel,
        grid_spec=pltpu.PrefetchScalarGridSpec(
            num_scalar_prefetch=1,
            grid=(blocks,),
            in_specs=[
                pl.BlockSpec((1, GROUP, LANES, LANES), lambda i, s: (i, 0, 0, 0)),
                pl.BlockSpec(own.shape, lambda i, s: (0, 0, 0)),
                pl.BlockSpec(own.shape, lambda i, s: (0, 0, 0)),
                pl.BlockSpec((1, LANES, 1), lambda i, s: (i, 0, 0)),
                pl.BlockSpec(w.shape, lambda i, s: (0, 0)),
            ],
            out_specs=[
                pl.BlockSpec((1, LANES, wide), lambda i, s: (i, 0, 0)),
                pl.BlockSpec((1, GROUP * LANES, 1), lambda i, s: (i, 0, 0)),
                pl.BlockSpec((1, LANES, width), lambda i, s: (i, 0, 0)),
            ],
            scratch_shapes=[pltpu.VMEM((wide, width), BF16)],
        ),
        out_shape=(
            jax.ShapeDtypeStruct((blocks, LANES, wide), BF16),
            jax.ShapeDtypeStruct((blocks, GROUP * LANES, 1), F32),
            jax.ShapeDtypeStruct((blocks, LANES, width), BF16),
        ),
        name="attend",
    )(info, q, own, other, begin, w)


def attend_back_kernel(
    info_ref, q_ref, own_ref, other_ref, begin_ref, att_ref, lse_ref, datt_ref, cos_ref, sin_ref,
    dq_ref, d_own_ref, mail_ref, d_other_ref,
):
    step = pl.program_id(0)
    core = info_ref[0]
    block = 2 * step + core
    first = info_ref[1 + step] // (2 * LANES)

    @pl.when(step == 0)
    def _():
        d_own_ref[...] = jnp.zeros_like(d_own_ref)
        d_other_ref[...] = jnp.zeros_like(d_other_ref)

    q = q_ref[0].reshape(GROUP * LANES, LANES)
    begin = jnp.concatenate([begin_ref[0]] * GROUP, 0)

    def spread(wide):
        front, back = wide[:, :LANES], wide[:, LANES:]
        low = lanes_of(front) < HD
        parts = [jnp.where(low, 0.0, part) for part in (turn(front), front, turn(back))]
        return jnp.concatenate(parts, 0)

    datt = spread(datt_ref[0].astype(F32)).astype(BF16)
    att = spread(att_ref[0].astype(F32))
    delta = jnp.sum(datt.astype(F32) * att, -1, keepdims=True)
    lse = lse_ref[0]
    both = jnp.concatenate([q, datt], 0)

    def one(chunk, acc):
        keys = jnp.concatenate([own_ref[chunk], other_ref[chunk]], 0)
        allowed = allowed_keys(begin, block, chunk, core)
        weights = jnp.where(allowed, jnp.exp(dot(q, keys, NT) - lse), 0.0)
        slope = (weights * (dot(datt, keys, NT) - delta)).astype(BF16)
        d_keys = dot(jnp.concatenate([slope, weights.astype(BF16)], 0), both, TN)
        d_own_ref[chunk] += d_keys[:LANES]
        d_other_ref[chunk] += d_keys[LANES:]
        return acc + dot(slope, keys)

    acc = lax.fori_loop(first, step + 1, one, jnp.zeros((GROUP * LANES, LANES), F32))
    heads = [acc[h * LANES : (h + 1) * LANES] * (HD**-0.5) for h in range(GROUP)]
    low = lanes_of(heads[0]) < HD
    cosine, sine = cos_ref[0], -sin_ref[0]
    front = spin(jnp.where(low, heads[0], turn(heads[1])), cosine, sine)
    back = spin(jnp.where(low, heads[2], 0.0), cosine, sine)
    dq_ref[0] = jnp.concatenate([front, back], 1).astype(BF16)

    @pl.when(step == pl.num_programs(0) - 1)
    def _():
        mail_ref[...] = d_other_ref[...].astype(BF16)


def attend_back(info, q, own, other, begin, att, lse, datt, cosine, sine):
    blocks = q.shape[0]
    wide = 2 * LANES

    def block(*shape):
        return pl.BlockSpec((1,) + shape, lambda i, s: (i,) + (0,) * len(shape))

    whole = pl.BlockSpec(own.shape, lambda i, s: (0, 0, 0))
    return pl.pallas_call(
        attend_back_kernel,
        grid_spec=pltpu.PrefetchScalarGridSpec(
            num_scalar_prefetch=1,
            grid=(blocks,),
            in_specs=[
                block(GROUP, LANES, LANES),
                whole,
                whole,
                block(LANES, 1),
                block(LANES, wide),
                block(GROUP * LANES, 1),
                block(LANES, wide),
                block(LANES, LANES),
                block(LANES, LANES),
            ],
            out_specs=[block(LANES, wide), whole, whole],
            scratch_shapes=[pltpu.VMEM(own.shape, F32)],
        ),
        out_shape=(
            jax.ShapeDtypeStruct((blocks, LANES, wide), BF16),
            jax.ShapeDtypeStruct(own.shape, F32),
            jax.ShapeDtypeStruct(own.shape, BF16),
        ),
        name="attend_back",
    )(info, q, own, other, begin, att, lse, datt, cosine, sine)


def add_kernel(layers, *refs):
    o_ref = refs[-1]
    for layer in range(layers):
        own, got = refs[2 * layer], refs[2 * layer + 1]
        o_ref[layer, 0] = own[...].astype(F32) + got[...].astype(F32)


def add_layers(pairs):
    layers = len(pairs)
    rows, columns = pairs[0][0].shape
    tile = rows // 4
    flat = [array for pair in pairs for array in pair]
    return pl.pallas_call(
        functools.partial(add_kernel, layers),
        grid=(4,),
        out_shape=jax.ShapeDtypeStruct((layers, 1, rows, columns), F32),
        in_specs=[pl.BlockSpec((tile, columns), lambda i: (i, 0))] * len(flat),
        out_specs=pl.BlockSpec((layers, 1, tile, columns), lambda i: (0, 0, i, 0)),
        name="add_layers",
    )(*flat)


def on_device(
    tokens,
    cotangent,
    positions,
    segments,
    routes,
    attn_gain,
    w_query,
    w_key,
    w_value,
    w_out,
    ffn_gain,
    router,
    w_gate,
    w_up,
    w_down,
):
    rows, width = tokens.shape
    devices = lax.axis_size("fsdp")
    replicas = lax.axis_size("rep")
    count = devices // 2
    me = lax.axis_index("fsdp")
    chip, core = me // 2, lax.rem(me, 2)
    shard = w_query.shape[1]
    experts = devices
    columns = 3 * LANES
    used = (GROUP + 2) * HD
    pairs = [(index, index ^ 1) for index in range(devices)]

    def swap(array):
        return lax.ppermute(array, "fsdp", pairs)

    small = jnp.concatenate(
        [attn_gain, ffn_gain, router.transpose(0, 2, 1).reshape(LAYERS * experts, shard)], 0
    )
    small = jnp.pad(small, ((0, 48 - small.shape[0]), (0, LANES - shard)))
    rate = jnp.exp(-jnp.log(10000.0) * jnp.arange(HD // 2, dtype=F32) / (HD // 2))
    angle = rate[:, None] * positions.astype(F32)[None, :]
    table = jnp.concatenate([jnp.cos(angle), jnp.sin(angle)], 0)
    slabs = jnp.concatenate(
        [
            w_query.reshape(LAYERS, shard, count, GROUP * HD),
            w_key.reshape(LAYERS, shard, count, HD),
            w_value.reshape(LAYERS, shard, count, HD),
            jnp.zeros((LAYERS, shard, count, columns - used), BF16),
        ],
        -1,
    ).transpose(2, 0, 1, 3)
    heads_w, outs_w, smalls, tables = exchange_weights(count, slabs, w_out, small, table)
    heads_w = heads_w.reshape(LAYERS, width, columns)
    w_heads = [heads_w[layer] for layer in range(LAYERS)]
    w_outs = [outs_w[:, layer].reshape(2 * shard, width) for layer in range(LAYERS)]
    smalls = smalls[:, : (2 + experts) * LAYERS, :shard].transpose(1, 0, 2).reshape(-1, width)
    smalls = smalls.astype(F32)
    gains_one, gains_two = smalls[:LAYERS], smalls[LAYERS : 2 * LAYERS]
    routers = smalls[2 * LAYERS :].reshape(LAYERS, experts, width)
    tables = tables.transpose(0, 2, 1).reshape(count * rows, HD)
    cosine = jnp.concatenate([tables[:, : HD // 2]] * 4, 1).reshape(count, rows, LANES)
    sine = jnp.concatenate([tables[:, HD // 2 :]] * 4, 1).reshape(count, rows, LANES)
    experts_w = []
    for layer in range(LAYERS):
        own = [w_gate[layer, 0], w_up[layer, 0], w_down[layer, 0]]
        experts_w.append(own + [swap(w) for w in own])
    mine = [2 * chip + core, 2 * chip + 1 - core]

    flat = segments.reshape(1, -1)
    kinds = jnp.arange(8, dtype=jnp.int32)[:, None]
    starts = jnp.sum((flat < kinds).astype(jnp.int32), 1, keepdims=True)
    begin = jnp.sum(jnp.where(flat == kinds, starts, 0), 0).reshape(count, 2, rows)
    begin = lax.dynamic_index_in_dim(begin, core, 1, False)
    info = jnp.concatenate([core[None], begin[:, 0]]).astype(jnp.int32)
    begin = begin[:, :, None]

    hidden = tokens.astype(F32)
    saved = []

    def normal(values):
        inverse = lax.rsqrt(jnp.mean(values * values, -1, keepdims=True) + EPS)
        return inverse, values * inverse

    for layer in range(LAYERS):
        inverse_one, normed_one = normal(hidden)
        x_attn = (normed_one * gains_one[layer][None, :]).astype(BF16)
        query, kv, kv_other, x_all = gather_project(count, x_attn, w_heads[layer], cosine, sine)
        att, lse, partial = attend(info, query, kv, kv_other, begin, w_outs[layer])
        (added,) = ring_scatter(count, partial)
        middle = hidden + added
        inverse_two, normed_two = normal(middle)
        x_moe = (normed_two * gains_two[layer][None, :]).astype(BF16)
        logits = dot(routers[layer].astype(BF16), x_moe, NT)
        named = jnp.any(
            jnp.arange(experts, dtype=jnp.int32)[:, None, None] == routes[layer].T[None, :, :], 1
        )
        share = jax.nn.softmax(jnp.where(named, logits, -jnp.inf), axis=0)
        mixed, m_all, share_all = gather_mix_scatter(count, x_moe, share, experts_w[layer])
        saved.append(
            (inverse_one, normed_one, x_all, query, kv, kv_other, att, lse)
            + (inverse_two, normed_two, m_all, share_all, mixed)
        )
        hidden = middle + mixed
    activations = hidden.astype(BF16)

    grad = cotangent.astype(F32)
    waiting = []
    own_sums = [[None] * 4 for _ in range(LAYERS)]
    peer_sums = [[None] * 4 for _ in range(LAYERS)]
    heads_sums = [None] * LAYERS

    def send(kernel, *arguments, most=1):
        taken = []
        while replicas == 2 and waiting and len(taken) < most:
            taken.append(waiting.pop(0))
        rides = [(own_sums[layer][index], "rep") for layer, index in taken]
        results = kernel(count, *arguments, rides)
        for place, (layer, index) in enumerate(taken):
            peer_sums[layer][index] = results[len(results) - len(taken) + place]
        return results[: len(results) - len(taken)]

    for layer in reversed(range(LAYERS)):
        (inverse_one, normed_one, x_all, query, kv, kv_other, att, lse) = saved[layer][:8]
        (inverse_two, normed_two, m_all, share_all, mixed) = saved[layer][8:]
        d_mix = grad.astype(BF16)
        balance = jnp.sum(mixed * d_mix.astype(F32), -1)
        side = jnp.broadcast_to(balance[None, :], (8, rows))
        router_mine = jnp.concatenate(
            [lax.dynamic_slice_in_dim(routers[layer], e, 1, 0) for e in mine], 0
        )
        d_x, *expert_grads, g_router = send(
            gather_mix_back_scatter, d_mix, side, m_all, share_all, router_mine, experts_w[layer],
            most=2,
        )
        own_sums[layer][:3] = expert_grads
        waiting.extend((layer, index) for index in range(3))
        gain = gains_two[layer][None, :]
        d_norm = d_x * gain
        d_gain_two = jnp.sum(d_x * normed_two, 0)
        grad_mid = grad + inverse_two * (
            d_norm - normed_two * jnp.mean(d_norm * normed_two, -1, keepdims=True)
        )
        datt, own_sums[layer][3] = send(
            gather_branch_back, grad_mid.astype(BF16), w_outs[layer], att
        )
        d_query, d_own, d_other = attend_back(
            info, query, kv, kv_other, begin, att, lse, datt, cosine, sine
        )
        d_x, g_heads = send(
            join_scatter, d_query, d_own, d_other, cosine, sine, w_heads[layer], x_all
        )
        waiting.append((layer, 3))
        gain = gains_one[layer][None, :]
        d_norm = d_x * gain
        d_gain_one = jnp.sum(d_x * normed_one, 0)
        grad = grad_mid + inverse_one * (
            d_norm - normed_one * jnp.mean(d_norm * normed_one, -1, keepdims=True)
        )
        g_router = jnp.where(core == 0, g_router, g_router[::-1])
        extra = jnp.concatenate(
            [g_router, d_gain_one[None, :], d_gain_two[None, :]], 0
        ).T
        heads_sums[layer] = jnp.concatenate(
            [g_heads[:, :used], extra, jnp.zeros((width, columns - used - 4), F32)], 1
        ).astype(BF16).reshape(count, 2, shard, columns)
    heads_sums = jnp.stack(heads_sums, 2).transpose(1, 0, 2, 3, 4)
    total = finish_heads(count, replicas, heads_sums)
    for layer, index in waiting:
        if replicas == 2:
            peer_sums[layer][index] = lax.ppermute(own_sums[layer][index], "rep", [(0, 1), (1, 0)])
    if replicas == 2:
        g_gate, g_up = add_wide(
            [
                (own_sums[layer][index], peer_sums[layer][index])
                for layer in range(LAYERS)
                for index in range(2)
            ]
        )
        g_down, g_out = [
            add_layers([(own_sums[layer][index], peer_sums[layer][index]) for layer in range(LAYERS)])
            for index in (2, 3)
        ]
    else:
        total = lax.psum(total.astype(BF16), "rep").astype(F32)
        summed = [
            jnp.stack(
                [lax.psum(own_sums[layer][index], "rep").astype(F32) for layer in range(LAYERS)]
            )[:, None]
            for index in range(4)
        ]
        wide = jnp.concatenate(summed[:2], 2)
        ff = w_gate.shape[3]
        g_gate, g_up, g_down, g_out = wide[..., :ff], wide[..., ff:], summed[2], summed[3]
    total = total.transpose(1, 2, 0, 3)

    def part(first, last):
        return total[..., first:last].reshape(LAYERS, shard, -1)

    key_edge = GROUP * HD
    gains = jnp.sum(total[..., used + 2 : used + 4], 2)
    return (
        activations,
        grad,
        gains[..., 0],
        part(0, key_edge),
        part(key_edge, key_edge + HD),
        part(key_edge + HD, used),
        g_out[:, 0],
        gains[..., 1],
        part(used, used + 2),
        g_gate,
        g_up,
        g_down,
    )


def solution(mesh):
    placed = (
        P(("rep", "fsdp"), None),
        P(("rep", "fsdp"), None),
        P(("rep", "fsdp")),
        P("rep", None),
        P(None, ("rep", "fsdp"), None),
        P(None, "fsdp"),
        P(None, "fsdp", None),
        P(None, "fsdp", None),
        P(None, "fsdp", None),
        P(None, "fsdp", None),
        P(None, "fsdp"),
        P(None, "fsdp", None),
        P(None, "fsdp", None, None),
        P(None, "fsdp", None, None),
        P(None, "fsdp", None, None),
    )
    return jax.shard_map(
        on_device,
        mesh=mesh,
        in_specs=placed,
        out_specs=(
            P(("rep", "fsdp"), None),
            P(("rep", "fsdp"), None),
            P(None, "fsdp"),
            P(None, "fsdp", None),
            P(None, "fsdp", None),
            P(None, "fsdp", None),
            P(None, "fsdp", None),
            P(None, "fsdp"),
            P(None, "fsdp", None),
            P(None, "fsdp", None, None),
            P(None, "fsdp", None, None),
            P(None, "fsdp", None, None),
        ),
        check_vma=False,
    )
```

```python
import functools

import jax
import jax.numpy as jnp
from jax import lax
from jax.experimental import pallas as pl
from jax.experimental.pallas import tpu as pltpu
from jax.sharding import PartitionSpec as P

HEADS = 24
KV_HEADS = 8
HD = 64
LAYERS = 2
GROUP = HEADS // KV_HEADS
LANES = 128
EPS = 1e-06
MASKED = -1e30
MESH = pl.DeviceIdType.MESH
F32 = jnp.float32
BF16 = jnp.bfloat16


def ring_place(chip, count):
    return lax.select(lax.rem(chip, 2) == 0, chip // 2, count - 1 - chip // 2)


def ring_chip(place, count):
    return lax.select(place < count // 2, 2 * place, 2 * (count - 1 - place) + 1)


def ring_setup(count):
    me = lax.axis_index("fsdp")
    chip, core = me // 2, lax.rem(me, 2)
    place = ring_place(chip, count)

    def at(offset):
        return ring_chip(lax.rem(place + offset + 2 * count, count), count)

    near = [{"fsdp": at(1) * 2 + core}, {"fsdp": at(-1) * 2 + core}]
    return chip, at, near


def partner_of(axis):
    if axis == "rep":
        return {"rep": 1 - lax.axis_index("rep")}
    me = lax.axis_index("fsdp")
    return {"fsdp": me + 1 - 2 * lax.rem(me, 2)}


def meet(others):
    barrier = pltpu.get_barrier_semaphore()
    for other in others:
        pl.semaphore_signal(barrier, inc=1, device_id=other, device_id_type=MESH)
    pl.semaphore_wait(barrier, len(others))


def remote(src, dst, send_sem, recv_sem, device):
    return pltpu.make_async_remote_copy(
        src_ref=src,
        dst_ref=dst,
        send_sem=send_sem,
        recv_sem=recv_sem,
        device_id=device,
        device_id_type=MESH,
    )


def ring_hops(count):
    half = count // 2
    return {(0, 0): half, (1, 1): half, (0, 1): half - 1, (1, 0): half - 1}


IDENTITIES = {}


def identity(key):
    return IDENTITIES.setdefault(key, len(IDENTITIES))


class Ring:
    def __init__(self, count, riders=()):
        self.count = count
        self.riders = riders
        self.steps = count // 2
        self.chip, self.at, self.near = ring_setup(count)

    def meet(self, partner=False):
        others = self.near + ([partner_of("fsdp")] if partner else [])
        meet(others + ([partner_of("rep")] if self.riders else []))
        for rider in self.riders:
            rider.start()

    def gather(self, x_ref, buf, sems, side=None, first=None, second=None):
        own_sem, send_sem, recv_sem = sems[:3]
        half_rows = x_ref.shape[0] // 2
        steps = self.steps
        own = [pltpu.make_async_copy(x_ref, buf.at[self.chip], own_sem.at[0])]
        if side is not None:
            side_ref, side_buf = side
            side_send, side_recv = sems[3:]
            own.append(pltpu.make_async_copy(side_ref, side_buf.at[self.chip], own_sem.at[1]))
        for copy in own:
            copy.start()

        def piece(key, step, block, source=None):
            direction, part = key
            rows = pl.ds(part * half_rows, half_rows)
            target = buf.at[block, rows]
            return remote(
                target if source is None else source.at[rows],
                target,
                send_sem.at[direction, part, step],
                recv_sem.at[direction, part, step],
                self.near[direction],
            )

        def side_piece(direction, step, block, source=None):
            target = side_buf.at[block]
            return remote(
                target if source is None else source,
                target,
                side_send.at[direction, step],
                side_recv.at[direction, step],
                self.near[direction],
            )

        def toward(key, places):
            return self.at(-places if key[0] == 0 else places)

        early, late = [(0, 0), (1, 1)], [(0, 1), (1, 0)]
        if side is not None:
            for direction in range(2):
                side_piece(direction, 0, self.chip, side_ref).start()
        for key in early + late:
            piece(key, 0, self.chip, x_ref).start()

        def step(s, carry):
            if side is not None:
                for direction in range(2):

                    @pl.when(s <= steps - direction)
                    def _():
                        block = toward((direction, 0), s)
                        side_piece(direction, s - 1, block).wait_recv()

                        @pl.when(s < steps - direction)
                        def _():
                            side_piece(direction, s, block).start()

            for key in early:
                block = toward(key, s)
                piece(key, s - 1, block).wait_recv()

                @pl.when(s < steps)
                def _():
                    piece(key, s, block).start()

            if first is not None:
                first(s)

            @pl.when(s < steps)
            def _():
                for key in late:
                    block = toward(key, s)
                    piece(key, s - 1, block).wait_recv()

                    @pl.when(s < steps - 1)
                    def _():
                        piece(key, s, block).start()

            if second is not None:
                second(s)
            return carry

        for copy in own:
            copy.wait()
        lax.fori_loop(1, steps + 1, step, 0)

        def drain():
            for s in range(steps):
                for key in early + (late if s < steps - 1 else []):
                    piece(key, s, toward(key, s)).wait_send()
                if side is not None:
                    for direction in range(2):
                        if s < steps - direction:
                            side_piece(direction, s, toward((direction, 0), s)).wait_send()

        return drain

    def pair(self, s):
        return self.at(s), self.at(-s)

    def meanwhile(self, compute, place):
        def run(s):
            @pl.when(s == 1)
            def _():
                compute(place, (self.chip,))

            @pl.when(s > 1)
            def _():
                compute(place, self.pair(s - 1))

        return run

    def scatter(self, partial, land, sems, work=None, source=None, ready=None):
        send_sem, recv_sem = sems
        source = partial if source is None else source
        half_rows = partial.shape[1] // 2
        steps = self.steps
        hops = ring_hops(self.count)

        def ahead(key, s):
            places = hops[key] - s
            return self.at(places if key[0] == 0 else -places)

        def piece(key, s, source):
            direction, part = key
            return remote(
                source,
                land.at[direction, part, s],
                send_sem.at[direction, part, s],
                recv_sem.at[direction, part, s],
                self.near[direction],
            )

        def rows_of(key):
            return pl.ds(key[1] * half_rows, half_rows)

        for key in hops:
            piece(key, 0, source.at[ahead(key, 0), rows_of(key)]).start()
        if ready is not None:
            ready()

        def step(s, carry):
            for place, key in enumerate(hops):
                if work is not None:
                    work(s - 1, place)

                @pl.when(s < hops[key])
                def _():
                    slot = land.at[key[0], key[1], s - 1]
                    piece(key, s - 1, slot).wait_recv()
                    mine = partial[ahead(key, s), rows_of(key)]
                    slot[...] = (slot[...].astype(F32) + mine.astype(F32)).astype(BF16)
                    piece(key, s, slot).start()

            return carry

        lax.fori_loop(1, steps + 1, step, 0)
        for key in hops:
            slot = land.at[key[0], key[1], hops[key] - 1]
            piece(key, hops[key] - 1, slot).wait_recv()
        halves = []
        for part in range(2):
            rows = pl.ds(part * half_rows, half_rows)
            total = partial[self.chip, rows].astype(F32)
            for direction in range(2):
                total = total + land[direction, part, hops[direction, part] - 1].astype(F32)
            halves.append(total)
        summed = jnp.concatenate(halves, 0)

        def drain():
            for key in hops:
                for s in range(hops[key]):
                    piece(key, s, land.at[key[0], key[1], s]).wait_send()

        return summed, drain


def dmas(*shapes):
    return [pltpu.SemaphoreType.DMA(shape) for shape in shapes]


def gather_sems(count, sided=False):
    steps = count // 2
    shapes = [(2,), (2, 2, steps), (2, 2, steps)]
    return dmas(*(shapes + ([(2, steps), (2, steps)] if sided else [])))


def scatter_sems(count):
    return dmas((2, 2, count // 2), (2, 2, count // 2))


ANYWHERE = pl.BlockSpec(memory_space=pl.ANY)
HERE = pl.BlockSpec(memory_space=pltpu.VMEM)


FREE = pl.CostEstimate(flops=0, bytes_accessed=0, transcendentals=0)


def ring_call(body, key, inputs, outputs, scratch, megabytes, rides=()):
    n_in, n_out, n_rides = len(inputs), len(outputs), len(rides)

    def kernel(*refs):
        ins, ride_in, outs, ride_out, rest = split(refs, n_in, n_rides, n_out, n_rides)
        riders = []
        if n_rides:
            *rest, send_sem, recv_sem = rest
            riders = [
                remote(ride_in[i], ride_out[i], send_sem.at[i], recv_sem.at[i], partner_of("rep"))
                for i in range(n_rides)
            ]
        body(riders, *ins, *outs, *rest)
        for rider in riders:
            rider.wait()

    return pl.pallas_call(
        kernel,
        out_shape=tuple(shape for shape, _ in outputs) + tuple(cells(a.shape, a.dtype) for a in rides),
        in_specs=[spec for _, spec in inputs] + [ANYWHERE] * n_rides,
        out_specs=[spec for _, spec in outputs] + [ANYWHERE] * n_rides,
        scratch_shapes=list(scratch) + (dmas((n_rides,), (n_rides,)) if n_rides else []),
        compiler_params=pltpu.CompilerParams(
            collective_id=identity(key),
            has_side_effects=True,
            vmem_limit_bytes=megabytes << 20,
        ),
        cost_estimate=FREE,
        name=key[0],
    )(*[array for array, _ in inputs], *rides)


def split(refs, *sizes):
    parts, place = [], 0
    for size in sizes:
        parts.append(refs[place : place + size])
        place += size
    return parts + [refs[place:]]


def cells(shape, dtype):
    return jax.ShapeDtypeStruct(shape, dtype)


def setup_kernel(
    count, slab_ref, out_w_ref, small_ref, table_ref,
    heads_ref, outs_ref, smalls_ref, tables_ref,
    own_sem, slab_send, slab_recv, pass_send, pass_recv,
    small_send, small_recv, table_send, table_recv, out_send, out_recv,
):
    devices = 2 * count
    me = lax.axis_index("fsdp")
    chip, core = me // 2, lax.rem(me, 2)
    layers = slab_ref.shape[1]

    def device(offset):
        return {"fsdp": lax.rem(me + offset, devices)}

    def chip_at(offset):
        return lax.rem(chip + offset + count, count)

    partner = partner_of("fsdp")
    meet([device(offset) for offset in range(1, devices)])
    copies = [
        pltpu.make_async_copy(slab_ref.at[chip, layer], heads_ref.at[layer, me], own_sem.at[layer])
        for layer in range(layers)
    ] + [
        pltpu.make_async_copy(small_ref, smalls_ref.at[me], own_sem.at[layers]),
        pltpu.make_async_copy(table_ref, tables_ref.at[chip], own_sem.at[layers + 1]),
        pltpu.make_async_copy(out_w_ref, outs_ref.at[core], own_sem.at[layers + 2]),
    ]
    sends = [
        remote(small_ref, smalls_ref.at[me], small_send.at[offset], small_recv.at[offset], device(offset))
        for offset in range(1, devices)
    ]
    for offset in range(1, count):
        there = {"fsdp": chip_at(offset) * 2 + core}
        sends.append(
            remote(table_ref, tables_ref.at[chip], table_send.at[offset], table_recv.at[offset], there)
        )
        for layer in range(layers):
            sends.append(
                remote(
                    slab_ref.at[chip_at(offset), layer], heads_ref.at[layer, me],
                    slab_send.at[offset, layer], slab_recv.at[offset, layer], there,
                )
            )
    for layer in range(layers):
        sends.append(
            remote(
                slab_ref.at[chip, layer], heads_ref.at[layer, me],
                pass_send.at[0, layer], pass_recv.at[0, layer], partner,
            )
        )
    sends.append(remote(out_w_ref, outs_ref.at[core], out_send.at[0], out_recv.at[0], partner))
    for copy in copies + sends:
        copy.start()
    for offset in range(1, count):
        origin = chip_at(-offset) * 2 + core
        for layer in range(layers):
            slot = heads_ref.at[layer, origin]
            remote(slot, slot, slab_send.at[offset, layer], slab_recv.at[offset, layer], partner).wait_recv()
            forward = remote(slot, slot, pass_send.at[offset, layer], pass_recv.at[offset, layer], partner)
            forward.start()
    for offset in range(1, count):
        origin = chip_at(-offset)
        table = tables_ref.at[origin]
        remote(table, table, table_send.at[offset], table_recv.at[offset], partner).wait_recv()
    for offset in range(count):
        origin = chip_at(-offset) * 2 + 1 - core
        mine = chip_at(-offset) * 2 + core
        for layer in range(layers):
            slot, sent = heads_ref.at[layer, origin], heads_ref.at[layer, mine]
            if offset > 0:
                remote(sent, sent, pass_send.at[offset, layer], pass_recv.at[offset, layer], partner).wait_send()
            remote(slot, slot, pass_send.at[offset, layer], pass_recv.at[offset, layer], partner).wait_recv()
    for offset in range(1, devices):
        slot = smalls_ref.at[lax.rem(me - offset + devices, devices)]
        remote(slot, slot, small_send.at[offset], small_recv.at[offset], partner).wait_recv()
    other = outs_ref.at[1 - core]
    remote(other, other, out_send.at[0], out_recv.at[0], partner).wait_recv()
    for copy in copies:
        copy.wait()
    for send in sends:
        send.wait_send()


def exchange_weights(count, slabs, out_w, small, table):
    layers = slabs.shape[1]
    devices = 2 * count
    dma = pltpu.SemaphoreType.DMA
    anywhere = pl.BlockSpec(memory_space=pl.ANY)
    return pl.pallas_call(
        functools.partial(setup_kernel, count),
        out_shape=(
            jax.ShapeDtypeStruct((layers, devices) + slabs.shape[2:], slabs.dtype),
            jax.ShapeDtypeStruct((2,) + out_w.shape, out_w.dtype),
            jax.ShapeDtypeStruct((devices,) + small.shape, small.dtype),
            jax.ShapeDtypeStruct((count,) + table.shape, table.dtype),
        ),
        in_specs=[anywhere] * 4,
        out_specs=[anywhere] * 4,
        scratch_shapes=[
            dma((layers + 3,)),
            dma((count, layers)),
            dma((count, layers)),
            dma((count, layers)),
            dma((count, layers)),
            dma((devices,)),
            dma((devices,)),
            dma((count,)),
            dma((count,)),
            dma((1,)),
            dma((1,)),
        ],
        compiler_params=pltpu.CompilerParams(
            collective_id=identity(("setup",)), has_side_effects=True
        ),
        cost_estimate=FREE,
        name="exchange_weights",
    )(slabs, out_w, small, table)


def dot(left, right, contract=((1,), (0,))):
    return lax.dot_general(left, right, (contract, ((), ())), preferred_element_type=F32)


NT = ((1,), (1,))
TN = ((0,), (0,))


def lanes_of(field):
    return lax.broadcasted_iota(jnp.int32, field.shape, 1)


def turn(field):
    return pltpu.roll(field, HD, 1)


def spin(field, cosine, sine):
    swapped = jnp.where(
        lax.rem(lanes_of(field), HD) < HD // 2,
        -pltpu.roll(field, LANES - HD // 2, 1),
        pltpu.roll(field, HD // 2, 1),
    )
    return field * cosine + swapped * sine


def project_rows(rows, cosine, sine):
    first = spin(rows[:, :LANES], cosine, sine)
    second = spin(rows[:, LANES : 2 * LANES], cosine, sine)
    third = rows[:, 2 * LANES :]
    low = lanes_of(first) < HD
    heads = []
    for field in (first, turn(first), second):
        rounded = jnp.where(low, field, 0.0).astype(BF16).astype(F32)
        heads.append((rounded * (HD**-0.5)).astype(BF16))
    return heads, jnp.where(low, turn(second), turn(third)).astype(BF16)


def angles(table):
    rows = jnp.concatenate([table, table], 0).T
    early = lax.rem(lanes_of(rows), HD) < HD // 2
    cosine = jnp.where(early, rows, pltpu.roll(rows, HD // 2, 1))
    sine = jnp.where(early, pltpu.roll(rows, LANES - HD // 2, 1), rows)
    return cosine, sine


def normal(values):
    inverse = lax.rsqrt(jnp.mean(values * values, -1, keepdims=True) + EPS)
    return inverse, values * inverse


def normal_back(d_x, values, gain):
    inverse, normed = normal(values)
    d_norm = d_x * gain
    d_values = inverse * (d_norm - normed * jnp.mean(d_norm * normed, -1, keepdims=True))
    return d_values, jnp.sum(d_x * normed, 0, keepdims=True)


def diagonal():
    shape = (LANES, LANES)
    return lax.broadcasted_iota(jnp.int32, shape, 0) == lax.broadcasted_iota(jnp.int32, shape, 1)


def as_column(line):
    return jnp.sum(jnp.where(diagonal(), jnp.broadcast_to(line, (LANES, LANES)), 0.0), 1, keepdims=True)


def as_line(column):
    return jnp.sum(jnp.where(diagonal(), jnp.broadcast_to(column, (LANES, LANES)), 0.0), 0, keepdims=True)


def flat(value):
    return value.reshape(value.shape[0] * value.shape[1], value.shape[2])


def stack(ref, blocks):
    parts = [ref[b] for b in blocks]
    return parts[0] if len(parts) == 1 else jnp.concatenate(parts, 0)


def cut(value, blocks):
    return [(b, value[i * LANES : (i + 1) * LANES]) for i, b in enumerate(blocks)]


def gain_row(params_ref, kind, layer):
    row = kind * LAYERS + layer
    return params_ref[row : row + 1, :]


def router_rows(experts, layer):
    first = 2 * LAYERS + layer * experts
    return slice(first, first + experts)


def project_kernel(count, layer, riders, *refs):
    inputs, outputs, scratch = split(refs, 3, 4)
    x_ref, w_ref, table_ref = inputs
    q_ref, own_ref, other_ref, all_ref = outputs
    buf, weights = scratch[:2]
    sems, pair_sems, out_sem, load_sem = split(scratch[2:], 3, 2, 1)
    ring = Ring(count, riders)
    load = pltpu.make_async_copy(w_ref.at[layer], weights, load_sem[0].at[0])
    load.start()
    ring.meet(True)
    partner = partner_of("fsdp")

    def pass_on(block):
        return remote(
            own_ref.at[block], other_ref.at[block], pair_sems[0].at[block], pair_sems[1].at[block], partner
        )

    def compute(place, blocks):
        rows = dot(stack(buf, blocks), weights[...])
        tables = [angles(table_ref[b]) for b in blocks]
        cosine = jnp.concatenate([t[0] for t in tables], 0)
        sine = jnp.concatenate([t[1] for t in tables], 0)
        heads, pair = project_rows(rows, cosine, sine)
        for index, head in enumerate(heads):
            for block, part in cut(head, blocks):
                q_ref[block, index] = part
        for block, part in cut(pair, blocks):
            own_ref[block] = part
            pass_on(block).start()

    def first(s):
        @pl.when(s == 1)
        def _():
            load.wait()

    drain = ring.gather(x_ref, buf, sems, None, first, ring.meanwhile(compute, 0))
    keep = pltpu.make_async_copy(buf, all_ref, out_sem[0].at[0])
    keep.start()
    compute(0, (ring.at(ring.steps),))
    drain()
    for block in range(count):
        pass_on(block).wait()
    keep.wait()


def gather_project(count, layer, x, w, tables):
    rows, width = x.shape
    block = cells((count, rows, LANES), BF16)
    return ring_call(
        functools.partial(project_kernel, count, layer),
        ("project", layer),
        [(x, ANYWHERE), (w, ANYWHERE), (tables, HERE)],
        [
            (cells((count, GROUP, rows, LANES), BF16), HERE),
            (block, HERE),
            (block, HERE),
            (cells((count, rows, width), BF16), ANYWHERE),
        ],
        [pltpu.VMEM((count, rows, width), BF16), pltpu.VMEM(w.shape[1:], BF16)]
        + gather_sems(count)
        + dmas((count,), (count,), (1,), (1,)),
        20,
    )


def route_kernel(count, layer, riders, *refs):
    inputs, outputs, scratch = split(refs, 4, 3)
    p_ref, hidden_ref, params_ref, routes_ref = inputs
    middle_ref, x_ref, share_ref = outputs
    partial, land = scratch[:2]
    sems, load_sem = split(scratch[2:], 2)
    ring = Ring(count, riders)
    load = pltpu.make_async_copy(p_ref, partial, load_sem[0].at[0])
    load.start()
    ring.meet()
    added, drain = ring.scatter(partial, land, sems, None, p_ref, load.wait)
    middle = hidden_ref[...] + added
    middle_ref[...] = middle
    x = (normal(middle)[1] * gain_row(params_ref, 1, layer)).astype(BF16)
    x_ref[...] = x
    experts = share_ref.shape[0]
    logits = dot(params_ref[router_rows(experts, layer), :].astype(BF16), x, NT)
    expert = lax.broadcasted_iota(jnp.int32, logits.shape, 0)
    named = expert < 0
    for choice in range(routes_ref.shape[1]):
        named = named | (expert == routes_ref[layer, choice : choice + 1, :])
    scores = jnp.where(named, logits, MASKED)
    weights = jnp.where(named, jnp.exp(scores - jnp.max(scores, 0, keepdims=True)), 0.0)
    share_ref[...] = weights / jnp.sum(weights, 0, keepdims=True)
    drain()


def scatter_route(count, layer, partial, hidden, params, routes):
    _, rows, width = partial.shape
    experts = 2 * count
    return ring_call(
        functools.partial(route_kernel, count, layer),
        ("route", layer),
        [(partial, ANYWHERE), (hidden, HERE), (params, HERE), (routes, HERE)],
        [
            (cells((rows, width), F32), HERE),
            (cells((rows, width), BF16), HERE),
            (cells((experts, rows), F32), HERE),
        ],
        [pltpu.VMEM(partial.shape, BF16), land_scratch(count, rows, width)]
        + scatter_sems(count)
        + dmas((1,)),
        20,
    )


def load_experts(refs, layer, gates, ups, downs, sem):
    copies = []
    for e in range(2):
        for place, buf in enumerate((gates, ups, downs)):
            source = refs[3 * e + place].at[layer, 0]
            copies.append(pltpu.make_async_copy(source, buf.at[e], sem.at[3 * e + place]))
    for copy in copies:
        copy.start()
    return copies


def expert_of(e):
    me = lax.axis_index("fsdp")
    return me if e == 0 else me + 1 - 2 * lax.rem(me, 2)


def share_of(share_ref, e, blocks):
    columns = [as_column(share_ref[b, pl.ds(expert_of(e), 1), :]) for b in blocks]
    return jnp.concatenate(columns, 0) if len(columns) > 1 else columns[0]


def after_loads(loads, run):
    def first(s):
        @pl.when(s == 1)
        def _():
            for load in loads:
                load.wait()

        run(s)

    return first


def mix_kernel(count, layer, riders, *refs):
    inputs, outputs, scratch = split(refs, 10, 5)
    x_ref, side_ref, middle_ref, params_ref = inputs[:4]
    mixed_ref, hidden_ref, next_ref, all_ref, share_ref = outputs
    buf, partial, land, acc, gates, ups, downs = scratch[:7]
    sems, scatter_sem, load_sem, out_sem = split(scratch[7:], 5, 2, 1)
    ring = Ring(count, riders)
    loads = load_experts(inputs[4:], layer, gates, ups, downs, load_sem[0])
    ring.meet()

    def compute(e, blocks):
        x = stack(buf, blocks)
        act_gate, act_up = dot(x, gates[e]), dot(x, ups[e])
        hidden = jax.nn.silu(act_gate) * act_up * share_of(share_ref, e, blocks)
        part = dot(hidden.astype(BF16), downs[e])
        if e == 0:
            acc[: x.shape[0]] = part
        else:
            total = (acc[: x.shape[0]] + part).astype(BF16)
            for block, rows in cut(total, blocks):
                partial[block] = rows

    drain = ring.gather(
        x_ref, buf, sems, (side_ref, share_ref),
        after_loads(loads, ring.meanwhile(compute, 0)), ring.meanwhile(compute, 1),
    )
    keep = pltpu.make_async_copy(buf, all_ref, out_sem[0].at[0])
    keep.start()
    for e in range(2):
        compute(e, (ring.at(ring.steps),))
    mixed, finish = ring.scatter(partial, land, scatter_sem)
    mixed_ref[...] = mixed
    hidden = middle_ref[...] + mixed
    hidden_ref[...] = hidden
    if layer + 1 < LAYERS:
        next_ref[...] = (normal(hidden)[1] * gain_row(params_ref, 0, layer + 1)).astype(BF16)
    else:
        next_ref[...] = hidden.astype(BF16)
    drain()
    finish()
    keep.wait()


def expert_scratch(weights):
    return [pltpu.VMEM((2,) + w.shape[2:], BF16) for w in weights[:3]]


def land_scratch(count, rows, width):
    return pltpu.VMEM((2, 2, count // 2, rows // 2, width), BF16)


def gather_mix_scatter(count, layer, x, share, middle, params, weights):
    rows, width = x.shape
    everyone = pltpu.VMEM((count, rows, width), BF16)
    own = cells((rows, width), F32)
    return ring_call(
        functools.partial(mix_kernel, count, layer),
        ("mix", layer),
        [(x, ANYWHERE), (share, ANYWHERE), (middle, HERE), (params, HERE)]
        + [(w, ANYWHERE) for w in weights],
        [
            (own, HERE),
            (own, HERE),
            (cells((rows, width), BF16), HERE),
            (cells((count, rows, width), BF16), ANYWHERE),
            (cells((count,) + share.shape, F32), HERE),
        ],
        [everyone, everyone, land_scratch(count, rows, width), pltpu.VMEM((2 * rows, width), F32)]
        + expert_scratch(weights)
        + gather_sems(count, True)
        + scatter_sems(count)
        + dmas((6,), (1,)),
        56,
    )


def mix_back_kernel(count, layer, riders, *refs):
    inputs, outputs, scratch = split(refs, 13, 5)
    d_ref, side_ref, m_ref, share_ref, params_ref, grad_ref, middle_ref = inputs[:7]
    mid_ref, branch_ref, gain_ref, sum_ref, g_router_ref = outputs
    buf, partial, land, acc, gates, ups, downs = scratch[:7]
    tokens, acts, hiddens, balance_ref, totals, got = scratch[7:13]
    sems, scatter_sem, load_sem, pair_sem, out_sem = split(scratch[13:], 5, 2, 1, 2)
    ring = Ring(count, riders)
    loads = load_experts(inputs[7:], layer, gates, ups, downs, load_sem[0])
    loads.append(pltpu.make_async_copy(m_ref, tokens, load_sem[0].at[6]))
    loads[-1].start()
    ring.meet(True)
    ff = gates.shape[2]
    width = buf.shape[2]
    g_router_ref[...] = jnp.zeros_like(g_router_ref)
    routers = 2 * LAYERS + layer * 2 * count

    def compute(e, blocks):
        d, x = stack(buf, blocks), stack(tokens, blocks)
        share = share_of(share_ref, e, blocks)
        balance = [as_column(balance_ref[b, 0:1, :]) for b in blocks]
        balance = jnp.concatenate(balance, 0) if len(balance) > 1 else balance[0]
        act_gate, act_up = dot(x, gates[e]), dot(x, ups[e])
        sig = jax.nn.sigmoid(act_gate)
        swish = act_gate * sig
        hidden = swish * act_up
        raw = dot(d, downs[e], NT)
        d_logit = share * (jnp.sum(hidden * raw, -1, keepdims=True) - balance)
        d_hidden = raw * share
        d_gate = (d_hidden * act_up * sig * (1.0 + act_gate * (1.0 - sig))).astype(BF16)
        d_up = (d_hidden * swish).astype(BF16)
        weighted = (hidden * share).astype(BF16)
        part = dot(d_gate, gates[e], NT) + dot(d_up, ups[e], NT)
        part = part + d_logit * params_ref[pl.ds(routers + expert_of(e), 1), :]
        g_router_ref[e : e + 1, :] += jnp.sum(d_logit * x.astype(F32), 0, keepdims=True)
        for place, block in enumerate(blocks):
            here = slice(place * LANES, (place + 1) * LANES)
            acts[e, block, :, :ff] = d_gate[here]
            acts[e, block, :, ff:] = d_up[here]
            hiddens[e, block] = weighted[here]
        if e == 0:
            acc[: x.shape[0]] = part
        else:
            total = (acc[: x.shape[0]] + part).astype(BF16)
            for block, rows in cut(total, blocks):
                partial[block] = rows

    drain = ring.gather(
        d_ref, buf, sems, (side_ref, balance_ref),
        after_loads(loads, ring.meanwhile(compute, 0)), ring.meanwhile(compute, 1),
    )
    for e in range(2):
        compute(e, (ring.at(ring.steps),))

    partner = partner_of("fsdp")
    strip = 2 * LANES
    strips = width // (2 * strip)
    groups = width // ff

    def regions(half):
        regions = [(group * width + half * (width // 2), width // 2) for group in range(2)]
        return regions + [(2 * width + group * ff + half * (ff // 2), ff // 2) for group in range(groups)]

    def swap(half):
        return [
            remote(
                totals.at[1, pl.ds(first, length)], got.at[pl.ds(first, length)],
                pair_sem[0].at[half, index], pair_sem[1].at[half, index], partner,
            )
            for index, (first, length) in enumerate(regions(half))
        ]

    def store(half):
        return [
            pltpu.make_async_copy(
                totals.at[0, pl.ds(first, length)], sum_ref.at[pl.ds(first, length)], out_sem[0].at[half, index]
            )
            for index, (first, length) in enumerate(regions(half))
        ]

    def work(s, place):
        e = 1 - s // 2
        half = lax.rem(s, 2)

        def put(first, value):
            rows = pl.ds(pl.multiple_of(first, strip), strip)

            @pl.when(s < 2)
            def _():
                totals[1, rows] = value.astype(BF16)

            @pl.when(s >= 2)
            def _():
                totals[0, rows] = (value + got[rows].astype(F32)).astype(BF16)

        if place == 0:
            for h in range(2):

                @pl.when(s == 2 + h)
                def _():
                    for copy in swap(h):
                        copy.wait_recv()

        if place < strips:
            first = (half * strips + place) * strip
            columns = pl.ds(pl.multiple_of(first, strip), strip)
            value = dot(flat(tokens[:, :, columns]), flat(acts[e]), TN)
            for group in range(2):
                put(group * width + first, value[:, group * ff : (group + 1) * ff])
        if place == 3:
            columns = pl.ds(pl.multiple_of(half * strip, strip), strip)
            value = dot(flat(hiddens[e, :, :, columns]), flat(buf[...]), TN)
            for group in range(groups):
                put(2 * width + group * ff + half * strip, value[:, group * ff : (group + 1) * ff])
            for h in range(2):

                @pl.when(s == h)
                def _():
                    for copy in swap(h):
                        copy.start()

                @pl.when(s == 2 + h)
                def _():
                    for copy in store(h):
                        copy.start()

    d_x, finish = ring.scatter(partial, land, scatter_sem, work)
    d_values, gain_ref[...] = normal_back(d_x, middle_ref[...], gain_row(params_ref, 1, layer))
    grad = grad_ref[...] + d_values
    mid_ref[...] = grad
    branch_ref[...] = grad.astype(BF16)
    drain()
    finish()
    for half in range(2):
        for copy in swap(half):
            copy.wait_send()
        for copy in store(half):
            copy.wait()


def gather_mix_back_scatter(count, layer, d, side, m_all, share, params, grad, middle, weights, rides):
    rows, width = d.shape
    ff = weights[0].shape[3]
    everyone = pltpu.VMEM((count, rows, width), BF16)
    groups = width // ff
    own = cells((rows, width), F32)
    return ring_call(
        functools.partial(mix_back_kernel, count, layer),
        ("mix_back", layer),
        [(d, ANYWHERE), (side, ANYWHERE), (m_all, ANYWHERE), (share, HERE), (params, HERE), (grad, HERE), (middle, HERE)]
        + [(w, ANYWHERE) for w in weights],
        [
            (own, HERE),
            (cells((rows, width), BF16), HERE),
            (cells((1, width), F32), HERE),
            (cells((3 * width, ff), BF16), ANYWHERE),
            (cells((2, width), F32), HERE),
        ],
        [everyone, everyone, land_scratch(count, rows, width), pltpu.VMEM((2 * rows, width), F32)]
        + expert_scratch(weights)
        + [
            everyone,
            pltpu.VMEM((2, count, rows, 2 * ff), BF16),
            pltpu.VMEM((2, count, rows, ff), BF16),
            pltpu.VMEM((count,) + side.shape, F32),
            pltpu.VMEM((2, 3 * width, ff), BF16),
            pltpu.VMEM((3 * width, ff), BF16),
        ]
        + gather_sems(count, True)
        + scatter_sems(count)
        + dmas((7,), (2, 2 + groups), (2, 2 + groups), (2, 2 + groups)),
        60,
        rides,
    )


def branch_back_kernel(count, layer, riders, *refs):
    inputs, outputs, scratch = split(refs, 3, 2)
    d_ref, w_ref, att_ref = inputs
    datt_ref, g_ref = outputs
    buf, wide_w, acc, mail, got = scratch[:5]
    sems, pair_sem, load_sem = split(scratch[5:], 3, 2)
    ring = Ring(count, riders)
    shard = g_ref.shape[0]
    loads = load_out_weights(w_ref, layer, wide_w, load_sem[0])
    ring.meet(True)
    acc[...] = jnp.zeros_like(acc)

    def compute(place, blocks):
        d = stack(buf, blocks)
        datt = dot(d, wide_w[...], NT).astype(BF16)
        for block, rows in cut(datt, blocks):
            datt_ref[block] = rows
        acc[...] += dot(stack(att_ref, blocks), d, TN)

    drain = ring.gather(
        d_ref, buf, sems, None, after_loads(loads, lambda s: None), ring.meanwhile(compute, 0)
    )
    compute(0, (ring.at(ring.steps),))
    core = lax.rem(lax.axis_index("fsdp"), 2)
    mail[...] = acc[pl.ds(pl.multiple_of((1 - core) * shard, 8), shard), :].astype(BF16)
    swap = remote(mail, got, pair_sem[0].at[0], pair_sem[1].at[0], partner_of("fsdp"))
    swap.start()
    drain()
    swap.wait()
    own = acc[pl.ds(pl.multiple_of(core * shard, 8), shard), :]
    g_ref[...] = (own + got[...].astype(F32)).astype(BF16)


def gather_branch_back(count, layer, d, w, att):
    rows, width = d.shape
    shard = w.shape[2]
    return ring_call(
        functools.partial(branch_back_kernel, count, layer),
        ("branch_back", layer),
        [(d, ANYWHERE), (w, ANYWHERE), (att, HERE)],
        [
            (cells((count, rows, 2 * LANES), BF16), HERE),
            (cells((shard, width), BF16), HERE),
        ],
        [
            pltpu.VMEM((count, rows, width), BF16),
            pltpu.VMEM((2 * LANES, width), BF16),
            pltpu.VMEM((2 * LANES, width), F32),
            pltpu.VMEM((shard, width), BF16),
            pltpu.VMEM((shard, width), BF16),
        ]
        + gather_sems(count)
        + dmas((1,), (1,), (2,)),
        20,
    )


def load_out_weights(w_ref, layer, wide_ref, sem):
    shard = w_ref.shape[2]
    copies = [
        pltpu.make_async_copy(w_ref.at[core, layer], wide_ref.at[pl.ds(core * shard, shard)], sem.at[core])
        for core in range(2)
    ]
    for copy in copies:
        copy.start()
    used = 2 * shard
    wide_ref[used:] = jnp.zeros((wide_ref.shape[0] - used, wide_ref.shape[1]), BF16)
    return copies


def join_kernel(count, layer, riders, *refs):
    inputs, outputs, scratch = split(refs, 13, 4)
    dq_ref, own_ref, other_ref, table_ref, w_ref, x_ref, params_ref, mid_ref, hidden_ref = inputs[:9]
    mixed_ref, router_ref, gain_two_ref = inputs[9:12]
    grad_ref, d_mix_ref, side_ref, g_ref = outputs
    partial, land, rows_ref, tokens, got, weights, last_ref = scratch[:7]
    scatter_sem, pair_sem, load_sem = split(scratch[7:], 2, 2)
    ring = Ring(count, riders)
    loads = [
        pltpu.make_async_copy(x_ref, tokens, load_sem[0].at[0]),
        pltpu.make_async_copy(w_ref.at[layer], weights, load_sem[0].at[1]),
    ]
    for load in loads:
        load.start()
    ring.meet(True)
    swap = remote(other_ref, got, pair_sem[0].at[0], pair_sem[1].at[0], partner_of("fsdp"))
    swap.start()
    swap.wait()
    loads[1].wait()

    def compute(index, carry):
        blocks = 2 * index, 2 * index + 1
        rows = []
        for b in blocks:
            pair = own_ref[b] + got[b].astype(F32)
            cosine, sine = angles(table_ref[b])
            keys = spin(pair, cosine, -sine)
            low = lanes_of(pair) < HD
            middle = jnp.where(low, dq_ref[b, :, LANES:].astype(F32), turn(keys))
            last = jnp.where(low, turn(pair), 0.0)
            rows.append(
                jnp.concatenate([dq_ref[b, :, :LANES], middle.astype(BF16), last.astype(BF16)], 1)
            )
            rows_ref[b] = rows[-1]
        total = dot(jnp.concatenate(rows, 0), weights[...], NT).astype(BF16)
        for block, part in cut(total, blocks):
            partial[block] = part
        return carry

    lax.fori_loop(0, count // 2, compute, 0)
    loads[0].wait()
    strip = g_ref.shape[0] // ring.steps
    tile = 2 * LANES

    def work(s, place):
        if place == 0:
            rows = pl.ds(pl.multiple_of(s * strip, LANES), strip)
            value = dot(flat(tokens[:, :, rows]), flat(rows_ref[...]), TN)
            g_ref[rows, :tile] = value[:, :tile].astype(BF16)
            last_ref[rows] = value[:, tile:]

    d_x, drain = ring.scatter(partial, land, scatter_sem, work)
    d_values, gain_one = normal_back(d_x, hidden_ref[...], gain_row(params_ref, 0, layer))
    grad = mid_ref[...] + d_values
    grad_ref[...] = grad
    d_mix = grad.astype(BF16)
    d_mix_ref[...] = d_mix
    balance = jnp.sum(mixed_ref[...] * d_mix.astype(F32), -1, keepdims=True)
    side_ref[...] = jnp.broadcast_to(as_line(balance), side_ref.shape)
    core = lax.rem(lax.axis_index("fsdp"), 2)
    routers = router_ref[...]
    first, second = routers[0:1], routers[1:2]
    lines = [
        jnp.where(core == 0, first, second),
        jnp.where(core == 0, second, first),
        gain_one,
        gain_two_ref[...],
    ]
    width = g_ref.shape[0]
    tall = jnp.concatenate(
        [jnp.zeros((HD, width), F32)] + lines + [jnp.zeros((HD - len(lines), width), F32)], 0
    )
    g_ref[:, tile:] = (last_ref[...] + tall.T).astype(BF16)
    drain()


def join_scatter(count, layer, dq, own, other, tables, w, x_all, params, mid, hidden, mixed, g_router, gain_two):
    _, rows, width = x_all.shape
    everyone = pltpu.VMEM((count, rows, width), BF16)
    here = [dq, own, other, tables]
    late = [params, mid, hidden, mixed, g_router, gain_two]
    nothing = jnp.zeros((8, LANES), F32)
    return ring_call(
        functools.partial(join_kernel, count, layer),
        ("join", layer),
        [(a, HERE) for a in here] + [(w, ANYWHERE), (x_all, ANYWHERE)] + [(a, HERE) for a in late]
        + [(nothing, HERE)],
        [
            (cells((rows, width), F32), HERE),
            (cells((rows, width), BF16), HERE),
            (cells((8, rows), F32), HERE),
            (cells(w.shape[1:], BF16), HERE),
        ],
        [
            everyone,
            land_scratch(count, rows, width),
            pltpu.VMEM((count, rows, w.shape[2]), BF16),
            everyone,
            pltpu.VMEM(other.shape, BF16),
            pltpu.VMEM(w.shape[1:], BF16),
            pltpu.VMEM((width, LANES), F32),
        ]
        + scatter_sems(count)
        + dmas((1,), (1,), (2,)),
        28,
    )


def finish_kernel(count, replicas, *refs):
    inputs, outputs, scratch = split(refs, 3, 4)
    g_ref, early_ref, early_peer_ref = inputs
    q_out, k_out, v_out, rest_out = outputs
    early, land, total, mine, peer = scratch[:5]
    pair_send, pair_recv, part_send, part_recv, rep_send, rep_recv = scratch[5:]
    me = lax.axis_index("fsdp")
    chip, core = me // 2, lax.rem(me, 2)
    partner = partner_of("fsdp")

    def chip_at(offset):
        return lax.rem(chip + offset + count, count)

    def device(offset):
        return {"fsdp": chip_at(offset) * 2 + core}

    across = [partner_of("rep")] if replicas == 2 else []
    meet([device(offset) for offset in range(1, count)] + [partner] + across)
    swaps = [remote(g_ref.at[:, 1 - core], land.at[0], pair_send.at[0], pair_recv.at[0], partner)]
    swaps[0].start()
    for block in range(count):
        for half in range(2):
            both = early_ref[block, half].astype(F32)
            if replicas == 2:
                both = both + early_peer_ref[block, half].astype(F32)
            early[half, block] = both.astype(BF16)
    swaps.append(remote(early.at[1 - core], land.at[1], pair_send.at[1], pair_recv.at[1], partner))
    swaps[1].start()
    for swap in swaps:
        swap.wait()
    for block in range(count):
        total[block, 0] = (g_ref[block, core].astype(F32) + land[0, block].astype(F32)).astype(BF16)
        total[block, 1] = (early[core, block].astype(F32) + land[1, block].astype(F32)).astype(BF16)
    sends = [
        remote(
            total.at[chip_at(offset)], mine.at[chip],
            part_send.at[offset], part_recv.at[offset], device(offset),
        )
        for offset in range(1, count)
    ]
    for send in sends:
        send.start()
    mine[chip] = total[chip]

    def to_peer(offset):
        slot = chip_at(-offset)
        return remote(mine.at[slot, 0], peer.at[slot], rep_send.at[offset], rep_recv.at[offset], across[0])

    for offset in range(count):
        if offset > 0:
            slot = mine.at[chip_at(-offset)]
            remote(slot, slot, part_send.at[offset], part_recv.at[offset], partner).wait_recv()
        if replicas == 2:
            to_peer(offset).start()
    if replicas == 2:
        for offset in range(count):
            to_peer(offset).wait()

    def tiles(block, layer):
        value = mine[block, layer].astype(F32)
        if replicas == 2 and layer == 0:
            value = value + peer[block].astype(F32)
        return [value[:, i * LANES : (i + 1) * LANES] for i in range(3)]

    for layer in range(LAYERS):
        for half in range(count // 2):
            a, b = tiles(2 * half, layer), tiles(2 * half + 1, layer)
            low = lanes_of(a[0]) < HD
            q_out[layer, :, 3 * half * LANES : 3 * (half + 1) * LANES] = jnp.concatenate(
                [a[0], jnp.where(low, a[1], turn(b[0])), jnp.where(low, turn(b[0]), turn(b[1]))], 1
            )
            here = slice(half * LANES, (half + 1) * LANES)
            k_out[layer, :, here] = jnp.where(low, turn(a[1]), b[1])
            v_out[layer, :, here] = jnp.where(low, a[2], turn(b[2]))
            rest_out[layer, 2 * half] = a[2]
            rest_out[layer, 2 * half + 1] = b[2]
    for send in sends:
        send.wait_send()


def finish_heads(count, replicas, g, early, early_peer):
    _, _, rows, columns = g.shape
    width = count * GROUP * HD
    part = (count, LAYERS, rows, columns)
    dma = pltpu.SemaphoreType.DMA
    return pl.pallas_call(
        functools.partial(finish_kernel, count, replicas),
        out_shape=(
            cells((LAYERS, rows, width), F32),
            cells((LAYERS, rows, count * HD), F32),
            cells((LAYERS, rows, count * HD), F32),
            cells((LAYERS, count, rows, LANES), F32),
        ),
        in_specs=[HERE] * 3,
        out_specs=[HERE] * 4,
        scratch_shapes=[
            pltpu.VMEM((2, count, rows, columns), BF16),
            pltpu.VMEM((2, count, rows, columns), BF16),
            pltpu.VMEM(part, BF16),
            pltpu.VMEM(part, BF16),
            pltpu.VMEM((count, rows, columns), BF16),
            dma((2,)), dma((2,)), dma((count,)), dma((count,)), dma((count,)), dma((count,)),
        ],
        compiler_params=pltpu.CompilerParams(
            collective_id=identity(("finish",)), has_side_effects=True, vmem_limit_bytes=32 << 20
        ),
        cost_estimate=FREE,
        name="finish_heads",
    )(g, early, early_peer)


def add_kernel(layers, *refs):
    out_refs = refs[-3:]
    for layer in range(layers):
        pairs = refs[layer * 10 : (layer + 1) * 10]
        sums = [pairs[i][...].astype(F32) + pairs[i + 5][...].astype(F32) for i in range(5)]
        out_refs[0][layer, 0] = sums[0]
        out_refs[1][layer, 0] = sums[1]
        out_refs[2][layer, 0] = jnp.concatenate(sums[2:], 1)


def add_experts(pairs):
    layers = len(pairs)
    rows, ff = pairs[0][0].shape
    width = rows // 3
    steps = 4
    tall, short = width // steps, ff // steps

    def at(first, length):
        return pl.BlockSpec((length, ff), lambda i: (first // length + i, 0))

    specs = [at(0, tall), at(width, tall)] + [at(2 * width + g * ff, short) for g in range(3)]
    arrays = [array for pair in pairs for array in pair for _ in range(5)]
    return pl.pallas_call(
        functools.partial(add_kernel, layers),
        grid=(steps,),
        out_shape=(
            cells((layers, 1, width, ff), F32),
            cells((layers, 1, width, ff), F32),
            cells((layers, 1, ff, width), F32),
        ),
        in_specs=specs * (2 * layers),
        out_specs=[
            pl.BlockSpec((layers, 1, tall, ff), lambda i: (0, 0, i, 0)),
            pl.BlockSpec((layers, 1, tall, ff), lambda i: (0, 0, i, 0)),
            pl.BlockSpec((layers, 1, short, width), lambda i: (0, 0, i, 0)),
        ],
        cost_estimate=FREE,
        name="add_experts",
    )(*arrays)


def allowed_keys(begin, block, chunk, core):
    shape = (GROUP * LANES, 2 * LANES)
    place = lax.broadcasted_iota(jnp.int32, shape, 1)
    shift = jnp.where(place < LANES, core, -core)
    key = chunk * 2 * LANES + place + shift * LANES
    query = block * LANES + lax.rem(lax.broadcasted_iota(jnp.int32, shape, 0), LANES)
    return (key >= begin) & (key <= query)


def attend_kernel(layer, info_ref, q_ref, own_ref, other_ref, begin_ref, w_ref, att_ref, lse_ref, out_ref, wide_ref, sem):
    step = pl.program_id(0)
    core = info_ref[0]
    block = 2 * step + core
    first = info_ref[1 + step] // (2 * LANES)

    @pl.when(step == 0)
    def _():
        for load in load_out_weights(w_ref, layer, wide_ref, sem):
            load.wait()

    q = q_ref[0].reshape(GROUP * LANES, LANES)
    begin = jnp.concatenate([begin_ref[0]] * GROUP, 0)

    def one(chunk, state):
        top, total, acc = state
        keys = jnp.concatenate([own_ref[chunk], other_ref[chunk]], 0)
        allowed = allowed_keys(begin, block, chunk, core)
        scores = jnp.where(allowed, dot(q, keys, NT), MASKED)
        new_top = jnp.maximum(top, jnp.max(scores, -1, keepdims=True))
        weights = jnp.where(allowed, jnp.exp(scores - new_top), 0.0)
        shrink = jnp.exp(top - new_top)
        total = total * shrink + jnp.sum(weights, -1, keepdims=True)
        return new_top, total, acc * shrink + dot(weights.astype(BF16), keys)

    rows = GROUP * LANES
    top, total, acc = lax.fori_loop(
        first,
        step + 1,
        one,
        (jnp.full((rows, 1), MASKED, F32), jnp.zeros((rows, 1), F32), jnp.zeros((rows, LANES), F32)),
    )
    lse_ref[0] = top + jnp.log(total)
    att = acc / total
    heads = [att[h * LANES : (h + 1) * LANES] for h in range(GROUP)]
    low = lanes_of(heads[0]) < HD
    wide = jnp.concatenate(
        [jnp.where(low, turn(heads[0]), heads[1]), jnp.where(low, turn(heads[2]), 0.0)], 1
    ).astype(BF16)
    att_ref[0] = wide
    out_ref[0] = dot(wide, wide_ref[...]).astype(BF16)


def attend(layer, info, q, own, other, begin, w):
    blocks = q.shape[0]
    width = w.shape[3]
    wide = 2 * LANES
    return pl.pallas_call(
        functools.partial(attend_kernel, layer),
        grid_spec=pltpu.PrefetchScalarGridSpec(
            num_scalar_prefetch=1,
            grid=(blocks,),
            in_specs=[
                pl.BlockSpec((1, GROUP, LANES, LANES), lambda i, s: (i, 0, 0, 0)),
                pl.BlockSpec(own.shape, lambda i, s: (0, 0, 0)),
                pl.BlockSpec(own.shape, lambda i, s: (0, 0, 0)),
                pl.BlockSpec((1, LANES, 1), lambda i, s: (i, 0, 0)),
                ANYWHERE,
            ],
            out_specs=[
                pl.BlockSpec((1, LANES, wide), lambda i, s: (i, 0, 0)),
                pl.BlockSpec((1, GROUP * LANES, 1), lambda i, s: (i, 0, 0)),
                pl.BlockSpec((1, LANES, width), lambda i, s: (i, 0, 0)),
            ],
            scratch_shapes=[pltpu.VMEM((wide, width), BF16), pltpu.SemaphoreType.DMA((2,))],
        ),
        out_shape=(
            jax.ShapeDtypeStruct((blocks, LANES, wide), BF16),
            jax.ShapeDtypeStruct((blocks, GROUP * LANES, 1), F32),
            jax.ShapeDtypeStruct((blocks, LANES, width), BF16),
        ),
        cost_estimate=FREE,
        name="attend",
    )(info, q, own, other, begin, w)


def attend_back_kernel(
    info_ref, q_ref, own_ref, other_ref, begin_ref, att_ref, lse_ref, datt_ref, table_ref,
    dq_ref, d_own_ref, mail_ref, d_other_ref,
):
    step = pl.program_id(0)
    core = info_ref[0]
    block = 2 * step + core
    first = info_ref[1 + step] // (2 * LANES)

    @pl.when(step == 0)
    def _():
        d_own_ref[...] = jnp.zeros_like(d_own_ref)
        d_other_ref[...] = jnp.zeros_like(d_other_ref)

    q = q_ref[0].reshape(GROUP * LANES, LANES)
    begin = jnp.concatenate([begin_ref[0]] * GROUP, 0)

    def spread(wide):
        front, back = wide[:, :LANES], wide[:, LANES:]
        low = lanes_of(front) < HD
        parts = [jnp.where(low, 0.0, part) for part in (turn(front), front, turn(back))]
        return jnp.concatenate(parts, 0)

    datt = spread(datt_ref[0].astype(F32)).astype(BF16)
    att = spread(att_ref[0].astype(F32))
    delta = jnp.sum(datt.astype(F32) * att, -1, keepdims=True)
    lse = lse_ref[0]
    both = jnp.concatenate([q, datt], 0)

    def one(chunk, acc):
        keys = jnp.concatenate([own_ref[chunk], other_ref[chunk]], 0)
        allowed = allowed_keys(begin, block, chunk, core)
        weights = jnp.where(allowed, jnp.exp(dot(q, keys, NT) - lse), 0.0)
        slope = (weights * (dot(datt, keys, NT) - delta)).astype(BF16)
        d_keys = dot(jnp.concatenate([slope, weights.astype(BF16)], 0), both, TN)
        d_own_ref[chunk] += d_keys[:LANES]
        d_other_ref[chunk] += d_keys[LANES:]
        return acc + dot(slope, keys)

    acc = lax.fori_loop(first, step + 1, one, jnp.zeros((GROUP * LANES, LANES), F32))
    heads = [acc[h * LANES : (h + 1) * LANES] * (HD**-0.5) for h in range(GROUP)]
    low = lanes_of(heads[0]) < HD
    cosine, sine = angles(table_ref[0])
    front = spin(jnp.where(low, heads[0], turn(heads[1])), cosine, -sine)
    back = spin(jnp.where(low, heads[2], 0.0), cosine, -sine)
    dq_ref[0] = jnp.concatenate([front, back], 1).astype(BF16)

    @pl.when(step == pl.num_programs(0) - 1)
    def _():
        mail_ref[...] = d_other_ref[...].astype(BF16)


def attend_back(info, q, own, other, begin, att, lse, datt, tables):
    blocks = q.shape[0]
    wide = 2 * LANES

    def block(*shape):
        return pl.BlockSpec((1,) + shape, lambda i, s: (i,) + (0,) * len(shape))

    whole = pl.BlockSpec(own.shape, lambda i, s: (0, 0, 0))
    return pl.pallas_call(
        attend_back_kernel,
        grid_spec=pltpu.PrefetchScalarGridSpec(
            num_scalar_prefetch=1,
            grid=(blocks,),
            in_specs=[
                block(GROUP, LANES, LANES),
                whole,
                whole,
                block(LANES, 1),
                block(LANES, wide),
                block(GROUP * LANES, 1),
                block(LANES, wide),
                block(HD, LANES),
            ],
            out_specs=[block(LANES, wide), whole, whole],
            scratch_shapes=[pltpu.VMEM(own.shape, F32)],
        ),
        out_shape=(
            jax.ShapeDtypeStruct((blocks, LANES, wide), BF16),
            jax.ShapeDtypeStruct(own.shape, F32),
            jax.ShapeDtypeStruct(own.shape, BF16),
        ),
        cost_estimate=FREE,
        name="attend_back",
    )(info, q, own, other, begin, att, lse, datt, tables)


def on_device(
    tokens,
    cotangent,
    positions,
    segments,
    routes,
    attn_gain,
    w_query,
    w_key,
    w_value,
    w_out,
    ffn_gain,
    router,
    w_gate,
    w_up,
    w_down,
):
    rows, width = tokens.shape
    devices = lax.axis_size("fsdp")
    replicas = lax.axis_size("rep")
    count = devices // 2
    me = lax.axis_index("fsdp")
    chip, core = me // 2, lax.rem(me, 2)
    shard = w_query.shape[1]
    experts = devices
    columns = 3 * LANES
    used = (GROUP + 2) * HD
    pairs = [(index, index ^ 1) for index in range(devices)]

    def swap(array):
        return lax.ppermute(array, "fsdp", pairs)

    small = jnp.concatenate(
        [attn_gain, ffn_gain, router.transpose(0, 2, 1).reshape(LAYERS * experts, shard)], 0
    )
    small = jnp.pad(small, ((0, 48 - small.shape[0]), (0, LANES - shard)))
    rate = jnp.exp(-jnp.log(10000.0) * jnp.arange(HD // 2, dtype=F32) / (HD // 2))
    angle = rate[:, None] * positions.astype(F32)[None, :]
    table = jnp.concatenate([jnp.cos(angle), jnp.sin(angle)], 0)
    slabs = jnp.concatenate(
        [
            w_query.reshape(LAYERS, shard, count, GROUP * HD),
            w_key.reshape(LAYERS, shard, count, HD),
            w_value.reshape(LAYERS, shard, count, HD),
            jnp.zeros((LAYERS, shard, count, columns - used), BF16),
        ],
        -1,
    ).transpose(2, 0, 1, 3)
    heads_w, outs_w, smalls, tables = exchange_weights(count, slabs, w_out, small, table)
    heads_w = heads_w.reshape(LAYERS, width, columns)
    params = smalls[:, : (2 + experts) * LAYERS, :shard].transpose(1, 0, 2).reshape(-1, width)
    params = params.astype(F32)
    own_w, _ = lax.optimization_barrier(([w_gate, w_up, w_down], smalls))
    experts_w = own_w + [swap(w) for w in own_w]

    flat_segments = segments.reshape(1, -1)
    kinds = jnp.arange(8, dtype=jnp.int32)[:, None]
    starts = jnp.sum((flat_segments < kinds).astype(jnp.int32), 1, keepdims=True)
    begin = jnp.sum(jnp.where(flat_segments == kinds, starts, 0), 0).reshape(count, 2, rows)
    begin = lax.dynamic_index_in_dim(begin, core, 1, False)
    info = jnp.concatenate([core[None], begin[:, 0]]).astype(jnp.int32)
    begin = begin[:, :, None]

    hidden = tokens.astype(F32)
    x_attn = (normal(hidden)[1] * params[0:1]).astype(BF16)
    chosen = routes.transpose(0, 2, 1)
    saved = []
    for layer in range(LAYERS):
        query, kv, kv_other, x_all = gather_project(count, layer, x_attn, heads_w, tables)
        att, lse, partial = attend(layer, info, query, kv, kv_other, begin, outs_w)
        middle, x_moe, share = scatter_route(count, layer, partial, hidden, params, chosen)
        mixed, after, x_attn, m_all, share_all = gather_mix_scatter(
            count, layer, x_moe, share, middle, params, experts_w
        )
        saved.append((hidden, x_all, query, kv, kv_other, att, lse, middle, mixed, m_all, share_all))
        hidden = after
    activations = x_attn

    def across(array):
        return lax.ppermute(array, "rep", [(0, 1), (1, 0)]) if replicas == 2 else array

    grad, d_mix = cotangent.astype(F32), cotangent
    balance = jnp.sum(saved[-1][8] * grad, -1)
    side = jnp.broadcast_to(balance[None, :], (8, rows))
    expert_sums = [None] * LAYERS
    out_sums = [None] * LAYERS
    for layer in reversed(range(LAYERS)):
        hidden, x_all, query, kv, kv_other, att, lse, middle, mixed, m_all, share_all = saved[layer]
        rides = [out_sums[layer + 1], early] if layer + 1 < LAYERS and replicas == 2 else []
        grad_mid, d_branch, gain_two, expert_sum, g_router, *rode = gather_mix_back_scatter(
            count, layer, d_mix, side, m_all, share_all, params, grad, middle, experts_w, rides
        )
        if layer + 1 < LAYERS:
            d_branch, expert_sums[layer + 1] = lax.optimization_barrier(
                (d_branch, expert_sums[layer + 1])
            )
        expert_sums[layer] = (expert_sum, across(expert_sum))
        datt, out_sum = gather_branch_back(count, layer, d_branch, outs_w, att)
        out_sums[layer] = out_sum
        d_query, d_own, d_other = attend_back(
            info, query, kv, kv_other, begin, att, lse, datt, tables
        )
        grad, d_mix, side, heads = join_scatter(
            count, layer, d_query, d_own, d_other, tables, heads_w, x_all, params, grad_mid, hidden,
            saved[max(layer - 1, 0)][8], g_router, gain_two,
        )
        heads = heads.reshape(count, 2, shard, columns)
        early = heads if layer > 0 else early
    g_query, g_key, g_value, rest = finish_heads(
        count, replicas, heads, early, rode[1] if rode else early
    )
    if replicas == 2:
        g_gate, g_up, g_down = add_experts(expert_sums)
        arrived = [across(out_sums[0]), rode[0]]
        g_out = jnp.stack([a.astype(F32) + b.astype(F32) for a, b in zip(out_sums, arrived)])
    else:
        g_query, g_key, g_value, rest, g_out, flat_sums = [
            lax.psum(array.astype(BF16), "rep").astype(F32)
            for array in (
                g_query, g_key, g_value, rest,
                jnp.stack(out_sums),
                jnp.stack([own for own, _ in expert_sums]),
            )
        ]
        ff = w_gate.shape[3]
        g_gate, g_up = flat_sums[:, None, :width], flat_sums[:, None, width : 2 * width]
        g_down = flat_sums[:, 2 * width :].reshape(LAYERS, width // ff, ff, ff)
        g_down = g_down.transpose(0, 2, 1, 3).reshape(LAYERS, 1, ff, width)
    rest = rest[..., HD : HD + 4]
    gains = jnp.sum(rest, 1)
    g_router = rest[..., :2].transpose(0, 2, 1, 3).reshape(LAYERS, shard, experts)
    return (
        activations,
        grad,
        gains[..., 2],
        g_query,
        g_key,
        g_value,
        g_out,
        gains[..., 3],
        g_router,
        g_gate,
        g_up,
        g_down,
    )


def solution(mesh):
    placed = (
        P(("rep", "fsdp"), None),
        P(("rep", "fsdp"), None),
        P(("rep", "fsdp")),
        P("rep", None),
        P(None, ("rep", "fsdp"), None),
        P(None, "fsdp"),
        P(None, "fsdp", None),
        P(None, "fsdp", None),
        P(None, "fsdp", None),
        P(None, "fsdp", None),
        P(None, "fsdp"),
        P(None, "fsdp", None),
        P(None, "fsdp", None, None),
        P(None, "fsdp", None, None),
        P(None, "fsdp", None, None),
    )
    return jax.shard_map(
        on_device,
        mesh=mesh,
        in_specs=placed,
        out_specs=(
            P(("rep", "fsdp"), None),
            P(("rep", "fsdp"), None),
            P(None, "fsdp"),
            P(None, "fsdp", None),
            P(None, "fsdp", None),
            P(None, "fsdp", None),
            P(None, "fsdp", None),
            P(None, "fsdp"),
            P(None, "fsdp", None),
            P(None, "fsdp", None, None),
            P(None, "fsdp", None, None),
            P(None, "fsdp", None, None),
        ),
        check_vma=False,
    )
```

```python
import functools

import jax
import jax.numpy as jnp
from jax import lax
from jax.experimental import pallas as pl
from jax.experimental.pallas import tpu as pltpu
from jax.sharding import PartitionSpec as P

HEADS = 24
KV_HEADS = 8
HD = 64
LAYERS = 2
GROUP = HEADS // KV_HEADS
LANES = 128
PAIR = 2
EPS = 1e-06
MASKED = -1e30
MESH = pl.DeviceIdType.MESH
F32 = jnp.float32
BF16 = jnp.bfloat16


def ring_place(chip, count):
    return lax.select(lax.rem(chip, 2) == 0, chip // 2, count - 1 - chip // 2)


def ring_chip(place, count):
    return lax.select(place < count // 2, 2 * place, 2 * (count - 1 - place) + 1)


def ring_setup(count):
    me = lax.axis_index("fsdp")
    chip, core = me // 2, lax.rem(me, 2)
    place = ring_place(chip, count)

    def at(offset):
        return ring_chip(lax.rem(place + offset + 2 * count, count), count)

    near = [{"fsdp": at(1) * 2 + core}, {"fsdp": at(-1) * 2 + core}]
    return chip, at, near


def partner_of(axis):
    if axis == "rep":
        return {"rep": 1 - lax.axis_index("rep")}
    me = lax.axis_index("fsdp")
    return {"fsdp": me + 1 - 2 * lax.rem(me, 2)}


def meet(others):
    barrier = pltpu.get_barrier_semaphore()
    for other in others:
        pl.semaphore_signal(barrier, inc=1, device_id=other, device_id_type=MESH)
    pl.semaphore_wait(barrier, len(others))


def remote(src, dst, send_sem, recv_sem, device):
    return pltpu.make_async_remote_copy(
        src_ref=src,
        dst_ref=dst,
        send_sem=send_sem,
        recv_sem=recv_sem,
        device_id=device,
        device_id_type=MESH,
    )


def ring_hops(count):
    half = count // 2
    return {(0, 0): half, (1, 1): half, (0, 1): half - 1, (1, 0): half - 1}


IDENTITIES = {}


def identity(key):
    return IDENTITIES.setdefault(key, len(IDENTITIES))


class Ring:
    def __init__(self, count, traffic):
        self.count = count
        self.riders, self.early, self.late = traffic
        self.steps = count // 2
        self.chip, self.at, self.near = ring_setup(count)

    def meet(self, partner=False):
        others = self.near + ([partner_of("fsdp")] if partner else [])
        meet(others + ([partner_of("rep")] if self.riders else []))
        for rider in self.riders:
            rider.start()
        for copy in self.early:
            copy.wait()

    def settle(self):
        for copy in self.late:
            copy.wait()

    def gather(self, x_ref, buf, sems, side=None, first=None, second=None):
        own_sem, send_sem, recv_sem = sems[:3]
        half_rows = x_ref.shape[0] // 2
        steps = self.steps
        own = [pltpu.make_async_copy(x_ref, buf.at[self.chip], own_sem.at[0])]
        if side is not None:
            side_ref, side_buf = side
            side_send, side_recv = sems[3:]
            own.append(pltpu.make_async_copy(side_ref, side_buf.at[self.chip], own_sem.at[1]))
        for copy in own:
            copy.start()

        def piece(key, step, block, source=None):
            direction, part = key
            rows = pl.ds(part * half_rows, half_rows)
            target = buf.at[block, rows]
            return remote(
                target if source is None else source.at[rows],
                target,
                send_sem.at[direction, part, step],
                recv_sem.at[direction, part, step],
                self.near[direction],
            )

        def side_piece(direction, step, block, source=None):
            target = side_buf.at[block]
            return remote(
                target if source is None else source,
                target,
                side_send.at[direction, step],
                side_recv.at[direction, step],
                self.near[direction],
            )

        def toward(key, places):
            return self.at(-places if key[0] == 0 else places)

        early, late = [(0, 0), (1, 1)], [(0, 1), (1, 0)]
        if side is not None:
            for direction in range(2):
                side_piece(direction, 0, self.chip, side_ref).start()
        for key in early + late:
            piece(key, 0, self.chip, x_ref).start()

        def step(s, carry):
            if side is not None:
                for direction in range(2):

                    @pl.when(s <= steps - direction)
                    def _():
                        block = toward((direction, 0), s)
                        side_piece(direction, s - 1, block).wait_recv()

                        @pl.when(s < steps - direction)
                        def _():
                            side_piece(direction, s, block).start()

            for key in early:
                block = toward(key, s)
                piece(key, s - 1, block).wait_recv()

                @pl.when(s < steps)
                def _():
                    piece(key, s, block).start()

            if first is not None:
                first(s)

            @pl.when(s < steps)
            def _():
                for key in late:
                    block = toward(key, s)
                    piece(key, s - 1, block).wait_recv()

                    @pl.when(s < steps - 1)
                    def _():
                        piece(key, s, block).start()

            if second is not None:
                second(s)
            return carry

        for copy in own:
            copy.wait()
        lax.fori_loop(1, steps + 1, step, 0)

        def drain():
            for s in range(steps):
                for key in early + (late if s < steps - 1 else []):
                    piece(key, s, toward(key, s)).wait_send()
                if side is not None:
                    for direction in range(2):
                        if s < steps - direction:
                            side_piece(direction, s, toward((direction, 0), s)).wait_send()

        return drain

    def pair(self, s):
        return self.at(s), self.at(-s)

    def meanwhile(self, compute, place):
        def run(s):
            @pl.when(s == 1)
            def _():
                compute(place, (self.chip,))

            @pl.when(s > 1)
            def _():
                compute(place, self.pair(s - 1))

        return run

    def scatter(self, partial, land, sems, work=None, source=None, ready=None):
        send_sem, recv_sem = sems
        source = partial if source is None else source
        half_rows = partial.shape[1] // 2
        steps = self.steps
        hops = ring_hops(self.count)

        def ahead(key, s):
            places = hops[key] - s
            return self.at(places if key[0] == 0 else -places)

        def piece(key, s, source):
            direction, part = key
            return remote(
                source,
                land.at[direction, part, s],
                send_sem.at[direction, part, s],
                recv_sem.at[direction, part, s],
                self.near[direction],
            )

        def rows_of(key):
            return pl.ds(key[1] * half_rows, half_rows)

        for key in hops:
            piece(key, 0, source.at[ahead(key, 0), rows_of(key)]).start()
        if ready is not None:
            ready()

        def step(s, carry):
            for place, key in enumerate(hops):
                if work is not None:
                    work(s - 1, place)

                @pl.when(s < hops[key])
                def _():
                    slot = land.at[key[0], key[1], s - 1]
                    piece(key, s - 1, slot).wait_recv()
                    mine = partial[ahead(key, s), rows_of(key)]
                    slot[...] = (slot[...].astype(F32) + mine.astype(F32)).astype(BF16)
                    piece(key, s, slot).start()

            return carry

        lax.fori_loop(1, steps + 1, step, 0)
        for key in hops:
            slot = land.at[key[0], key[1], hops[key] - 1]
            piece(key, hops[key] - 1, slot).wait_recv()
        halves = []
        for part in range(2):
            rows = pl.ds(part * half_rows, half_rows)
            total = partial[self.chip, rows].astype(F32)
            for direction in range(2):
                total = total + land[direction, part, hops[direction, part] - 1].astype(F32)
            halves.append(total)
        summed = jnp.concatenate(halves, 0)

        def drain():
            for key in hops:
                for s in range(hops[key]):
                    piece(key, s, land.at[key[0], key[1], s]).wait_send()

        return summed, drain


def dmas(*shapes):
    return [pltpu.SemaphoreType.DMA(shape) for shape in shapes]


def gather_sems(count, sided=False):
    steps = count // 2
    shapes = [(2,), (2, 2, steps), (2, 2, steps)]
    return dmas(*(shapes + ([(2, steps), (2, steps)] if sided else [])))


def scatter_sems(count):
    return dmas((2, 2, count // 2), (2, 2, count // 2))


ANYWHERE = pl.BlockSpec(memory_space=pltpu.HBM)
HERE = pl.BlockSpec(memory_space=pltpu.VMEM)
EARLY, LATE = "early", "late"
OUT = "out"


FREE = pl.CostEstimate(flops=0, bytes_accessed=0, transcendentals=0)


def ring_call(body, key, inputs, outputs, scratch, megabytes, rides=()):
    n_in, n_out, n_rides = len(inputs), len(outputs), len(rides)
    in_kinds = [kind for _, kind in inputs]
    out_kinds = [kind for _, kind in outputs]
    copied = [a for a, kind in inputs if kind in (EARLY, LATE)]
    returned = [a for a, kind in outputs if kind == OUT]
    moves = len(copied) + len(returned)

    def kernel(*refs):
        ins, ride_in, outs, ride_out, rest = split(refs, n_in, n_rides, n_out, n_rides)
        rest, own, rest_sems = rest[: len(scratch)], rest[len(scratch) : len(scratch) + moves], rest[len(scratch) + moves :]
        move_sem, rest_sems = rest_sems[0], rest_sems[1:]
        riders = []
        if n_rides:
            send_sem, recv_sem = rest_sems
            riders = [
                remote(ride_in[i], ride_out[i], send_sem.at[i], recv_sem.at[i], partner_of("rep"))
                for i in range(n_rides)
            ]
        used = 0
        early, late, leaving = [], [], []
        ins, outs = list(ins), list(outs)
        for i, kind in enumerate(in_kinds):
            if kind in (EARLY, LATE):
                copy = pltpu.make_async_copy(ins[i], own[used], move_sem.at[used])
                copy.start()
                (early if kind == EARLY else late).append(copy)
                ins[i] = own[used]
                used += 1
        for i, kind in enumerate(out_kinds):
            if kind == OUT:
                leaving.append(pltpu.make_async_copy(own[used], outs[i], move_sem.at[used]))
                outs[i] = own[used]
                used += 1
        body((riders, early, late), *ins, *outs, *rest)
        for copy in leaving:
            copy.start()
        for rider in riders:
            rider.wait()
        for copy in leaving:
            copy.wait()

    def spec(kind):
        return ANYWHERE if isinstance(kind, str) else kind

    return pl.pallas_call(
        kernel,
        out_shape=tuple(shape for shape, _ in outputs) + tuple(cells(a.shape, a.dtype) for a in rides),
        in_specs=[spec(kind) for kind in in_kinds] + [ANYWHERE] * n_rides,
        out_specs=[spec(kind) for kind in out_kinds] + [ANYWHERE] * n_rides,
        scratch_shapes=list(scratch)
        + [pltpu.VMEM(a.shape, a.dtype) for a in copied + returned]
        + dmas((max(moves, 1),))
        + (dmas((n_rides,), (n_rides,)) if n_rides else []),
        compiler_params=pltpu.CompilerParams(
            collective_id=identity(key),
            has_side_effects=True,
            vmem_limit_bytes=megabytes << 20,
        ),
        cost_estimate=FREE,
        name=key[0],
    )(*[array for array, _ in inputs], *rides)


def split(refs, *sizes):
    parts, place = [], 0
    for size in sizes:
        parts.append(refs[place : place + size])
        place += size
    return parts + [refs[place:]]


def cells(shape, dtype):
    return jax.ShapeDtypeStruct(shape, dtype)


def setup_kernel(
    count, slab_ref, out_w_ref, small_ref, table_ref,
    heads_ref, outs_ref, smalls_ref, tables_ref,
    own_sem, slab_send, slab_recv, pass_send, pass_recv,
    small_send, small_recv, table_send, table_recv, out_send, out_recv,
):
    devices = 2 * count
    me = lax.axis_index("fsdp")
    chip, core = me // 2, lax.rem(me, 2)
    layers = slab_ref.shape[1]

    def device(offset):
        return {"fsdp": lax.rem(me + offset, devices)}

    def chip_at(offset):
        return lax.rem(chip + offset + count, count)

    partner = partner_of("fsdp")
    meet([device(offset) for offset in range(1, devices)])
    copies = [
        pltpu.make_async_copy(slab_ref.at[chip, layer], heads_ref.at[layer, me], own_sem.at[layer])
        for layer in range(layers)
    ] + [
        pltpu.make_async_copy(small_ref, smalls_ref.at[me], own_sem.at[layers]),
        pltpu.make_async_copy(table_ref, tables_ref.at[chip], own_sem.at[layers + 1]),
        pltpu.make_async_copy(out_w_ref, outs_ref.at[core], own_sem.at[layers + 2]),
    ]
    sends = [
        remote(small_ref, smalls_ref.at[me], small_send.at[offset], small_recv.at[offset], device(offset))
        for offset in range(1, devices)
    ]
    for offset in range(1, count):
        there = {"fsdp": chip_at(offset) * 2 + core}
        sends.append(
            remote(table_ref, tables_ref.at[chip], table_send.at[offset], table_recv.at[offset], there)
        )
        for layer in range(layers):
            sends.append(
                remote(
                    slab_ref.at[chip_at(offset), layer], heads_ref.at[layer, me],
                    slab_send.at[offset, layer], slab_recv.at[offset, layer], there,
                )
            )
    for layer in range(layers):
        sends.append(
            remote(
                slab_ref.at[chip, layer], heads_ref.at[layer, me],
                pass_send.at[0, layer], pass_recv.at[0, layer], partner,
            )
        )
    sends.append(remote(out_w_ref, outs_ref.at[core], out_send.at[0], out_recv.at[0], partner))
    for copy in copies + sends:
        copy.start()
    for offset in range(1, count):
        origin = chip_at(-offset) * 2 + core
        for layer in range(layers):
            slot = heads_ref.at[layer, origin]
            remote(slot, slot, slab_send.at[offset, layer], slab_recv.at[offset, layer], partner).wait_recv()
            forward = remote(slot, slot, pass_send.at[offset, layer], pass_recv.at[offset, layer], partner)
            forward.start()
    for offset in range(1, count):
        origin = chip_at(-offset)
        table = tables_ref.at[origin]
        remote(table, table, table_send.at[offset], table_recv.at[offset], partner).wait_recv()
    for offset in range(count):
        origin = chip_at(-offset) * 2 + 1 - core
        mine = chip_at(-offset) * 2 + core
        for layer in range(layers):
            slot, sent = heads_ref.at[layer, origin], heads_ref.at[layer, mine]
            if offset > 0:
                remote(sent, sent, pass_send.at[offset, layer], pass_recv.at[offset, layer], partner).wait_send()
            remote(slot, slot, pass_send.at[offset, layer], pass_recv.at[offset, layer], partner).wait_recv()
    for offset in range(1, devices):
        slot = smalls_ref.at[lax.rem(me - offset + devices, devices)]
        remote(slot, slot, small_send.at[offset], small_recv.at[offset], partner).wait_recv()
    other = outs_ref.at[1 - core]
    remote(other, other, out_send.at[0], out_recv.at[0], partner).wait_recv()
    for copy in copies:
        copy.wait()
    for send in sends:
        send.wait_send()


def exchange_weights(count, slabs, out_w, small, table):
    layers = slabs.shape[1]
    devices = 2 * count
    dma = pltpu.SemaphoreType.DMA
    anywhere = pl.BlockSpec(memory_space=pl.ANY)
    return pl.pallas_call(
        functools.partial(setup_kernel, count),
        out_shape=(
            jax.ShapeDtypeStruct((layers, devices) + slabs.shape[2:], slabs.dtype),
            jax.ShapeDtypeStruct((2,) + out_w.shape, out_w.dtype),
            jax.ShapeDtypeStruct((devices,) + small.shape, small.dtype),
            jax.ShapeDtypeStruct((count,) + table.shape, table.dtype),
        ),
        in_specs=[anywhere] * 4,
        out_specs=[anywhere] * 4,
        scratch_shapes=[
            dma((layers + 3,)),
            dma((count, layers)),
            dma((count, layers)),
            dma((count, layers)),
            dma((count, layers)),
            dma((devices,)),
            dma((devices,)),
            dma((count,)),
            dma((count,)),
            dma((1,)),
            dma((1,)),
        ],
        compiler_params=pltpu.CompilerParams(
            collective_id=identity(("setup",)), has_side_effects=True
        ),
        cost_estimate=FREE,
        name="exchange_weights",
    )(slabs, out_w, small, table)


def dot(left, right, contract=((1,), (0,))):
    return lax.dot_general(left, right, (contract, ((), ())), preferred_element_type=F32)


NT = ((1,), (1,))
TN = ((0,), (0,))


def lanes_of(field):
    return lax.broadcasted_iota(jnp.int32, field.shape, 1)


def turn(field):
    return pltpu.roll(field, HD, 1)


def spin(field, cosine, sine):
    swapped = jnp.where(
        lax.rem(lanes_of(field), HD) < HD // 2,
        -pltpu.roll(field, LANES - HD // 2, 1),
        pltpu.roll(field, HD // 2, 1),
    )
    return field * cosine + swapped * sine


def project_rows(rows, cosine, sine):
    first = spin(rows[:, :LANES], cosine, sine)
    second = spin(rows[:, LANES : 2 * LANES], cosine, sine)
    third = rows[:, 2 * LANES :]
    low = lanes_of(first) < HD
    heads = []
    for field in (first, turn(first), second):
        rounded = jnp.where(low, field, 0.0).astype(BF16).astype(F32)
        heads.append((rounded * (HD**-0.5)).astype(BF16))
    return heads, jnp.where(low, turn(second), turn(third)).astype(BF16)


def angles(table):
    rows = jnp.concatenate([table, table], 0).T
    early = lax.rem(lanes_of(rows), HD) < HD // 2
    cosine = jnp.where(early, rows, pltpu.roll(rows, HD // 2, 1))
    sine = jnp.where(early, pltpu.roll(rows, LANES - HD // 2, 1), rows)
    return cosine, sine


def normal(values):
    inverse = lax.rsqrt(jnp.mean(values * values, -1, keepdims=True) + EPS)
    return inverse, values * inverse


def normal_back(d_x, values, gain):
    inverse, normed = normal(values)
    d_norm = d_x * gain
    d_values = inverse * (d_norm - normed * jnp.mean(d_norm * normed, -1, keepdims=True))
    return d_values, jnp.sum(d_x * normed, 0, keepdims=True)


def diagonal():
    shape = (LANES, LANES)
    return lax.broadcasted_iota(jnp.int32, shape, 0) == lax.broadcasted_iota(jnp.int32, shape, 1)


def as_column(line):
    return jnp.sum(jnp.where(diagonal(), jnp.broadcast_to(line, (LANES, LANES)), 0.0), 1, keepdims=True)


def as_line(column):
    return jnp.sum(jnp.where(diagonal(), jnp.broadcast_to(column, (LANES, LANES)), 0.0), 0, keepdims=True)


def flat(value):
    return value.reshape(value.shape[0] * value.shape[1], value.shape[2])


def stack(ref, blocks):
    parts = [ref[b] for b in blocks]
    return parts[0] if len(parts) == 1 else jnp.concatenate(parts, 0)


def cut(value, blocks):
    return [(b, value[i * LANES : (i + 1) * LANES]) for i, b in enumerate(blocks)]


def gain_row(params_ref, kind, layer):
    row = kind * LAYERS + layer
    return params_ref[row : row + 1, :]


def router_rows(experts, layer):
    first = 2 * LAYERS + layer * experts
    return slice(first, first + experts)


def project_kernel(count, layer, traffic, *refs):
    inputs, outputs, scratch = split(refs, 3, 4)
    x_ref, w_ref, table_ref = inputs
    q_ref, own_ref, other_ref, all_ref = outputs
    buf, weights, q_buf, own_buf = scratch[:4]
    sems, pair_sems, out_sem, load_sem = split(scratch[4:], 3, 2, 1)
    ring = Ring(count, traffic)
    load = pltpu.make_async_copy(w_ref.at[layer], weights, load_sem[0].at[0])
    load.start()
    ring.meet(True)
    partner = partner_of("fsdp")

    def pass_on(block):
        return [
            remote(
                own_buf.at[block], other_ref.at[block], pair_sems[0].at[block], pair_sems[1].at[block], partner
            ),
            pltpu.make_async_copy(own_buf.at[block], own_ref.at[block], out_sem[0].at[0, block]),
            pltpu.make_async_copy(q_buf.at[block], q_ref.at[block], out_sem[0].at[1, block]),
        ]

    def compute(place, blocks):
        rows = dot(stack(buf, blocks), weights[...])
        tables = [angles(table_ref[b]) for b in blocks]
        cosine = jnp.concatenate([t[0] for t in tables], 0)
        sine = jnp.concatenate([t[1] for t in tables], 0)
        heads, pair = project_rows(rows, cosine, sine)
        for index, head in enumerate(heads):
            for block, part in cut(head, blocks):
                q_buf[block, index] = part
        for block, part in cut(pair, blocks):
            own_buf[block] = part
            for copy in pass_on(block):
                copy.start()

    def first(s):
        @pl.when(s == 1)
        def _():
            load.wait()

    drain = ring.gather(x_ref, buf, sems, None, first, ring.meanwhile(compute, 0))
    keep = pltpu.make_async_copy(buf, all_ref, out_sem[0].at[2, 0])
    keep.start()
    compute(0, (ring.at(ring.steps),))
    drain()
    for block in range(count):
        for copy in pass_on(block):
            copy.wait()
    keep.wait()


def gather_project(count, layer, x, w, tables):
    rows, width = x.shape
    block = cells((count, rows, LANES), BF16)
    queries = (count, GROUP, rows, LANES)
    return ring_call(
        functools.partial(project_kernel, count, layer),
        ("project", layer),
        [(x, ANYWHERE), (w, ANYWHERE), (tables, EARLY)],
        [
            (cells(queries, BF16), ANYWHERE),
            (block, ANYWHERE),
            (block, ANYWHERE),
            (cells((count, rows, width), BF16), ANYWHERE),
        ],
        [
            pltpu.VMEM((count, rows, width), BF16),
            pltpu.VMEM(w.shape[1:], BF16),
            pltpu.VMEM(queries, BF16),
            pltpu.VMEM(block.shape, BF16),
        ]
        + gather_sems(count)
        + dmas((count,), (count,), (3, count), (1,)),
        20,
    )


def route_kernel(count, layer, traffic, *refs):
    inputs, outputs, scratch = split(refs, 4, 3)
    p_ref, hidden_ref, params_ref, routes_ref = inputs
    middle_ref, x_ref, share_ref = outputs
    partial, land = scratch[:2]
    sems, load_sem = split(scratch[2:], 2)
    ring = Ring(count, traffic)
    load = pltpu.make_async_copy(p_ref, partial, load_sem[0].at[0])
    load.start()
    ring.meet()
    added, drain = ring.scatter(partial, land, sems, None, p_ref, load.wait)
    ring.settle()
    middle = hidden_ref[...] + added
    middle_ref[...] = middle
    x = (normal(middle)[1] * gain_row(params_ref, 1, layer)).astype(BF16)
    x_ref[...] = x
    experts = share_ref.shape[0]
    logits = dot(params_ref[router_rows(experts, layer), :].astype(BF16), x, NT)
    expert = lax.broadcasted_iota(jnp.int32, logits.shape, 0)
    named = expert < 0
    for choice in range(routes_ref.shape[1]):
        named = named | (expert == routes_ref[layer, choice : choice + 1, :])
    scores = jnp.where(named, logits, MASKED)
    weights = jnp.where(named, jnp.exp(scores - jnp.max(scores, 0, keepdims=True)), 0.0)
    share_ref[...] = weights / jnp.sum(weights, 0, keepdims=True)
    drain()


def scatter_route(count, layer, partial, hidden, params, routes):
    _, rows, width = partial.shape
    experts = 2 * count
    return ring_call(
        functools.partial(route_kernel, count, layer),
        ("route", layer),
        [(partial, ANYWHERE), (hidden, LATE), (params, LATE), (routes, LATE)],
        [
            (cells((rows, width), F32), OUT),
            (cells((rows, width), BF16), OUT),
            (cells((experts, rows), F32), OUT),
        ],
        [pltpu.VMEM(partial.shape, BF16), land_scratch(count, rows, width)]
        + scatter_sems(count)
        + dmas((1,)),
        20,
    )


def load_experts(refs, layer, gates, ups, downs, sem):
    copies = []
    for e in range(2):
        for place, buf in enumerate((gates, ups, downs)):
            source = refs[3 * e + place].at[layer, 0]
            copies.append(pltpu.make_async_copy(source, buf.at[e], sem.at[3 * e + place]))
    for copy in copies:
        copy.start()
    return copies


def expert_of(e):
    me = lax.axis_index("fsdp")
    return me if e == 0 else me + 1 - 2 * lax.rem(me, 2)


def share_of(share_ref, e, blocks):
    columns = [as_column(share_ref[b, pl.ds(expert_of(e), 1), :]) for b in blocks]
    return jnp.concatenate(columns, 0) if len(columns) > 1 else columns[0]


def after_loads(loads, run):
    def first(s):
        @pl.when(s == 1)
        def _():
            for load in loads:
                load.wait()

        run(s)

    return first


def mix_kernel(count, layer, traffic, *refs):
    inputs, outputs, scratch = split(refs, 10, 5)
    x_ref, side_ref, middle_ref, params_ref = inputs[:4]
    mixed_ref, hidden_ref, next_ref, all_ref, share_ref = outputs
    buf, partial, land, acc, gates, ups, downs = scratch[:7]
    sems, scatter_sem, load_sem, out_sem = split(scratch[7:], 5, 2, 1)
    ring = Ring(count, traffic)
    loads = load_experts(inputs[4:], layer, gates, ups, downs, load_sem[0])
    ring.meet()

    def compute(e, blocks):
        x = stack(buf, blocks)
        act_gate, act_up = dot(x, gates[e]), dot(x, ups[e])
        hidden = jax.nn.silu(act_gate) * act_up * share_of(share_ref, e, blocks)
        part = dot(hidden.astype(BF16), downs[e])
        if e == 0:
            acc[: x.shape[0]] = part
        else:
            total = (acc[: x.shape[0]] + part).astype(BF16)
            for block, rows in cut(total, blocks):
                partial[block] = rows

    drain = ring.gather(
        x_ref, buf, sems, (side_ref, share_ref),
        after_loads(loads, ring.meanwhile(compute, 0)), ring.meanwhile(compute, 1),
    )
    keep = pltpu.make_async_copy(buf, all_ref, out_sem[0].at[0])
    keep.start()
    for e in range(2):
        compute(e, (ring.at(ring.steps),))
    mixed, finish = ring.scatter(partial, land, scatter_sem)
    ring.settle()
    mixed_ref[...] = mixed
    hidden = middle_ref[...] + mixed
    hidden_ref[...] = hidden
    if layer + 1 < LAYERS:
        next_ref[...] = (normal(hidden)[1] * gain_row(params_ref, 0, layer + 1)).astype(BF16)
    else:
        next_ref[...] = hidden.astype(BF16)
    drain()
    finish()
    keep.wait()


def expert_scratch(weights):
    return [pltpu.VMEM((2,) + w.shape[2:], BF16) for w in weights[:3]]


def land_scratch(count, rows, width):
    return pltpu.VMEM((2, 2, count // 2, rows // 2, width), BF16)


def gather_mix_scatter(count, layer, x, share, middle, params, weights):
    rows, width = x.shape
    everyone = pltpu.VMEM((count, rows, width), BF16)
    own = cells((rows, width), F32)
    return ring_call(
        functools.partial(mix_kernel, count, layer),
        ("mix", layer),
        [(x, ANYWHERE), (share, ANYWHERE), (middle, LATE), (params, LATE)]
        + [(w, ANYWHERE) for w in weights],
        [
            (own, OUT),
            (own, OUT),
            (cells((rows, width), BF16), OUT),
            (cells((count, rows, width), BF16), ANYWHERE),
            (cells((count,) + share.shape, F32), OUT),
        ],
        [everyone, everyone, land_scratch(count, rows, width), pltpu.VMEM((2 * rows, width), F32)]
        + expert_scratch(weights)
        + gather_sems(count, True)
        + scatter_sems(count)
        + dmas((6,), (1,)),
        56,
    )


def mix_back_kernel(count, layer, traffic, *refs):
    inputs, outputs, scratch = split(refs, 13, 5)
    d_ref, side_ref, m_ref, share_ref, params_ref, grad_ref, middle_ref = inputs[:7]
    mid_ref, branch_ref, gain_ref, sum_ref, g_router_ref = outputs
    buf, partial, land, acc, gates, ups, downs = scratch[:7]
    tokens, acts, hiddens, balance_ref, totals, got = scratch[7:13]
    sems, scatter_sem, load_sem, pair_sem, out_sem = split(scratch[13:], 5, 2, 1, 2)
    ring = Ring(count, traffic)
    loads = load_experts(inputs[7:], layer, gates, ups, downs, load_sem[0])
    loads.append(pltpu.make_async_copy(m_ref, tokens, load_sem[0].at[6]))
    loads[-1].start()
    ring.meet(True)
    ff = gates.shape[2]
    width = buf.shape[2]
    g_router_ref[...] = jnp.zeros_like(g_router_ref)
    routers = 2 * LAYERS + layer * 2 * count

    def compute(e, blocks):
        d, x = stack(buf, blocks), stack(tokens, blocks)
        share = share_of(share_ref, e, blocks)
        balance = [as_column(balance_ref[b, 0:1, :]) for b in blocks]
        balance = jnp.concatenate(balance, 0) if len(balance) > 1 else balance[0]
        act_gate, act_up = dot(x, gates[e]), dot(x, ups[e])
        sig = jax.nn.sigmoid(act_gate)
        swish = act_gate * sig
        hidden = swish * act_up
        raw = dot(d, downs[e], NT)
        d_logit = share * (jnp.sum(hidden * raw, -1, keepdims=True) - balance)
        d_hidden = raw * share
        d_gate = (d_hidden * act_up * sig * (1.0 + act_gate * (1.0 - sig))).astype(BF16)
        d_up = (d_hidden * swish).astype(BF16)
        weighted = (hidden * share).astype(BF16)
        part = dot(d_gate, gates[e], NT) + dot(d_up, ups[e], NT)
        part = part + d_logit * params_ref[pl.ds(routers + expert_of(e), 1), :]
        g_router_ref[e : e + 1, :] += jnp.sum(d_logit * x.astype(F32), 0, keepdims=True)
        for place, block in enumerate(blocks):
            here = slice(place * LANES, (place + 1) * LANES)
            acts[e, block, :, :ff] = d_gate[here]
            acts[e, block, :, ff:] = d_up[here]
            hiddens[e, block] = weighted[here]
        if e == 0:
            acc[: x.shape[0]] = part
        else:
            total = (acc[: x.shape[0]] + part).astype(BF16)
            for block, rows in cut(total, blocks):
                partial[block] = rows

    drain = ring.gather(
        d_ref, buf, sems, (side_ref, balance_ref),
        after_loads(loads, ring.meanwhile(compute, 0)), ring.meanwhile(compute, 1),
    )
    for e in range(2):
        compute(e, (ring.at(ring.steps),))

    partner = partner_of("fsdp")
    strip = 2 * LANES
    strips = width // (2 * strip)
    groups = width // ff

    def regions(half):
        regions = [(group * width + half * (width // 2), width // 2) for group in range(2)]
        return regions + [(2 * width + group * ff + half * (ff // 2), ff // 2) for group in range(groups)]

    def swap(half):
        return [
            remote(
                totals.at[1, pl.ds(first, length)], got.at[pl.ds(first, length)],
                pair_sem[0].at[half, index], pair_sem[1].at[half, index], partner,
            )
            for index, (first, length) in enumerate(regions(half))
        ]

    def store(half):
        return [
            pltpu.make_async_copy(
                totals.at[0, pl.ds(first, length)], sum_ref.at[pl.ds(first, length)], out_sem[0].at[half, index]
            )
            for index, (first, length) in enumerate(regions(half))
        ]

    def work(s, place):
        e = 1 - s // 2
        half = lax.rem(s, 2)

        def put(first, value):
            rows = pl.ds(pl.multiple_of(first, strip), strip)

            @pl.when(s < 2)
            def _():
                totals[1, rows] = value.astype(BF16)

            @pl.when(s >= 2)
            def _():
                totals[0, rows] = (value + got[rows].astype(F32)).astype(BF16)

        if place == 0:
            for h in range(2):

                @pl.when(s == 2 + h)
                def _():
                    for copy in swap(h):
                        copy.wait_recv()

        if place < strips:
            first = (half * strips + place) * strip
            columns = pl.ds(pl.multiple_of(first, strip), strip)
            value = dot(flat(tokens[:, :, columns]), flat(acts[e]), TN)
            for group in range(2):
                put(group * width + first, value[:, group * ff : (group + 1) * ff])
        if place == 3:
            columns = pl.ds(pl.multiple_of(half * strip, strip), strip)
            value = dot(flat(hiddens[e, :, :, columns]), flat(buf[...]), TN)
            for group in range(groups):
                put(2 * width + group * ff + half * strip, value[:, group * ff : (group + 1) * ff])
            for h in range(2):

                @pl.when(s == h)
                def _():
                    for copy in swap(h):
                        copy.start()

                @pl.when(s == 2 + h)
                def _():
                    for copy in store(h):
                        copy.start()

    d_x, finish = ring.scatter(partial, land, scatter_sem, work)
    ring.settle()
    d_values, gain_ref[...] = normal_back(d_x, middle_ref[...], gain_row(params_ref, 1, layer))
    grad = grad_ref[...] + d_values
    mid_ref[...] = grad
    branch_ref[...] = grad.astype(BF16)
    drain()
    finish()
    for half in range(2):
        for copy in swap(half):
            copy.wait_send()
        for copy in store(half):
            copy.wait()


def gather_mix_back_scatter(count, layer, d, side, m_all, share, params, grad, middle, weights, rides):
    rows, width = d.shape
    ff = weights[0].shape[3]
    everyone = pltpu.VMEM((count, rows, width), BF16)
    groups = width // ff
    own = cells((rows, width), F32)
    return ring_call(
        functools.partial(mix_back_kernel, count, layer),
        ("mix_back", layer),
        [(d, ANYWHERE), (side, ANYWHERE), (m_all, ANYWHERE), (share, EARLY), (params, EARLY), (grad, LATE), (middle, LATE)]
        + [(w, ANYWHERE) for w in weights],
        [
            (own, OUT),
            (cells((rows, width), BF16), OUT),
            (cells((1, width), F32), OUT),
            (cells((3 * width, ff), BF16), ANYWHERE),
            (cells((2, width), F32), OUT),
        ],
        [everyone, everyone, land_scratch(count, rows, width), pltpu.VMEM((2 * rows, width), F32)]
        + expert_scratch(weights)
        + [
            everyone,
            pltpu.VMEM((2, count, rows, 2 * ff), BF16),
            pltpu.VMEM((2, count, rows, ff), BF16),
            pltpu.VMEM((count,) + side.shape, F32),
            pltpu.VMEM((2, 3 * width, ff), BF16),
            pltpu.VMEM((3 * width, ff), BF16),
        ]
        + gather_sems(count, True)
        + scatter_sems(count)
        + dmas((7,), (2, 2 + groups), (2, 2 + groups), (2, 2 + groups)),
        60,
        rides,
    )


def branch_back_kernel(count, layer, traffic, *refs):
    inputs, outputs, scratch = split(refs, 3, 2)
    d_ref, w_ref, att_ref = inputs
    datt_ref, g_ref = outputs
    buf, wide_w, acc, mail, got = scratch[:5]
    sems, pair_sem, load_sem = split(scratch[5:], 3, 2)
    ring = Ring(count, traffic)
    shard = g_ref.shape[0]
    loads = load_out_weights(w_ref, layer, wide_w, load_sem[0])
    ring.meet(True)
    acc[...] = jnp.zeros_like(acc)

    def compute(place, blocks):
        d = stack(buf, blocks)
        datt = dot(d, wide_w[...], NT).astype(BF16)
        for block, rows in cut(datt, blocks):
            datt_ref[block] = rows
        acc[...] += dot(stack(att_ref, blocks), d, TN)

    drain = ring.gather(
        d_ref, buf, sems, None, after_loads(loads, lambda s: None), ring.meanwhile(compute, 0)
    )
    compute(0, (ring.at(ring.steps),))
    core = lax.rem(lax.axis_index("fsdp"), 2)
    mail[...] = acc[pl.ds(pl.multiple_of((1 - core) * shard, 8), shard), :].astype(BF16)
    swap = remote(mail, got, pair_sem[0].at[0], pair_sem[1].at[0], partner_of("fsdp"))
    swap.start()
    drain()
    swap.wait()
    own = acc[pl.ds(pl.multiple_of(core * shard, 8), shard), :]
    g_ref[...] = (own + got[...].astype(F32)).astype(BF16)


def gather_branch_back(count, layer, d, w, att):
    rows, width = d.shape
    shard = w.shape[2]
    return ring_call(
        functools.partial(branch_back_kernel, count, layer),
        ("branch_back", layer),
        [(d, ANYWHERE), (w, ANYWHERE), (att, EARLY)],
        [
            (cells((count, rows, 2 * LANES), BF16), OUT),
            (cells((shard, width), BF16), OUT),
        ],
        [
            pltpu.VMEM((count, rows, width), BF16),
            pltpu.VMEM((2 * LANES, width), BF16),
            pltpu.VMEM((2 * LANES, width), F32),
            pltpu.VMEM((shard, width), BF16),
            pltpu.VMEM((shard, width), BF16),
        ]
        + gather_sems(count)
        + dmas((1,), (1,), (2,)),
        20,
    )


def load_out_weights(w_ref, layer, wide_ref, sem):
    shard = w_ref.shape[2]
    copies = [
        pltpu.make_async_copy(w_ref.at[core, layer], wide_ref.at[pl.ds(core * shard, shard)], sem.at[core])
        for core in range(2)
    ]
    for copy in copies:
        copy.start()
    used = 2 * shard
    wide_ref[used:] = jnp.zeros((wide_ref.shape[0] - used, wide_ref.shape[1]), BF16)
    return copies


def join_kernel(count, layer, traffic, *refs):
    inputs, outputs, scratch = split(refs, 12, 4)
    dq_ref, own_ref, other_ref, table_ref, w_ref, x_ref, params_ref, mid_ref, hidden_ref = inputs[:9]
    mixed_ref, router_ref, gain_two_ref = inputs[9:12]
    grad_ref, d_mix_ref, side_ref, g_ref = outputs
    partial, land, rows_ref, tokens, got, weights, last_ref = scratch[:7]
    scatter_sem, pair_sem, load_sem = split(scratch[7:], 2, 2)
    ring = Ring(count, traffic)
    loads = [
        pltpu.make_async_copy(x_ref, tokens, load_sem[0].at[0]),
        pltpu.make_async_copy(w_ref.at[layer], weights, load_sem[0].at[1]),
    ]
    for load in loads:
        load.start()
    ring.meet(True)
    swap = remote(other_ref, got, pair_sem[0].at[0], pair_sem[1].at[0], partner_of("fsdp"))
    swap.start()
    swap.wait()
    loads[1].wait()

    def compute(index, carry):
        blocks = 2 * index, 2 * index + 1
        rows = []
        for b in blocks:
            pair = own_ref[b] + got[b].astype(F32)
            cosine, sine = angles(table_ref[b])
            keys = spin(pair, cosine, -sine)
            low = lanes_of(pair) < HD
            middle = jnp.where(low, dq_ref[b, :, LANES:].astype(F32), turn(keys))
            last = jnp.where(low, turn(pair), 0.0)
            rows.append(
                jnp.concatenate([dq_ref[b, :, :LANES], middle.astype(BF16), last.astype(BF16)], 1)
            )
            rows_ref[b] = rows[-1]
        total = dot(jnp.concatenate(rows, 0), weights[...], NT).astype(BF16)
        for block, part in cut(total, blocks):
            partial[block] = part
        return carry

    lax.fori_loop(0, count // 2, compute, 0)
    loads[0].wait()
    strip = g_ref.shape[0] // ring.steps
    tile = 2 * LANES

    def work(s, place):
        if place == 0:
            rows = pl.ds(pl.multiple_of(s * strip, LANES), strip)
            value = dot(flat(tokens[:, :, rows]), flat(rows_ref[...]), TN)
            g_ref[rows, :tile] = value[:, :tile].astype(BF16)
            last_ref[rows] = value[:, tile:]

    d_x, drain = ring.scatter(partial, land, scatter_sem, work)
    ring.settle()
    d_values, gain_one = normal_back(d_x, hidden_ref[...], gain_row(params_ref, 0, layer))
    grad = mid_ref[...] + d_values
    grad_ref[...] = grad
    d_mix = grad.astype(BF16)
    d_mix_ref[...] = d_mix
    balance = jnp.sum(mixed_ref[...] * d_mix.astype(F32), -1, keepdims=True)
    side_ref[...] = jnp.broadcast_to(as_line(balance), side_ref.shape)
    core = lax.rem(lax.axis_index("fsdp"), 2)
    routers = router_ref[...]
    first, second = routers[0:1], routers[1:2]
    lines = [
        jnp.where(core == 0, first, second),
        jnp.where(core == 0, second, first),
        gain_one,
        gain_two_ref[...],
    ]
    width = g_ref.shape[0]
    tall = jnp.concatenate(
        [jnp.zeros((HD, width), F32)] + lines + [jnp.zeros((HD - len(lines), width), F32)], 0
    )
    g_ref[:, tile:] = (last_ref[...] + tall.T).astype(BF16)
    drain()


def join_scatter(count, layer, dq, own, other, tables, w, x_all, params, mid, hidden, mixed, g_router, gain_two):
    _, rows, width = x_all.shape
    everyone = pltpu.VMEM((count, rows, width), BF16)
    late = [params, mid, hidden, mixed, g_router, gain_two]
    return ring_call(
        functools.partial(join_kernel, count, layer),
        ("join", layer),
        [(dq, EARLY), (own, EARLY), (other, ANYWHERE), (tables, EARLY), (w, ANYWHERE), (x_all, ANYWHERE)]
        + [(a, LATE) for a in late],
        [
            (cells((rows, width), F32), OUT),
            (cells((rows, width), BF16), OUT),
            (cells((8, rows), F32), OUT),
            (cells(w.shape[1:], BF16), OUT),
        ],
        [
            everyone,
            land_scratch(count, rows, width),
            pltpu.VMEM((count, rows, w.shape[2]), BF16),
            everyone,
            pltpu.VMEM(other.shape, BF16),
            pltpu.VMEM(w.shape[1:], BF16),
            pltpu.VMEM((width, LANES), F32),
        ]
        + scatter_sems(count)
        + dmas((1,), (1,), (2,)),
        28,
    )


def finish_kernel(count, replicas, *refs):
    inputs, outputs, scratch = split(refs, 3, 4)
    g_ref, early_ref, early_peer_ref = inputs
    q_out, k_out, v_out, rest_out = outputs
    early, land, total, mine, peer = scratch[:5]
    pair_send, pair_recv, part_send, part_recv, rep_send, rep_recv = scratch[5:]
    me = lax.axis_index("fsdp")
    chip, core = me // 2, lax.rem(me, 2)
    partner = partner_of("fsdp")

    def chip_at(offset):
        return lax.rem(chip + offset + count, count)

    def device(offset):
        return {"fsdp": chip_at(offset) * 2 + core}

    across = [partner_of("rep")] if replicas == 2 else []
    meet([device(offset) for offset in range(1, count)] + [partner] + across)
    swaps = [remote(g_ref.at[:, 1 - core], land.at[0], pair_send.at[0], pair_recv.at[0], partner)]
    swaps[0].start()
    for block in range(count):
        for half in range(2):
            both = early_ref[block, half].astype(F32)
            if replicas == 2:
                both = both + early_peer_ref[block, half].astype(F32)
            early[half, block] = both.astype(BF16)
    swaps.append(remote(early.at[1 - core], land.at[1], pair_send.at[1], pair_recv.at[1], partner))
    swaps[1].start()
    for swap in swaps:
        swap.wait()
    for block in range(count):
        total[block, 0] = (g_ref[block, core].astype(F32) + land[0, block].astype(F32)).astype(BF16)
        total[block, 1] = (early[core, block].astype(F32) + land[1, block].astype(F32)).astype(BF16)
    sends = [
        remote(
            total.at[chip_at(offset)], mine.at[chip],
            part_send.at[offset], part_recv.at[offset], device(offset),
        )
        for offset in range(1, count)
    ]
    for send in sends:
        send.start()
    mine[chip] = total[chip]

    def to_peer(offset):
        slot = chip_at(-offset)
        return remote(mine.at[slot, 0], peer.at[slot], rep_send.at[offset], rep_recv.at[offset], across[0])

    for offset in range(count):
        if offset > 0:
            slot = mine.at[chip_at(-offset)]
            remote(slot, slot, part_send.at[offset], part_recv.at[offset], partner).wait_recv()
        if replicas == 2:
            to_peer(offset).start()
    if replicas == 2:
        for offset in range(count):
            to_peer(offset).wait()

    def tiles(block, layer):
        value = mine[block, layer].astype(F32)
        if replicas == 2 and layer == 0:
            value = value + peer[block].astype(F32)
        return [value[:, i * LANES : (i + 1) * LANES] for i in range(3)]

    for layer in range(LAYERS):
        for half in range(count // 2):
            a, b = tiles(2 * half, layer), tiles(2 * half + 1, layer)
            low = lanes_of(a[0]) < HD
            q_out[layer, :, 3 * half * LANES : 3 * (half + 1) * LANES] = jnp.concatenate(
                [a[0], jnp.where(low, a[1], turn(b[0])), jnp.where(low, turn(b[0]), turn(b[1]))], 1
            )
            here = slice(half * LANES, (half + 1) * LANES)
            k_out[layer, :, here] = jnp.where(low, turn(a[1]), b[1])
            v_out[layer, :, here] = jnp.where(low, a[2], turn(b[2]))
            rest_out[layer, 2 * half] = a[2]
            rest_out[layer, 2 * half + 1] = b[2]
    for send in sends:
        send.wait_send()


def finish_heads(count, replicas, g, early, early_peer):
    _, _, rows, columns = g.shape
    width = count * GROUP * HD
    part = (count, LAYERS, rows, columns)
    dma = pltpu.SemaphoreType.DMA
    return pl.pallas_call(
        functools.partial(finish_kernel, count, replicas),
        out_shape=(
            cells((LAYERS, rows, width), F32),
            cells((LAYERS, rows, count * HD), F32),
            cells((LAYERS, rows, count * HD), F32),
            cells((LAYERS, count, rows, LANES), F32),
        ),
        in_specs=[HERE] * 3,
        out_specs=[HERE] * 4,
        scratch_shapes=[
            pltpu.VMEM((2, count, rows, columns), BF16),
            pltpu.VMEM((2, count, rows, columns), BF16),
            pltpu.VMEM(part, BF16),
            pltpu.VMEM(part, BF16),
            pltpu.VMEM((count, rows, columns), BF16),
            dma((2,)), dma((2,)), dma((count,)), dma((count,)), dma((count,)), dma((count,)),
        ],
        compiler_params=pltpu.CompilerParams(
            collective_id=identity(("finish",)), has_side_effects=True, vmem_limit_bytes=32 << 20
        ),
        cost_estimate=FREE,
        name="finish_heads",
    )(g, early, early_peer)


def add_kernel(layers, *refs):
    out_refs = refs[-3:]
    for layer in range(layers):
        pairs = refs[layer * 10 : (layer + 1) * 10]
        sums = [pairs[i][...].astype(F32) + pairs[i + 5][...].astype(F32) for i in range(5)]
        out_refs[0][layer, 0] = sums[0]
        out_refs[1][layer, 0] = sums[1]
        out_refs[2][layer, 0] = jnp.concatenate(sums[2:], 1)


def add_experts(pairs):
    layers = len(pairs)
    rows, ff = pairs[0][0].shape
    width = rows // 3
    steps = 4
    tall, short = width // steps, ff // steps

    def at(first, length):
        return pl.BlockSpec((length, ff), lambda i: (first // length + i, 0))

    specs = [at(0, tall), at(width, tall)] + [at(2 * width + g * ff, short) for g in range(3)]
    arrays = [array for pair in pairs for array in pair for _ in range(5)]
    return pl.pallas_call(
        functools.partial(add_kernel, layers),
        grid=(steps,),
        out_shape=(
            cells((layers, 1, width, ff), F32),
            cells((layers, 1, width, ff), F32),
            cells((layers, 1, ff, width), F32),
        ),
        in_specs=specs * (2 * layers),
        out_specs=[
            pl.BlockSpec((layers, 1, tall, ff), lambda i: (0, 0, i, 0)),
            pl.BlockSpec((layers, 1, tall, ff), lambda i: (0, 0, i, 0)),
            pl.BlockSpec((layers, 1, short, width), lambda i: (0, 0, i, 0)),
        ],
        cost_estimate=FREE,
        name="add_experts",
    )(*arrays)


def chunk_keys(own_ref, other_ref, chunk):
    return jnp.concatenate([own_ref[chunk], other_ref[chunk]], 0)


def allowed_keys(begin, query, chunk, core):
    shape = (2 * LANES, begin.shape[1])
    place = lax.broadcasted_iota(jnp.int32, shape, 0)
    shift = jnp.where(place < LANES, core, -core)
    key = chunk * 2 * LANES + place + shift * LANES
    return (key >= begin) & (key <= query)


def block_info(info_ref, begin_ref):
    step = pl.program_id(0)
    core = info_ref[0]
    lane = lax.broadcasted_iota(jnp.int32, (1, LANES), 1)
    begin, query = [], []
    for part in range(PAIR):
        begin += [begin_ref[part]] * GROUP
        query += [(2 * (PAIR * step + part) + core) * LANES + lane] * GROUP
    first = info_ref[1 + PAIR * step] // (2 * LANES)
    return core, jnp.concatenate(begin, 1), jnp.concatenate(query, 1), first, PAIR * (step + 1)


def chunk_keys(own_ref, other_ref, chunk):
    return jnp.concatenate([own_ref[chunk], other_ref[chunk]], 0)


def turn_keys(own_ref, other_ref, turned_ref):
    for chunk in range(turned_ref.shape[0]):
        turned_ref[chunk] = chunk_keys(own_ref, other_ref, chunk).astype(F32).T.astype(BF16)


def by_head(field):
    return [field[:, h * LANES : (h + 1) * LANES].T for h in range(GROUP)]


def attend_kernel(layer, info_ref, q_ref, own_ref, other_ref, begin_ref, w_ref, att_ref, lse_ref, out_ref, wide_ref, turned_ref, score_ref, sem):
    core, begin, query, first, last = block_info(info_ref, begin_ref)
    width = PAIR * GROUP * LANES

    @pl.when(pl.program_id(0) == 0)
    def _():
        loads = load_out_weights(w_ref, layer, wide_ref, sem)
        turn_keys(own_ref, other_ref, turned_ref)
        for load in loads:
            load.wait()

    q = q_ref[...].reshape(width, LANES)

    def score(chunk, top):
        keys = chunk_keys(own_ref, other_ref, chunk)
        scores = jnp.where(allowed_keys(begin, query, chunk, core), dot(keys, q, NT), MASKED)
        score_ref[chunk] = scores
        return jnp.maximum(top, jnp.max(scores, 0, keepdims=True))

    top = lax.fori_loop(first, last, score, jnp.full((1, width), MASKED, F32))

    def add(chunk, state):
        total, acc = state
        weights = jnp.exp(score_ref[chunk] - top)
        total = total + jnp.sum(weights, 0, keepdims=True)
        return total, acc + dot(turned_ref[chunk], weights.astype(BF16))

    total, acc = lax.fori_loop(
        first, last, add, (jnp.zeros((1, width), F32), jnp.zeros((LANES, width), F32))
    )
    lse = top + jnp.log(total)
    att = acc / total
    rows = []
    for part in range(PAIR):
        here = slice(part * GROUP * LANES, (part + 1) * GROUP * LANES)
        lse_ref[part] = lse[:, here]
        heads = by_head(att[:, here])
        low = lanes_of(heads[0]) < HD
        rows.append(
            jnp.concatenate(
                [jnp.where(low, turn(heads[0]), heads[1]), jnp.where(low, turn(heads[2]), 0.0)], 1
            ).astype(BF16)
        )
        att_ref[part] = rows[-1]
    out = dot(jnp.concatenate(rows, 0), wide_ref[...]).astype(BF16)
    for part in range(PAIR):
        out_ref[part] = out[part * LANES : (part + 1) * LANES]


def blocks_of(*shape):
    return pl.BlockSpec((PAIR,) + shape, lambda i, s: (i,) + (0,) * len(shape))


def attend(layer, info, q, own, other, begin, w):
    blocks = q.shape[0]
    width = w.shape[3]
    wide = 2 * LANES
    whole = pl.BlockSpec(own.shape, lambda i, s: (0, 0, 0))
    return pl.pallas_call(
        functools.partial(attend_kernel, layer),
        grid_spec=pltpu.PrefetchScalarGridSpec(
            num_scalar_prefetch=1,
            grid=(blocks // PAIR,),
            in_specs=[
                blocks_of(GROUP, LANES, LANES), whole, whole, blocks_of(1, LANES), ANYWHERE,
            ],
            out_specs=[
                blocks_of(LANES, wide), blocks_of(1, GROUP * LANES), blocks_of(LANES, width),
            ],
            scratch_shapes=[
                pltpu.VMEM((wide, width), BF16),
                pltpu.VMEM((blocks, LANES, wide), BF16),
                pltpu.VMEM((blocks, wide, PAIR * GROUP * LANES), F32),
                pltpu.SemaphoreType.DMA((2,)),
            ],
        ),
        out_shape=(
            cells((blocks, LANES, wide), BF16),
            cells((blocks, 1, GROUP * LANES), F32),
            cells((blocks, LANES, width), BF16),
        ),
        compiler_params=pltpu.CompilerParams(vmem_limit_bytes=28 << 20),
        cost_estimate=FREE,
        name="attend",
    )(info, q, own, other, begin, w)


def attend_back_kernel(
    info_ref, q_ref, own_ref, other_ref, begin_ref, att_ref, lse_ref, datt_ref, table_ref,
    dq_ref, d_own_ref, mail_ref, d_other_ref, turned_ref,
):
    core, begin, query, first, last = block_info(info_ref, begin_ref)
    width = PAIR * GROUP * LANES

    @pl.when(pl.program_id(0) == 0)
    def _():
        turn_keys(own_ref, other_ref, turned_ref)
        d_own_ref[...] = jnp.zeros_like(d_own_ref)
        d_other_ref[...] = jnp.zeros_like(d_other_ref)

    q = q_ref[...].reshape(width, LANES)

    def spread(wide):
        front, back = wide[:, :LANES], wide[:, LANES:]
        low = lanes_of(front) < HD
        return [jnp.where(low, 0.0, part) for part in (turn(front), front, turn(back))]

    slopes, deltas = [], []
    for part in range(PAIR):
        for d, a in zip(spread(datt_ref[part].astype(F32)), spread(att_ref[part].astype(F32))):
            slopes.append(d)
            deltas.append(jnp.sum((d * a).T, 0, keepdims=True))
    datt = jnp.concatenate(slopes, 0).astype(BF16)
    delta = jnp.concatenate(deltas, 1)
    lse = jnp.concatenate([lse_ref[part] for part in range(PAIR)], 1)
    both = jnp.concatenate([q, datt], 0)

    def one(chunk, acc):
        keys = chunk_keys(own_ref, other_ref, chunk)
        scores = jnp.where(allowed_keys(begin, query, chunk, core), dot(keys, q, NT), MASKED)
        weights = jnp.exp(scores - lse)
        slope = (weights * (dot(keys, datt, NT) - delta)).astype(BF16)
        d_keys = dot(jnp.concatenate([slope, weights.astype(BF16)], 1), both)
        d_own_ref[chunk] += d_keys[:LANES]
        d_other_ref[chunk] += d_keys[LANES:]
        return acc + dot(turned_ref[chunk], slope)

    acc = lax.fori_loop(first, last, one, jnp.zeros((LANES, width), F32)) * (HD**-0.5)
    for part in range(PAIR):
        heads = by_head(acc[:, part * GROUP * LANES : (part + 1) * GROUP * LANES])
        low = lanes_of(heads[0]) < HD
        cosine, sine = angles(table_ref[part])
        front = spin(jnp.where(low, heads[0], turn(heads[1])), cosine, -sine)
        back = spin(jnp.where(low, heads[2], 0.0), cosine, -sine)
        dq_ref[part] = jnp.concatenate([front, back], 1).astype(BF16)

    @pl.when(pl.program_id(0) == pl.num_programs(0) - 1)
    def _():
        mail_ref[...] = d_other_ref[...].astype(BF16)


def attend_back(info, q, own, other, begin, att, lse, datt, tables):
    blocks = q.shape[0]
    wide = 2 * LANES
    whole = pl.BlockSpec(own.shape, lambda i, s: (0, 0, 0))
    return pl.pallas_call(
        attend_back_kernel,
        grid_spec=pltpu.PrefetchScalarGridSpec(
            num_scalar_prefetch=1,
            grid=(blocks // PAIR,),
            in_specs=[
                blocks_of(GROUP, LANES, LANES),
                whole,
                whole,
                blocks_of(1, LANES),
                blocks_of(LANES, wide),
                blocks_of(1, GROUP * LANES),
                blocks_of(LANES, wide),
                blocks_of(HD, LANES),
            ],
            out_specs=[blocks_of(LANES, wide), whole, whole],
            scratch_shapes=[pltpu.VMEM(own.shape, F32), pltpu.VMEM((blocks, LANES, wide), BF16)],
        ),
        out_shape=(
            cells((blocks, LANES, wide), BF16),
            cells(own.shape, F32),
            cells(own.shape, BF16),
        ),
        compiler_params=pltpu.CompilerParams(vmem_limit_bytes=28 << 20),
        cost_estimate=FREE,
        name="attend_back",
    )(info, q, own, other, begin, att, lse, datt, tables)


def on_device(
    tokens,
    cotangent,
    positions,
    segments,
    routes,
    attn_gain,
    w_query,
    w_key,
    w_value,
    w_out,
    ffn_gain,
    router,
    w_gate,
    w_up,
    w_down,
):
    rows, width = tokens.shape
    devices = lax.axis_size("fsdp")
    replicas = lax.axis_size("rep")
    count = devices // 2
    me = lax.axis_index("fsdp")
    chip, core = me // 2, lax.rem(me, 2)
    shard = w_query.shape[1]
    experts = devices
    columns = 3 * LANES
    used = (GROUP + 2) * HD
    pairs = [(index, index ^ 1) for index in range(devices)]

    def swap(array):
        return lax.ppermute(array, "fsdp", pairs)

    small = jnp.concatenate(
        [attn_gain, ffn_gain, router.transpose(0, 2, 1).reshape(LAYERS * experts, shard)], 0
    )
    small = jnp.pad(small, ((0, 48 - small.shape[0]), (0, LANES - shard)))
    rate = jnp.exp(-jnp.log(10000.0) * jnp.arange(HD // 2, dtype=F32) / (HD // 2))
    angle = rate[:, None] * positions.astype(F32)[None, :]
    table = jnp.concatenate([jnp.cos(angle), jnp.sin(angle)], 0)
    slabs = jnp.concatenate(
        [
            w_query.reshape(LAYERS, shard, count, GROUP * HD),
            w_key.reshape(LAYERS, shard, count, HD),
            w_value.reshape(LAYERS, shard, count, HD),
            jnp.zeros((LAYERS, shard, count, columns - used), BF16),
        ],
        -1,
    ).transpose(2, 0, 1, 3)
    heads_w, outs_w, smalls, tables = exchange_weights(count, slabs, w_out, small, table)
    heads_w = heads_w.reshape(LAYERS, width, columns)
    params = smalls[:, : (2 + experts) * LAYERS, :shard].transpose(1, 0, 2).reshape(-1, width)
    params = params.astype(F32)
    own_w, _ = lax.optimization_barrier(([w_gate, w_up, w_down], smalls))
    experts_w = own_w + [swap(w) for w in own_w]

    flat_segments = segments.reshape(1, -1)
    kinds = jnp.arange(8, dtype=jnp.int32)[:, None]
    starts = jnp.sum((flat_segments < kinds).astype(jnp.int32), 1, keepdims=True)
    begin = jnp.sum(jnp.where(flat_segments == kinds, starts, 0), 0).reshape(count, 2, rows)
    begin = lax.dynamic_index_in_dim(begin, core, 1, False)
    info = jnp.concatenate([core[None], begin[:, 0]]).astype(jnp.int32)
    begin = begin[:, None, :]

    hidden = tokens.astype(F32)
    x_attn = (normal(hidden)[1] * params[0:1]).astype(BF16)
    chosen = routes.transpose(0, 2, 1)
    saved = []
    for layer in range(LAYERS):
        query, kv, kv_other, x_all = gather_project(count, layer, x_attn, heads_w, tables)
        att, lse, partial = attend(layer, info, query, kv, kv_other, begin, outs_w)
        middle, x_moe, share = scatter_route(count, layer, partial, hidden, params, chosen)
        mixed, after, x_attn, m_all, share_all = gather_mix_scatter(
            count, layer, x_moe, share, middle, params, experts_w
        )
        saved.append((hidden, x_all, query, kv, kv_other, att, lse, middle, mixed, m_all, share_all))
        hidden = after
    activations = x_attn

    def across(array):
        return lax.ppermute(array, "rep", [(0, 1), (1, 0)]) if replicas == 2 else array

    grad, d_mix = cotangent.astype(F32), cotangent
    balance = jnp.sum(saved[-1][8] * grad, -1)
    side = jnp.broadcast_to(balance[None, :], (8, rows))
    expert_sums = [None] * LAYERS
    out_sums = [None] * LAYERS
    for layer in reversed(range(LAYERS)):
        hidden, x_all, query, kv, kv_other, att, lse, middle, mixed, m_all, share_all = saved[layer]
        rides = [out_sums[layer + 1], early] if layer + 1 < LAYERS and replicas == 2 else []
        grad_mid, d_branch, gain_two, expert_sum, g_router, *rode = gather_mix_back_scatter(
            count, layer, d_mix, side, m_all, share_all, params, grad, middle, experts_w, rides
        )
        if layer + 1 < LAYERS:
            d_branch, expert_sums[layer + 1] = lax.optimization_barrier(
                (d_branch, expert_sums[layer + 1])
            )
        expert_sums[layer] = (expert_sum, across(expert_sum))
        datt, out_sum = gather_branch_back(count, layer, d_branch, outs_w, att)
        out_sums[layer] = out_sum
        d_query, d_own, d_other = attend_back(
            info, query, kv, kv_other, begin, att, lse, datt, tables
        )
        grad, d_mix, side, heads = join_scatter(
            count, layer, d_query, d_own, d_other, tables, heads_w, x_all, params, grad_mid, hidden,
            saved[max(layer - 1, 0)][8], g_router, gain_two,
        )
        heads = heads.reshape(count, 2, shard, columns)
        early = heads if layer > 0 else early
    g_query, g_key, g_value, rest = finish_heads(
        count, replicas, heads, early, rode[1] if rode else early
    )
    if replicas == 2:
        g_gate, g_up, g_down = add_experts(expert_sums)
        arrived = [across(out_sums[0]), rode[0]]
        g_out = jnp.stack([a.astype(F32) + b.astype(F32) for a, b in zip(out_sums, arrived)])
    else:
        g_query, g_key, g_value, rest, g_out, flat_sums = [
            lax.psum(array.astype(BF16), "rep").astype(F32)
            for array in (
                g_query, g_key, g_value, rest,
                jnp.stack(out_sums),
                jnp.stack([own for own, _ in expert_sums]),
            )
        ]
        ff = w_gate.shape[3]
        g_gate, g_up = flat_sums[:, None, :width], flat_sums[:, None, width : 2 * width]
        g_down = flat_sums[:, 2 * width :].reshape(LAYERS, width // ff, ff, ff)
        g_down = g_down.transpose(0, 2, 1, 3).reshape(LAYERS, 1, ff, width)
    rest = rest[..., HD : HD + 4]
    gains = jnp.sum(rest, 1)
    g_router = rest[..., :2].transpose(0, 2, 1, 3).reshape(LAYERS, shard, experts)
    return (
        activations,
        grad,
        gains[..., 2],
        g_query,
        g_key,
        g_value,
        g_out,
        gains[..., 3],
        g_router,
        g_gate,
        g_up,
        g_down,
    )


def solution(mesh):
    placed = (
        P(("rep", "fsdp"), None),
        P(("rep", "fsdp"), None),
        P(("rep", "fsdp")),
        P("rep", None),
        P(None, ("rep", "fsdp"), None),
        P(None, "fsdp"),
        P(None, "fsdp", None),
        P(None, "fsdp", None),
        P(None, "fsdp", None),
        P(None, "fsdp", None),
        P(None, "fsdp"),
        P(None, "fsdp", None),
        P(None, "fsdp", None, None),
        P(None, "fsdp", None, None),
        P(None, "fsdp", None, None),
    )
    return jax.shard_map(
        on_device,
        mesh=mesh,
        in_specs=placed,
        out_specs=(
            P(("rep", "fsdp"), None),
            P(("rep", "fsdp"), None),
            P(None, "fsdp"),
            P(None, "fsdp", None),
            P(None, "fsdp", None),
            P(None, "fsdp", None),
            P(None, "fsdp", None),
            P(None, "fsdp"),
            P(None, "fsdp", None),
            P(None, "fsdp", None, None),
            P(None, "fsdp", None, None),
            P(None, "fsdp", None, None),
        ),
        check_vma=False,
    )
```

```python
import functools

import jax
import jax.numpy as jnp
from jax import lax
from jax.experimental import pallas as pl
from jax.experimental.pallas import tpu as pltpu
from jax.sharding import PartitionSpec as P

HEADS = 24
KV_HEADS = 8
HD = 64
LAYERS = 2
GROUP = HEADS // KV_HEADS
LANES = 128
EPS = 1e-06
MASKED = -1e30
MESH = pl.DeviceIdType.MESH
F32 = jnp.float32
BF16 = jnp.bfloat16


def ring_place(chip, count):
    return lax.select(lax.rem(chip, 2) == 0, chip // 2, count - 1 - chip // 2)


def ring_chip(place, count):
    return lax.select(place < count // 2, 2 * place, 2 * (count - 1 - place) + 1)


def ring_setup(count):
    me = lax.axis_index("fsdp")
    chip, core = me // 2, lax.rem(me, 2)
    place = ring_place(chip, count)

    def at(offset):
        return ring_chip(lax.rem(place + offset + 2 * count, count), count)

    near = [{"fsdp": at(1) * 2 + core}, {"fsdp": at(-1) * 2 + core}]
    return chip, at, near


def partner_of(axis):
    if axis == "rep":
        return {"rep": 1 - lax.axis_index("rep")}
    me = lax.axis_index("fsdp")
    return {"fsdp": me + 1 - 2 * lax.rem(me, 2)}


def meet(others):
    barrier = pltpu.get_barrier_semaphore()
    for other in others:
        pl.semaphore_signal(barrier, inc=1, device_id=other, device_id_type=MESH)
    pl.semaphore_wait(barrier, len(others))


def remote(src, dst, send_sem, recv_sem, device):
    return pltpu.make_async_remote_copy(
        src_ref=src,
        dst_ref=dst,
        send_sem=send_sem,
        recv_sem=recv_sem,
        device_id=device,
        device_id_type=MESH,
    )


def ring_hops(count):
    half = count // 2
    return {(0, 0): half, (1, 1): half, (0, 1): half - 1, (1, 0): half - 1}


IDENTITIES = {}


def identity(key):
    return IDENTITIES.setdefault(key, len(IDENTITIES))


class Ring:
    def __init__(self, count, traffic):
        self.count = count
        self.riders, self.early, self.late, self.soon = traffic
        self.steps = count // 2
        self.chip, self.at, self.near = ring_setup(count)

    def meet(self, partner=False):
        others = self.near + ([partner_of("fsdp")] if partner else [])
        meet(others + ([partner_of("rep")] if self.riders else []))
        for rider in self.riders:
            rider.start()
        for copy in self.early:
            copy.wait()

    def settle(self):
        for copy in self.late:
            copy.wait()

    def depart(self):
        for copy in self.soon:
            copy.start()

    def gather(self, x_ref, buf, sems, side=None, first=None, second=None):
        own_sem, send_sem, recv_sem = sems[:3]
        half_rows = x_ref.shape[0] // 2
        steps = self.steps
        own = [pltpu.make_async_copy(x_ref, buf.at[self.chip], own_sem.at[0])]
        if side is not None:
            side_ref, side_buf = side
            side_send, side_recv = sems[3:]
            own.append(pltpu.make_async_copy(side_ref, side_buf.at[self.chip], own_sem.at[1]))
        for copy in own:
            copy.start()

        def piece(key, step, block, source=None):
            direction, part = key
            rows = pl.ds(part * half_rows, half_rows)
            target = buf.at[block, rows]
            return remote(
                target if source is None else source.at[rows],
                target,
                send_sem.at[direction, part, step],
                recv_sem.at[direction, part, step],
                self.near[direction],
            )

        def side_piece(direction, step, block, source=None):
            target = side_buf.at[block]
            return remote(
                target if source is None else source,
                target,
                side_send.at[direction, step],
                side_recv.at[direction, step],
                self.near[direction],
            )

        def toward(key, places):
            return self.at(-places if key[0] == 0 else places)

        early, late = [(0, 0), (1, 1)], [(0, 1), (1, 0)]
        if side is not None:
            for direction in range(2):
                side_piece(direction, 0, self.chip, side_ref).start()
        for key in early + late:
            piece(key, 0, self.chip, x_ref).start()

        def step(s, carry):
            if side is not None:
                for direction in range(2):

                    @pl.when(s <= steps - direction)
                    def _():
                        block = toward((direction, 0), s)
                        side_piece(direction, s - 1, block).wait_recv()

                        @pl.when(s < steps - direction)
                        def _():
                            side_piece(direction, s, block).start()

            for key in early:
                block = toward(key, s)
                piece(key, s - 1, block).wait_recv()

                @pl.when(s < steps)
                def _():
                    piece(key, s, block).start()

            if first is not None:
                first(s)

            @pl.when(s < steps)
            def _():
                for key in late:
                    block = toward(key, s)
                    piece(key, s - 1, block).wait_recv()

                    @pl.when(s < steps - 1)
                    def _():
                        piece(key, s, block).start()

            if second is not None:
                second(s)
            return carry

        for copy in own:
            copy.wait()
        lax.fori_loop(1, steps + 1, step, 0)

        def drain():
            for s in range(steps):
                for key in early + (late if s < steps - 1 else []):
                    piece(key, s, toward(key, s)).wait_send()
                if side is not None:
                    for direction in range(2):
                        if s < steps - direction:
                            side_piece(direction, s, toward((direction, 0), s)).wait_send()

        return drain

    def pair(self, s):
        return self.at(s), self.at(-s)

    def meanwhile(self, compute, place):
        def run(s):
            @pl.when(s == 1)
            def _():
                compute(place, (self.chip,))

            @pl.when(s > 1)
            def _():
                compute(place, self.pair(s - 1))

        return run

    def scatter(self, partial, land, sems, work=None, between=None):
        send_sem, recv_sem = sems
        half_rows = partial.shape[1] // 2
        steps = self.steps
        hops = ring_hops(self.count)

        def ahead(key, s):
            places = hops[key] - s
            return self.at(places if key[0] == 0 else -places)

        def piece(key, s, source):
            direction, part = key
            return remote(
                source,
                land.at[direction, part, s],
                send_sem.at[direction, part, s],
                recv_sem.at[direction, part, s],
                self.near[direction],
            )

        def rows_of(key):
            return pl.ds(key[1] * half_rows, half_rows)

        for place, key in enumerate(hops):
            if place == 2 and between is not None:
                between()
            piece(key, 0, partial.at[ahead(key, 0), rows_of(key)]).start()

        def step(s, carry):
            for place, key in enumerate(hops):
                if work is not None:
                    work(s - 1, place)

                @pl.when(s < hops[key])
                def _():
                    slot = land.at[key[0], key[1], s - 1]
                    piece(key, s - 1, slot).wait_recv()
                    mine = partial[ahead(key, s), rows_of(key)]
                    slot[...] = (slot[...].astype(F32) + mine.astype(F32)).astype(BF16)
                    piece(key, s, slot).start()

            return carry

        lax.fori_loop(1, steps + 1, step, 0)
        for key in hops:
            slot = land.at[key[0], key[1], hops[key] - 1]
            piece(key, hops[key] - 1, slot).wait_recv()
        halves = []
        for part in range(2):
            rows = pl.ds(part * half_rows, half_rows)
            total = partial[self.chip, rows].astype(F32)
            for direction in range(2):
                total = total + land[direction, part, hops[direction, part] - 1].astype(F32)
            halves.append(total)
        summed = jnp.concatenate(halves, 0)

        def drain():
            for key in hops:
                for s in range(hops[key]):
                    piece(key, s, land.at[key[0], key[1], s]).wait_send()

        return summed, drain


def dmas(*shapes):
    return [pltpu.SemaphoreType.DMA(shape) for shape in shapes]


def gather_sems(count, sided=False):
    steps = count // 2
    shapes = [(2,), (2, 2, steps), (2, 2, steps)]
    return dmas(*(shapes + ([(2, steps), (2, steps)] if sided else [])))


def scatter_sems(count):
    return dmas((2, 2, count // 2), (2, 2, count // 2))


ANYWHERE = pl.BlockSpec(memory_space=pltpu.HBM)
HERE = pl.BlockSpec(memory_space=pltpu.VMEM)
EARLY, LATE = "early", "late"
OUT, SOON = "out", "soon"


FREE = pl.CostEstimate(flops=0, bytes_accessed=0, transcendentals=0)


def ring_call(body, key, inputs, outputs, scratch, megabytes, rides=()):
    n_in, n_out, n_rides = len(inputs), len(outputs), len(rides)
    in_kinds = [kind for _, kind in inputs]
    out_kinds = [kind for _, kind in outputs]
    copied = [a for a, kind in inputs if kind in (EARLY, LATE)]
    returned = [a for a, kind in outputs if kind in (OUT, SOON)]
    moves = len(copied) + len(returned)

    def kernel(*refs):
        ins, ride_in, outs, ride_out, rest = split(refs, n_in, n_rides, n_out, n_rides)
        rest, own, rest_sems = rest[: len(scratch)], rest[len(scratch) : len(scratch) + moves], rest[len(scratch) + moves :]
        move_sem, rest_sems = rest_sems[0], rest_sems[1:]
        riders = []
        if n_rides:
            send_sem, recv_sem = rest_sems
            riders = [
                remote(ride_in[i], ride_out[i], send_sem.at[i], recv_sem.at[i], partner_of("rep"))
                for i in range(n_rides)
            ]
        used = 0
        early, late, leaving, soon = [], [], [], []
        ins, outs = list(ins), list(outs)
        for i, kind in enumerate(in_kinds):
            if kind in (EARLY, LATE):
                copy = pltpu.make_async_copy(ins[i], own[used], move_sem.at[used])
                copy.start()
                (early if kind == EARLY else late).append(copy)
                ins[i] = own[used]
                used += 1
        for i, kind in enumerate(out_kinds):
            if kind in (OUT, SOON):
                copy = pltpu.make_async_copy(own[used], outs[i], move_sem.at[used])
                (leaving if kind == OUT else soon).append(copy)
                outs[i] = own[used]
                used += 1
        body((riders, early, late, soon), *ins, *outs, *rest)
        for copy in leaving:
            copy.start()
        for rider in riders:
            rider.wait()
        for copy in leaving + soon:
            copy.wait()

    def spec(kind):
        return ANYWHERE if isinstance(kind, str) else kind

    return pl.pallas_call(
        kernel,
        out_shape=tuple(shape for shape, _ in outputs) + tuple(cells(a.shape, a.dtype) for a in rides),
        in_specs=[spec(kind) for kind in in_kinds] + [ANYWHERE] * n_rides,
        out_specs=[spec(kind) for kind in out_kinds] + [ANYWHERE] * n_rides,
        scratch_shapes=list(scratch)
        + [pltpu.VMEM(a.shape, a.dtype) for a in copied + returned]
        + dmas((max(moves, 1),))
        + (dmas((n_rides,), (n_rides,)) if n_rides else []),
        compiler_params=pltpu.CompilerParams(
            collective_id=identity(key),
            has_side_effects=True,
            vmem_limit_bytes=megabytes << 20,
        ),
        cost_estimate=FREE,
        name=key[0],
    )(*[array for array, _ in inputs], *rides)


def split(refs, *sizes):
    parts, place = [], 0
    for size in sizes:
        parts.append(refs[place : place + size])
        place += size
    return parts + [refs[place:]]


def cells(shape, dtype):
    return jax.ShapeDtypeStruct(shape, dtype)


def setup_kernel(
    count, slab_ref, out_w_ref, small_ref, table_ref,
    heads_ref, outs_ref, smalls_ref, tables_ref,
    own_sem, slab_send, slab_recv, pass_send, pass_recv,
    small_send, small_recv, table_send, table_recv, out_send, out_recv,
):
    devices = 2 * count
    me = lax.axis_index("fsdp")
    chip, core = me // 2, lax.rem(me, 2)
    layers = slab_ref.shape[1]

    def device(offset):
        return {"fsdp": lax.rem(me + offset, devices)}

    def chip_at(offset):
        return lax.rem(chip + offset + count, count)

    partner = partner_of("fsdp")
    meet([device(offset) for offset in range(1, devices)])
    copies = [
        pltpu.make_async_copy(slab_ref.at[chip, layer], heads_ref.at[layer, me], own_sem.at[layer])
        for layer in range(layers)
    ] + [
        pltpu.make_async_copy(small_ref, smalls_ref.at[me], own_sem.at[layers]),
        pltpu.make_async_copy(table_ref, tables_ref.at[chip], own_sem.at[layers + 1]),
        pltpu.make_async_copy(out_w_ref, outs_ref.at[core], own_sem.at[layers + 2]),
    ]
    sends = [
        remote(small_ref, smalls_ref.at[me], small_send.at[offset], small_recv.at[offset], device(offset))
        for offset in range(1, devices)
    ]
    for offset in range(1, count):
        there = {"fsdp": chip_at(offset) * 2 + core}
        sends.append(
            remote(table_ref, tables_ref.at[chip], table_send.at[offset], table_recv.at[offset], there)
        )
        for layer in range(layers):
            sends.append(
                remote(
                    slab_ref.at[chip_at(offset), layer], heads_ref.at[layer, me],
                    slab_send.at[offset, layer], slab_recv.at[offset, layer], there,
                )
            )
    for layer in range(layers):
        sends.append(
            remote(
                slab_ref.at[chip, layer], heads_ref.at[layer, me],
                pass_send.at[0, layer], pass_recv.at[0, layer], partner,
            )
        )
    sends.append(remote(out_w_ref, outs_ref.at[core], out_send.at[0], out_recv.at[0], partner))
    for copy in copies + sends:
        copy.start()
    for offset in range(1, count):
        origin = chip_at(-offset) * 2 + core
        for layer in range(layers):
            slot = heads_ref.at[layer, origin]
            remote(slot, slot, slab_send.at[offset, layer], slab_recv.at[offset, layer], partner).wait_recv()
            forward = remote(slot, slot, pass_send.at[offset, layer], pass_recv.at[offset, layer], partner)
            forward.start()
    for offset in range(1, count):
        origin = chip_at(-offset)
        table = tables_ref.at[origin]
        remote(table, table, table_send.at[offset], table_recv.at[offset], partner).wait_recv()
    for offset in range(count):
        origin = chip_at(-offset) * 2 + 1 - core
        mine = chip_at(-offset) * 2 + core
        for layer in range(layers):
            slot, sent = heads_ref.at[layer, origin], heads_ref.at[layer, mine]
            if offset > 0:
                remote(sent, sent, pass_send.at[offset, layer], pass_recv.at[offset, layer], partner).wait_send()
            remote(slot, slot, pass_send.at[offset, layer], pass_recv.at[offset, layer], partner).wait_recv()
    for offset in range(1, devices):
        slot = smalls_ref.at[lax.rem(me - offset + devices, devices)]
        remote(slot, slot, small_send.at[offset], small_recv.at[offset], partner).wait_recv()
    other = outs_ref.at[1 - core]
    remote(other, other, out_send.at[0], out_recv.at[0], partner).wait_recv()
    for copy in copies:
        copy.wait()
    for send in sends:
        send.wait_send()


def exchange_weights(count, slabs, out_w, small, table):
    layers = slabs.shape[1]
    devices = 2 * count
    dma = pltpu.SemaphoreType.DMA
    anywhere = pl.BlockSpec(memory_space=pl.ANY)
    return pl.pallas_call(
        functools.partial(setup_kernel, count),
        out_shape=(
            jax.ShapeDtypeStruct((layers, devices) + slabs.shape[2:], slabs.dtype),
            jax.ShapeDtypeStruct((2,) + out_w.shape, out_w.dtype),
            jax.ShapeDtypeStruct((devices,) + small.shape, small.dtype),
            jax.ShapeDtypeStruct((count,) + table.shape, table.dtype),
        ),
        in_specs=[anywhere] * 4,
        out_specs=[anywhere] * 4,
        scratch_shapes=[
            dma((layers + 3,)),
            dma((count, layers)),
            dma((count, layers)),
            dma((count, layers)),
            dma((count, layers)),
            dma((devices,)),
            dma((devices,)),
            dma((count,)),
            dma((count,)),
            dma((1,)),
            dma((1,)),
        ],
        compiler_params=pltpu.CompilerParams(
            collective_id=identity(("setup",)), has_side_effects=True, vmem_limit_bytes=60 << 20
        ),
        cost_estimate=FREE,
        name="exchange_weights",
    )(slabs, out_w, small, table)


def dot(left, right, contract=((1,), (0,))):
    return lax.dot_general(left, right, (contract, ((), ())), preferred_element_type=F32)


NT = ((1,), (1,))
TN = ((0,), (0,))


def lanes_of(field):
    return lax.broadcasted_iota(jnp.int32, field.shape, 1)


def turn(field):
    return pltpu.roll(field, HD, 1)


def spin(field, cosine, sine):
    swapped = jnp.where(
        lax.rem(lanes_of(field), HD) < HD // 2,
        -pltpu.roll(field, LANES - HD // 2, 1),
        pltpu.roll(field, HD // 2, 1),
    )
    return field * cosine + swapped * sine


def project_rows(rows, cosine, sine):
    first = spin(rows[:, :LANES], cosine, sine)
    second = spin(rows[:, LANES : 2 * LANES], cosine, sine)
    third = rows[:, 2 * LANES :]
    low = lanes_of(first) < HD
    heads = []
    for field in (first, turn(first), second):
        rounded = jnp.where(low, field, 0.0).astype(BF16).astype(F32)
        heads.append((rounded * (HD**-0.5)).astype(BF16))
    return heads, jnp.where(low, turn(second), turn(third)).astype(BF16)


def angles(table):
    rows = jnp.concatenate([table, table], 0).T
    early = lax.rem(lanes_of(rows), HD) < HD // 2
    cosine = jnp.where(early, rows, pltpu.roll(rows, HD // 2, 1))
    sine = jnp.where(early, pltpu.roll(rows, LANES - HD // 2, 1), rows)
    return cosine, sine


def normal(values):
    inverse = lax.rsqrt(jnp.mean(values * values, -1, keepdims=True) + EPS)
    return inverse, values * inverse


def normal_back(d_x, values, gain):
    inverse, normed = normal(values)
    d_norm = d_x * gain
    d_values = inverse * (d_norm - normed * jnp.mean(d_norm * normed, -1, keepdims=True))
    return d_values, jnp.sum(d_x * normed, 0, keepdims=True)


def diagonal():
    shape = (LANES, LANES)
    return lax.broadcasted_iota(jnp.int32, shape, 0) == lax.broadcasted_iota(jnp.int32, shape, 1)


def as_column(line):
    return jnp.sum(jnp.where(diagonal(), jnp.broadcast_to(line, (LANES, LANES)), 0.0), 1, keepdims=True)


def as_line(column):
    return jnp.sum(jnp.where(diagonal(), jnp.broadcast_to(column, (LANES, LANES)), 0.0), 0, keepdims=True)


def flat(value):
    return value.reshape(value.shape[0] * value.shape[1], value.shape[2])


def stack(ref, blocks):
    parts = [ref[b] for b in blocks]
    return parts[0] if len(parts) == 1 else jnp.concatenate(parts, 0)


def cut(value, blocks):
    return [(b, value[i * LANES : (i + 1) * LANES]) for i, b in enumerate(blocks)]


def gain_row(params_ref, kind, layer):
    row = kind * LAYERS + layer
    return params_ref[row : row + 1, :]


def router_rows(experts, layer):
    first = 2 * LAYERS + layer * experts
    return slice(first, first + experts)


def allowed_keys(begin, query, chunk, core):
    shape = (2 * LANES, begin.shape[1])
    place = lax.broadcasted_iota(jnp.int32, shape, 0)
    shift = jnp.where(place < LANES, core, -core)
    key = chunk * 2 * LANES + place + shift * LANES
    return (key >= begin) & (key <= query)


def query_rows(begin_ref, blocks, core):
    lane = lax.broadcasted_iota(jnp.int32, (1, LANES), 1)
    begin, query = [], []
    for block in blocks:
        begin += [begin_ref[block]] * GROUP
        query += [(2 * block + core) * LANES + lane] * GROUP
    return jnp.concatenate(begin, 1), jnp.concatenate(query, 1)


def chunk_keys(own_ref, other_ref, chunk):
    return jnp.concatenate([own_ref[chunk], other_ref[chunk]], 0)


def turn_keys(own_ref, other_ref, turned_ref):
    def one(chunk, carry):
        turned_ref[chunk] = chunk_keys(own_ref, other_ref, chunk).astype(F32).T.astype(BF16)
        return carry

    lax.fori_loop(0, turned_ref.shape[0], one, 0)


def by_head(field):
    return [field[:, h * LANES : (h + 1) * LANES].T for h in range(GROUP)]


def last_chunk(blocks):
    return blocks[0] if len(blocks) == 1 else jnp.maximum(*blocks)


def attend_kernel(count, layer, traffic, *refs):
    inputs, outputs, scratch = split(refs, 8, 9)
    x_ref, w_ref, w_out_ref, table_ref, begin_ref, hidden_ref, params_ref, routes_ref = inputs
    q_ref, own_ref, other_ref, all_ref, att_ref, lse_ref, middle_ref, x_out_ref, share_ref = outputs
    buf, weights, wide_w, turned_ref, score_ref, partial, land = scratch[:7]
    sems, pair_sems, scatter_sem, out_sem, load_sem = split(scratch[7:], 3, 2, 2, 1)
    ring = Ring(count, traffic)
    loads = [pltpu.make_async_copy(w_ref.at[layer], weights, load_sem[0].at[2])]
    loads[0].start()
    loads += load_out_weights(w_out_ref, layer, wide_w, load_sem[0])
    ring.meet(True)
    partner = partner_of("fsdp")
    core = lax.rem(lax.axis_index("fsdp"), 2)

    def pass_on(block):
        return remote(
            own_ref.at[block], other_ref.at[block], pair_sems[0].at[block], pair_sems[1].at[block], partner
        )

    def project(place, blocks):
        rows = dot(stack(buf, blocks), weights[...])
        tables = [angles(table_ref[b]) for b in blocks]
        cosine = jnp.concatenate([t[0] for t in tables], 0)
        sine = jnp.concatenate([t[1] for t in tables], 0)
        heads, pair = project_rows(rows, cosine, sine)
        for index, head in enumerate(heads):
            for block, part in cut(head, blocks):
                q_ref[block, index] = part
        for block, part in cut(pair, blocks):
            own_ref[block] = part
            pass_on(block).start()

    drain = ring.gather(
        x_ref, buf, sems, None, after_loads(loads, lambda s: None), ring.meanwhile(project, 0)
    )
    keep = pltpu.make_async_copy(buf, all_ref, out_sem[0].at[0])
    keep.start()
    project(0, (ring.at(ring.steps),))
    for block in range(count):
        pass_on(block).wait()
    ring.depart()
    turn_keys(own_ref, other_ref, turned_ref)

    def attend(blocks):
        width = len(blocks) * GROUP * LANES
        q = jnp.concatenate([q_ref[b].reshape(GROUP * LANES, LANES) for b in blocks], 0)
        begin, query = query_rows(begin_ref, blocks, core)
        end = last_chunk(blocks) + 1

        def score(chunk, top):
            keys = chunk_keys(own_ref, other_ref, chunk)
            scores = jnp.where(allowed_keys(begin, query, chunk, core), dot(keys, q, NT), MASKED)
            score_ref[chunk, :, :width] = scores
            return jnp.maximum(top, jnp.max(scores, 0, keepdims=True))

        top = lax.fori_loop(0, end, score, jnp.full((1, width), MASKED, F32))

        def add(chunk, state):
            total, acc = state
            weights = jnp.exp(score_ref[chunk, :, :width] - top)
            total = total + jnp.sum(weights, 0, keepdims=True)
            return total, acc + dot(turned_ref[chunk], weights.astype(BF16))

        total, acc = lax.fori_loop(
            0, end, add, (jnp.zeros((1, width), F32), jnp.zeros((LANES, width), F32))
        )
        lse = top + jnp.log(total)
        att = acc / total
        rows = []
        for place, block in enumerate(blocks):
            here = slice(place * GROUP * LANES, (place + 1) * GROUP * LANES)
            lse_ref[block] = lse[:, here]
            heads = by_head(att[:, here])
            low = lanes_of(heads[0]) < HD
            rows.append(
                jnp.concatenate(
                    [jnp.where(low, turn(heads[0]), heads[1]), jnp.where(low, turn(heads[2]), 0.0)], 1
                ).astype(BF16)
            )
            att_ref[block] = rows[-1]
        out = dot(jnp.concatenate(rows, 0) if len(rows) > 1 else rows[0], wide_w[...]).astype(BF16)
        for block, part in cut(out, blocks):
            partial[block] = part

    attend((ring.at(ring.steps),))

    def between():
        attend(ring.pair(ring.steps - 1))

    def work(s, place):
        if place == 2:

            @pl.when(s < ring.steps - 2)
            def _():
                attend(ring.pair(ring.steps - 2 - s))

            @pl.when(s == ring.steps - 2)
            def _():
                attend((ring.chip,))

    added, finish = ring.scatter(partial, land, scatter_sem, work, between)
    ring.settle()
    middle = hidden_ref[...] + added
    middle_ref[...] = middle
    x = (normal(middle)[1] * gain_row(params_ref, 1, layer)).astype(BF16)
    x_out_ref[...] = x
    experts = share_ref.shape[0]
    logits = dot(params_ref[router_rows(experts, layer), :].astype(BF16), x, NT)
    expert = lax.broadcasted_iota(jnp.int32, logits.shape, 0)
    named = expert < 0
    for choice in range(routes_ref.shape[1]):
        named = named | (expert == routes_ref[layer, choice : choice + 1, :])
    scores = jnp.where(named, logits, MASKED)
    weighted = jnp.where(named, jnp.exp(scores - jnp.max(scores, 0, keepdims=True)), 0.0)
    share_ref[...] = weighted / jnp.sum(weighted, 0, keepdims=True)
    drain()
    finish()
    keep.wait()


def gather_attend_scatter(count, layer, x, w, w_out, tables, begin, hidden, params, routes):
    rows, width = x.shape
    block = cells((count, rows, LANES), BF16)
    everyone = pltpu.VMEM((count, rows, width), BF16)
    wide = 2 * LANES
    return ring_call(
        functools.partial(attend_kernel, count, layer),
        ("attend", layer),
        [
            (x, ANYWHERE), (w, ANYWHERE), (w_out, ANYWHERE), (tables, EARLY), (begin, EARLY),
            (hidden, LATE), (params, LATE), (routes, LATE),
        ],
        [
            (cells((count, GROUP, rows, LANES), BF16), SOON),
            (block, SOON),
            (block, SOON),
            (cells((count, rows, width), BF16), ANYWHERE),
            (cells((count, rows, wide), BF16), OUT),
            (cells((count, 1, GROUP * rows), F32), OUT),
            (cells((rows, width), F32), OUT),
            (cells((rows, width), BF16), OUT),
            (cells((2 * count, rows), F32), OUT),
        ],
        [
            everyone,
            pltpu.VMEM(w.shape[1:], BF16),
            pltpu.VMEM((wide, width), BF16),
            pltpu.VMEM((count, LANES, wide), BF16),
            pltpu.VMEM((count, wide, 2 * GROUP * LANES), F32),
            everyone,
            land_scratch(count, rows, width),
        ]
        + gather_sems(count)
        + dmas((count,), (count,))
        + scatter_sems(count)
        + dmas((1,), (3,)),
        60,
    )


def load_experts(refs, layer, gates, ups, downs, sem):
    copies = []
    for e in range(2):
        for place, buf in enumerate((gates, ups, downs)):
            source = refs[3 * e + place].at[layer, 0]
            copies.append(pltpu.make_async_copy(source, buf.at[e], sem.at[3 * e + place]))
    for copy in copies:
        copy.start()
    return copies


def expert_of(e):
    me = lax.axis_index("fsdp")
    return me if e == 0 else me + 1 - 2 * lax.rem(me, 2)


def share_of(share_ref, e, blocks):
    columns = [as_column(share_ref[b, pl.ds(expert_of(e), 1), :]) for b in blocks]
    return jnp.concatenate(columns, 0) if len(columns) > 1 else columns[0]


def after_loads(loads, run):
    def first(s):
        @pl.when(s == 1)
        def _():
            for load in loads:
                load.wait()

        run(s)

    return first


def mix_kernel(count, layer, traffic, *refs):
    inputs, outputs, scratch = split(refs, 10, 5)
    x_ref, side_ref, middle_ref, params_ref = inputs[:4]
    mixed_ref, hidden_ref, next_ref, all_ref, share_ref = outputs
    buf, partial, land, acc, gates, ups, downs = scratch[:7]
    sems, scatter_sem, load_sem, out_sem = split(scratch[7:], 5, 2, 1)
    ring = Ring(count, traffic)
    loads = load_experts(inputs[4:], layer, gates, ups, downs, load_sem[0])
    ring.meet()

    def compute(e, blocks):
        x = stack(buf, blocks)
        act_gate, act_up = dot(x, gates[e]), dot(x, ups[e])
        hidden = jax.nn.silu(act_gate) * act_up * share_of(share_ref, e, blocks)
        part = dot(hidden.astype(BF16), downs[e])
        if e == 0:
            acc[: x.shape[0]] = part
        else:
            total = (acc[: x.shape[0]] + part).astype(BF16)
            for block, rows in cut(total, blocks):
                partial[block] = rows

    drain = ring.gather(
        x_ref, buf, sems, (side_ref, share_ref),
        after_loads(loads, ring.meanwhile(compute, 0)), ring.meanwhile(compute, 1),
    )
    keep = pltpu.make_async_copy(buf, all_ref, out_sem[0].at[0])
    keep.start()
    for e in range(2):
        compute(e, (ring.at(ring.steps),))
    mixed, finish = ring.scatter(partial, land, scatter_sem)
    ring.settle()
    mixed_ref[...] = mixed
    hidden = middle_ref[...] + mixed
    hidden_ref[...] = hidden
    if layer + 1 < LAYERS:
        next_ref[...] = (normal(hidden)[1] * gain_row(params_ref, 0, layer + 1)).astype(BF16)
    else:
        next_ref[...] = hidden.astype(BF16)
    drain()
    finish()
    keep.wait()


def expert_scratch(weights):
    return [pltpu.VMEM((2,) + w.shape[2:], BF16) for w in weights[:3]]


def land_scratch(count, rows, width):
    return pltpu.VMEM((2, 2, count // 2, rows // 2, width), BF16)


def gather_mix_scatter(count, layer, x, share, middle, params, weights):
    rows, width = x.shape
    everyone = pltpu.VMEM((count, rows, width), BF16)
    own = cells((rows, width), F32)
    return ring_call(
        functools.partial(mix_kernel, count, layer),
        ("mix", layer),
        [(x, ANYWHERE), (share, ANYWHERE), (middle, LATE), (params, LATE)]
        + [(w, ANYWHERE) for w in weights],
        [
            (own, OUT),
            (own, OUT),
            (cells((rows, width), BF16), OUT),
            (cells((count, rows, width), BF16), ANYWHERE),
            (cells((count,) + share.shape, F32), OUT),
        ],
        [everyone, everyone, land_scratch(count, rows, width), pltpu.VMEM((2 * rows, width), F32)]
        + expert_scratch(weights)
        + gather_sems(count, True)
        + scatter_sems(count)
        + dmas((6,), (1,)),
        60,
    )


def mix_back_kernel(count, layer, traffic, *refs):
    inputs, outputs, scratch = split(refs, 13, 5)
    d_ref, side_ref, m_ref, share_ref, params_ref, grad_ref, middle_ref = inputs[:7]
    mid_ref, branch_ref, gain_ref, sum_ref, g_router_ref = outputs
    buf, partial, land, acc, gates, ups, downs = scratch[:7]
    tokens, acts, hiddens, balance_ref, totals, got = scratch[7:13]
    sems, scatter_sem, load_sem, pair_sem, out_sem = split(scratch[13:], 5, 2, 1, 2)
    ring = Ring(count, traffic)
    loads = load_experts(inputs[7:], layer, gates, ups, downs, load_sem[0])
    loads.append(pltpu.make_async_copy(m_ref, tokens, load_sem[0].at[6]))
    loads[-1].start()
    ring.meet(True)
    ff = gates.shape[2]
    width = buf.shape[2]
    g_router_ref[...] = jnp.zeros_like(g_router_ref)
    routers = 2 * LAYERS + layer * 2 * count

    def compute(e, blocks):
        d, x = stack(buf, blocks), stack(tokens, blocks)
        share = share_of(share_ref, e, blocks)
        balance = [as_column(balance_ref[b, 0:1, :]) for b in blocks]
        balance = jnp.concatenate(balance, 0) if len(balance) > 1 else balance[0]
        act_gate, act_up = dot(x, gates[e]), dot(x, ups[e])
        sig = jax.nn.sigmoid(act_gate)
        swish = act_gate * sig
        hidden = swish * act_up
        raw = dot(d, downs[e], NT)
        d_logit = share * (jnp.sum(hidden * raw, -1, keepdims=True) - balance)
        d_hidden = raw * share
        d_gate = (d_hidden * act_up * sig * (1.0 + act_gate * (1.0 - sig))).astype(BF16)
        d_up = (d_hidden * swish).astype(BF16)
        weighted = (hidden * share).astype(BF16)
        part = dot(d_gate, gates[e], NT) + dot(d_up, ups[e], NT)
        part = part + d_logit * params_ref[pl.ds(routers + expert_of(e), 1), :]
        g_router_ref[e : e + 1, :] += jnp.sum(d_logit * x.astype(F32), 0, keepdims=True)
        for place, block in enumerate(blocks):
            here = slice(place * LANES, (place + 1) * LANES)
            acts[e, block, :, :ff] = d_gate[here]
            acts[e, block, :, ff:] = d_up[here]
            hiddens[e, block] = weighted[here]
        if e == 0:
            acc[: x.shape[0]] = part
        else:
            total = (acc[: x.shape[0]] + part).astype(BF16)
            for block, rows in cut(total, blocks):
                partial[block] = rows

    drain = ring.gather(
        d_ref, buf, sems, (side_ref, balance_ref),
        after_loads(loads, ring.meanwhile(compute, 0)), ring.meanwhile(compute, 1),
    )
    for e in range(2):
        compute(e, (ring.at(ring.steps),))

    partner = partner_of("fsdp")
    strip = 2 * LANES
    strips = width // (2 * strip)
    groups = width // ff

    def regions(half):
        regions = [(group * width + half * (width // 2), width // 2) for group in range(2)]
        return regions + [(2 * width + group * ff + half * (ff // 2), ff // 2) for group in range(groups)]

    def swap(half):
        return [
            remote(
                totals.at[1, pl.ds(first, length)], got.at[pl.ds(first, length)],
                pair_sem[0].at[half, index], pair_sem[1].at[half, index], partner,
            )
            for index, (first, length) in enumerate(regions(half))
        ]

    def store(half):
        return [
            pltpu.make_async_copy(
                totals.at[0, pl.ds(first, length)], sum_ref.at[pl.ds(first, length)], out_sem[0].at[half, index]
            )
            for index, (first, length) in enumerate(regions(half))
        ]

    def work(s, place):
        e = 1 - s // 2
        half = lax.rem(s, 2)

        def put(first, value):
            rows = pl.ds(pl.multiple_of(first, strip), strip)

            @pl.when(s < 2)
            def _():
                totals[1, rows] = value.astype(BF16)

            @pl.when(s >= 2)
            def _():
                totals[0, rows] = (value + got[rows].astype(F32)).astype(BF16)

        if place == 0:
            for h in range(2):

                @pl.when(s == 2 + h)
                def _():
                    for copy in swap(h):
                        copy.wait_recv()

        if place < strips:
            first = (half * strips + place) * strip
            columns = pl.ds(pl.multiple_of(first, strip), strip)
            value = dot(flat(tokens[:, :, columns]), flat(acts[e]), TN)
            for group in range(2):
                put(group * width + first, value[:, group * ff : (group + 1) * ff])
        if place == 3:
            columns = pl.ds(pl.multiple_of(half * strip, strip), strip)
            value = dot(flat(hiddens[e, :, :, columns]), flat(buf[...]), TN)
            for group in range(groups):
                put(2 * width + group * ff + half * strip, value[:, group * ff : (group + 1) * ff])
            for h in range(2):

                @pl.when(s == h)
                def _():
                    for copy in swap(h):
                        copy.start()

                @pl.when(s == 2 + h)
                def _():
                    for copy in store(h):
                        copy.start()

    d_x, finish = ring.scatter(partial, land, scatter_sem, work)
    ring.settle()
    d_values, gain_ref[...] = normal_back(d_x, middle_ref[...], gain_row(params_ref, 1, layer))
    grad = grad_ref[...] + d_values
    mid_ref[...] = grad
    branch_ref[...] = grad.astype(BF16)
    drain()
    finish()
    for half in range(2):
        for copy in swap(half):
            copy.wait_send()
        for copy in store(half):
            copy.wait()


def gather_mix_back_scatter(count, layer, d, side, m_all, share, params, grad, middle, weights, rides):
    rows, width = d.shape
    ff = weights[0].shape[3]
    everyone = pltpu.VMEM((count, rows, width), BF16)
    groups = width // ff
    own = cells((rows, width), F32)
    return ring_call(
        functools.partial(mix_back_kernel, count, layer),
        ("mix_back", layer),
        [(d, ANYWHERE), (side, ANYWHERE), (m_all, ANYWHERE), (share, EARLY), (params, EARLY), (grad, LATE), (middle, LATE)]
        + [(w, ANYWHERE) for w in weights],
        [
            (own, OUT),
            (cells((rows, width), BF16), OUT),
            (cells((1, width), F32), OUT),
            (cells((3 * width, ff), BF16), ANYWHERE),
            (cells((2, width), F32), OUT),
        ],
        [everyone, everyone, land_scratch(count, rows, width), pltpu.VMEM((2 * rows, width), F32)]
        + expert_scratch(weights)
        + [
            everyone,
            pltpu.VMEM((2, count, rows, 2 * ff), BF16),
            pltpu.VMEM((2, count, rows, ff), BF16),
            pltpu.VMEM((count,) + side.shape, F32),
            pltpu.VMEM((2, 3 * width, ff), BF16),
            pltpu.VMEM((3 * width, ff), BF16),
        ]
        + gather_sems(count, True)
        + scatter_sems(count)
        + dmas((7,), (2, 2 + groups), (2, 2 + groups), (2, 2 + groups)),
        60,
        rides,
    )


def load_out_weights(w_ref, layer, wide_ref, sem):
    shard = w_ref.shape[2]
    copies = [
        pltpu.make_async_copy(w_ref.at[core, layer], wide_ref.at[pl.ds(core * shard, shard)], sem.at[core])
        for core in range(2)
    ]
    for copy in copies:
        copy.start()
    used = 2 * shard
    wide_ref[used:] = jnp.zeros((wide_ref.shape[0] - used, wide_ref.shape[1]), BF16)
    return copies


def attend_back_kernel(count, layer, traffic, *refs):
    inputs, outputs, scratch = split(refs, 17, 5)
    d_ref, w_out_ref, w_ref, x_ref, att_ref, q_ref, own_ref, other_ref, begin_ref, lse_ref, table_ref = inputs[:11]
    params_ref, mid_ref, hidden_ref, mixed_ref, router_ref, gain_two_ref = inputs[11:]
    g_out_ref, grad_ref, d_mix_ref, side_ref, g_ref = outputs
    buf, wide_w, g_acc, out_mail, out_got, turned_ref, d_own, d_other, mail, got, dq_ref = scratch[:11]
    partial, land, rows_ref, tokens, weights, last_ref = scratch[11:17]
    sems, scatter_sem, pair_sem, load_sem = split(scratch[17:], 3, 2, 2)
    ring = Ring(count, traffic)
    shard = g_out_ref.shape[0]
    loads = load_out_weights(w_out_ref, layer, wide_w, load_sem[0])
    later = [
        pltpu.make_async_copy(x_ref, tokens, load_sem[0].at[2]),
        pltpu.make_async_copy(w_ref.at[layer], weights, load_sem[0].at[3]),
    ]
    for load in later:
        load.start()
    ring.meet(True)
    core = lax.rem(lax.axis_index("fsdp"), 2)
    width = GROUP * LANES

    def spread(wide):
        front, back = wide[:, :LANES], wide[:, LANES:]
        low = lanes_of(front) < HD
        return [jnp.where(low, 0.0, part) for part in (turn(front), front, turn(back))]

    def compute(block):
        d = buf[block]
        wide = dot(d, wide_w[...], NT).astype(BF16)
        g_acc[...] += dot(att_ref[block], d, TN)
        slopes, deltas = [], []
        for piece, a in zip(spread(wide.astype(F32)), spread(att_ref[block].astype(F32))):
            slopes.append(piece)
            deltas.append(jnp.sum((piece * a).T, 0, keepdims=True))
        datt = jnp.concatenate(slopes, 0).astype(BF16)
        delta = jnp.concatenate(deltas, 1)
        q = q_ref[block].reshape(width, LANES)
        both = jnp.concatenate([q, datt], 0)
        begin, query = query_rows(begin_ref, (block,), core)
        lse = lse_ref[block]

        def one(chunk, acc):
            keys = chunk_keys(own_ref, other_ref, chunk)
            scores = jnp.where(allowed_keys(begin, query, chunk, core), dot(keys, q, NT), MASKED)
            weight = jnp.exp(scores - lse)
            slope = (weight * (dot(keys, datt, NT) - delta)).astype(BF16)
            d_keys = dot(jnp.concatenate([slope, weight.astype(BF16)], 1), both)
            d_own[chunk] += d_keys[:LANES]
            d_other[chunk] += d_keys[LANES:]
            return acc + dot(turned_ref[chunk], slope)

        acc = lax.fori_loop(0, block + 1, one, jnp.zeros((LANES, width), F32)) * (HD**-0.5)
        heads = by_head(acc)
        low = lanes_of(heads[0]) < HD
        cosine, sine = angles(table_ref[block])
        front = spin(jnp.where(low, heads[0], turn(heads[1])), cosine, -sine)
        back = spin(jnp.where(low, heads[2], 0.0), cosine, -sine)
        dq_ref[block] = jnp.concatenate([front, back], 1).astype(BF16)

    def first(s):
        @pl.when(s == 1)
        def _():
            for load in loads:
                load.wait()
            turn_keys(own_ref, other_ref, turned_ref)
            g_acc[...] = jnp.zeros_like(g_acc)
            d_own[...] = jnp.zeros_like(d_own)
            d_other[...] = jnp.zeros_like(d_other)

        @pl.when(s > 1)
        def _():
            compute(ring.at(s - 1))

    def second(s):
        compute(ring.at(1 - s))

    drain = ring.gather(d_ref, buf, sems, None, first, second)
    compute(ring.at(ring.steps))
    partner = partner_of("fsdp")
    mail[...] = d_other[...].astype(BF16)
    out_mail[...] = g_acc[pl.ds(pl.multiple_of((1 - core) * shard, 8), shard), :].astype(BF16)
    swaps = [
        remote(mail, got, pair_sem[0].at[0], pair_sem[1].at[0], partner),
        remote(out_mail, out_got, pair_sem[0].at[1], pair_sem[1].at[1], partner),
    ]
    for swap in swaps:
        swap.start()
    for load in later:
        load.wait()
    drain()
    swaps[0].wait()

    def join(blocks):
        rows = []
        for b in blocks:
            pair = d_own[b] + got[b].astype(F32)
            cosine, sine = angles(table_ref[b])
            keys = spin(pair, cosine, -sine)
            low = lanes_of(pair) < HD
            middle = jnp.where(low, dq_ref[b, :, LANES:].astype(F32), turn(keys))
            last = jnp.where(low, turn(pair), 0.0)
            rows.append(
                jnp.concatenate([dq_ref[b, :, :LANES], middle.astype(BF16), last.astype(BF16)], 1)
            )
            rows_ref[b] = rows[-1]
        total = dot(jnp.concatenate(rows, 0), weights[...], NT).astype(BF16)
        for block, part in cut(total, blocks):
            partial[block] = part

    join((ring.at(ring.steps), ring.chip))
    strip = g_ref.shape[0] // ring.steps
    tile = 2 * LANES

    def between():
        def one(index, carry):
            join(ring.pair(ring.steps - 1 - index))
            return carry

        lax.fori_loop(0, ring.steps - 1, one, 0)

    def work(s, place):
        if place == 0:
            rows = pl.ds(pl.multiple_of(s * strip, LANES), strip)
            value = dot(flat(tokens[:, :, rows]), flat(rows_ref[...]), TN)
            g_ref[rows, :tile] = value[:, :tile].astype(BF16)
            last_ref[rows] = value[:, tile:]

    d_x, finish = ring.scatter(partial, land, scatter_sem, work, between)
    swaps[1].wait()
    own = g_acc[pl.ds(pl.multiple_of(core * shard, 8), shard), :]
    g_out_ref[...] = (own + out_got[...].astype(F32)).astype(BF16)
    ring.settle()
    d_values, gain_one = normal_back(d_x, hidden_ref[...], gain_row(params_ref, 0, layer))
    grad = mid_ref[...] + d_values
    grad_ref[...] = grad
    d_mix = grad.astype(BF16)
    d_mix_ref[...] = d_mix
    balance = jnp.sum(mixed_ref[...] * d_mix.astype(F32), -1, keepdims=True)
    side_ref[...] = jnp.broadcast_to(as_line(balance), side_ref.shape)
    routers = router_ref[...]
    lines = [
        jnp.where(core == 0, routers[0:1], routers[1:2]),
        jnp.where(core == 0, routers[1:2], routers[0:1]),
        gain_one,
        gain_two_ref[...],
    ]
    features = g_ref.shape[0]
    tall = jnp.concatenate(
        [jnp.zeros((HD, features), F32)] + lines + [jnp.zeros((HD - len(lines), features), F32)], 0
    )
    g_ref[:, tile:] = (last_ref[...] + tall.T).astype(BF16)
    finish()


def gather_attend_back_scatter(
    count, layer, d, w_out, w, x_all, att, q, own, other, begin, lse, tables, late, rides=()
):
    _, rows, width = x_all.shape
    shard = w_out.shape[2]
    columns = w.shape[2]
    everyone = pltpu.VMEM((count, rows, width), BF16)
    early = [att, q, own, other, begin, lse, tables]
    pairs = cells((count, rows, LANES), BF16)
    return ring_call(
        functools.partial(attend_back_kernel, count, layer),
        ("attend_back", layer),
        [(a, ANYWHERE) for a in (d, w_out, w, x_all)] + [(a, EARLY) for a in early] + [(a, LATE) for a in late],
        [
            (cells((shard, width), BF16), OUT),
            (cells((rows, width), F32), OUT),
            (cells((rows, width), BF16), OUT),
            (cells((8, rows), F32), OUT),
            (cells(w.shape[1:], BF16), OUT),
        ],
        [
            everyone,
            pltpu.VMEM((2 * LANES, width), BF16),
            pltpu.VMEM((2 * LANES, width), F32),
            pltpu.VMEM((shard, width), BF16),
            pltpu.VMEM((shard, width), BF16),
            pltpu.VMEM((count, LANES, 2 * LANES), BF16),
            pltpu.VMEM(pairs.shape, F32),
            pltpu.VMEM(pairs.shape, F32),
            pltpu.VMEM(pairs.shape, BF16),
            pltpu.VMEM(pairs.shape, BF16),
            pltpu.VMEM((count, rows, 2 * LANES), BF16),
            everyone,
            land_scratch(count, rows, width),
            pltpu.VMEM((count, rows, columns), BF16),
            everyone,
            pltpu.VMEM(w.shape[1:], BF16),
            pltpu.VMEM((width, LANES), F32),
        ]
        + gather_sems(count)
        + scatter_sems(count)
        + dmas((2,), (2,), (4,)),
        60,
        rides,
    )


def finish_kernel(count, replicas, *refs):
    inputs, outputs, scratch = split(refs, 3, 4)
    g_ref, early_ref, early_peer_ref = inputs
    q_out, k_out, v_out, rest_out = outputs
    early, land, total, mine, peer = scratch[:5]
    pair_send, pair_recv, part_send, part_recv, rep_send, rep_recv = scratch[5:]
    me = lax.axis_index("fsdp")
    chip, core = me // 2, lax.rem(me, 2)
    partner = partner_of("fsdp")

    def chip_at(offset):
        return lax.rem(chip + offset + count, count)

    def device(offset):
        return {"fsdp": chip_at(offset) * 2 + core}

    across = [partner_of("rep")] if replicas == 2 else []
    meet([device(offset) for offset in range(1, count)] + [partner] + across)
    swaps = [remote(g_ref.at[:, 1 - core], land.at[0], pair_send.at[0], pair_recv.at[0], partner)]
    swaps[0].start()
    for block in range(count):
        for half in range(2):
            both = early_ref[block, half].astype(F32)
            if replicas == 2:
                both = both + early_peer_ref[block, half].astype(F32)
            early[half, block] = both.astype(BF16)
    swaps.append(remote(early.at[1 - core], land.at[1], pair_send.at[1], pair_recv.at[1], partner))
    swaps[1].start()
    for swap in swaps:
        swap.wait()
    for block in range(count):
        total[block, 0] = (g_ref[block, core].astype(F32) + land[0, block].astype(F32)).astype(BF16)
        total[block, 1] = (early[core, block].astype(F32) + land[1, block].astype(F32)).astype(BF16)
    sends = [
        remote(
            total.at[chip_at(offset)], mine.at[chip],
            part_send.at[offset], part_recv.at[offset], device(offset),
        )
        for offset in range(1, count)
    ]
    for send in sends:
        send.start()
    mine[chip] = total[chip]

    def to_peer(offset):
        slot = chip_at(-offset)
        return remote(mine.at[slot, 0], peer.at[slot], rep_send.at[offset], rep_recv.at[offset], across[0])

    for offset in range(count):
        if offset > 0:
            slot = mine.at[chip_at(-offset)]
            remote(slot, slot, part_send.at[offset], part_recv.at[offset], partner).wait_recv()
        if replicas == 2:
            to_peer(offset).start()
    if replicas == 2:
        for offset in range(count):
            to_peer(offset).wait()

    def tiles(block, layer):
        value = mine[block, layer].astype(F32)
        if replicas == 2 and layer == 0:
            value = value + peer[block].astype(F32)
        return [value[:, i * LANES : (i + 1) * LANES] for i in range(3)]

    for layer in range(LAYERS):
        for half in range(count // 2):
            a, b = tiles(2 * half, layer), tiles(2 * half + 1, layer)
            low = lanes_of(a[0]) < HD
            q_out[layer, :, 3 * half * LANES : 3 * (half + 1) * LANES] = jnp.concatenate(
                [a[0], jnp.where(low, a[1], turn(b[0])), jnp.where(low, turn(b[0]), turn(b[1]))], 1
            )
            here = slice(half * LANES, (half + 1) * LANES)
            k_out[layer, :, here] = jnp.where(low, turn(a[1]), b[1])
            v_out[layer, :, here] = jnp.where(low, a[2], turn(b[2]))
            rest_out[layer, 2 * half] = a[2]
            rest_out[layer, 2 * half + 1] = b[2]
    for send in sends:
        send.wait_send()


def finish_heads(count, replicas, g, early, early_peer):
    _, _, rows, columns = g.shape
    width = count * GROUP * HD
    part = (count, LAYERS, rows, columns)
    dma = pltpu.SemaphoreType.DMA
    return pl.pallas_call(
        functools.partial(finish_kernel, count, replicas),
        out_shape=(
            cells((LAYERS, rows, width), F32),
            cells((LAYERS, rows, count * HD), F32),
            cells((LAYERS, rows, count * HD), F32),
            cells((LAYERS, count, rows, LANES), F32),
        ),
        in_specs=[HERE] * 3,
        out_specs=[HERE] * 4,
        scratch_shapes=[
            pltpu.VMEM((2, count, rows, columns), BF16),
            pltpu.VMEM((2, count, rows, columns), BF16),
            pltpu.VMEM(part, BF16),
            pltpu.VMEM(part, BF16),
            pltpu.VMEM((count, rows, columns), BF16),
            dma((2,)), dma((2,)), dma((count,)), dma((count,)), dma((count,)), dma((count,)),
        ],
        compiler_params=pltpu.CompilerParams(
            collective_id=identity(("finish",)), has_side_effects=True, vmem_limit_bytes=60 << 20
        ),
        cost_estimate=FREE,
        name="finish_heads",
    )(g, early, early_peer)


def add_kernel(layers, *refs):
    out_refs = refs[-3:]
    for layer in range(layers):
        pairs = refs[layer * 10 : (layer + 1) * 10]
        sums = [pairs[i][...].astype(F32) + pairs[i + 5][...].astype(F32) for i in range(5)]
        out_refs[0][layer, 0] = sums[0]
        out_refs[1][layer, 0] = sums[1]
        out_refs[2][layer, 0] = jnp.concatenate(sums[2:], 1)


def add_experts(pairs):
    layers = len(pairs)
    rows, ff = pairs[0][0].shape
    width = rows // 3
    steps = 4
    tall, short = width // steps, ff // steps

    def at(first, length):
        return pl.BlockSpec((length, ff), lambda i: (first // length + i, 0))

    specs = [at(0, tall), at(width, tall)] + [at(2 * width + g * ff, short) for g in range(3)]
    arrays = [array for pair in pairs for array in pair for _ in range(5)]
    return pl.pallas_call(
        functools.partial(add_kernel, layers),
        grid=(steps,),
        out_shape=(
            cells((layers, 1, width, ff), F32),
            cells((layers, 1, width, ff), F32),
            cells((layers, 1, ff, width), F32),
        ),
        in_specs=specs * (2 * layers),
        out_specs=[
            pl.BlockSpec((layers, 1, tall, ff), lambda i: (0, 0, i, 0)),
            pl.BlockSpec((layers, 1, tall, ff), lambda i: (0, 0, i, 0)),
            pl.BlockSpec((layers, 1, short, width), lambda i: (0, 0, i, 0)),
        ],
        cost_estimate=FREE,
        name="add_experts",
    )(*arrays)


def chunk_keys(own_ref, other_ref, chunk):
    return jnp.concatenate([own_ref[chunk], other_ref[chunk]], 0)


def on_device(
    tokens,
    cotangent,
    positions,
    segments,
    routes,
    attn_gain,
    w_query,
    w_key,
    w_value,
    w_out,
    ffn_gain,
    router,
    w_gate,
    w_up,
    w_down,
):
    rows, width = tokens.shape
    devices = lax.axis_size("fsdp")
    replicas = lax.axis_size("rep")
    count = devices // 2
    me = lax.axis_index("fsdp")
    chip, core = me // 2, lax.rem(me, 2)
    shard = w_query.shape[1]
    experts = devices
    columns = 3 * LANES
    used = (GROUP + 2) * HD
    pairs = [(index, index ^ 1) for index in range(devices)]

    def swap(array):
        return lax.ppermute(array, "fsdp", pairs)

    small = jnp.concatenate(
        [attn_gain, ffn_gain, router.transpose(0, 2, 1).reshape(LAYERS * experts, shard)], 0
    )
    small = jnp.pad(small, ((0, 48 - small.shape[0]), (0, LANES - shard)))
    rate = jnp.exp(-jnp.log(10000.0) * jnp.arange(HD // 2, dtype=F32) / (HD // 2))
    angle = rate[:, None] * positions.astype(F32)[None, :]
    table = jnp.concatenate([jnp.cos(angle), jnp.sin(angle)], 0)
    slabs = jnp.concatenate(
        [
            w_query.reshape(LAYERS, shard, count, GROUP * HD),
            w_key.reshape(LAYERS, shard, count, HD),
            w_value.reshape(LAYERS, shard, count, HD),
            jnp.zeros((LAYERS, shard, count, columns - used), BF16),
        ],
        -1,
    ).transpose(2, 0, 1, 3)
    heads_w, outs_w, smalls, tables = exchange_weights(count, slabs, w_out, small, table)
    heads_w = heads_w.reshape(LAYERS, width, columns)
    params = smalls[:, : (2 + experts) * LAYERS, :shard].transpose(1, 0, 2).reshape(-1, width)
    params = params.astype(F32)
    own_w, _ = lax.optimization_barrier(([w_gate, w_up, w_down], smalls))
    experts_w = own_w + [swap(w) for w in own_w]

    flat_segments = segments.reshape(1, -1)
    kinds = jnp.arange(8, dtype=jnp.int32)[:, None]
    starts = jnp.sum((flat_segments < kinds).astype(jnp.int32), 1, keepdims=True)
    begin = jnp.sum(jnp.where(flat_segments == kinds, starts, 0), 0).reshape(count, 2, rows)
    begin = lax.dynamic_index_in_dim(begin, core, 1, True)

    hidden = tokens.astype(F32)
    x_attn = (normal(hidden)[1] * params[0:1]).astype(BF16)
    chosen = routes.transpose(0, 2, 1)
    saved = []
    for layer in range(LAYERS):
        query, kv, kv_other, x_all, att, lse, middle, x_moe, share = gather_attend_scatter(
            count, layer, x_attn, heads_w, outs_w, tables, begin, hidden, params, chosen
        )
        mixed, after, x_attn, m_all, share_all = gather_mix_scatter(
            count, layer, x_moe, share, middle, params, experts_w
        )
        saved.append((hidden, x_all, query, kv, kv_other, att, lse, middle, mixed, m_all, share_all))
        hidden = after
    activations = x_attn

    def across(array):
        return lax.ppermute(array, "rep", [(0, 1), (1, 0)]) if replicas == 2 else array

    grad, d_mix = cotangent.astype(F32), cotangent
    balance = jnp.sum(saved[-1][8] * grad, -1)
    side = jnp.broadcast_to(balance[None, :], (8, rows))
    expert_sums = [None] * LAYERS
    out_sums = [None] * LAYERS
    for layer in reversed(range(LAYERS)):
        hidden, x_all, query, kv, kv_other, att, lse, middle, mixed, m_all, share_all = saved[layer]
        rides = [out_sums[layer + 1], early] if layer + 1 < LAYERS and replicas == 2 else []
        grad_mid, d_branch, gain_two, expert_sum, g_router, *rode = gather_mix_back_scatter(
            count, layer, d_mix, side, m_all, share_all, params, grad, middle, experts_w, rides
        )
        if layer + 1 < LAYERS:
            d_branch, expert_sums[layer + 1] = lax.optimization_barrier(
                (d_branch, expert_sums[layer + 1])
            )
        expert_sums[layer] = (expert_sum, across(expert_sum))
        out_sum, grad, d_mix, side, heads = gather_attend_back_scatter(
            count, layer, d_branch, outs_w, heads_w, x_all, att, query, kv, kv_other, begin, lse, tables,
            [params, grad_mid, hidden, saved[max(layer - 1, 0)][8], g_router, gain_two],
        )
        out_sums[layer] = out_sum
        heads = heads.reshape(count, 2, shard, columns)
        early = heads if layer > 0 else early
    g_query, g_key, g_value, rest = finish_heads(
        count, replicas, heads, early, rode[1] if rode else early
    )
    if replicas == 2:
        g_gate, g_up, g_down = add_experts(expert_sums)
        arrived = [across(out_sums[0]), rode[0]]
        g_out = jnp.stack([a.astype(F32) + b.astype(F32) for a, b in zip(out_sums, arrived)])
    else:
        g_query, g_key, g_value, rest, g_out, flat_sums = [
            lax.psum(array.astype(BF16), "rep").astype(F32)
            for array in (
                g_query, g_key, g_value, rest,
                jnp.stack(out_sums),
                jnp.stack([own for own, _ in expert_sums]),
            )
        ]
        ff = w_gate.shape[3]
        g_gate, g_up = flat_sums[:, None, :width], flat_sums[:, None, width : 2 * width]
        g_down = flat_sums[:, 2 * width :].reshape(LAYERS, width // ff, ff, ff)
        g_down = g_down.transpose(0, 2, 1, 3).reshape(LAYERS, 1, ff, width)
    rest = rest[..., HD : HD + 4]
    gains = jnp.sum(rest, 1)
    g_router = rest[..., :2].transpose(0, 2, 1, 3).reshape(LAYERS, shard, experts)
    return (
        activations,
        grad,
        gains[..., 2],
        g_query,
        g_key,
        g_value,
        g_out,
        gains[..., 3],
        g_router,
        g_gate,
        g_up,
        g_down,
    )


def solution(mesh):
    placed = (
        P(("rep", "fsdp"), None),
        P(("rep", "fsdp"), None),
        P(("rep", "fsdp")),
        P("rep", None),
        P(None, ("rep", "fsdp"), None),
        P(None, "fsdp"),
        P(None, "fsdp", None),
        P(None, "fsdp", None),
        P(None, "fsdp", None),
        P(None, "fsdp", None),
        P(None, "fsdp"),
        P(None, "fsdp", None),
        P(None, "fsdp", None, None),
        P(None, "fsdp", None, None),
        P(None, "fsdp", None, None),
    )
    return jax.shard_map(
        on_device,
        mesh=mesh,
        in_specs=placed,
        out_specs=(
            P(("rep", "fsdp"), None),
            P(("rep", "fsdp"), None),
            P(None, "fsdp"),
            P(None, "fsdp", None),
            P(None, "fsdp", None),
            P(None, "fsdp", None),
            P(None, "fsdp", None),
            P(None, "fsdp"),
            P(None, "fsdp", None),
            P(None, "fsdp", None, None),
            P(None, "fsdp", None, None),
            P(None, "fsdp", None, None),
        ),
        check_vma=False,
    )
```

```python
import functools

import jax
import jax.numpy as jnp
from jax import lax
from jax.experimental import pallas as pl
from jax.experimental.pallas import tpu as pltpu
from jax.sharding import PartitionSpec as P

HEADS = 24
KV_HEADS = 8
HD = 64
LAYERS = 2
GROUP = HEADS // KV_HEADS
LANES = 128
SPAN = 2
EPS = 1e-06
MASKED = -1e30
MESH = pl.DeviceIdType.MESH
F32 = jnp.float32
BF16 = jnp.bfloat16


def ring_place(chip, count):
    return lax.select(lax.rem(chip, 2) == 0, chip // 2, count - 1 - chip // 2)


def ring_chip(place, count):
    return lax.select(place < count // 2, 2 * place, 2 * (count - 1 - place) + 1)


def ring_setup(count):
    me = lax.axis_index("fsdp")
    chip, core = me // 2, lax.rem(me, 2)
    place = ring_place(chip, count)

    def at(offset):
        return ring_chip(lax.rem(place + offset + 2 * count, count), count)

    near = [{"fsdp": at(1) * 2 + core}, {"fsdp": at(-1) * 2 + core}]
    return chip, at, near


def partner_of(axis):
    if axis == "rep":
        return {"rep": 1 - lax.axis_index("rep")}
    me = lax.axis_index("fsdp")
    return {"fsdp": me + 1 - 2 * lax.rem(me, 2)}


def meet(others):
    barrier = pltpu.get_barrier_semaphore()
    for other in others:
        pl.semaphore_signal(barrier, inc=1, device_id=other, device_id_type=MESH)
    pl.semaphore_wait(barrier, len(others))


def remote(src, dst, send_sem, recv_sem, device):
    return pltpu.make_async_remote_copy(
        src_ref=src,
        dst_ref=dst,
        send_sem=send_sem,
        recv_sem=recv_sem,
        device_id=device,
        device_id_type=MESH,
    )


def ring_hops(count):
    half = count // 2
    return {(0, 0): half, (1, 1): half, (0, 1): half - 1, (1, 0): half - 1}


IDENTITIES = {}


def identity(key):
    return IDENTITIES.setdefault(key, len(IDENTITIES))


class Ring:
    def __init__(self, count, traffic):
        self.count = count
        self.riders, self.early, self.late, self.soon = traffic
        self.steps = count // 2
        self.chip, self.at, self.near = ring_setup(count)

    def meet(self, partner=False):
        others = self.near + ([partner_of("fsdp")] if partner else [])
        meet(others + ([partner_of("rep")] if self.riders else []))
        for rider in self.riders:
            rider.start()
        for copy in self.early:
            copy.wait()

    def settle(self):
        for copy in self.late:
            copy.wait()

    def depart(self):
        for copy in self.soon:
            copy.start()

    def gather(self, x_ref, buf, sems, side=None, first=None, second=None):
        own_sem, send_sem, recv_sem = sems[:3]
        half_rows = x_ref.shape[0] // 2
        steps = self.steps
        own = [pltpu.make_async_copy(x_ref, buf.at[self.chip], own_sem.at[0])]
        if side is not None:
            side_ref, side_buf = side
            side_send, side_recv = sems[3:]
            own.append(pltpu.make_async_copy(side_ref, side_buf.at[self.chip], own_sem.at[1]))
        for copy in own:
            copy.start()

        def piece(key, step, block, source=None):
            direction, part = key
            rows = pl.ds(part * half_rows, half_rows)
            target = buf.at[block, rows]
            return remote(
                target if source is None else source.at[rows],
                target,
                send_sem.at[direction, part, step],
                recv_sem.at[direction, part, step],
                self.near[direction],
            )

        def side_piece(direction, step, block, source=None):
            target = side_buf.at[block]
            return remote(
                target if source is None else source,
                target,
                side_send.at[direction, step],
                side_recv.at[direction, step],
                self.near[direction],
            )

        def toward(key, places):
            return self.at(-places if key[0] == 0 else places)

        early, late = [(0, 0), (1, 1)], [(0, 1), (1, 0)]
        if side is not None:
            for direction in range(2):
                side_piece(direction, 0, self.chip, side_ref).start()
        for key in early + late:
            piece(key, 0, self.chip, x_ref).start()

        def take(keys, s, last):
            for key in keys:
                block = toward(key, s)
                piece(key, s - 1, block).wait_recv()

                @pl.when(s < last)
                def _():
                    piece(key, s, block).start()

        def take_side(s):
            if side is not None:
                for direction in range(2):

                    @pl.when(s <= steps - direction)
                    def _():
                        block = toward((direction, 0), s)
                        side_piece(direction, s - 1, block).wait_recv()

                        @pl.when(s < steps - direction)
                        def _():
                            side_piece(direction, s, block).start()

        def step(s, carry):
            take_side(s)
            take(early, s, steps)
            first(s)
            take(late, s, steps - 1)
            second(s)
            return carry

        for copy in own:
            copy.wait()
        lax.fori_loop(1, steps, step, 0)
        first(steps)
        take_side(steps)
        take(early, steps, steps)

        def drain():
            for s in range(steps):
                for key in early + (late if s < steps - 1 else []):
                    piece(key, s, toward(key, s)).wait_send()
                if side is not None:
                    for direction in range(2):
                        if s < steps - direction:
                            side_piece(direction, s, toward((direction, 0), s)).wait_send()

        return drain

    def pair(self, s):
        return self.at(s), self.at(-s)

    def meanwhile(self, compute):
        def first(s):
            @pl.when(s == 1)
            def _():
                for part in range(2):
                    compute(part, (self.chip,))

            @pl.when(s > 1)
            def _():
                compute(1, self.pair(s - 1))

        return first, lambda s: compute(0, self.pair(s))

    def scatter(self, partial, land, sems, work=None, between=None):
        send_sem, recv_sem = sems
        half_rows = partial.shape[1] // 2
        steps = self.steps
        hops = ring_hops(self.count)

        def ahead(key, s):
            places = hops[key] - s
            return self.at(places if key[0] == 0 else -places)

        def piece(key, s, source):
            direction, part = key
            return remote(
                source,
                land.at[direction, part, s],
                send_sem.at[direction, part, s],
                recv_sem.at[direction, part, s],
                self.near[direction],
            )

        def rows_of(key):
            return pl.ds(key[1] * half_rows, half_rows)

        for place, key in enumerate(hops):
            if place == 2 and between is not None:
                between()
            piece(key, 0, partial.at[ahead(key, 0), rows_of(key)]).start()

        def step(s, carry):
            for place, key in enumerate(hops):
                if work is not None:
                    work(s - 1, place)

                @pl.when(s < hops[key])
                def _():
                    slot = land.at[key[0], key[1], s - 1]
                    piece(key, s - 1, slot).wait_recv()
                    mine = partial[ahead(key, s), rows_of(key)]
                    slot[...] = (slot[...].astype(F32) + mine.astype(F32)).astype(BF16)
                    piece(key, s, slot).start()

            return carry

        lax.fori_loop(1, steps + 1, step, 0)
        for key in hops:
            slot = land.at[key[0], key[1], hops[key] - 1]
            piece(key, hops[key] - 1, slot).wait_recv()
        halves = []
        for part in range(2):
            rows = pl.ds(part * half_rows, half_rows)
            total = partial[self.chip, rows].astype(F32)
            for direction in range(2):
                total = total + land[direction, part, hops[direction, part] - 1].astype(F32)
            halves.append(total)
        summed = jnp.concatenate(halves, 0)

        def drain():
            for key in hops:
                for s in range(hops[key]):
                    piece(key, s, land.at[key[0], key[1], s]).wait_send()

        return summed, drain


def dmas(*shapes):
    return [pltpu.SemaphoreType.DMA(shape) for shape in shapes]


def gather_sems(count, sided=False):
    steps = count // 2
    shapes = [(2,), (2, 2, steps), (2, 2, steps)]
    return dmas(*(shapes + ([(2, steps), (2, steps)] if sided else [])))


def scatter_sems(count):
    return dmas((2, 2, count // 2), (2, 2, count // 2))


ANYWHERE = pl.BlockSpec(memory_space=pltpu.HBM)
HERE = pl.BlockSpec(memory_space=pltpu.VMEM)
EARLY, LATE = "early", "late"
OUT, SOON = "out", "soon"


FREE = pl.CostEstimate(flops=0, bytes_accessed=0, transcendentals=0)


def ring_call(body, key, inputs, outputs, scratch, megabytes, rides=()):
    n_in, n_out, n_rides = len(inputs), len(outputs), len(rides)
    in_kinds = [kind for _, kind in inputs]
    out_kinds = [kind for _, kind in outputs]
    copied = [a for a, kind in inputs if kind in (EARLY, LATE)]
    returned = [a for a, kind in outputs if kind in (OUT, SOON)]
    moves = len(copied) + len(returned)

    def kernel(*refs):
        ins, ride_in, outs, ride_out, rest = split(refs, n_in, n_rides, n_out, n_rides)
        rest, own, rest_sems = rest[: len(scratch)], rest[len(scratch) : len(scratch) + moves], rest[len(scratch) + moves :]
        move_sem, rest_sems = rest_sems[0], rest_sems[1:]
        riders = []
        if n_rides:
            send_sem, recv_sem = rest_sems
            riders = [
                remote(ride_in[i], ride_out[i], send_sem.at[i], recv_sem.at[i], partner_of("rep"))
                for i in range(n_rides)
            ]
        used = 0
        early, late, leaving, soon = [], [], [], []
        ins, outs = list(ins), list(outs)
        for i, kind in enumerate(in_kinds):
            if kind in (EARLY, LATE):
                copy = pltpu.make_async_copy(ins[i], own[used], move_sem.at[used])
                copy.start()
                (early if kind == EARLY else late).append(copy)
                ins[i] = own[used]
                used += 1
        for i, kind in enumerate(out_kinds):
            if kind in (OUT, SOON):
                copy = pltpu.make_async_copy(own[used], outs[i], move_sem.at[used])
                (leaving if kind == OUT else soon).append(copy)
                outs[i] = own[used]
                used += 1
        body((riders, early, late, soon), *ins, *outs, *rest)
        for copy in leaving:
            copy.start()
        for rider in riders:
            rider.wait()
        for copy in leaving + soon:
            copy.wait()

    def spec(kind):
        return ANYWHERE if isinstance(kind, str) else kind

    return pl.pallas_call(
        kernel,
        out_shape=tuple(shape for shape, _ in outputs) + tuple(cells(a.shape, a.dtype) for a in rides),
        in_specs=[spec(kind) for kind in in_kinds] + [ANYWHERE] * n_rides,
        out_specs=[spec(kind) for kind in out_kinds] + [ANYWHERE] * n_rides,
        scratch_shapes=list(scratch)
        + [pltpu.VMEM(a.shape, a.dtype) for a in copied + returned]
        + dmas((max(moves, 1),))
        + (dmas((n_rides,), (n_rides,)) if n_rides else []),
        compiler_params=pltpu.CompilerParams(
            collective_id=identity(key),
            has_side_effects=True,
            vmem_limit_bytes=megabytes << 20,
        ),
        cost_estimate=FREE,
        name=key[0],
    )(*[array for array, _ in inputs], *rides)


def split(refs, *sizes):
    parts, place = [], 0
    for size in sizes:
        parts.append(refs[place : place + size])
        place += size
    return parts + [refs[place:]]


def cells(shape, dtype):
    return jax.ShapeDtypeStruct(shape, dtype)


def setup_kernel(
    count, slab_ref, out_w_ref, small_ref, table_ref,
    heads_ref, outs_ref, smalls_ref, tables_ref,
    own_sem, slab_send, slab_recv, pass_send, pass_recv,
    small_send, small_recv, table_send, table_recv, out_send, out_recv,
):
    devices = 2 * count
    me = lax.axis_index("fsdp")
    chip, core = me // 2, lax.rem(me, 2)
    layers = slab_ref.shape[1]

    def device(offset):
        return {"fsdp": lax.rem(me + offset, devices)}

    def chip_at(offset):
        return lax.rem(chip + offset + count, count)

    partner = partner_of("fsdp")
    meet([device(offset) for offset in range(1, devices)])
    copies = [
        pltpu.make_async_copy(slab_ref.at[chip, layer], heads_ref.at[layer, me], own_sem.at[layer])
        for layer in range(layers)
    ] + [
        pltpu.make_async_copy(small_ref, smalls_ref.at[me], own_sem.at[layers]),
        pltpu.make_async_copy(table_ref, tables_ref.at[chip], own_sem.at[layers + 1]),
        pltpu.make_async_copy(out_w_ref, outs_ref.at[core], own_sem.at[layers + 2]),
    ]
    sends = [
        remote(small_ref, smalls_ref.at[me], small_send.at[offset], small_recv.at[offset], device(offset))
        for offset in range(1, devices)
    ]
    for offset in range(1, count):
        there = {"fsdp": chip_at(offset) * 2 + core}
        sends.append(
            remote(table_ref, tables_ref.at[chip], table_send.at[offset], table_recv.at[offset], there)
        )
        for layer in range(layers):
            sends.append(
                remote(
                    slab_ref.at[chip_at(offset), layer], heads_ref.at[layer, me],
                    slab_send.at[offset, layer], slab_recv.at[offset, layer], there,
                )
            )
    for layer in range(layers):
        sends.append(
            remote(
                slab_ref.at[chip, layer], heads_ref.at[layer, me],
                pass_send.at[0, layer], pass_recv.at[0, layer], partner,
            )
        )
    sends.append(remote(out_w_ref, outs_ref.at[core], out_send.at[0], out_recv.at[0], partner))
    for copy in copies + sends:
        copy.start()
    for offset in range(1, count):
        origin = chip_at(-offset) * 2 + core
        for layer in range(layers):
            slot = heads_ref.at[layer, origin]
            remote(slot, slot, slab_send.at[offset, layer], slab_recv.at[offset, layer], partner).wait_recv()
            forward = remote(slot, slot, pass_send.at[offset, layer], pass_recv.at[offset, layer], partner)
            forward.start()
    for offset in range(1, count):
        origin = chip_at(-offset)
        table = tables_ref.at[origin]
        remote(table, table, table_send.at[offset], table_recv.at[offset], partner).wait_recv()
    for offset in range(count):
        origin = chip_at(-offset) * 2 + 1 - core
        mine = chip_at(-offset) * 2 + core
        for layer in range(layers):
            slot, sent = heads_ref.at[layer, origin], heads_ref.at[layer, mine]
            if offset > 0:
                remote(sent, sent, pass_send.at[offset, layer], pass_recv.at[offset, layer], partner).wait_send()
            remote(slot, slot, pass_send.at[offset, layer], pass_recv.at[offset, layer], partner).wait_recv()
    for offset in range(1, devices):
        slot = smalls_ref.at[lax.rem(me - offset + devices, devices)]
        remote(slot, slot, small_send.at[offset], small_recv.at[offset], partner).wait_recv()
    other = outs_ref.at[1 - core]
    remote(other, other, out_send.at[0], out_recv.at[0], partner).wait_recv()
    for copy in copies:
        copy.wait()
    for send in sends:
        send.wait_send()


def exchange_weights(count, slabs, out_w, small, table):
    layers = slabs.shape[1]
    devices = 2 * count
    dma = pltpu.SemaphoreType.DMA
    anywhere = pl.BlockSpec(memory_space=pl.ANY)
    return pl.pallas_call(
        functools.partial(setup_kernel, count),
        out_shape=(
            jax.ShapeDtypeStruct((layers, devices) + slabs.shape[2:], slabs.dtype),
            jax.ShapeDtypeStruct((2,) + out_w.shape, out_w.dtype),
            jax.ShapeDtypeStruct((devices,) + small.shape, small.dtype),
            jax.ShapeDtypeStruct((count,) + table.shape, table.dtype),
        ),
        in_specs=[anywhere] * 4,
        out_specs=[anywhere] * 4,
        scratch_shapes=[
            dma((layers + 3,)),
            dma((count, layers)),
            dma((count, layers)),
            dma((count, layers)),
            dma((count, layers)),
            dma((devices,)),
            dma((devices,)),
            dma((count,)),
            dma((count,)),
            dma((1,)),
            dma((1,)),
        ],
        compiler_params=pltpu.CompilerParams(
            collective_id=identity(("setup",)), has_side_effects=True, vmem_limit_bytes=60 << 20
        ),
        cost_estimate=FREE,
        name="exchange_weights",
    )(slabs, out_w, small, table)


def dot(left, right, contract=((1,), (0,))):
    return lax.dot_general(left, right, (contract, ((), ())), preferred_element_type=F32)


NT = ((1,), (1,))
TN = ((0,), (0,))


def lanes_of(field):
    return lax.broadcasted_iota(jnp.int32, field.shape, 1)


def turn(field):
    return pltpu.roll(field, HD, 1)


def spin(field, cosine, sine):
    swapped = jnp.where(
        lax.rem(lanes_of(field), HD) < HD // 2,
        -pltpu.roll(field, LANES - HD // 2, 1),
        pltpu.roll(field, HD // 2, 1),
    )
    return field * cosine + swapped * sine


def project_rows(rows, cosine, sine):
    first = spin(rows[:, :LANES], cosine, sine)
    second = spin(rows[:, LANES : 2 * LANES], cosine, sine)
    third = rows[:, 2 * LANES :]
    low = lanes_of(first) < HD
    heads = []
    for field in (first, turn(first), second):
        rounded = jnp.where(low, field, 0.0).astype(BF16).astype(F32)
        heads.append((rounded * (HD**-0.5)).astype(BF16))
    return heads, jnp.where(low, turn(second), turn(third)).astype(BF16)


def angles(table):
    rows = jnp.concatenate([table, table], 0).T
    early = lax.rem(lanes_of(rows), HD) < HD // 2
    cosine = jnp.where(early, rows, pltpu.roll(rows, HD // 2, 1))
    sine = jnp.where(early, pltpu.roll(rows, LANES - HD // 2, 1), rows)
    return cosine, sine


def normal(values):
    inverse = lax.rsqrt(jnp.mean(values * values, -1, keepdims=True) + EPS)
    return inverse, values * inverse


def normal_back(d_x, values, gain):
    inverse, normed = normal(values)
    d_norm = d_x * gain
    d_values = inverse * (d_norm - normed * jnp.mean(d_norm * normed, -1, keepdims=True))
    return d_values, jnp.sum(d_x * normed, 0, keepdims=True)


def diagonal():
    shape = (LANES, LANES)
    return lax.broadcasted_iota(jnp.int32, shape, 0) == lax.broadcasted_iota(jnp.int32, shape, 1)


def as_column(line):
    return jnp.sum(jnp.where(diagonal(), jnp.broadcast_to(line, (LANES, LANES)), 0.0), 1, keepdims=True)


def as_line(column):
    return jnp.sum(jnp.where(diagonal(), jnp.broadcast_to(column, (LANES, LANES)), 0.0), 0, keepdims=True)


def flat(value):
    return value.reshape(value.shape[0] * value.shape[1], value.shape[2])


def stack(ref, blocks):
    parts = [ref[b] for b in blocks]
    return parts[0] if len(parts) == 1 else jnp.concatenate(parts, 0)


def cut(value, blocks):
    return [(b, value[i * LANES : (i + 1) * LANES]) for i, b in enumerate(blocks)]


def gain_row(params_ref, kind, layer):
    row = kind * LAYERS + layer
    return params_ref[row : row + 1, :]


def router_rows(experts, layer):
    first = 2 * LAYERS + layer * experts
    return slice(first, first + experts)


def allowed_keys(begin, query, chunk, core):
    half = SPAN * LANES
    shape = (2 * half, begin.shape[1])
    place = lax.broadcasted_iota(jnp.int32, (2 * half, 1), 0)
    inner = lax.rem(place, half)
    whose = jnp.where(place < half, core, 1 - core)
    key = chunk * 2 * half + inner // LANES * (2 * LANES) + whose * LANES + lax.rem(inner, LANES)
    key = jnp.broadcast_to(key, shape)
    return (key >= begin) & (key <= query)


def query_rows(begin_ref, blocks, core):
    lane = lax.broadcasted_iota(jnp.int32, (1, LANES), 1)
    begin, query = [], []
    for block in blocks:
        begin += [begin_ref[block]] * GROUP
        query += [(2 * block + core) * LANES + lane] * GROUP
    return jnp.concatenate(begin, 1), jnp.concatenate(query, 1)


def chunk_keys(own_ref, other_ref, chunk):
    chips = pl.ds(chunk * SPAN, SPAN)
    return jnp.concatenate([flat(own_ref[chips]), flat(other_ref[chips])], 0)


def turn_keys(own_ref, other_ref, turned_ref):
    def one(chunk, carry):
        turned_ref[chunk] = chunk_keys(own_ref, other_ref, chunk).astype(F32).T.astype(BF16)
        return carry

    lax.fori_loop(0, turned_ref.shape[0], one, 0)


def by_head(field):
    return [field[:, h * LANES : (h + 1) * LANES].T for h in range(GROUP)]


def chunks_of(blocks):
    last = blocks[0] if len(blocks) == 1 else jnp.maximum(*blocks)
    return last // SPAN + 1


def attend_kernel(count, layer, traffic, *refs):
    inputs, outputs, scratch = split(refs, 8, 9)
    x_ref, w_ref, w_out_ref, table_ref, begin_ref, hidden_ref, params_ref, routes_ref = inputs
    q_ref, own_ref, other_ref, all_ref, att_ref, lse_ref, middle_ref, x_out_ref, share_ref = outputs
    buf, weights, wide_w, turned_ref, score_ref, partial, land = scratch[:7]
    sems, pair_sems, scatter_sem, out_sem, load_sem = split(scratch[7:], 3, 2, 2, 1)
    ring = Ring(count, traffic)
    loads = [pltpu.make_async_copy(w_ref.at[layer], weights, load_sem[0].at[2])]
    loads[0].start()
    loads += load_out_weights(w_out_ref, layer, wide_w, load_sem[0])
    ring.meet(True)
    partner = partner_of("fsdp")
    core = lax.rem(lax.axis_index("fsdp"), 2)

    def pass_on(block):
        return remote(
            own_ref.at[block], other_ref.at[block], pair_sems[0].at[block], pair_sems[1].at[block], partner
        )

    def project(blocks):
        rows = dot(stack(buf, blocks), weights[...])
        tables = [angles(table_ref[b]) for b in blocks]
        cosine = jnp.concatenate([t[0] for t in tables], 0)
        sine = jnp.concatenate([t[1] for t in tables], 0)
        heads, pair = project_rows(rows, cosine, sine)
        for index, head in enumerate(heads):
            for block, part in cut(head, blocks):
                q_ref[block, index] = part
        for block, part in cut(pair, blocks):
            own_ref[block] = part
            pass_on(block).start()

    def first(s):
        @pl.when(s == 1)
        def _():
            for load in loads:
                load.wait()
            project((ring.chip,))

    drain = ring.gather(x_ref, buf, sems, None, first, lambda s: project(ring.pair(s)))
    keep = pltpu.make_async_copy(buf, all_ref, out_sem[0].at[0])
    keep.start()
    project((ring.at(ring.steps),))
    for block in range(count):
        pass_on(block).wait()
    ring.depart()
    turn_keys(own_ref, other_ref, turned_ref)

    def attend(blocks):
        width = len(blocks) * GROUP * LANES
        q = jnp.concatenate([q_ref[b].reshape(GROUP * LANES, LANES) for b in blocks], 0)
        begin, query = query_rows(begin_ref, blocks, core)
        end = chunks_of(blocks)

        def score(chunk, top):
            keys = chunk_keys(own_ref, other_ref, chunk)
            scores = jnp.where(allowed_keys(begin, query, chunk, core), dot(keys, q, NT), MASKED)
            score_ref[chunk, :, :width] = scores
            return jnp.maximum(top, jnp.max(scores, 0, keepdims=True))

        top = lax.fori_loop(0, end, score, jnp.full((1, width), MASKED, F32))

        def add(chunk, state):
            total, acc = state
            weights = jnp.exp(score_ref[chunk, :, :width] - top)
            total = total + jnp.sum(weights, 0, keepdims=True)
            return total, acc + dot(turned_ref[chunk], weights.astype(BF16))

        total, acc = lax.fori_loop(
            0, end, add, (jnp.zeros((1, width), F32), jnp.zeros((LANES, width), F32))
        )
        lse = top + jnp.log(total)
        att = acc / total
        rows = []
        for place, block in enumerate(blocks):
            here = slice(place * GROUP * LANES, (place + 1) * GROUP * LANES)
            lse_ref[block] = lse[:, here]
            heads = by_head(att[:, here])
            low = lanes_of(heads[0]) < HD
            rows.append(
                jnp.concatenate(
                    [jnp.where(low, turn(heads[0]), heads[1]), jnp.where(low, turn(heads[2]), 0.0)], 1
                ).astype(BF16)
            )
            att_ref[block] = rows[-1]
        out = dot(jnp.concatenate(rows, 0) if len(rows) > 1 else rows[0], wide_w[...]).astype(BF16)
        for block, part in cut(out, blocks):
            partial[block] = part

    attend((ring.at(ring.steps),))

    def between():
        attend(ring.pair(ring.steps - 1))

    def work(s, place):
        if place == 2:

            @pl.when(s < ring.steps - 2)
            def _():
                attend(ring.pair(ring.steps - 2 - s))

            @pl.when(s == ring.steps - 2)
            def _():
                attend((ring.chip,))

    added, finish = ring.scatter(partial, land, scatter_sem, work, between)
    ring.settle()
    middle = hidden_ref[...] + added
    middle_ref[...] = middle
    x = (normal(middle)[1] * gain_row(params_ref, 1, layer)).astype(BF16)
    x_out_ref[...] = x
    experts = share_ref.shape[0]
    logits = dot(params_ref[router_rows(experts, layer), :].astype(BF16), x, NT)
    expert = lax.broadcasted_iota(jnp.int32, logits.shape, 0)
    named = expert < 0
    for choice in range(routes_ref.shape[1]):
        named = named | (expert == routes_ref[layer, choice : choice + 1, :])
    scores = jnp.where(named, logits, MASKED)
    weighted = jnp.where(named, jnp.exp(scores - jnp.max(scores, 0, keepdims=True)), 0.0)
    share_ref[...] = weighted / jnp.sum(weighted, 0, keepdims=True)
    drain()
    finish()
    keep.wait()


def gather_attend_scatter(count, layer, x, w, w_out, tables, begin, hidden, params, routes):
    rows, width = x.shape
    block = cells((count, rows, LANES), BF16)
    everyone = pltpu.VMEM((count, rows, width), BF16)
    wide = 2 * LANES
    return ring_call(
        functools.partial(attend_kernel, count, layer),
        ("attend", layer),
        [
            (x, ANYWHERE), (w, ANYWHERE), (w_out, ANYWHERE), (tables, EARLY), (begin, EARLY),
            (hidden, LATE), (params, LATE), (routes, LATE),
        ],
        [
            (cells((count, GROUP, rows, LANES), BF16), SOON),
            (block, SOON),
            (block, SOON),
            (cells((count, rows, width), BF16), ANYWHERE),
            (cells((count, rows, wide), BF16), OUT),
            (cells((count, 1, GROUP * rows), F32), OUT),
            (cells((rows, width), F32), OUT),
            (cells((rows, width), BF16), OUT),
            (cells((2 * count, rows), F32), OUT),
        ],
        [
            everyone,
            pltpu.VMEM(w.shape[1:], BF16),
            pltpu.VMEM((wide, width), BF16),
            pltpu.VMEM((count // SPAN, LANES, SPAN * wide), BF16),
            pltpu.VMEM((count // SPAN, SPAN * wide, 2 * GROUP * LANES), F32),
            everyone,
            land_scratch(count, rows, width),
        ]
        + gather_sems(count)
        + dmas((count,), (count,))
        + scatter_sems(count)
        + dmas((1,), (3,)),
        60,
    )


def load_experts(refs, layer, gates, ups, downs, sem):
    copies = []
    for e in range(2):
        for place, buf in enumerate((gates, ups, downs)):
            source = refs[3 * e + place].at[layer, 0]
            copies.append(pltpu.make_async_copy(source, buf.at[e], sem.at[3 * e + place]))
    for copy in copies:
        copy.start()
    return copies


def expert_of(e):
    me = lax.axis_index("fsdp")
    return me if e == 0 else me + 1 - 2 * lax.rem(me, 2)


def share_of(share_ref, e, blocks):
    columns = [as_column(share_ref[b, pl.ds(expert_of(e), 1), :]) for b in blocks]
    return jnp.concatenate(columns, 0) if len(columns) > 1 else columns[0]


def after_loads(loads, run):
    def first(s):
        @pl.when(s == 1)
        def _():
            for load in loads:
                load.wait()

        run(s)

    return first


def mix_kernel(count, layer, traffic, *refs):
    inputs, outputs, scratch = split(refs, 10, 5)
    x_ref, side_ref, middle_ref, params_ref = inputs[:4]
    mixed_ref, hidden_ref, next_ref, all_ref, share_ref = outputs
    buf, partial, land, acc, gates, ups, downs = scratch[:7]
    sems, scatter_sem, load_sem, out_sem = split(scratch[7:], 5, 2, 1)
    ring = Ring(count, traffic)
    loads = load_experts(inputs[4:], layer, gates, ups, downs, load_sem[0])
    ring.meet()

    def compute(e, blocks):
        x = stack(buf, blocks)
        act_gate, act_up = dot(x, gates[e]), dot(x, ups[e])
        hidden = jax.nn.silu(act_gate) * act_up * share_of(share_ref, e, blocks)
        part = dot(hidden.astype(BF16), downs[e])
        if e == 0:
            acc[: x.shape[0]] = part
        else:
            total = (acc[: x.shape[0]] + part).astype(BF16)
            for block, rows in cut(total, blocks):
                partial[block] = rows

    first, second = ring.meanwhile(compute)
    drain = ring.gather(x_ref, buf, sems, (side_ref, share_ref), after_loads(loads, first), second)
    keep = pltpu.make_async_copy(buf, all_ref, out_sem[0].at[0])
    keep.start()
    for e in range(2):
        compute(e, (ring.at(ring.steps),))
    mixed, finish = ring.scatter(partial, land, scatter_sem)
    ring.settle()
    mixed_ref[...] = mixed
    hidden = middle_ref[...] + mixed
    hidden_ref[...] = hidden
    if layer + 1 < LAYERS:
        next_ref[...] = (normal(hidden)[1] * gain_row(params_ref, 0, layer + 1)).astype(BF16)
    else:
        next_ref[...] = hidden.astype(BF16)
    drain()
    finish()
    keep.wait()


def expert_scratch(weights):
    return [pltpu.VMEM((2,) + w.shape[2:], BF16) for w in weights[:3]]


def land_scratch(count, rows, width):
    return pltpu.VMEM((2, 2, count // 2, rows // 2, width), BF16)


def gather_mix_scatter(count, layer, x, share, middle, params, weights):
    rows, width = x.shape
    everyone = pltpu.VMEM((count, rows, width), BF16)
    own = cells((rows, width), F32)
    return ring_call(
        functools.partial(mix_kernel, count, layer),
        ("mix", layer),
        [(x, ANYWHERE), (share, ANYWHERE), (middle, LATE), (params, LATE)]
        + [(w, ANYWHERE) for w in weights],
        [
            (own, OUT),
            (own, OUT),
            (cells((rows, width), BF16), OUT),
            (cells((count, rows, width), BF16), ANYWHERE),
            (cells((count,) + share.shape, F32), OUT),
        ],
        [everyone, everyone, land_scratch(count, rows, width), pltpu.VMEM((2 * rows, width), F32)]
        + expert_scratch(weights)
        + gather_sems(count, True)
        + scatter_sems(count)
        + dmas((6,), (1,)),
        60,
    )


def mix_back_kernel(count, layer, traffic, *refs):
    inputs, outputs, scratch = split(refs, 13, 5)
    d_ref, side_ref, m_ref, share_ref, params_ref, grad_ref, middle_ref = inputs[:7]
    mid_ref, branch_ref, gain_ref, sum_ref, g_router_ref = outputs
    buf, partial, land, acc, gates, ups, downs = scratch[:7]
    tokens, acts, hiddens, balance_ref, totals, got = scratch[7:13]
    sems, scatter_sem, load_sem, pair_sem, out_sem = split(scratch[13:], 5, 2, 1, 2)
    ring = Ring(count, traffic)
    loads = load_experts(inputs[7:], layer, gates, ups, downs, load_sem[0])
    loads.append(pltpu.make_async_copy(m_ref, tokens, load_sem[0].at[6]))
    loads[-1].start()
    ring.meet(True)
    ff = gates.shape[2]
    width = buf.shape[2]
    g_router_ref[...] = jnp.zeros_like(g_router_ref)
    routers = 2 * LAYERS + layer * 2 * count

    def compute(e, blocks):
        d, x = stack(buf, blocks), stack(tokens, blocks)
        share = share_of(share_ref, e, blocks)
        balance = [as_column(balance_ref[b, 0:1, :]) for b in blocks]
        balance = jnp.concatenate(balance, 0) if len(balance) > 1 else balance[0]
        act_gate, act_up = dot(x, gates[e]), dot(x, ups[e])
        sig = jax.nn.sigmoid(act_gate)
        swish = act_gate * sig
        hidden = swish * act_up
        raw = dot(d, downs[e], NT)
        d_logit = share * (jnp.sum(hidden * raw, -1, keepdims=True) - balance)
        d_hidden = raw * share
        d_gate = (d_hidden * act_up * sig * (1.0 + act_gate * (1.0 - sig))).astype(BF16)
        d_up = (d_hidden * swish).astype(BF16)
        weighted = (hidden * share).astype(BF16)
        part = dot(d_gate, gates[e], NT) + dot(d_up, ups[e], NT)
        part = part + d_logit * params_ref[pl.ds(routers + expert_of(e), 1), :]
        g_router_ref[e : e + 1, :] += jnp.sum(d_logit * x.astype(F32), 0, keepdims=True)
        for place, block in enumerate(blocks):
            here = slice(place * LANES, (place + 1) * LANES)
            acts[e, block, :, :ff] = d_gate[here]
            acts[e, block, :, ff:] = d_up[here]
            hiddens[e, block] = weighted[here]
        if e == 0:
            acc[: x.shape[0]] = part
        else:
            total = (acc[: x.shape[0]] + part).astype(BF16)
            for block, rows in cut(total, blocks):
                partial[block] = rows

    first, second = ring.meanwhile(compute)
    drain = ring.gather(d_ref, buf, sems, (side_ref, balance_ref), after_loads(loads, first), second)
    for e in range(2):
        compute(e, (ring.at(ring.steps),))

    partner = partner_of("fsdp")
    strip = 2 * LANES
    strips = width // (2 * strip)
    groups = width // ff

    def regions(half):
        regions = [(group * width + half * (width // 2), width // 2) for group in range(2)]
        return regions + [(2 * width + group * ff + half * (ff // 2), ff // 2) for group in range(groups)]

    def swap(half):
        return [
            remote(
                totals.at[1, pl.ds(first, length)], got.at[pl.ds(first, length)],
                pair_sem[0].at[half, index], pair_sem[1].at[half, index], partner,
            )
            for index, (first, length) in enumerate(regions(half))
        ]

    def store(half):
        return [
            pltpu.make_async_copy(
                totals.at[0, pl.ds(first, length)], sum_ref.at[pl.ds(first, length)], out_sem[0].at[half, index]
            )
            for index, (first, length) in enumerate(regions(half))
        ]

    def work(s, place):
        e = 1 - s // 2
        half = lax.rem(s, 2)

        def put(first, value):
            rows = pl.ds(pl.multiple_of(first, strip), strip)

            @pl.when(s < 2)
            def _():
                totals[1, rows] = value.astype(BF16)

            @pl.when(s >= 2)
            def _():
                totals[0, rows] = (value + got[rows].astype(F32)).astype(BF16)

        if place == 0:
            for h in range(2):

                @pl.when(s == 2 + h)
                def _():
                    for copy in swap(h):
                        copy.wait_recv()

        if place < strips:
            first = (half * strips + place) * strip
            columns = pl.ds(pl.multiple_of(first, strip), strip)
            value = dot(flat(tokens[:, :, columns]), flat(acts[e]), TN)
            for group in range(2):
                put(group * width + first, value[:, group * ff : (group + 1) * ff])
        if place == 3:
            columns = pl.ds(pl.multiple_of(half * strip, strip), strip)
            value = dot(flat(hiddens[e, :, :, columns]), flat(buf[...]), TN)
            for group in range(groups):
                put(2 * width + group * ff + half * strip, value[:, group * ff : (group + 1) * ff])
            for h in range(2):

                @pl.when(s == h)
                def _():
                    for copy in swap(h):
                        copy.start()

                @pl.when(s == 2 + h)
                def _():
                    for copy in store(h):
                        copy.start()

    d_x, finish = ring.scatter(partial, land, scatter_sem, work)
    ring.settle()
    d_values, gain_ref[...] = normal_back(d_x, middle_ref[...], gain_row(params_ref, 1, layer))
    grad = grad_ref[...] + d_values
    mid_ref[...] = grad
    branch_ref[...] = grad.astype(BF16)
    drain()
    finish()
    for half in range(2):
        for copy in swap(half):
            copy.wait_send()
        for copy in store(half):
            copy.wait()


def gather_mix_back_scatter(count, layer, d, side, m_all, share, params, grad, middle, weights, rides):
    rows, width = d.shape
    ff = weights[0].shape[3]
    everyone = pltpu.VMEM((count, rows, width), BF16)
    groups = width // ff
    own = cells((rows, width), F32)
    return ring_call(
        functools.partial(mix_back_kernel, count, layer),
        ("mix_back", layer),
        [(d, ANYWHERE), (side, ANYWHERE), (m_all, ANYWHERE), (share, EARLY), (params, EARLY), (grad, LATE), (middle, LATE)]
        + [(w, ANYWHERE) for w in weights],
        [
            (own, OUT),
            (cells((rows, width), BF16), OUT),
            (cells((1, width), F32), OUT),
            (cells((3 * width, ff), BF16), ANYWHERE),
            (cells((2, width), F32), OUT),
        ],
        [everyone, everyone, land_scratch(count, rows, width), pltpu.VMEM((2 * rows, width), F32)]
        + expert_scratch(weights)
        + [
            everyone,
            pltpu.VMEM((2, count, rows, 2 * ff), BF16),
            pltpu.VMEM((2, count, rows, ff), BF16),
            pltpu.VMEM((count,) + side.shape, F32),
            pltpu.VMEM((2, 3 * width, ff), BF16),
            pltpu.VMEM((3 * width, ff), BF16),
        ]
        + gather_sems(count, True)
        + scatter_sems(count)
        + dmas((7,), (2, 2 + groups), (2, 2 + groups), (2, 2 + groups)),
        60,
        rides,
    )


def load_out_weights(w_ref, layer, wide_ref, sem):
    shard = w_ref.shape[2]
    copies = [
        pltpu.make_async_copy(w_ref.at[core, layer], wide_ref.at[pl.ds(core * shard, shard)], sem.at[core])
        for core in range(2)
    ]
    for copy in copies:
        copy.start()
    used = 2 * shard
    wide_ref[used:] = jnp.zeros((wide_ref.shape[0] - used, wide_ref.shape[1]), BF16)
    return copies


def attend_back_kernel(count, layer, traffic, *refs):
    inputs, outputs, scratch = split(refs, 17, 5)
    d_ref, w_out_ref, w_ref, x_ref, att_ref, q_ref, own_ref, other_ref, begin_ref, lse_ref, table_ref = inputs[:11]
    params_ref, mid_ref, hidden_ref, mixed_ref, router_ref, gain_two_ref = inputs[11:]
    g_out_ref, grad_ref, d_mix_ref, side_ref, g_ref = outputs
    buf, wide_w, g_acc, out_mail, out_got, turned_ref, d_own, d_other, mail, got, dq_ref = scratch[:11]
    partial, land, rows_ref, tokens, weights, last_ref = scratch[11:17]
    sems, scatter_sem, pair_sem, load_sem = split(scratch[17:], 3, 2, 2)
    ring = Ring(count, traffic)
    shard = g_out_ref.shape[0]
    loads = load_out_weights(w_out_ref, layer, wide_w, load_sem[0])
    later = [
        pltpu.make_async_copy(x_ref, tokens, load_sem[0].at[2]),
        pltpu.make_async_copy(w_ref.at[layer], weights, load_sem[0].at[3]),
    ]
    for load in later:
        load.start()
    ring.meet(True)
    core = lax.rem(lax.axis_index("fsdp"), 2)
    width = GROUP * LANES

    def spread(wide):
        front, back = wide[:, :LANES], wide[:, LANES:]
        low = lanes_of(front) < HD
        return [jnp.where(low, 0.0, part) for part in (turn(front), front, turn(back))]

    def compute(block):
        d = buf[block]
        wide = dot(d, wide_w[...], NT).astype(BF16)
        g_acc[...] += dot(att_ref[block], d, TN)
        slopes, deltas = [], []
        for piece, a in zip(spread(wide.astype(F32)), spread(att_ref[block].astype(F32))):
            slopes.append(piece)
            deltas.append(jnp.sum((piece * a).T, 0, keepdims=True))
        datt = jnp.concatenate(slopes, 0).astype(BF16)
        delta = jnp.concatenate(deltas, 1)
        q = q_ref[block].reshape(width, LANES)
        both = jnp.concatenate([q, datt], 0)
        begin, query = query_rows(begin_ref, (block,), core)
        lse = lse_ref[block]

        def one(chunk, acc):
            keys = chunk_keys(own_ref, other_ref, chunk)
            scores = jnp.where(allowed_keys(begin, query, chunk, core), dot(keys, q, NT), MASKED)
            weight = jnp.exp(scores - lse)
            slope = (weight * (dot(keys, datt, NT) - delta)).astype(BF16)
            d_keys = dot(jnp.concatenate([slope, weight.astype(BF16)], 1), both)
            half = SPAN * LANES
            chips = pl.ds(chunk * SPAN, SPAN)
            d_own[chips] += d_keys[:half].reshape(SPAN, LANES, LANES)
            d_other[chips] += d_keys[half:].reshape(SPAN, LANES, LANES)
            return acc + dot(turned_ref[chunk], slope)

        acc = lax.fori_loop(0, chunks_of((block,)), one, jnp.zeros((LANES, width), F32)) * (HD**-0.5)
        heads = by_head(acc)
        low = lanes_of(heads[0]) < HD
        cosine, sine = angles(table_ref[block])
        front = spin(jnp.where(low, heads[0], turn(heads[1])), cosine, -sine)
        back = spin(jnp.where(low, heads[2], 0.0), cosine, -sine)
        dq_ref[block] = jnp.concatenate([front, back], 1).astype(BF16)

    def first(s):
        @pl.when(s == 1)
        def _():
            for load in loads:
                load.wait()
            turn_keys(own_ref, other_ref, turned_ref)
            g_acc[...] = jnp.zeros_like(g_acc)
            d_own[...] = jnp.zeros_like(d_own)
            d_other[...] = jnp.zeros_like(d_other)

        compute(ring.at(1 - s))

    def second(s):
        compute(ring.at(s))

    drain = ring.gather(d_ref, buf, sems, None, first, second)
    compute(ring.at(ring.steps))
    partner = partner_of("fsdp")
    mail[...] = d_other[...].astype(BF16)
    out_mail[...] = g_acc[pl.ds(pl.multiple_of((1 - core) * shard, 8), shard), :].astype(BF16)
    swaps = [
        remote(mail, got, pair_sem[0].at[0], pair_sem[1].at[0], partner),
        remote(out_mail, out_got, pair_sem[0].at[1], pair_sem[1].at[1], partner),
    ]
    for swap in swaps:
        swap.start()
    for load in later:
        load.wait()
    drain()
    swaps[0].wait()

    def join(blocks):
        rows = []
        for b in blocks:
            pair = d_own[b] + got[b].astype(F32)
            cosine, sine = angles(table_ref[b])
            keys = spin(pair, cosine, -sine)
            low = lanes_of(pair) < HD
            middle = jnp.where(low, dq_ref[b, :, LANES:].astype(F32), turn(keys))
            last = jnp.where(low, turn(pair), 0.0)
            rows.append(
                jnp.concatenate([dq_ref[b, :, :LANES], middle.astype(BF16), last.astype(BF16)], 1)
            )
            rows_ref[b] = rows[-1]
        total = dot(jnp.concatenate(rows, 0), weights[...], NT).astype(BF16)
        for block, part in cut(total, blocks):
            partial[block] = part

    join((ring.at(ring.steps), ring.chip))
    strip = g_ref.shape[0] // ring.steps
    tile = 2 * LANES

    def between():
        def one(index, carry):
            join(ring.pair(ring.steps - 1 - index))
            return carry

        lax.fori_loop(0, ring.steps - 1, one, 0)

    def work(s, place):
        if place == 0:
            rows = pl.ds(pl.multiple_of(s * strip, LANES), strip)
            value = dot(flat(tokens[:, :, rows]), flat(rows_ref[...]), TN)
            g_ref[rows, :tile] = value[:, :tile].astype(BF16)
            last_ref[rows] = value[:, tile:]

    d_x, finish = ring.scatter(partial, land, scatter_sem, work, between)
    swaps[1].wait()
    own = g_acc[pl.ds(pl.multiple_of(core * shard, 8), shard), :]
    g_out_ref[...] = (own + out_got[...].astype(F32)).astype(BF16)
    ring.settle()
    d_values, gain_one = normal_back(d_x, hidden_ref[...], gain_row(params_ref, 0, layer))
    grad = mid_ref[...] + d_values
    grad_ref[...] = grad
    d_mix = grad.astype(BF16)
    d_mix_ref[...] = d_mix
    balance = jnp.sum(mixed_ref[...] * d_mix.astype(F32), -1, keepdims=True)
    side_ref[...] = jnp.broadcast_to(as_line(balance), side_ref.shape)
    routers = router_ref[...]
    lines = [
        jnp.where(core == 0, routers[0:1], routers[1:2]),
        jnp.where(core == 0, routers[1:2], routers[0:1]),
        gain_one,
        gain_two_ref[...],
    ]
    features = g_ref.shape[0]
    tall = jnp.concatenate(
        [jnp.zeros((HD, features), F32)] + lines + [jnp.zeros((HD - len(lines), features), F32)], 0
    )
    g_ref[:, tile:] = (last_ref[...] + tall.T).astype(BF16)
    finish()


def gather_attend_back_scatter(
    count, layer, d, w_out, w, x_all, att, q, own, other, begin, lse, tables, late, rides=()
):
    _, rows, width = x_all.shape
    shard = w_out.shape[2]
    columns = w.shape[2]
    everyone = pltpu.VMEM((count, rows, width), BF16)
    early = [att, q, own, other, begin, lse, tables]
    pairs = cells((count, rows, LANES), BF16)
    return ring_call(
        functools.partial(attend_back_kernel, count, layer),
        ("attend_back", layer),
        [(a, ANYWHERE) for a in (d, w_out, w, x_all)] + [(a, EARLY) for a in early] + [(a, LATE) for a in late],
        [
            (cells((shard, width), BF16), OUT),
            (cells((rows, width), F32), OUT),
            (cells((rows, width), BF16), OUT),
            (cells((8, rows), F32), OUT),
            (cells(w.shape[1:], BF16), OUT),
        ],
        [
            everyone,
            pltpu.VMEM((2 * LANES, width), BF16),
            pltpu.VMEM((2 * LANES, width), F32),
            pltpu.VMEM((shard, width), BF16),
            pltpu.VMEM((shard, width), BF16),
            pltpu.VMEM((count // SPAN, LANES, SPAN * 2 * LANES), BF16),
            pltpu.VMEM(pairs.shape, F32),
            pltpu.VMEM(pairs.shape, F32),
            pltpu.VMEM(pairs.shape, BF16),
            pltpu.VMEM(pairs.shape, BF16),
            pltpu.VMEM((count, rows, 2 * LANES), BF16),
            everyone,
            land_scratch(count, rows, width),
            pltpu.VMEM((count, rows, columns), BF16),
            everyone,
            pltpu.VMEM(w.shape[1:], BF16),
            pltpu.VMEM((width, LANES), F32),
        ]
        + gather_sems(count)
        + scatter_sems(count)
        + dmas((2,), (2,), (4,)),
        60,
        rides,
    )


def finish_kernel(count, replicas, *refs):
    inputs, outputs, scratch = split(refs, 3, 2)
    g_ref, early_ref, early_peer_ref = inputs
    mine, peer = outputs
    early, land, total = scratch[:3]
    pair_send, pair_recv, part_send, part_recv, rep_send, rep_recv = scratch[3:]
    me = lax.axis_index("fsdp")
    chip, core = me // 2, lax.rem(me, 2)
    partner = partner_of("fsdp")

    def chip_at(offset):
        return lax.rem(chip + offset + count, count)

    def device(offset):
        return {"fsdp": chip_at(offset) * 2 + core}

    across = [partner_of("rep")] if replicas == 2 else []
    meet([device(offset) for offset in range(1, count)] + [partner] + across)
    swaps = [remote(g_ref.at[:, 1 - core], land.at[0], pair_send.at[0], pair_recv.at[0], partner)]
    swaps[0].start()
    for block in range(count):
        for half in range(2):
            both = early_ref[block, half].astype(F32)
            if replicas == 2:
                both = both + early_peer_ref[block, half].astype(F32)
            early[half, block] = both.astype(BF16)
    if replicas != 2:
        peer[...] = jnp.zeros_like(peer)
    swaps.append(remote(early.at[1 - core], land.at[1], pair_send.at[1], pair_recv.at[1], partner))
    swaps[1].start()
    for swap in swaps:
        swap.wait()
    for block in range(count):
        total[block, 0] = (g_ref[block, core].astype(F32) + land[0, block].astype(F32)).astype(BF16)
        total[block, 1] = (early[core, block].astype(F32) + land[1, block].astype(F32)).astype(BF16)
    sends = [
        remote(
            total.at[chip_at(offset)], mine.at[chip],
            part_send.at[offset], part_recv.at[offset], device(offset),
        )
        for offset in range(1, count)
    ]
    for send in sends:
        send.start()
    mine[chip] = total[chip]

    def to_peer(offset):
        slot = chip_at(-offset)
        return remote(mine.at[slot, 0], peer.at[slot], rep_send.at[offset], rep_recv.at[offset], across[0])

    for offset in range(count):
        if offset > 0:
            slot = mine.at[chip_at(-offset)]
            remote(slot, slot, part_send.at[offset], part_recv.at[offset], partner).wait_recv()
        if replicas == 2:
            to_peer(offset).start()
    if replicas == 2:
        for offset in range(count):
            to_peer(offset).wait()

    for send in sends:
        send.wait_send()


def finish_heads(count, replicas, g, early, early_peer):
    _, _, rows, columns = g.shape
    part = (count, LAYERS, rows, columns)
    dma = pltpu.SemaphoreType.DMA
    return pl.pallas_call(
        functools.partial(finish_kernel, count, replicas),
        out_shape=(cells(part, BF16), cells((count, rows, columns), BF16)),
        in_specs=[HERE] * 3,
        out_specs=[HERE] * 2,
        scratch_shapes=[
            pltpu.VMEM((2, count, rows, columns), BF16),
            pltpu.VMEM((2, count, rows, columns), BF16),
            pltpu.VMEM(part, BF16),
            dma((2,)), dma((2,)), dma((count,)), dma((count,)), dma((count,)), dma((count,)),
        ],
        compiler_params=pltpu.CompilerParams(
            collective_id=identity(("finish",)), has_side_effects=True, vmem_limit_bytes=60 << 20
        ),
        cost_estimate=FREE,
        name="finish_heads",
    )(g, early, early_peer)


def close_kernel(layers, count, *refs):
    n_experts = 0 if len(refs) == 2 * layers + 7 else 10 * layers
    inputs, heads_in, experts_in, outputs = split(refs, 2 * layers, 2, n_experts)
    mine, peer = heads_in
    out_ref, q_out, k_out, v_out, rest_out = outputs[:5]

    @pl.when(pl.program_id(0) == 0)
    def _():
        for layer in range(layers):
            own, got = inputs[2 * layer : 2 * layer + 2]
            out_ref[layer] = own[...].astype(F32) + got[...].astype(F32)

            def tiles(block):
                value = mine[block, layer].astype(F32)
                if layer == 0:
                    value = value + peer[block].astype(F32)
                return [value[:, i * LANES : (i + 1) * LANES] for i in range(3)]

            for half in range(count // 2):
                a, b = tiles(2 * half), tiles(2 * half + 1)
                low = lanes_of(a[0]) < HD
                q_out[layer, :, 3 * half * LANES : 3 * (half + 1) * LANES] = jnp.concatenate(
                    [a[0], jnp.where(low, a[1], turn(b[0])), jnp.where(low, turn(b[0]), turn(b[1]))], 1
                )
                here = slice(half * LANES, (half + 1) * LANES)
                k_out[layer, :, here] = jnp.where(low, turn(a[1]), b[1])
                v_out[layer, :, here] = jnp.where(low, a[2], turn(b[2]))
                rest_out[layer, 2 * half] = a[2]
                rest_out[layer, 2 * half + 1] = b[2]

    if experts_in:
        expert_refs = outputs[5:]
        for layer in range(layers):
            pairs = experts_in[layer * 10 : (layer + 1) * 10]
            sums = [pairs[i][...].astype(F32) + pairs[i + 5][...].astype(F32) for i in range(5)]
            expert_refs[0][layer, 0] = sums[0]
            expert_refs[1][layer, 0] = sums[1]
            expert_refs[2][layer, 0] = jnp.concatenate(sums[2:], 1)


def close(count, outs, mine, peer, experts):
    layers = len(outs)
    shard, width = outs[0][0].shape
    steps = 4

    def whole(shape):
        return pl.BlockSpec(shape, lambda i: (0,) * len(shape))

    arrays = [array for pair in outs for array in pair] + [mine, peer]
    specs = [whole(a.shape) for a in arrays]
    shapes = [
        (layers, shard, width),
        (layers, shard, count * GROUP * HD),
        (layers, shard, count * HD),
        (layers, shard, count * HD),
        (layers, count, shard, LANES),
    ]
    out_specs = [whole(shape) for shape in shapes]
    if experts:
        rows, ff = experts[0][0].shape
        tall, short = width // steps, ff // steps
        groups = (rows - 2 * width) // ff

        def at(first, length):
            return pl.BlockSpec((length, ff), lambda i: (first // length + i, 0))

        parts = [at(0, tall), at(width, tall)] + [at(2 * width + g * ff, short) for g in range(groups)]
        arrays += [array for pair in experts for array in pair for _ in parts]
        specs += parts * (2 * layers)
        shapes += [(layers, 1, width, ff), (layers, 1, width, ff), (layers, 1, ff, width)]
        tile = pl.BlockSpec((layers, 1, tall, ff), lambda i: (0, 0, i, 0))
        out_specs += [tile, tile, pl.BlockSpec((layers, 1, short, width), lambda i: (0, 0, i, 0))]
    return pl.pallas_call(
        functools.partial(close_kernel, layers, count),
        grid=(steps if experts else 1,),
        out_shape=tuple(cells(shape, F32) for shape in shapes),
        in_specs=specs,
        out_specs=out_specs,
        compiler_params=pltpu.CompilerParams(vmem_limit_bytes=60 << 20),
        cost_estimate=FREE,
        name="close",
    )(*arrays)


def on_device(
    tokens,
    cotangent,
    positions,
    segments,
    routes,
    attn_gain,
    w_query,
    w_key,
    w_value,
    w_out,
    ffn_gain,
    router,
    w_gate,
    w_up,
    w_down,
):
    rows, width = tokens.shape
    devices = lax.axis_size("fsdp")
    replicas = lax.axis_size("rep")
    count = devices // 2
    me = lax.axis_index("fsdp")
    chip, core = me // 2, lax.rem(me, 2)
    shard = w_query.shape[1]
    experts = devices
    columns = 3 * LANES
    used = (GROUP + 2) * HD
    pairs = [(index, index ^ 1) for index in range(devices)]

    def swap(array):
        return lax.ppermute(array, "fsdp", pairs)

    small = jnp.concatenate(
        [attn_gain, ffn_gain, router.transpose(0, 2, 1).reshape(LAYERS * experts, shard)], 0
    )
    small = jnp.pad(small, ((0, 48 - small.shape[0]), (0, LANES - shard)))
    rate = jnp.exp(-jnp.log(10000.0) * jnp.arange(HD // 2, dtype=F32) / (HD // 2))
    angle = rate[:, None] * positions.astype(F32)[None, :]
    table = jnp.concatenate([jnp.cos(angle), jnp.sin(angle)], 0)
    slabs = jnp.concatenate(
        [
            w_query.reshape(LAYERS, shard, count, GROUP * HD),
            w_key.reshape(LAYERS, shard, count, HD),
            w_value.reshape(LAYERS, shard, count, HD),
            jnp.zeros((LAYERS, shard, count, columns - used), BF16),
        ],
        -1,
    ).transpose(2, 0, 1, 3)
    heads_w, outs_w, smalls, tables = exchange_weights(count, slabs, w_out, small, table)
    heads_w = heads_w.reshape(LAYERS, width, columns)
    params = smalls[:, : (2 + experts) * LAYERS, :shard].transpose(1, 0, 2).reshape(-1, width)
    params = params.astype(F32)
    own_w, _ = lax.optimization_barrier(([w_gate, w_up, w_down], smalls))
    experts_w = own_w + [swap(w) for w in own_w]

    flat_segments = segments.reshape(1, -1)
    kinds = jnp.arange(8, dtype=jnp.int32)[:, None]
    starts = jnp.sum((flat_segments < kinds).astype(jnp.int32), 1, keepdims=True)
    begin = jnp.sum(jnp.where(flat_segments == kinds, starts, 0), 0).reshape(count, 2, rows)
    begin = lax.dynamic_index_in_dim(begin, core, 1, True)

    hidden = tokens.astype(F32)
    x_attn = (normal(hidden)[1] * params[0:1]).astype(BF16)
    chosen = routes.transpose(0, 2, 1)
    saved = []
    for layer in range(LAYERS):
        query, kv, kv_other, x_all, att, lse, middle, x_moe, share = gather_attend_scatter(
            count, layer, x_attn, heads_w, outs_w, tables, begin, hidden, params, chosen
        )
        mixed, after, x_attn, m_all, share_all = gather_mix_scatter(
            count, layer, x_moe, share, middle, params, experts_w
        )
        saved.append((hidden, x_all, query, kv, kv_other, att, lse, middle, mixed, m_all, share_all))
        hidden = after
    activations = x_attn

    def across(array):
        return lax.ppermute(array, "rep", [(0, 1), (1, 0)]) if replicas == 2 else array

    grad, d_mix = cotangent.astype(F32), cotangent
    balance = jnp.sum(saved[-1][8] * grad, -1)
    side = jnp.broadcast_to(balance[None, :], (8, rows))
    expert_sums = [None] * LAYERS
    out_sums = [None] * LAYERS
    for layer in reversed(range(LAYERS)):
        hidden, x_all, query, kv, kv_other, att, lse, middle, mixed, m_all, share_all = saved[layer]
        rides = [out_sums[layer + 1], early] if layer + 1 < LAYERS and replicas == 2 else []
        grad_mid, d_branch, gain_two, expert_sum, g_router, *rode = gather_mix_back_scatter(
            count, layer, d_mix, side, m_all, share_all, params, grad, middle, experts_w, rides
        )
        if layer + 1 < LAYERS:
            d_branch, expert_sums[layer + 1] = lax.optimization_barrier(
                (d_branch, expert_sums[layer + 1])
            )
        expert_sums[layer] = (expert_sum, across(expert_sum))
        out_sum, grad, d_mix, side, heads = gather_attend_back_scatter(
            count, layer, d_branch, outs_w, heads_w, x_all, att, query, kv, kv_other, begin, lse, tables,
            [params, grad_mid, hidden, saved[max(layer - 1, 0)][8], g_router, gain_two],
        )
        out_sums[layer] = out_sum
        heads = heads.reshape(count, 2, shard, columns)
        early = heads if layer > 0 else early
    arrived, peer = finish_heads(count, replicas, heads, early, rode[1] if rode else early)
    if replicas == 2:
        outs = list(zip(out_sums, [across(out_sums[0]), rode[0]]))
        g_out, g_query, g_key, g_value, rest, g_gate, g_up, g_down = close(
            count, outs, arrived, peer, expert_sums
        )
    else:
        outs = [(own, jnp.zeros_like(own)) for own in out_sums]
        summed = close(count, outs, arrived, peer, [])
        g_out, g_query, g_key, g_value, rest, flat_sums = [
            lax.psum(array.astype(BF16), "rep").astype(F32)
            for array in (*summed, jnp.stack([own for own, _ in expert_sums]))
        ]
        ff = w_gate.shape[3]
        g_gate, g_up = flat_sums[:, None, :width], flat_sums[:, None, width : 2 * width]
        g_down = flat_sums[:, 2 * width :].reshape(LAYERS, width // ff, ff, ff)
        g_down = g_down.transpose(0, 2, 1, 3).reshape(LAYERS, 1, ff, width)
    rest = rest[..., HD : HD + 4]
    gains = jnp.sum(rest, 1)
    g_router = rest[..., :2].transpose(0, 2, 1, 3).reshape(LAYERS, shard, experts)
    return (
        activations,
        grad,
        gains[..., 2],
        g_query,
        g_key,
        g_value,
        g_out,
        gains[..., 3],
        g_router,
        g_gate,
        g_up,
        g_down,
    )


def solution(mesh):
    placed = (
        P(("rep", "fsdp"), None),
        P(("rep", "fsdp"), None),
        P(("rep", "fsdp")),
        P("rep", None),
        P(None, ("rep", "fsdp"), None),
        P(None, "fsdp"),
        P(None, "fsdp", None),
        P(None, "fsdp", None),
        P(None, "fsdp", None),
        P(None, "fsdp", None),
        P(None, "fsdp"),
        P(None, "fsdp", None),
        P(None, "fsdp", None, None),
        P(None, "fsdp", None, None),
        P(None, "fsdp", None, None),
    )
    return jax.shard_map(
        on_device,
        mesh=mesh,
        in_specs=placed,
        out_specs=(
            P(("rep", "fsdp"), None),
            P(("rep", "fsdp"), None),
            P(None, "fsdp"),
            P(None, "fsdp", None),
            P(None, "fsdp", None),
            P(None, "fsdp", None),
            P(None, "fsdp", None),
            P(None, "fsdp"),
            P(None, "fsdp", None),
            P(None, "fsdp", None, None),
            P(None, "fsdp", None, None),
            P(None, "fsdp", None, None),
        ),
        check_vma=False,
    )
```

```python
import functools

import jax
import jax.numpy as jnp
from jax import lax
from jax.experimental import pallas as pl
from jax.experimental.pallas import tpu as pltpu
from jax.sharding import PartitionSpec as P

HEADS = 24
KV_HEADS = 8
HD = 64
LAYERS = 2
GROUP = HEADS // KV_HEADS
LANES = 128
SPAN = 2
EPS = 1e-06
MASKED = -1e30
MESH = pl.DeviceIdType.MESH
F32 = jnp.float32
BF16 = jnp.bfloat16


def ring_place(chip, count):
    return lax.select(lax.rem(chip, 2) == 0, chip // 2, count - 1 - chip // 2)


def ring_chip(place, count):
    return lax.select(place < count // 2, 2 * place, 2 * (count - 1 - place) + 1)


def ring_setup(count):
    me = lax.axis_index("fsdp")
    chip, core = me // 2, lax.rem(me, 2)
    place = ring_place(chip, count)

    def at(offset):
        return ring_chip(lax.rem(place + offset + 2 * count, count), count)

    near = [{"fsdp": at(1) * 2 + core}, {"fsdp": at(-1) * 2 + core}]
    return chip, at, near


def partner_of(axis):
    if axis == "rep":
        return {"rep": 1 - lax.axis_index("rep")}
    me = lax.axis_index("fsdp")
    return {"fsdp": me + 1 - 2 * lax.rem(me, 2)}


def meet(others):
    barrier = pltpu.get_barrier_semaphore()
    for other in others:
        pl.semaphore_signal(barrier, inc=1, device_id=other, device_id_type=MESH)
    pl.semaphore_wait(barrier, len(others))


def remote(src, dst, send_sem, recv_sem, device):
    return pltpu.make_async_remote_copy(
        src_ref=src,
        dst_ref=dst,
        send_sem=send_sem,
        recv_sem=recv_sem,
        device_id=device,
        device_id_type=MESH,
    )


def ring_hops(count):
    half = count // 2
    return {(0, 0): half, (1, 1): half, (0, 1): half - 1, (1, 0): half - 1}


IDENTITIES = {}


def identity(key):
    return IDENTITIES.setdefault(key, len(IDENTITIES))


class Ring:
    def __init__(self, count, traffic):
        self.count = count
        self.riders, self.early, self.late, self.soon = traffic
        self.steps = count // 2
        self.chip, self.at, self.near = ring_setup(count)

    def meet(self, partner=False, everyone=None):
        others = everyone or self.near + ([partner_of("fsdp")] if partner else [])
        meet(others + ([partner_of("rep")] if self.riders else []))
        for rider in self.riders:
            rider.start()
        for copy in self.early:
            copy.wait()

    def settle(self):
        for copy in self.late:
            copy.wait()

    def depart(self):
        for copy in self.soon:
            copy.start()

    def gather(self, x_ref, buf, sems, side=None, first=None, second=None):
        own_sem, send_sem, recv_sem = sems[:3]
        half_rows = x_ref.shape[0] // 2
        steps = self.steps
        own = [pltpu.make_async_copy(x_ref, buf.at[self.chip], own_sem.at[0])]
        if side is not None:
            side_ref, side_buf = side
            side_send, side_recv = sems[3:]
            own.append(pltpu.make_async_copy(side_ref, side_buf.at[self.chip], own_sem.at[1]))
        for copy in own:
            copy.start()

        def piece(key, step, block, source=None):
            direction, part = key
            rows = pl.ds(part * half_rows, half_rows)
            target = buf.at[block, rows]
            return remote(
                target if source is None else source.at[rows],
                target,
                send_sem.at[direction, part, step],
                recv_sem.at[direction, part, step],
                self.near[direction],
            )

        def side_piece(direction, step, block, source=None):
            target = side_buf.at[block]
            return remote(
                target if source is None else source,
                target,
                side_send.at[direction, step],
                side_recv.at[direction, step],
                self.near[direction],
            )

        def toward(key, places):
            return self.at(-places if key[0] == 0 else places)

        early, late = [(0, 0), (1, 1)], [(0, 1), (1, 0)]
        if side is not None:
            for direction in range(2):
                side_piece(direction, 0, self.chip, side_ref).start()
        for key in early + late:
            piece(key, 0, self.chip, x_ref).start()

        def take(keys, s, last):
            for key in keys:
                block = toward(key, s)
                piece(key, s - 1, block).wait_recv()

                @pl.when(s < last)
                def _():
                    piece(key, s, block).start()

        def take_side(s):
            if side is not None:
                for direction in range(2):

                    @pl.when(s <= steps - direction)
                    def _():
                        block = toward((direction, 0), s)
                        side_piece(direction, s - 1, block).wait_recv()

                        @pl.when(s < steps - direction)
                        def _():
                            side_piece(direction, s, block).start()

        def step(s, carry):
            take_side(s)
            take(early, s, steps)
            first(s)
            take(late, s, steps - 1)
            second(s)
            return carry

        for copy in own:
            copy.wait()
        lax.fori_loop(1, steps, step, 0)
        first(steps)
        take_side(steps)
        take(early, steps, steps)

        def drain():
            for s in range(steps):
                for key in early + (late if s < steps - 1 else []):
                    piece(key, s, toward(key, s)).wait_send()
                if side is not None:
                    for direction in range(2):
                        if s < steps - direction:
                            side_piece(direction, s, toward((direction, 0), s)).wait_send()

        return drain

    def pair(self, s):
        return self.at(s), self.at(-s)

    def meanwhile(self, compute, ready):
        def first(s):
            @pl.when(s == 1)
            def _():
                compute(0, (self.chip,))

            @pl.when(s > 1)
            def _():
                compute(1, self.pair(s - 1))

        def second(s):
            @pl.when(s == 1)
            def _():
                ready()
                compute(1, (self.chip,))

            compute(0, self.pair(s))

        return first, second

    def scatter(self, partial, land, sems, work=None, between=None):
        send_sem, recv_sem = sems
        half_rows = partial.shape[1] // 2
        steps = self.steps
        hops = ring_hops(self.count)

        def ahead(key, s):
            places = hops[key] - s
            return self.at(places if key[0] == 0 else -places)

        def piece(key, s, source):
            direction, part = key
            return remote(
                source,
                land.at[direction, part, s],
                send_sem.at[direction, part, s],
                recv_sem.at[direction, part, s],
                self.near[direction],
            )

        def rows_of(key):
            return pl.ds(key[1] * half_rows, half_rows)

        for place, key in enumerate(hops):
            if place == 2 and between is not None:
                between()
            piece(key, 0, partial.at[ahead(key, 0), rows_of(key)]).start()

        def step(s, carry):
            for place, key in enumerate(hops):
                if work is not None:
                    work(s - 1, place)

                @pl.when(s < hops[key])
                def _():
                    slot = land.at[key[0], key[1], s - 1]
                    piece(key, s - 1, slot).wait_recv()
                    mine = partial[ahead(key, s), rows_of(key)]
                    slot[...] = (slot[...].astype(F32) + mine.astype(F32)).astype(BF16)
                    piece(key, s, slot).start()

            return carry

        lax.fori_loop(1, steps + 1, step, 0)
        for key in hops:
            slot = land.at[key[0], key[1], hops[key] - 1]
            piece(key, hops[key] - 1, slot).wait_recv()
        halves = []
        for part in range(2):
            rows = pl.ds(part * half_rows, half_rows)
            total = partial[self.chip, rows].astype(F32)
            for direction in range(2):
                total = total + land[direction, part, hops[direction, part] - 1].astype(F32)
            halves.append(total)
        summed = jnp.concatenate(halves, 0)

        def drain():
            for key in hops:
                for s in range(hops[key]):
                    piece(key, s, land.at[key[0], key[1], s]).wait_send()

        return summed, drain


def dmas(*shapes):
    return [pltpu.SemaphoreType.DMA(shape) for shape in shapes]


def gather_sems(count, sided=False):
    steps = count // 2
    shapes = [(2,), (2, 2, steps), (2, 2, steps)]
    return dmas(*(shapes + ([(2, steps), (2, steps)] if sided else [])))


def scatter_sems(count):
    return dmas((2, 2, count // 2), (2, 2, count // 2))


ANYWHERE = pl.BlockSpec(memory_space=pltpu.HBM)
HERE = pl.BlockSpec(memory_space=pltpu.VMEM)
EARLY, LATE = "early", "late"
OUT, SOON = "out", "soon"


FREE = pl.CostEstimate(flops=0, bytes_accessed=0, transcendentals=0)


def ring_call(body, key, inputs, outputs, scratch, megabytes, rides=()):
    n_in, n_out, n_rides = len(inputs), len(outputs), len(rides)
    in_kinds = [kind for _, kind in inputs]
    out_kinds = [kind for _, kind in outputs]
    copied = [a for a, kind in inputs if kind in (EARLY, LATE)]
    returned = [a for a, kind in outputs if kind in (OUT, SOON)]
    moves = len(copied) + len(returned)

    def kernel(*refs):
        ins, ride_in, outs, ride_out, rest = split(refs, n_in, n_rides, n_out, n_rides)
        rest, own, rest_sems = rest[: len(scratch)], rest[len(scratch) : len(scratch) + moves], rest[len(scratch) + moves :]
        move_sem, rest_sems = rest_sems[0], rest_sems[1:]
        riders = []
        if n_rides:
            send_sem, recv_sem = rest_sems
            riders = [
                remote(ride_in[i], ride_out[i], send_sem.at[i], recv_sem.at[i], partner_of("rep"))
                for i in range(n_rides)
            ]
        used = 0
        early, late, leaving, soon = [], [], [], []
        ins, outs = list(ins), list(outs)
        for i, kind in enumerate(in_kinds):
            if kind in (EARLY, LATE):
                copy = pltpu.make_async_copy(ins[i], own[used], move_sem.at[used])
                copy.start()
                (early if kind == EARLY else late).append(copy)
                ins[i] = own[used]
                used += 1
        for i, kind in enumerate(out_kinds):
            if kind in (OUT, SOON):
                copy = pltpu.make_async_copy(own[used], outs[i], move_sem.at[used])
                (leaving if kind == OUT else soon).append(copy)
                outs[i] = own[used]
                used += 1
        body((riders, early, late, soon), *ins, *outs, *rest)
        for copy in leaving:
            copy.start()
        for rider in riders:
            rider.wait()
        for copy in leaving + soon:
            copy.wait()

    def spec(kind):
        return ANYWHERE if isinstance(kind, str) else kind

    return pl.pallas_call(
        kernel,
        out_shape=tuple(shape for shape, _ in outputs) + tuple(cells(a.shape, a.dtype) for a in rides),
        in_specs=[spec(kind) for kind in in_kinds] + [ANYWHERE] * n_rides,
        out_specs=[spec(kind) for kind in out_kinds] + [ANYWHERE] * n_rides,
        scratch_shapes=list(scratch)
        + [pltpu.VMEM(a.shape, a.dtype) for a in copied + returned]
        + dmas((max(moves, 1),))
        + (dmas((n_rides,), (n_rides,)) if n_rides else []),
        compiler_params=pltpu.CompilerParams(
            collective_id=identity(key),
            has_side_effects=True,
            vmem_limit_bytes=megabytes << 20,
        ),
        cost_estimate=FREE,
        name=key[0],
    )(*[array for array, _ in inputs], *rides)


def split(refs, *sizes):
    parts, place = [], 0
    for size in sizes:
        parts.append(refs[place : place + size])
        place += size
    return parts + [refs[place:]]


def cells(shape, dtype):
    return jax.ShapeDtypeStruct(shape, dtype)


def dot(left, right, contract=((1,), (0,))):
    return lax.dot_general(left, right, (contract, ((), ())), preferred_element_type=F32)


NT = ((1,), (1,))
TN = ((0,), (0,))


def lanes_of(field):
    return lax.broadcasted_iota(jnp.int32, field.shape, 1)


def turn(field):
    return pltpu.roll(field, HD, 1)


def spin(field, cosine, sine):
    swapped = jnp.where(
        lax.rem(lanes_of(field), HD) < HD // 2,
        -pltpu.roll(field, LANES - HD // 2, 1),
        pltpu.roll(field, HD // 2, 1),
    )
    return field * cosine + swapped * sine


def project_rows(rows, cosine, sine):
    first = spin(rows[:, :LANES], cosine, sine)
    second = spin(rows[:, LANES : 2 * LANES], cosine, sine)
    third = rows[:, 2 * LANES :]
    low = lanes_of(first) < HD
    heads = []
    for field in (first, turn(first), second):
        rounded = jnp.where(low, field, 0.0).astype(BF16).astype(F32)
        heads.append((rounded * (HD**-0.5)).astype(BF16))
    return heads, jnp.where(low, turn(second), turn(third)).astype(BF16)


def angles(table):
    rows = jnp.concatenate([table, table], 0).T
    early = lax.rem(lanes_of(rows), HD) < HD // 2
    cosine = jnp.where(early, rows, pltpu.roll(rows, HD // 2, 1))
    sine = jnp.where(early, pltpu.roll(rows, LANES - HD // 2, 1), rows)
    return cosine, sine


def normal(values):
    inverse = lax.rsqrt(jnp.mean(values * values, -1, keepdims=True) + EPS)
    return inverse, values * inverse


def normal_back(d_x, values, gain):
    inverse, normed = normal(values)
    d_norm = d_x * gain
    d_values = inverse * (d_norm - normed * jnp.mean(d_norm * normed, -1, keepdims=True))
    return d_values, jnp.sum(d_x * normed, 0, keepdims=True)


def diagonal():
    shape = (LANES, LANES)
    return lax.broadcasted_iota(jnp.int32, shape, 0) == lax.broadcasted_iota(jnp.int32, shape, 1)


def as_column(line):
    return jnp.sum(jnp.where(diagonal(), jnp.broadcast_to(line, (LANES, LANES)), 0.0), 1, keepdims=True)


def as_line(column):
    return jnp.sum(jnp.where(diagonal(), jnp.broadcast_to(column, (LANES, LANES)), 0.0), 0, keepdims=True)


def flat(value):
    return value.reshape(value.shape[0] * value.shape[1], value.shape[2])


def stack(ref, blocks):
    parts = [ref[b] for b in blocks]
    return parts[0] if len(parts) == 1 else jnp.concatenate(parts, 0)


def cut(value, blocks):
    return [(b, value[i * LANES : (i + 1) * LANES]) for i, b in enumerate(blocks)]


def gain_row(params_ref, kind, layer):
    row = kind * LAYERS + layer
    return params_ref[row : row + 1, :]


def router_rows(experts, layer):
    first = 2 * LAYERS + layer * experts
    return slice(first, first + experts)


def allowed_keys(begin, query, chunk, core):
    half = SPAN * LANES
    shape = (2 * half, begin.shape[1])
    place = lax.broadcasted_iota(jnp.int32, (2 * half, 1), 0)
    inner = lax.rem(place, half)
    whose = jnp.where(place < half, core, 1 - core)
    key = chunk * 2 * half + inner // LANES * (2 * LANES) + whose * LANES + lax.rem(inner, LANES)
    key = jnp.broadcast_to(key, shape)
    return (key >= begin) & (key <= query)


def query_rows(begin_ref, blocks, core):
    lane = lax.broadcasted_iota(jnp.int32, (1, LANES), 1)
    begin, query = [], []
    for block in blocks:
        begin += [begin_ref[block]] * GROUP
        query += [(2 * block + core) * LANES + lane] * GROUP
    return jnp.concatenate(begin, 1), jnp.concatenate(query, 1)


def chunk_keys(own_ref, other_ref, chunk):
    chips = pl.ds(chunk * SPAN, SPAN)
    return jnp.concatenate([flat(own_ref[chips]), flat(other_ref[chips])], 0)


def turn_keys(own_ref, other_ref, turned_ref):
    def one(chunk, carry):
        turned_ref[chunk] = chunk_keys(own_ref, other_ref, chunk).astype(F32).T.astype(BF16)
        return carry

    lax.fori_loop(0, turned_ref.shape[0], one, 0)


def by_head(field):
    return [field[:, h * LANES : (h + 1) * LANES].T for h in range(GROUP)]


def chunks_of(blocks):
    last = blocks[0] if len(blocks) == 1 else jnp.maximum(*blocks)
    return last // SPAN + 1


class Opening:
    def __init__(self, count, inputs, outputs, scratch):
        self.tokens_ref, *self.projections, self.out_w_ref, self.small_ref, self.table_ref = inputs
        self.heads_ref, self.outs_ref, self.tables_ref, self.params_ref = outputs
        (self.x_ref, self.slab_ref, self.smalls, self.weights, self.own_sem, self.slab_sem, self.pass_sem, self.small_sem,
         self.table_sem, self.out_sem) = scratch
        self.count = count
        self.devices = 2 * count
        self.me = lax.axis_index("fsdp")
        self.chip, self.core = self.me // 2, lax.rem(self.me, 2)
        self.partner = partner_of("fsdp")

    def device(self, offset):
        return {"fsdp": lax.rem(self.me + offset, self.devices)}

    def chip_at(self, offset):
        return lax.rem(self.chip + offset + self.count, self.count)

    def everyone(self):
        return [self.device(offset) for offset in range(1, self.devices)]

    def home(self, layer, origin):
        shard = self.slab_ref.shape[2]
        rows = pl.ds(pl.multiple_of(origin * shard, shard), shard)
        return self.weights.at[rows] if layer == 0 else self.heads_ref.at[layer, rows]

    def across(self, layer, offset, source=None, target=None):
        slot = self.home(layer, self.me) if source is None else source
        target = slot if target is None else target
        there = {"fsdp": self.chip_at(offset) * 2 + self.core}
        return remote(slot, target, self.slab_sem.at[0, offset, layer], self.slab_sem.at[1, offset, layer], there)

    def beside(self, layer, offset, slot, source=None):
        return remote(
            slot if source is None else source, slot,
            self.pass_sem.at[0, offset, layer], self.pass_sem.at[1, offset, layer], self.partner,
        )

    def small_to(self, offset, slot, source=None):
        return remote(
            slot if source is None else source, slot,
            self.small_sem.at[0, offset], self.small_sem.at[1, offset], self.device(offset),
        )

    def table_to(self, offset, slot, source=None):
        there = {"fsdp": self.chip_at(offset) * 2 + self.core}
        return remote(
            slot if source is None else source, slot,
            self.table_sem.at[0, offset], self.table_sem.at[1, offset], there,
        )

    def out_to(self, slot, source):
        return remote(source, slot, self.out_sem.at[0], self.out_sem.at[1], self.partner)

    def divide(self):
        for layer in range(LAYERS):
            query, key, value = [ref[layer].astype(F32) for ref in self.projections]
            for half in range(self.count // 2):
                first = 3 * half * LANES
                t = [query[:, first + i * LANES : first + (i + 1) * LANES] for i in range(3)]
                k, v = [a[:, half * LANES : (half + 1) * LANES] for a in (key, value)]
                low = lanes_of(k) < HD
                even = [t[0], jnp.where(low, t[1], turn(k)), jnp.where(low, v, 0.0)]
                odd = [
                    jnp.where(low, turn(t[1]), turn(t[2])),
                    jnp.where(low, turn(t[2]), k),
                    jnp.where(low, turn(v), 0.0),
                ]
                for place, tiles in enumerate((even, odd)):
                    self.slab_ref[2 * half + place, layer] = jnp.concatenate(tiles, 1).astype(BF16)

    def start(self):
        me, chip = self.me, self.chip
        self.divide()
        self.copies = [
            pltpu.make_async_copy(self.small_ref, self.smalls.at[me], self.own_sem.at[0]),
            pltpu.make_async_copy(self.table_ref, self.tables_ref.at[chip], self.own_sem.at[1]),
            pltpu.make_async_copy(self.out_w_ref, self.outs_ref.at[self.core], self.own_sem.at[2]),
        ] + [
            pltpu.make_async_copy(self.slab_ref.at[chip, layer], self.home(layer, me), self.own_sem.at[3 + layer])
            for layer in range(LAYERS)
        ]
        self.sends = [
            self.small_to(offset, self.smalls.at[me], self.small_ref) for offset in range(1, self.devices)
        ]
        for offset in range(1, self.count):
            self.sends.append(self.table_to(offset, self.tables_ref.at[chip], self.table_ref))
        for layer in range(LAYERS):
            for offset in range(1, self.count):
                slab = self.slab_ref.at[self.chip_at(offset), layer]
                self.sends.append(self.across(layer, offset, slab, self.home(layer, me)))
            self.sends.append(self.beside(layer, 0, self.home(layer, me), self.slab_ref.at[chip, layer]))
        self.sends.append(self.out_to(self.outs_ref.at[self.core], self.out_w_ref))
        for copy in self.copies + self.sends:
            copy.start()

    def parameters(self):
        for offset in range(1, self.devices):
            origin = lax.rem(self.me - offset + self.devices, self.devices)
            self.small_to(offset, self.smalls.at[origin]).wait_recv()
        self.copies[0].wait()
        shard = self.slab_ref.shape[2]
        width = self.params_ref.shape[1]
        shape = (LANES, width)
        feature = lax.broadcasted_iota(jnp.int32, shape, 1)
        spread = (lax.rem(feature, shard) == lax.broadcasted_iota(jnp.int32, shape, 0)).astype(F32).astype(BF16)
        owner = lax.broadcasted_iota(jnp.int32, self.params_ref.shape, 1) // shard
        self.params_ref[...] = jnp.zeros_like(self.params_ref)

        def one(device, carry):
            rows = dot(self.smalls[device], spread)
            self.params_ref[...] += jnp.where(owner == device, rows, 0.0)
            return carry

        lax.fori_loop(0, self.devices, one, 0)
        normed = normal(self.tokens_ref[...].astype(F32))[1]
        self.x_ref[...] = (normed * gain_row(self.params_ref, 0, 0)).astype(BF16)

    def forward(self, layer):
        for offset in range(1, self.count):
            slot = self.home(layer, self.chip_at(-offset) * 2 + self.core)
            self.across(layer, offset, slot).wait_recv()
            self.beside(layer, offset, slot).start()

    def arrived(self, layer):
        self.copies[3 + layer].wait()
        for offset in range(self.count):
            slot = self.home(layer, self.chip_at(-offset) * 2 + 1 - self.core)
            self.beside(layer, offset, slot).wait_recv()

    def rest(self):
        for offset in range(1, self.count):
            self.table_to(offset, self.tables_ref.at[self.chip_at(-offset)]).wait_recv()
        for copy in self.copies[1:3]:
            copy.wait()
        other = self.outs_ref.at[1 - self.core]
        self.out_to(other, other).wait_recv()

    def drain(self):
        for send in self.sends:
            send.wait_send()
        for layer in range(LAYERS):
            for offset in range(1, self.count):
                slot = self.home(layer, self.chip_at(-offset) * 2 + self.core)
                self.beside(layer, offset, slot).wait_send()


def attend_kernel(count, layer, traffic, *refs):
    if layer == 0:
        inputs, outputs, scratch = split(refs, 9, 13)
        begin_ref, routes_ref = inputs[7:]
        hidden_ref, table_ref, params_ref = inputs[0], outputs[11], outputs[12]
    else:
        inputs, outputs, scratch = split(refs, 8, 9)
        x_ref, w_ref, w_out_ref, table_ref, begin_ref, hidden_ref, params_ref, routes_ref = inputs
    q_ref, own_ref, other_ref, all_ref, att_ref, lse_ref, middle_ref, x_out_ref, share_ref = outputs[:9]
    buf, weights, wide_w, turned_ref, score_ref, partial, land = scratch[:7]
    sems, pair_sems, scatter_sem, out_sem, load_sem, more = split(scratch[7:], 3, 2, 2, 1, 1)
    ring = Ring(count, traffic)
    partner = partner_of("fsdp")
    core = lax.rem(lax.axis_index("fsdp"), 2)

    def pass_on(block):
        return remote(
            own_ref.at[block], other_ref.at[block], pair_sems[0].at[block], pair_sems[1].at[block], partner
        )

    def project(blocks):
        rows = dot(stack(buf, blocks), weights[...])
        tables = [angles(table_ref[b]) for b in blocks]
        cosine = jnp.concatenate([t[0] for t in tables], 0)
        sine = jnp.concatenate([t[1] for t in tables], 0)
        heads, pair = project_rows(rows, cosine, sine)
        for index, head in enumerate(heads):
            for block, part in cut(head, blocks):
                q_ref[block, index] = part
        for block, part in cut(pair, blocks):
            own_ref[block] = part
            pass_on(block).start()

    if layer == 0:
        more = scratch[7 + 9 :]
        opening = Opening(count, inputs[:7], outputs[9:], [*more[:3], weights, *more[3:]])
        ring.meet(True, opening.everyone())
        opening.start()
        opening.parameters()
        drain = ring.gather(opening.x_ref, buf, sems, None, lambda s: None, lambda s: None)
        keep = [pltpu.make_async_copy(buf, all_ref, out_sem[0].at[0])]
        keep[0].start()
        opening.forward(0)
        opening.rest()
        loads = load_out_weights(outputs[10], layer, wide_w, load_sem[0])
        opening.arrived(0)
        keep.append(pltpu.make_async_copy(weights, outputs[9].at[0], out_sem[0].at[1]))
        keep[1].start()

        def both(index, carry):
            project((2 * index, 2 * index + 1))
            return carry

        lax.fori_loop(0, count // 2, both, 0)
        for load in loads:
            load.wait()
    else:
        loads = [pltpu.make_async_copy(w_ref.at[layer], weights, load_sem[0].at[2])]
        loads[0].start()
        loads += load_out_weights(w_out_ref, layer, wide_w, load_sem[0])
        ring.meet(True)

        def first(s):
            @pl.when(s == 1)
            def _():
                for load in loads:
                    load.wait()
                project((ring.chip,))

        drain = ring.gather(x_ref, buf, sems, None, first, lambda s: project(ring.pair(s)))
        keep = [pltpu.make_async_copy(buf, all_ref, out_sem[0].at[0])]
        keep[0].start()
        project((ring.at(ring.steps),))
    for block in range(count):
        pass_on(block).wait()
    ring.depart()
    turn_keys(own_ref, other_ref, turned_ref)

    def attend(blocks):
        width = len(blocks) * GROUP * LANES
        q = jnp.concatenate([q_ref[b].reshape(GROUP * LANES, LANES) for b in blocks], 0)
        begin, query = query_rows(begin_ref, blocks, core)
        end = chunks_of(blocks)

        def score(chunk, top):
            keys = chunk_keys(own_ref, other_ref, chunk)
            scores = jnp.where(allowed_keys(begin, query, chunk, core), dot(keys, q, NT), MASKED)
            score_ref[chunk, :, :width] = scores
            return jnp.maximum(top, jnp.max(scores, 0, keepdims=True))

        top = lax.fori_loop(0, end, score, jnp.full((1, width), MASKED, F32))

        def add(chunk, state):
            total, acc = state
            weights = jnp.exp(score_ref[chunk, :, :width] - top)
            total = total + jnp.sum(weights, 0, keepdims=True)
            return total, acc + dot(turned_ref[chunk], weights.astype(BF16))

        total, acc = lax.fori_loop(
            0, end, add, (jnp.zeros((1, width), F32), jnp.zeros((LANES, width), F32))
        )
        lse = top + jnp.log(total)
        att = acc / total
        rows = []
        for place, block in enumerate(blocks):
            here = slice(place * GROUP * LANES, (place + 1) * GROUP * LANES)
            lse_ref[block] = lse[:, here]
            heads = by_head(att[:, here])
            low = lanes_of(heads[0]) < HD
            rows.append(
                jnp.concatenate(
                    [jnp.where(low, turn(heads[0]), heads[1]), jnp.where(low, turn(heads[2]), 0.0)], 1
                ).astype(BF16)
            )
            att_ref[block] = rows[-1]
        out = dot(jnp.concatenate(rows, 0) if len(rows) > 1 else rows[0], wide_w[...]).astype(BF16)
        for block, part in cut(out, blocks):
            partial[block] = part

    attend((ring.at(ring.steps),))

    def between():
        if layer == 0:
            for later in range(1, LAYERS):
                opening.forward(later)
        attend(ring.pair(ring.steps - 1))

    def work(s, place):
        if place == 2:

            @pl.when(s < ring.steps - 2)
            def _():
                attend(ring.pair(ring.steps - 2 - s))

            @pl.when(s == ring.steps - 2)
            def _():
                attend((ring.chip,))

    added, finish = ring.scatter(partial, land, scatter_sem, work, between)
    ring.settle()
    middle = hidden_ref[...].astype(F32) + added
    middle_ref[...] = middle
    x = (normal(middle)[1] * gain_row(params_ref, 1, layer)).astype(BF16)
    x_out_ref[...] = x
    experts = share_ref.shape[0]
    logits = dot(params_ref[router_rows(experts, layer), :].astype(BF16), x, NT)
    expert = lax.broadcasted_iota(jnp.int32, logits.shape, 0)
    named = expert < 0
    for choice in range(routes_ref.shape[1]):
        named = named | (expert == routes_ref[layer, choice : choice + 1, :])
    scores = jnp.where(named, logits, MASKED)
    weighted = jnp.where(named, jnp.exp(scores - jnp.max(scores, 0, keepdims=True)), 0.0)
    share_ref[...] = weighted / jnp.sum(weighted, 0, keepdims=True)
    drain()
    finish()
    for copy in keep:
        copy.wait()
    if layer == 0:
        for later in range(1, LAYERS):
            opening.arrived(later)
        opening.drain()


def gather_attend_scatter(count, layer, inputs, rows, width, columns, extra=()):
    block = cells((count, rows, LANES), BF16)
    everyone = pltpu.VMEM((count, rows, width), BF16)
    wide = 2 * LANES
    more_outputs, more_scratch = extra if extra else ([], [])
    return ring_call(
        functools.partial(attend_kernel, count, layer),
        ("attend", layer),
        inputs,
        [
            (cells((count, GROUP, rows, LANES), BF16), SOON),
            (block, SOON),
            (block, SOON),
            (cells((count, rows, width), BF16), ANYWHERE),
            (cells((count, rows, wide), BF16), OUT),
            (cells((count, 1, GROUP * rows), F32), OUT),
            (cells((rows, width), F32), OUT),
            (cells((rows, width), BF16), OUT),
            (cells((2 * count, rows), F32), OUT),
        ]
        + more_outputs,
        [
            everyone,
            pltpu.VMEM((width, columns), BF16),
            pltpu.VMEM((wide, width), BF16),
            pltpu.VMEM((count // SPAN, LANES, SPAN * wide), BF16),
            pltpu.VMEM((count // SPAN, SPAN * wide, 2 * GROUP * LANES), F32),
            everyone,
            land_scratch(count, rows, width),
        ]
        + gather_sems(count)
        + dmas((count,), (count,))
        + scatter_sems(count)
        + dmas((2,), (3,))
        + more_scratch,
        60,
    )


def open_attend_scatter(count, columns, tokens, projections, out_w, small, table, begin, routes):
    rows, width = tokens.shape
    layers, shard, _ = out_w.shape
    devices = 2 * count
    outputs = [
        (cells((layers, width, columns), BF16), ANYWHERE),
        (cells((2,) + out_w.shape, BF16), ANYWHERE),
        (cells((count,) + table.shape, F32), OUT),
        (cells((small.shape[0], width), F32), OUT),
    ]
    scratch = [
        pltpu.VMEM((rows, width), BF16),
        pltpu.VMEM((count, layers, shard, columns), BF16),
        pltpu.VMEM((devices,) + small.shape, BF16),
    ] + dmas(
        (3 + layers,), (2, count, layers), (2, count, layers), (2, devices), (2, count), (2,)
    )
    inputs = [(a, EARLY) for a in (tokens, *projections)] + [(a, ANYWHERE) for a in (out_w, small, table)]
    inputs += [(begin, EARLY), (routes, LATE)]
    return gather_attend_scatter(count, 0, inputs, rows, width, columns, (outputs, scratch))


def load_experts(refs, layer, bufs, sem):
    copies = [
        pltpu.make_async_copy(ref.at[layer, 0], buf.at[0], sem.at[place])
        for place, (ref, buf) in enumerate(zip(refs, bufs))
    ]
    for copy in copies:
        copy.start()
    return copies


def lend_experts(refs, layer, bufs, sems):
    copies = [
        remote(ref.at[layer, 0], buf.at[1], sems[0].at[place], sems[1].at[place], partner_of("fsdp"))
        for place, (ref, buf) in enumerate(zip(refs, bufs))
    ]
    for copy in copies:
        copy.start()
    return copies


def expert_of(e):
    me = lax.axis_index("fsdp")
    return me if e == 0 else me + 1 - 2 * lax.rem(me, 2)


def share_of(share_ref, e, blocks):
    columns = [as_column(share_ref[b, pl.ds(expert_of(e), 1), :]) for b in blocks]
    return jnp.concatenate(columns, 0) if len(columns) > 1 else columns[0]


def after_loads(loads, run):
    def first(s):
        @pl.when(s == 1)
        def _():
            for load in loads:
                load.wait()

        run(s)

    return first


def mix_kernel(count, layer, traffic, *refs):
    last = layer + 1 == LAYERS
    inputs, outputs, scratch = split(refs, 7 + last, 5 + last)
    x_ref, side_ref, middle_ref, params_ref = inputs[:4]
    mixed_ref, hidden_ref, next_ref, all_ref, share_ref = outputs[:5]
    buf, partial, land, acc, gates, ups, downs = scratch[:7]
    sems, scatter_sem, load_sem, lend_sem, out_sem = split(scratch[7:], 5, 2, 1, 2)
    ring = Ring(count, traffic)
    loads = load_experts(inputs[4:7], layer, (gates, ups, downs), load_sem[0])
    ring.meet(True)
    lent = lend_experts(inputs[4:7], layer, (gates, ups, downs), lend_sem)

    def ready():
        for copy in lent:
            copy.wait()

    def compute(e, blocks):
        x = stack(buf, blocks)
        act_gate, act_up = dot(x, gates[e]), dot(x, ups[e])
        hidden = jax.nn.silu(act_gate) * act_up * share_of(share_ref, e, blocks)
        part = dot(hidden.astype(BF16), downs[e])
        if e == 0:
            acc[: x.shape[0]] = part
        else:
            total = (acc[: x.shape[0]] + part).astype(BF16)
            for block, rows in cut(total, blocks):
                partial[block] = rows

    first, second = ring.meanwhile(compute, ready)
    drain = ring.gather(x_ref, buf, sems, (side_ref, share_ref), after_loads(loads, first), second)
    keep = pltpu.make_async_copy(buf, all_ref, out_sem[0].at[0])
    keep.start()
    for e in range(2):
        compute(e, (ring.at(ring.steps),))
    mixed, finish = ring.scatter(partial, land, scatter_sem)
    ring.settle()
    mixed_ref[...] = mixed
    hidden = middle_ref[...] + mixed
    hidden_ref[...] = hidden
    if layer + 1 < LAYERS:
        next_ref[...] = (normal(hidden)[1] * gain_row(params_ref, 0, layer + 1)).astype(BF16)
    else:
        next_ref[...] = hidden.astype(BF16)
        balance = jnp.sum(mixed * inputs[7][...].astype(F32), -1, keepdims=True)
        outputs[5][...] = jnp.broadcast_to(as_line(balance), outputs[5].shape)
    drain()
    finish()
    keep.wait()


def expert_scratch(weights):
    return [pltpu.VMEM((2,) + w.shape[2:], BF16) for w in weights]


def land_scratch(count, rows, width):
    return pltpu.VMEM((2, 2, count // 2, rows // 2, width), BF16)


def gather_mix_scatter(count, layer, x, share, middle, params, weights, cotangent):
    rows, width = x.shape
    everyone = pltpu.VMEM((count, rows, width), BF16)
    own = cells((rows, width), F32)
    return ring_call(
        functools.partial(mix_kernel, count, layer),
        ("mix", layer),
        [(x, ANYWHERE), (share, ANYWHERE), (middle, LATE), (params, LATE)]
        + [(w, ANYWHERE) for w in weights]
        + ([(cotangent, LATE)] if layer + 1 == LAYERS else []),
        [
            (own, OUT),
            (own, OUT),
            (cells((rows, width), BF16), OUT),
            (cells((count, rows, width), BF16), ANYWHERE),
            (cells((count,) + share.shape, F32), OUT),
        ]
        + ([(cells((8, rows), F32), OUT)] if layer + 1 == LAYERS else []),
        [everyone, everyone, land_scratch(count, rows, width), pltpu.VMEM((2 * rows, width), F32)]
        + expert_scratch(weights)
        + gather_sems(count, True)
        + scatter_sems(count)
        + dmas((3,), (3,), (3,), (1,)),
        60,
    )


def mix_back_kernel(count, layer, traffic, *refs):
    inputs, outputs, scratch = split(refs, 10, 5)
    d_ref, side_ref, m_ref, share_ref, params_ref, grad_ref, middle_ref = inputs[:7]
    mid_ref, branch_ref, gain_ref, sum_ref, g_router_ref = outputs
    buf, partial, land, acc, gates, ups, downs = scratch[:7]
    tokens, acts, hiddens, balance_ref, totals, got = scratch[7:13]
    sems, scatter_sem, load_sem, pair_sem, lend_sem, out_sem = split(scratch[13:], 5, 2, 1, 2, 2)
    ring = Ring(count, traffic)
    loads = load_experts(inputs[7:], layer, (gates, ups, downs), load_sem[0])
    loads.append(pltpu.make_async_copy(m_ref, tokens, load_sem[0].at[3]))
    loads[-1].start()
    ring.meet(True)
    lent = lend_experts(inputs[7:], layer, (gates, ups, downs), lend_sem)

    def ready():
        for copy in lent:
            copy.wait()

    ff = gates.shape[2]
    width = buf.shape[2]
    g_router_ref[...] = jnp.zeros_like(g_router_ref)
    routers = 2 * LAYERS + layer * 2 * count

    def compute(e, blocks):
        d, x = stack(buf, blocks), stack(tokens, blocks)
        share = share_of(share_ref, e, blocks)
        balance = [as_column(balance_ref[b, 0:1, :]) for b in blocks]
        balance = jnp.concatenate(balance, 0) if len(balance) > 1 else balance[0]
        act_gate, act_up = dot(x, gates[e]), dot(x, ups[e])
        sig = jax.nn.sigmoid(act_gate)
        swish = act_gate * sig
        hidden = swish * act_up
        raw = dot(d, downs[e], NT)
        d_logit = share * (jnp.sum(hidden * raw, -1, keepdims=True) - balance)
        d_hidden = raw * share
        d_gate = (d_hidden * act_up * sig * (1.0 + act_gate * (1.0 - sig))).astype(BF16)
        d_up = (d_hidden * swish).astype(BF16)
        weighted = (hidden * share).astype(BF16)
        part = dot(d_gate, gates[e], NT) + dot(d_up, ups[e], NT)
        part = part + d_logit * params_ref[pl.ds(routers + expert_of(e), 1), :]
        g_router_ref[e : e + 1, :] += jnp.sum(d_logit * x.astype(F32), 0, keepdims=True)
        for place, block in enumerate(blocks):
            here = slice(place * LANES, (place + 1) * LANES)
            acts[e, block, :, :ff] = d_gate[here]
            acts[e, block, :, ff:] = d_up[here]
            hiddens[e, block] = weighted[here]
        if e == 0:
            acc[: x.shape[0]] = part
        else:
            total = (acc[: x.shape[0]] + part).astype(BF16)
            for block, rows in cut(total, blocks):
                partial[block] = rows

    first, second = ring.meanwhile(compute, ready)
    drain = ring.gather(d_ref, buf, sems, (side_ref, balance_ref), after_loads(loads, first), second)
    for e in range(2):
        compute(e, (ring.at(ring.steps),))

    partner = partner_of("fsdp")
    strip = 2 * LANES
    strips = width // (2 * strip)
    groups = width // ff

    def regions(half):
        regions = [(group * width + half * (width // 2), width // 2) for group in range(2)]
        return regions + [(2 * width + group * ff + half * (ff // 2), ff // 2) for group in range(groups)]

    def swap(half):
        return [
            remote(
                totals.at[1, pl.ds(first, length)], got.at[pl.ds(first, length)],
                pair_sem[0].at[half, index], pair_sem[1].at[half, index], partner,
            )
            for index, (first, length) in enumerate(regions(half))
        ]

    def store(half):
        return [
            pltpu.make_async_copy(
                totals.at[0, pl.ds(first, length)], sum_ref.at[pl.ds(first, length)], out_sem[0].at[half, index]
            )
            for index, (first, length) in enumerate(regions(half))
        ]

    def work(s, place):
        e = 1 - s // 2
        half = lax.rem(s, 2)

        def put(first, value):
            rows = pl.ds(pl.multiple_of(first, strip), strip)

            @pl.when(s < 2)
            def _():
                totals[1, rows] = value.astype(BF16)

            @pl.when(s >= 2)
            def _():
                totals[0, rows] = (value + got[rows].astype(F32)).astype(BF16)

        if place == 0:
            for h in range(2):

                @pl.when(s == 2 + h)
                def _():
                    for copy in swap(h):
                        copy.wait_recv()

        if place < strips:
            first = (half * strips + place) * strip
            columns = pl.ds(pl.multiple_of(first, strip), strip)
            value = dot(flat(tokens[:, :, columns]), flat(acts[e]), TN)
            for group in range(2):
                put(group * width + first, value[:, group * ff : (group + 1) * ff])
        if place == 3:
            columns = pl.ds(pl.multiple_of(half * strip, strip), strip)
            value = dot(flat(hiddens[e, :, :, columns]), flat(buf[...]), TN)
            for group in range(groups):
                put(2 * width + group * ff + half * strip, value[:, group * ff : (group + 1) * ff])
            for h in range(2):

                @pl.when(s == h)
                def _():
                    for copy in swap(h):
                        copy.start()

                @pl.when(s == 2 + h)
                def _():
                    for copy in store(h):
                        copy.start()

    d_x, finish = ring.scatter(partial, land, scatter_sem, work)
    ring.settle()
    d_values, gain_ref[...] = normal_back(d_x, middle_ref[...], gain_row(params_ref, 1, layer))
    grad = grad_ref[...].astype(F32) + d_values
    mid_ref[...] = grad
    branch_ref[...] = grad.astype(BF16)
    drain()
    finish()
    for half in range(2):
        for copy in swap(half):
            copy.wait_send()
        for copy in store(half):
            copy.wait()


def gather_mix_back_scatter(count, layer, d, side, m_all, share, params, grad, middle, weights, rides):
    rows, width = d.shape
    ff = weights[0].shape[3]
    everyone = pltpu.VMEM((count, rows, width), BF16)
    groups = width // ff
    own = cells((rows, width), F32)
    return ring_call(
        functools.partial(mix_back_kernel, count, layer),
        ("mix_back", layer),
        [(d, ANYWHERE), (side, ANYWHERE), (m_all, ANYWHERE), (share, EARLY), (params, EARLY), (grad, LATE), (middle, LATE)]
        + [(w, ANYWHERE) for w in weights],
        [
            (own, OUT),
            (cells((rows, width), BF16), OUT),
            (cells((1, width), F32), OUT),
            (cells((3 * width, ff), BF16), ANYWHERE),
            (cells((2, width), F32), OUT),
        ],
        [everyone, everyone, land_scratch(count, rows, width), pltpu.VMEM((2 * rows, width), F32)]
        + expert_scratch(weights)
        + [
            everyone,
            pltpu.VMEM((2, count, rows, 2 * ff), BF16),
            pltpu.VMEM((2, count, rows, ff), BF16),
            pltpu.VMEM((count,) + side.shape, F32),
            pltpu.VMEM((2, 3 * width, ff), BF16),
            pltpu.VMEM((3 * width, ff), BF16),
        ]
        + gather_sems(count, True)
        + scatter_sems(count)
        + dmas((4,), (2, 2 + groups), (2, 2 + groups), (3,), (3,), (2, 2 + groups)),
        60,
        rides,
    )


def load_out_weights(w_ref, layer, wide_ref, sem):
    shard = w_ref.shape[2]
    copies = [
        pltpu.make_async_copy(w_ref.at[core, layer], wide_ref.at[pl.ds(core * shard, shard)], sem.at[core])
        for core in range(2)
    ]
    for copy in copies:
        copy.start()
    used = 2 * shard
    wide_ref[used:] = jnp.zeros((wide_ref.shape[0] - used, wide_ref.shape[1]), BF16)
    return copies


def attend_back_kernel(count, layer, traffic, *refs):
    inputs, outputs, scratch = split(refs, 17, 5)
    d_ref, w_out_ref, w_ref, x_ref, att_ref, q_ref, own_ref, other_ref, begin_ref, lse_ref, table_ref = inputs[:11]
    params_ref, mid_ref, hidden_ref, mixed_ref, router_ref, gain_two_ref = inputs[11:]
    g_out_ref, grad_ref, d_mix_ref, side_ref, g_ref = outputs
    buf, wide_w, g_acc, out_mail, out_got, turned_ref, d_own, d_other, mail, got, dq_ref = scratch[:11]
    partial, land, rows_ref, tokens, weights, last_ref = scratch[11:17]
    sems, scatter_sem, pair_sem, load_sem = split(scratch[17:], 3, 2, 2)
    ring = Ring(count, traffic)
    shard = g_out_ref.shape[0]
    loads = load_out_weights(w_out_ref, layer, wide_w, load_sem[0])
    later = [
        pltpu.make_async_copy(x_ref, tokens, load_sem[0].at[2]),
        pltpu.make_async_copy(w_ref.at[layer], weights, load_sem[0].at[3]),
    ]
    for load in later:
        load.start()
    ring.meet(True)
    core = lax.rem(lax.axis_index("fsdp"), 2)
    width = GROUP * LANES

    def spread(wide):
        front, back = wide[:, :LANES], wide[:, LANES:]
        low = lanes_of(front) < HD
        return [jnp.where(low, 0.0, part) for part in (turn(front), front, turn(back))]

    def compute(block):
        d = buf[block]
        wide = dot(d, wide_w[...], NT).astype(BF16)
        g_acc[...] += dot(att_ref[block], d, TN)
        slopes, deltas = [], []
        for piece, a in zip(spread(wide.astype(F32)), spread(att_ref[block].astype(F32))):
            slopes.append(piece)
            deltas.append(jnp.sum((piece * a).T, 0, keepdims=True))
        datt = jnp.concatenate(slopes, 0).astype(BF16)
        delta = jnp.concatenate(deltas, 1)
        q = q_ref[block].reshape(width, LANES)
        both = jnp.concatenate([q, datt], 0)
        begin, query = query_rows(begin_ref, (block,), core)
        lse = lse_ref[block]

        def one(chunk, acc):
            keys = chunk_keys(own_ref, other_ref, chunk)
            scores = jnp.where(allowed_keys(begin, query, chunk, core), dot(keys, q, NT), MASKED)
            weight = jnp.exp(scores - lse)
            slope = (weight * (dot(keys, datt, NT) - delta)).astype(BF16)
            d_keys = dot(jnp.concatenate([slope, weight.astype(BF16)], 1), both)
            half = SPAN * LANES
            chips = pl.ds(chunk * SPAN, SPAN)
            d_own[chips] += d_keys[:half].reshape(SPAN, LANES, LANES)
            d_other[chips] += d_keys[half:].reshape(SPAN, LANES, LANES)
            return acc + dot(turned_ref[chunk], slope)

        acc = lax.fori_loop(0, chunks_of((block,)), one, jnp.zeros((LANES, width), F32)) * (HD**-0.5)
        heads = by_head(acc)
        low = lanes_of(heads[0]) < HD
        cosine, sine = angles(table_ref[block])
        front = spin(jnp.where(low, heads[0], turn(heads[1])), cosine, -sine)
        back = spin(jnp.where(low, heads[2], 0.0), cosine, -sine)
        dq_ref[block] = jnp.concatenate([front, back], 1).astype(BF16)

    def first(s):
        @pl.when(s == 1)
        def _():
            for load in loads:
                load.wait()
            turn_keys(own_ref, other_ref, turned_ref)
            g_acc[...] = jnp.zeros_like(g_acc)
            d_own[...] = jnp.zeros_like(d_own)
            d_other[...] = jnp.zeros_like(d_other)

        compute(ring.at(1 - s))

    def second(s):
        compute(ring.at(s))

    drain = ring.gather(d_ref, buf, sems, None, first, second)
    compute(ring.at(ring.steps))
    partner = partner_of("fsdp")
    mail[...] = d_other[...].astype(BF16)
    out_mail[...] = g_acc[pl.ds(pl.multiple_of((1 - core) * shard, 8), shard), :].astype(BF16)
    swaps = [
        remote(mail, got, pair_sem[0].at[0], pair_sem[1].at[0], partner),
        remote(out_mail, out_got, pair_sem[0].at[1], pair_sem[1].at[1], partner),
    ]
    for swap in swaps:
        swap.start()
    for load in later:
        load.wait()
    drain()
    swaps[0].wait()

    def join(blocks):
        rows = []
        for b in blocks:
            pair = d_own[b] + got[b].astype(F32)
            cosine, sine = angles(table_ref[b])
            keys = spin(pair, cosine, -sine)
            low = lanes_of(pair) < HD
            middle = jnp.where(low, dq_ref[b, :, LANES:].astype(F32), turn(keys))
            last = jnp.where(low, turn(pair), 0.0)
            rows.append(
                jnp.concatenate([dq_ref[b, :, :LANES], middle.astype(BF16), last.astype(BF16)], 1)
            )
            rows_ref[b] = rows[-1]
        total = dot(jnp.concatenate(rows, 0), weights[...], NT).astype(BF16)
        for block, part in cut(total, blocks):
            partial[block] = part

    join((ring.at(ring.steps), ring.chip))
    strip = g_ref.shape[0] // ring.steps
    tile = 2 * LANES

    def between():
        def one(index, carry):
            join(ring.pair(ring.steps - 1 - index))
            return carry

        lax.fori_loop(0, ring.steps - 1, one, 0)

    def work(s, place):
        if place == 0:
            rows = pl.ds(pl.multiple_of(s * strip, LANES), strip)
            value = dot(flat(tokens[:, :, rows]), flat(rows_ref[...]), TN)
            g_ref[rows, :tile] = value[:, :tile].astype(BF16)
            last_ref[rows] = value[:, tile:]

    d_x, finish = ring.scatter(partial, land, scatter_sem, work, between)
    swaps[1].wait()
    own = g_acc[pl.ds(pl.multiple_of(core * shard, 8), shard), :]
    g_out_ref[...] = (own + out_got[...].astype(F32)).astype(BF16)
    ring.settle()
    d_values, gain_one = normal_back(d_x, hidden_ref[...].astype(F32), gain_row(params_ref, 0, layer))
    grad = mid_ref[...] + d_values
    grad_ref[...] = grad
    d_mix = grad.astype(BF16)
    d_mix_ref[...] = d_mix
    balance = jnp.sum(mixed_ref[...] * d_mix.astype(F32), -1, keepdims=True)
    side_ref[...] = jnp.broadcast_to(as_line(balance), side_ref.shape)
    routers = router_ref[...]
    lines = [
        jnp.where(core == 0, routers[0:1], routers[1:2]),
        jnp.where(core == 0, routers[1:2], routers[0:1]),
        gain_one,
        gain_two_ref[...],
    ]
    features = g_ref.shape[0]
    tall = jnp.concatenate(
        [jnp.zeros((HD, features), F32)] + lines + [jnp.zeros((HD - len(lines), features), F32)], 0
    )
    g_ref[:, tile:] = (last_ref[...] + tall.T).astype(BF16)
    finish()


def gather_attend_back_scatter(
    count, layer, d, w_out, w, x_all, att, q, own, other, begin, lse, tables, late, rides=()
):
    _, rows, width = x_all.shape
    shard = w_out.shape[2]
    columns = w.shape[2]
    everyone = pltpu.VMEM((count, rows, width), BF16)
    early = [att, q, own, other, begin, lse, tables]
    pairs = cells((count, rows, LANES), BF16)
    return ring_call(
        functools.partial(attend_back_kernel, count, layer),
        ("attend_back", layer),
        [(a, ANYWHERE) for a in (d, w_out, w, x_all)] + [(a, EARLY) for a in early] + [(a, LATE) for a in late],
        [
            (cells((shard, width), BF16), OUT),
            (cells((rows, width), F32), OUT),
            (cells((rows, width), BF16), OUT),
            (cells((8, rows), F32), OUT),
            (cells(w.shape[1:], BF16), OUT),
        ],
        [
            everyone,
            pltpu.VMEM((2 * LANES, width), BF16),
            pltpu.VMEM((2 * LANES, width), F32),
            pltpu.VMEM((shard, width), BF16),
            pltpu.VMEM((shard, width), BF16),
            pltpu.VMEM((count // SPAN, LANES, SPAN * 2 * LANES), BF16),
            pltpu.VMEM(pairs.shape, F32),
            pltpu.VMEM(pairs.shape, F32),
            pltpu.VMEM(pairs.shape, BF16),
            pltpu.VMEM(pairs.shape, BF16),
            pltpu.VMEM((count, rows, 2 * LANES), BF16),
            everyone,
            land_scratch(count, rows, width),
            pltpu.VMEM((count, rows, columns), BF16),
            everyone,
            pltpu.VMEM(w.shape[1:], BF16),
            pltpu.VMEM((width, LANES), F32),
        ]
        + gather_sems(count)
        + scatter_sems(count)
        + dmas((2,), (2,), (4,)),
        60,
        rides,
    )


def finish_kernel(count, replicas, *refs):
    inputs, outputs, scratch = split(refs, 3, 2)
    g_ref, early_ref, early_peer_ref = inputs
    mine, peer = outputs
    early, land, total = scratch[:3]
    pair_send, pair_recv, part_send, part_recv, rep_send, rep_recv = scratch[3:]
    me = lax.axis_index("fsdp")
    chip, core = me // 2, lax.rem(me, 2)
    partner = partner_of("fsdp")

    def chip_at(offset):
        return lax.rem(chip + offset + count, count)

    def device(offset):
        return {"fsdp": chip_at(offset) * 2 + core}

    across = [partner_of("rep")] if replicas == 2 else []
    meet([device(offset) for offset in range(1, count)] + [partner] + across)
    swaps = [remote(g_ref.at[:, 1 - core], land.at[0], pair_send.at[0], pair_recv.at[0], partner)]
    swaps[0].start()
    for block in range(count):
        for half in range(2):
            both = early_ref[block, half].astype(F32)
            if replicas == 2:
                both = both + early_peer_ref[block, half].astype(F32)
            early[half, block] = both.astype(BF16)
    if replicas != 2:
        peer[...] = jnp.zeros_like(peer)
    swaps.append(remote(early.at[1 - core], land.at[1], pair_send.at[1], pair_recv.at[1], partner))
    swaps[1].start()
    for swap in swaps:
        swap.wait()
    for block in range(count):
        total[block, 0] = (g_ref[block, core].astype(F32) + land[0, block].astype(F32)).astype(BF16)
        total[block, 1] = (early[core, block].astype(F32) + land[1, block].astype(F32)).astype(BF16)
    sends = [
        remote(
            total.at[chip_at(offset)], mine.at[chip],
            part_send.at[offset], part_recv.at[offset], device(offset),
        )
        for offset in range(1, count)
    ]
    for send in sends:
        send.start()
    mine[chip] = total[chip]

    def to_peer(offset):
        slot = chip_at(-offset)
        return remote(mine.at[slot, 0], peer.at[slot], rep_send.at[offset], rep_recv.at[offset], across[0])

    for offset in range(count):
        if offset > 0:
            slot = mine.at[chip_at(-offset)]
            remote(slot, slot, part_send.at[offset], part_recv.at[offset], partner).wait_recv()
        if replicas == 2:
            to_peer(offset).start()
    if replicas == 2:
        for offset in range(count):
            to_peer(offset).wait()

    for send in sends:
        send.wait_send()


def finish_heads(count, replicas, g, early, early_peer):
    _, _, rows, columns = g.shape
    part = (count, LAYERS, rows, columns)
    dma = pltpu.SemaphoreType.DMA
    return pl.pallas_call(
        functools.partial(finish_kernel, count, replicas),
        out_shape=(cells(part, BF16), cells((count, rows, columns), BF16)),
        in_specs=[HERE] * 3,
        out_specs=[HERE] * 2,
        scratch_shapes=[
            pltpu.VMEM((2, count, rows, columns), BF16),
            pltpu.VMEM((2, count, rows, columns), BF16),
            pltpu.VMEM(part, BF16),
            dma((2,)), dma((2,)), dma((count,)), dma((count,)), dma((count,)), dma((count,)),
        ],
        compiler_params=pltpu.CompilerParams(
            collective_id=identity(("finish",)), has_side_effects=True, vmem_limit_bytes=60 << 20
        ),
        cost_estimate=FREE,
        name="finish_heads",
    )(g, early, early_peer)


def close_kernel(layers, count, *refs):
    n_experts = 0 if len(refs) == 2 * layers + 7 else 10 * layers
    inputs, heads_in, experts_in, outputs = split(refs, 2 * layers, 2, n_experts)
    mine, peer = heads_in
    out_ref, q_out, k_out, v_out, rest_out = outputs[:5]

    @pl.when(pl.program_id(0) == 0)
    def _():
        for layer in range(layers):
            own, got = inputs[2 * layer : 2 * layer + 2]
            out_ref[layer] = own[...].astype(F32) + got[...].astype(F32)

            def tiles(block):
                value = mine[block, layer].astype(F32)
                if layer == 0:
                    value = value + peer[block].astype(F32)
                return [value[:, i * LANES : (i + 1) * LANES] for i in range(3)]

            for half in range(count // 2):
                a, b = tiles(2 * half), tiles(2 * half + 1)
                low = lanes_of(a[0]) < HD
                q_out[layer, :, 3 * half * LANES : 3 * (half + 1) * LANES] = jnp.concatenate(
                    [a[0], jnp.where(low, a[1], turn(b[0])), jnp.where(low, turn(b[0]), turn(b[1]))], 1
                )
                here = slice(half * LANES, (half + 1) * LANES)
                k_out[layer, :, here] = jnp.where(low, turn(a[1]), b[1])
                v_out[layer, :, here] = jnp.where(low, a[2], turn(b[2]))
                rest_out[layer, 2 * half] = a[2]
                rest_out[layer, 2 * half + 1] = b[2]

    if experts_in:
        expert_refs = outputs[5:]
        for layer in range(layers):
            pairs = experts_in[layer * 10 : (layer + 1) * 10]
            sums = [pairs[i][...].astype(F32) + pairs[i + 5][...].astype(F32) for i in range(5)]
            expert_refs[0][layer, 0] = sums[0]
            expert_refs[1][layer, 0] = sums[1]
            expert_refs[2][layer, 0] = jnp.concatenate(sums[2:], 1)


def close(count, outs, mine, peer, experts):
    layers = len(outs)
    shard, width = outs[0][0].shape
    steps = 4

    def whole(shape):
        return pl.BlockSpec(shape, lambda i: (0,) * len(shape))

    arrays = [array for pair in outs for array in pair] + [mine, peer]
    specs = [whole(a.shape) for a in arrays]
    shapes = [
        (layers, shard, width),
        (layers, shard, count * GROUP * HD),
        (layers, shard, count * HD),
        (layers, shard, count * HD),
        (layers, count, shard, LANES),
    ]
    out_specs = [whole(shape) for shape in shapes]
    if experts:
        rows, ff = experts[0][0].shape
        tall, short = width // steps, ff // steps
        groups = (rows - 2 * width) // ff

        def at(first, length):
            return pl.BlockSpec((length, ff), lambda i: (first // length + i, 0))

        parts = [at(0, tall), at(width, tall)] + [at(2 * width + g * ff, short) for g in range(groups)]
        arrays += [array for pair in experts for array in pair for _ in parts]
        specs += parts * (2 * layers)
        shapes += [(layers, 1, width, ff), (layers, 1, width, ff), (layers, 1, ff, width)]
        tile = pl.BlockSpec((layers, 1, tall, ff), lambda i: (0, 0, i, 0))
        out_specs += [tile, tile, pl.BlockSpec((layers, 1, short, width), lambda i: (0, 0, i, 0))]
    return pl.pallas_call(
        functools.partial(close_kernel, layers, count),
        grid=(steps if experts else 1,),
        out_shape=tuple(cells(shape, F32) for shape in shapes),
        in_specs=specs,
        out_specs=out_specs,
        compiler_params=pltpu.CompilerParams(vmem_limit_bytes=60 << 20),
        cost_estimate=FREE,
        name="close",
    )(*arrays)


def on_device(
    tokens,
    cotangent,
    positions,
    segments,
    routes,
    attn_gain,
    w_query,
    w_key,
    w_value,
    w_out,
    ffn_gain,
    router,
    w_gate,
    w_up,
    w_down,
):
    rows, width = tokens.shape
    devices = lax.axis_size("fsdp")
    replicas = lax.axis_size("rep")
    count = devices // 2
    me = lax.axis_index("fsdp")
    chip, core = me // 2, lax.rem(me, 2)
    shard = w_query.shape[1]
    experts = devices
    columns = 3 * LANES
    used = (GROUP + 2) * HD

    small = jnp.concatenate(
        [attn_gain, ffn_gain, router.transpose(0, 2, 1).reshape(LAYERS * experts, shard)], 0
    )
    small = jnp.pad(small, ((0, 48 - small.shape[0]), (0, LANES - shard)))
    rate = jnp.exp(-jnp.log(10000.0) * jnp.arange(HD // 2, dtype=F32) / (HD // 2))
    angle = rate[:, None] * positions.astype(F32)[None, :]
    table = jnp.concatenate([jnp.cos(angle), jnp.sin(angle)], 0)
    experts_w = [w_gate, w_up, w_down]

    flat_segments = segments.reshape(1, -1)
    kinds = jnp.arange(8, dtype=jnp.int32)[:, None]
    starts = jnp.sum((flat_segments < kinds).astype(jnp.int32), 1, keepdims=True)
    begin = jnp.sum(jnp.where(flat_segments == kinds, starts, 0), 0).reshape(count, 2, rows)
    begin = lax.dynamic_index_in_dim(begin, core, 1, True)

    chosen = routes.transpose(0, 2, 1)
    hidden = tokens
    saved = []
    for layer in range(LAYERS):
        if layer == 0:
            *results, heads_w, outs_w, tables, params = open_attend_scatter(
                count, columns, tokens, [w_query, w_key, w_value], w_out, small, table, begin, chosen
            )
        else:
            results = gather_attend_scatter(
                count,
                layer,
                [
                    (x_attn, ANYWHERE), (heads_w, ANYWHERE), (outs_w, ANYWHERE), (tables, EARLY),
                    (begin, EARLY), (hidden, LATE), (params, LATE), (chosen, LATE),
                ],
                rows,
                width,
                columns,
            )
        query, kv, kv_other, x_all, att, lse, middle, x_moe, share = results
        mixed, after, x_attn, m_all, share_all, *side = gather_mix_scatter(
            count, layer, x_moe, share, middle, params, experts_w, cotangent
        )
        saved.append((hidden, x_all, query, kv, kv_other, att, lse, middle, mixed, m_all, share_all))
        hidden = after
    activations = x_attn

    def across(array):
        return lax.ppermute(array, "rep", [(0, 1), (1, 0)]) if replicas == 2 else array

    grad = d_mix = cotangent
    (side,) = side
    expert_sums = [None] * LAYERS
    out_sums = [None] * LAYERS
    for layer in reversed(range(LAYERS)):
        hidden, x_all, query, kv, kv_other, att, lse, middle, mixed, m_all, share_all = saved[layer]
        rides = [out_sums[layer + 1], early] if layer + 1 < LAYERS and replicas == 2 else []
        grad_mid, d_branch, gain_two, expert_sum, g_router, *rode = gather_mix_back_scatter(
            count, layer, d_mix, side, m_all, share_all, params, grad, middle, experts_w, rides
        )
        if layer + 1 < LAYERS:
            d_branch, expert_sums[layer + 1] = lax.optimization_barrier(
                (d_branch, expert_sums[layer + 1])
            )
        expert_sums[layer] = (expert_sum, across(expert_sum))
        out_sum, grad, d_mix, side, heads = gather_attend_back_scatter(
            count, layer, d_branch, outs_w, heads_w, x_all, att, query, kv, kv_other, begin, lse, tables,
            [params, grad_mid, hidden, saved[max(layer - 1, 0)][8], g_router, gain_two],
        )
        out_sums[layer] = out_sum
        heads = heads.reshape(count, 2, shard, columns)
        early = heads if layer > 0 else early
    arrived, peer = finish_heads(count, replicas, heads, early, rode[1] if rode else early)
    if replicas == 2:
        outs = list(zip(out_sums, [across(out_sums[0]), rode[0]]))
        g_out, g_query, g_key, g_value, rest, g_gate, g_up, g_down = close(
            count, outs, arrived, peer, expert_sums
        )
    else:
        outs = [(own, jnp.zeros_like(own)) for own in out_sums]
        summed = close(count, outs, arrived, peer, [])
        g_out, g_query, g_key, g_value, rest, flat_sums = [
            lax.psum(array.astype(BF16), "rep").astype(F32)
            for array in (*summed, jnp.stack([own for own, _ in expert_sums]))
        ]
        ff = w_gate.shape[3]
        g_gate, g_up = flat_sums[:, None, :width], flat_sums[:, None, width : 2 * width]
        g_down = flat_sums[:, 2 * width :].reshape(LAYERS, width // ff, ff, ff)
        g_down = g_down.transpose(0, 2, 1, 3).reshape(LAYERS, 1, ff, width)
    rest = rest[..., HD : HD + 4]
    gains = jnp.sum(rest, 1)
    g_router = rest[..., :2].transpose(0, 2, 1, 3).reshape(LAYERS, shard, experts)
    return (
        activations,
        grad,
        gains[..., 2],
        g_query,
        g_key,
        g_value,
        g_out,
        gains[..., 3],
        g_router,
        g_gate,
        g_up,
        g_down,
    )


def solution(mesh):
    placed = (
        P(("rep", "fsdp"), None),
        P(("rep", "fsdp"), None),
        P(("rep", "fsdp")),
        P("rep", None),
        P(None, ("rep", "fsdp"), None),
        P(None, "fsdp"),
        P(None, "fsdp", None),
        P(None, "fsdp", None),
        P(None, "fsdp", None),
        P(None, "fsdp", None),
        P(None, "fsdp"),
        P(None, "fsdp", None),
        P(None, "fsdp", None, None),
        P(None, "fsdp", None, None),
        P(None, "fsdp", None, None),
    )
    return jax.shard_map(
        on_device,
        mesh=mesh,
        in_specs=placed,
        out_specs=(
            P(("rep", "fsdp"), None),
            P(("rep", "fsdp"), None),
            P(None, "fsdp"),
            P(None, "fsdp", None),
            P(None, "fsdp", None),
            P(None, "fsdp", None),
            P(None, "fsdp", None),
            P(None, "fsdp"),
            P(None, "fsdp", None),
            P(None, "fsdp", None, None),
            P(None, "fsdp", None, None),
            P(None, "fsdp", None, None),
        ),
        check_vma=False,
    )
```

```python
import functools

import jax
import jax.numpy as jnp
from jax import lax
from jax.experimental import pallas as pl
from jax.experimental.pallas import tpu as pltpu
from jax.sharding import PartitionSpec as P

HEADS = 24
KV_HEADS = 8
HD = 64
LAYERS = 2
GROUP = HEADS // KV_HEADS
LANES = 128
SPAN = 2
EPS = 1e-06
MASKED = -1e30
MESH = pl.DeviceIdType.MESH
F32 = jnp.float32
BF16 = jnp.bfloat16


def ring_place(chip, count):
    return lax.select(lax.rem(chip, 2) == 0, chip // 2, count - 1 - chip // 2)


def ring_chip(place, count):
    return lax.select(place < count // 2, 2 * place, 2 * (count - 1 - place) + 1)


def ring_setup(count):
    me = lax.axis_index("fsdp")
    chip, core = me // 2, lax.rem(me, 2)
    place = ring_place(chip, count)

    def at(offset):
        return ring_chip(lax.rem(place + offset + 2 * count, count), count)

    near = [{"fsdp": at(1) * 2 + core}, {"fsdp": at(-1) * 2 + core}]
    return chip, at, near


def partner_of(axis):
    if axis == "rep":
        return {"rep": 1 - lax.axis_index("rep")}
    me = lax.axis_index("fsdp")
    return {"fsdp": me + 1 - 2 * lax.rem(me, 2)}


def meet(others):
    barrier = pltpu.get_barrier_semaphore()
    for other in others:
        pl.semaphore_signal(barrier, inc=1, device_id=other, device_id_type=MESH)
    pl.semaphore_wait(barrier, len(others))


def remote(src, dst, send_sem, recv_sem, device):
    return pltpu.make_async_remote_copy(
        src_ref=src,
        dst_ref=dst,
        send_sem=send_sem,
        recv_sem=recv_sem,
        device_id=device,
        device_id_type=MESH,
    )


def ring_hops(count):
    half = count // 2
    return {(0, 0): half, (1, 1): half, (0, 1): half - 1, (1, 0): half - 1}


IDENTITIES = {}


def identity(key):
    return IDENTITIES.setdefault(key, len(IDENTITIES))


class Ring:
    def __init__(self, count, traffic):
        self.count = count
        self.riders, self.early, self.late, self.soon = traffic
        self.steps = count // 2
        self.chip, self.at, self.near = ring_setup(count)

    def meet(self, partner=False, everyone=None):
        others = everyone or self.near + ([partner_of("fsdp")] if partner else [])
        meet(others + ([partner_of("rep")] if self.riders else []))
        for rider in self.riders:
            rider.start()
        for copy in self.early:
            copy.wait()

    def settle(self):
        for copy in self.late:
            copy.wait()

    def depart(self):
        for copy in self.soon:
            copy.start()

    def gather(self, x_ref, buf, sems, side=None, first=None, second=None):
        own_sem, send_sem, recv_sem = sems[:3]
        half_rows = x_ref.shape[0] // 2
        steps = self.steps
        own = [pltpu.make_async_copy(x_ref, buf.at[self.chip], own_sem.at[0])]
        if side is not None:
            side_ref, side_buf = side
            side_send, side_recv = sems[3:]
            own.append(pltpu.make_async_copy(side_ref, side_buf.at[self.chip], own_sem.at[1]))
        for copy in own:
            copy.start()

        def piece(key, step, block, source=None):
            direction, part = key
            rows = pl.ds(part * half_rows, half_rows)
            target = buf.at[block, rows]
            return remote(
                target if source is None else source.at[rows],
                target,
                send_sem.at[direction, part, step],
                recv_sem.at[direction, part, step],
                self.near[direction],
            )

        def side_piece(direction, step, block, source=None):
            target = side_buf.at[block]
            return remote(
                target if source is None else source,
                target,
                side_send.at[direction, step],
                side_recv.at[direction, step],
                self.near[direction],
            )

        def toward(key, places):
            return self.at(-places if key[0] == 0 else places)

        early, late = [(0, 0), (1, 1)], [(0, 1), (1, 0)]
        if side is not None:
            for direction in range(2):
                side_piece(direction, 0, self.chip, side_ref).start()
        for key in early + late:
            piece(key, 0, self.chip, x_ref).start()

        def take(keys, s, last):
            for key in keys:
                block = toward(key, s)
                piece(key, s - 1, block).wait_recv()

                @pl.when(s < last)
                def _():
                    piece(key, s, block).start()

        def take_side(s):
            if side is not None:
                for direction in range(2):

                    @pl.when(s <= steps - direction)
                    def _():
                        block = toward((direction, 0), s)
                        side_piece(direction, s - 1, block).wait_recv()

                        @pl.when(s < steps - direction)
                        def _():
                            side_piece(direction, s, block).start()

        def step(s, carry):
            take_side(s)
            take(early, s, steps)
            first(s)
            take(late, s, steps - 1)
            second(s)
            return carry

        for copy in own:
            copy.wait()
        lax.fori_loop(1, steps, step, 0)
        first(steps)
        take_side(steps)
        take(early, steps, steps)

        def drain():
            for s in range(steps):
                for key in early + (late if s < steps - 1 else []):
                    piece(key, s, toward(key, s)).wait_send()
                if side is not None:
                    for direction in range(2):
                        if s < steps - direction:
                            side_piece(direction, s, toward((direction, 0), s)).wait_send()

        return drain

    def pair(self, s):
        return self.at(s), self.at(-s)

    def meanwhile(self, compute, ready):
        def first(s):
            @pl.when(s == 1)
            def _():
                compute(0, (self.chip,))

            @pl.when(s > 1)
            def _():
                compute(1, self.pair(s - 1))

        def second(s):
            @pl.when(s == 1)
            def _():
                ready()
                compute(1, (self.chip,))

            compute(0, self.pair(s))

        return first, second

    def scatter(self, partial, land, sems, work=None, between=None):
        send_sem, recv_sem = sems
        half_rows = partial.shape[1] // 2
        steps = self.steps
        hops = ring_hops(self.count)

        def ahead(key, s):
            places = hops[key] - s
            return self.at(places if key[0] == 0 else -places)

        def piece(key, s, source):
            direction, part = key
            return remote(
                source,
                land.at[direction, part, s],
                send_sem.at[direction, part, s],
                recv_sem.at[direction, part, s],
                self.near[direction],
            )

        def rows_of(key):
            return pl.ds(key[1] * half_rows, half_rows)

        for place, key in enumerate(hops):
            if place == 2 and between is not None:
                between()
            piece(key, 0, partial.at[ahead(key, 0), rows_of(key)]).start()

        def step(s, carry):
            for place, key in enumerate(hops):
                if work is not None:
                    work(s - 1, place)

                @pl.when(s < hops[key])
                def _():
                    slot = land.at[key[0], key[1], s - 1]
                    piece(key, s - 1, slot).wait_recv()
                    mine = partial[ahead(key, s), rows_of(key)]
                    slot[...] = (slot[...].astype(F32) + mine.astype(F32)).astype(BF16)
                    piece(key, s, slot).start()

            return carry

        lax.fori_loop(1, steps + 1, step, 0)
        for key in hops:
            slot = land.at[key[0], key[1], hops[key] - 1]
            piece(key, hops[key] - 1, slot).wait_recv()
        halves = []
        for part in range(2):
            rows = pl.ds(part * half_rows, half_rows)
            total = partial[self.chip, rows].astype(F32)
            for direction in range(2):
                total = total + land[direction, part, hops[direction, part] - 1].astype(F32)
            halves.append(total)
        summed = jnp.concatenate(halves, 0)

        def drain():
            for key in hops:
                for s in range(hops[key]):
                    piece(key, s, land.at[key[0], key[1], s]).wait_send()

        return summed, drain


def dmas(*shapes):
    return [pltpu.SemaphoreType.DMA(shape) for shape in shapes]


def gather_sems(count, sided=False):
    steps = count // 2
    shapes = [(2,), (2, 2, steps), (2, 2, steps)]
    return dmas(*(shapes + ([(2, steps), (2, steps)] if sided else [])))


def scatter_sems(count):
    return dmas((2, 2, count // 2), (2, 2, count // 2))


ANYWHERE = pl.BlockSpec(memory_space=pltpu.HBM)
HERE = pl.BlockSpec(memory_space=pltpu.VMEM)
EARLY, LATE = "early", "late"
OUT, SOON = "out", "soon"


FREE = pl.CostEstimate(flops=0, bytes_accessed=0, transcendentals=0)


def ring_call(body, key, inputs, outputs, scratch, megabytes, rides=()):
    n_in, n_out, n_rides = len(inputs), len(outputs), len(rides)
    in_kinds = [kind for _, kind in inputs]
    out_kinds = [kind for _, kind in outputs]
    copied = [a for a, kind in inputs if kind in (EARLY, LATE)]
    returned = [a for a, kind in outputs if kind in (OUT, SOON)]
    moves = len(copied) + len(returned)

    def kernel(*refs):
        ins, ride_in, outs, ride_out, rest = split(refs, n_in, n_rides, n_out, n_rides)
        rest, own, rest_sems = rest[: len(scratch)], rest[len(scratch) : len(scratch) + moves], rest[len(scratch) + moves :]
        move_sem, rest_sems = rest_sems[0], rest_sems[1:]
        riders = []
        if n_rides:
            send_sem, recv_sem = rest_sems
            riders = [
                remote(ride_in[i], ride_out[i], send_sem.at[i], recv_sem.at[i], partner_of("rep"))
                for i in range(n_rides)
            ]
        used = 0
        early, late, leaving, soon = [], [], [], []
        ins, outs = list(ins), list(outs)
        for i, kind in enumerate(in_kinds):
            if kind in (EARLY, LATE):
                copy = pltpu.make_async_copy(ins[i], own[used], move_sem.at[used])
                copy.start()
                (early if kind == EARLY else late).append(copy)
                ins[i] = own[used]
                used += 1
        for i, kind in enumerate(out_kinds):
            if kind in (OUT, SOON):
                copy = pltpu.make_async_copy(own[used], outs[i], move_sem.at[used])
                (leaving if kind == OUT else soon).append(copy)
                outs[i] = own[used]
                used += 1
        body((riders, early, late, soon), *ins, *outs, *rest)
        for copy in leaving:
            copy.start()
        for rider in riders:
            rider.wait()
        for copy in leaving + soon:
            copy.wait()

    def spec(kind):
        return ANYWHERE if isinstance(kind, str) else kind

    return pl.pallas_call(
        kernel,
        out_shape=tuple(shape for shape, _ in outputs) + tuple(cells(a.shape, a.dtype) for a in rides),
        in_specs=[spec(kind) for kind in in_kinds] + [ANYWHERE] * n_rides,
        out_specs=[spec(kind) for kind in out_kinds] + [ANYWHERE] * n_rides,
        scratch_shapes=list(scratch)
        + [pltpu.VMEM(a.shape, a.dtype) for a in copied + returned]
        + dmas((max(moves, 1),))
        + (dmas((n_rides,), (n_rides,)) if n_rides else []),
        compiler_params=pltpu.CompilerParams(
            collective_id=identity(key),
            has_side_effects=True,
            vmem_limit_bytes=megabytes << 20,
        ),
        cost_estimate=FREE,
        name=key[0],
    )(*[array for array, _ in inputs], *rides)


def split(refs, *sizes):
    parts, place = [], 0
    for size in sizes:
        parts.append(refs[place : place + size])
        place += size
    return parts + [refs[place:]]


def cells(shape, dtype):
    return jax.ShapeDtypeStruct(shape, dtype)


def dot(left, right, contract=((1,), (0,))):
    return lax.dot_general(left, right, (contract, ((), ())), preferred_element_type=F32)


NT = ((1,), (1,))
TN = ((0,), (0,))


def lanes_of(field):
    return lax.broadcasted_iota(jnp.int32, field.shape, 1)


def turn(field):
    return pltpu.roll(field, HD, 1)


def spin(field, cosine, sine):
    swapped = jnp.where(
        lax.rem(lanes_of(field), HD) < HD // 2,
        -pltpu.roll(field, LANES - HD // 2, 1),
        pltpu.roll(field, HD // 2, 1),
    )
    return field * cosine + swapped * sine


def project_rows(rows, cosine, sine):
    first = spin(rows[:, :LANES], cosine, sine)
    second = spin(rows[:, LANES : 2 * LANES], cosine, sine)
    third = rows[:, 2 * LANES :]
    low = lanes_of(first) < HD
    heads = []
    for field in (first, turn(first), second):
        rounded = jnp.where(low, field, 0.0).astype(BF16).astype(F32)
        heads.append((rounded * (HD**-0.5)).astype(BF16))
    return heads, jnp.where(low, turn(second), turn(third)).astype(BF16)


def angles(table):
    rows = jnp.concatenate([table, table], 0).T
    early = lax.rem(lanes_of(rows), HD) < HD // 2
    cosine = jnp.where(early, rows, pltpu.roll(rows, HD // 2, 1))
    sine = jnp.where(early, pltpu.roll(rows, LANES - HD // 2, 1), rows)
    return cosine, sine


def normal(values):
    inverse = lax.rsqrt(jnp.mean(values * values, -1, keepdims=True) + EPS)
    return inverse, values * inverse


def normal_back(d_x, values, gain):
    inverse, normed = normal(values)
    d_norm = d_x * gain
    d_values = inverse * (d_norm - normed * jnp.mean(d_norm * normed, -1, keepdims=True))
    return d_values, jnp.sum(d_x * normed, 0, keepdims=True)


def diagonal():
    shape = (LANES, LANES)
    return lax.broadcasted_iota(jnp.int32, shape, 0) == lax.broadcasted_iota(jnp.int32, shape, 1)


def as_column(line):
    return jnp.sum(jnp.where(diagonal(), jnp.broadcast_to(line, (LANES, LANES)), 0.0), 1, keepdims=True)


def as_line(column):
    return jnp.sum(jnp.where(diagonal(), jnp.broadcast_to(column, (LANES, LANES)), 0.0), 0, keepdims=True)


def flat(value):
    return value.reshape(value.shape[0] * value.shape[1], value.shape[2])


def stack(ref, blocks):
    parts = [ref[b] for b in blocks]
    return parts[0] if len(parts) == 1 else jnp.concatenate(parts, 0)


def cut(value, blocks):
    return [(b, value[i * LANES : (i + 1) * LANES]) for i, b in enumerate(blocks)]


def gain_row(params_ref, kind, layer):
    row = kind * LAYERS + layer
    return params_ref[row : row + 1, :]


def router_rows(experts, layer):
    first = 2 * LAYERS + layer * experts
    return slice(first, first + experts)


def allowed_keys(begin, query, chunk, core):
    half = SPAN * LANES
    shape = (2 * half, begin.shape[1])
    place = lax.broadcasted_iota(jnp.int32, (2 * half, 1), 0)
    inner = lax.rem(place, half)
    whose = jnp.where(place < half, core, 1 - core)
    key = chunk * 2 * half + inner // LANES * (2 * LANES) + whose * LANES + lax.rem(inner, LANES)
    key = jnp.broadcast_to(key, shape)
    return (key >= begin) & (key <= query)


def query_rows(begin_ref, blocks, core):
    lane = lax.broadcasted_iota(jnp.int32, (1, LANES), 1)
    begin, query = [], []
    for block in blocks:
        begin += [begin_ref[block]] * GROUP
        query += [(2 * block + core) * LANES + lane] * GROUP
    return jnp.concatenate(begin, 1), jnp.concatenate(query, 1)


def chunk_keys(own_ref, other_ref, chunk):
    chips = pl.ds(chunk * SPAN, SPAN)
    return jnp.concatenate([flat(own_ref[chips]), flat(other_ref[chips])], 0)


def turn_keys(own_ref, other_ref, turned_ref):
    def one(chunk, carry):
        turned_ref[chunk] = chunk_keys(own_ref, other_ref, chunk).astype(F32).T.astype(BF16)
        return carry

    lax.fori_loop(0, turned_ref.shape[0], one, 0)


def by_head(field):
    return [field[:, h * LANES : (h + 1) * LANES].T for h in range(GROUP)]


def chunks_of(blocks):
    last = blocks[0] if len(blocks) == 1 else jnp.maximum(*blocks)
    return last // SPAN + 1


class Opening:
    def __init__(self, count, inputs, outputs, scratch):
        self.tokens_ref, *self.projections, self.out_w_ref, self.small_ref, self.table_ref = inputs
        self.heads_ref, self.outs_ref, self.tables_ref, self.params_ref = outputs
        (self.x_ref, self.slab_ref, self.smalls, self.weights, self.own_sem, self.slab_sem, self.pass_sem, self.small_sem,
         self.table_sem, self.out_sem) = scratch
        self.count = count
        self.devices = 2 * count
        self.me = lax.axis_index("fsdp")
        self.chip, self.core = self.me // 2, lax.rem(self.me, 2)
        self.partner = partner_of("fsdp")

    def device(self, offset):
        return {"fsdp": lax.rem(self.me + offset, self.devices)}

    def chip_at(self, offset):
        return lax.rem(self.chip + offset + self.count, self.count)

    def everyone(self):
        return [self.device(offset) for offset in range(1, self.devices)]

    def home(self, layer, origin):
        shard = self.slab_ref.shape[2]
        rows = pl.ds(pl.multiple_of(origin * shard, shard), shard)
        return self.weights.at[rows] if layer == 0 else self.heads_ref.at[layer, rows]

    def across(self, layer, offset, source=None, target=None):
        slot = self.home(layer, self.me) if source is None else source
        target = slot if target is None else target
        there = {"fsdp": self.chip_at(offset) * 2 + self.core}
        return remote(slot, target, self.slab_sem.at[0, offset, layer], self.slab_sem.at[1, offset, layer], there)

    def beside(self, layer, offset, slot, source=None):
        return remote(
            slot if source is None else source, slot,
            self.pass_sem.at[0, offset, layer], self.pass_sem.at[1, offset, layer], self.partner,
        )

    def small_to(self, offset, slot, source=None):
        return remote(
            slot if source is None else source, slot,
            self.small_sem.at[0, offset], self.small_sem.at[1, offset], self.device(offset),
        )

    def table_to(self, offset, slot, source=None):
        there = {"fsdp": self.chip_at(offset) * 2 + self.core}
        return remote(
            slot if source is None else source, slot,
            self.table_sem.at[0, offset], self.table_sem.at[1, offset], there,
        )

    def out_to(self, slot, source):
        return remote(source, slot, self.out_sem.at[0], self.out_sem.at[1], self.partner)

    def divide(self):
        for layer in range(LAYERS):
            query, key, value = [ref[layer].astype(F32) for ref in self.projections]
            for half in range(self.count // 2):
                first = 3 * half * LANES
                t = [query[:, first + i * LANES : first + (i + 1) * LANES] for i in range(3)]
                k, v = [a[:, half * LANES : (half + 1) * LANES] for a in (key, value)]
                low = lanes_of(k) < HD
                even = [t[0], jnp.where(low, t[1], turn(k)), jnp.where(low, v, 0.0)]
                odd = [
                    jnp.where(low, turn(t[1]), turn(t[2])),
                    jnp.where(low, turn(t[2]), k),
                    jnp.where(low, turn(v), 0.0),
                ]
                for place, tiles in enumerate((even, odd)):
                    self.slab_ref[2 * half + place, layer] = jnp.concatenate(tiles, 1).astype(BF16)

    def start(self):
        me, chip = self.me, self.chip
        self.divide()
        self.copies = [
            pltpu.make_async_copy(self.small_ref, self.smalls.at[me], self.own_sem.at[0]),
            pltpu.make_async_copy(self.table_ref, self.tables_ref.at[chip], self.own_sem.at[1]),
            pltpu.make_async_copy(self.out_w_ref, self.outs_ref.at[self.core], self.own_sem.at[2]),
        ] + [
            pltpu.make_async_copy(self.slab_ref.at[chip, layer], self.home(layer, me), self.own_sem.at[3 + layer])
            for layer in range(LAYERS)
        ]
        self.sends = [
            self.small_to(offset, self.smalls.at[me], self.small_ref) for offset in range(1, self.devices)
        ]
        for offset in range(1, self.count):
            self.sends.append(self.table_to(offset, self.tables_ref.at[chip], self.table_ref))
        for layer in range(LAYERS):
            for offset in range(1, self.count):
                slab = self.slab_ref.at[self.chip_at(offset), layer]
                self.sends.append(self.across(layer, offset, slab, self.home(layer, me)))
            self.sends.append(self.beside(layer, 0, self.home(layer, me), self.slab_ref.at[chip, layer]))
        self.sends.append(self.out_to(self.outs_ref.at[self.core], self.out_w_ref))
        for copy in self.copies + self.sends:
            copy.start()

    def parameters(self):
        for offset in range(1, self.devices):
            origin = lax.rem(self.me - offset + self.devices, self.devices)
            self.small_to(offset, self.smalls.at[origin]).wait_recv()
        self.copies[0].wait()
        shard = self.slab_ref.shape[2]
        width = self.params_ref.shape[1]
        shape = (LANES, width)
        feature = lax.broadcasted_iota(jnp.int32, shape, 1)
        spread = (lax.rem(feature, shard) == lax.broadcasted_iota(jnp.int32, shape, 0)).astype(F32).astype(BF16)
        owner = lax.broadcasted_iota(jnp.int32, self.params_ref.shape, 1) // shard
        self.params_ref[...] = jnp.zeros_like(self.params_ref)

        def one(device, carry):
            rows = dot(self.smalls[device], spread)
            self.params_ref[...] += jnp.where(owner == device, rows, 0.0)
            return carry

        lax.fori_loop(0, self.devices, one, 0)
        normed = normal(self.tokens_ref[...].astype(F32))[1]
        self.x_ref[...] = (normed * gain_row(self.params_ref, 0, 0)).astype(BF16)

    def forward(self, layer):
        for offset in range(1, self.count):
            slot = self.home(layer, self.chip_at(-offset) * 2 + self.core)
            self.across(layer, offset, slot).wait_recv()
            self.beside(layer, offset, slot).start()

    def arrived(self, layer):
        self.copies[3 + layer].wait()
        for offset in range(self.count):
            slot = self.home(layer, self.chip_at(-offset) * 2 + 1 - self.core)
            self.beside(layer, offset, slot).wait_recv()

    def rest(self):
        for offset in range(1, self.count):
            self.table_to(offset, self.tables_ref.at[self.chip_at(-offset)]).wait_recv()
        for copy in self.copies[1:3]:
            copy.wait()
        other = self.outs_ref.at[1 - self.core]
        self.out_to(other, other).wait_recv()

    def drain(self):
        for send in self.sends:
            send.wait_send()
        for layer in range(LAYERS):
            for offset in range(1, self.count):
                slot = self.home(layer, self.chip_at(-offset) * 2 + self.core)
                self.beside(layer, offset, slot).wait_send()


def attend_kernel(count, layer, traffic, *refs):
    if layer == 0:
        inputs, outputs, scratch = split(refs, 9, 13)
        begin_ref, routes_ref = inputs[7:]
        hidden_ref, table_ref, params_ref = inputs[0], outputs[11], outputs[12]
    else:
        inputs, outputs, scratch = split(refs, 8, 9)
        x_ref, w_ref, w_out_ref, table_ref, begin_ref, hidden_ref, params_ref, routes_ref = inputs
    q_ref, own_ref, other_ref, all_ref, att_ref, lse_ref, middle_ref, x_out_ref, share_ref = outputs[:9]
    buf, weights, wide_w, turned_ref, score_ref, partial, land = scratch[:7]
    sems, pair_sems, scatter_sem, out_sem, load_sem, more = split(scratch[7:], 3, 2, 2, 1, 1)
    ring = Ring(count, traffic)
    partner = partner_of("fsdp")
    core = lax.rem(lax.axis_index("fsdp"), 2)

    def pass_on(block):
        return remote(
            own_ref.at[block], other_ref.at[block], pair_sems[0].at[block], pair_sems[1].at[block], partner
        )

    def project(blocks):
        rows = dot(stack(buf, blocks), weights[...])
        tables = [angles(table_ref[b]) for b in blocks]
        cosine = jnp.concatenate([t[0] for t in tables], 0)
        sine = jnp.concatenate([t[1] for t in tables], 0)
        heads, pair = project_rows(rows, cosine, sine)
        for index, head in enumerate(heads):
            for block, part in cut(head, blocks):
                q_ref[block, index] = part
        for block, part in cut(pair, blocks):
            own_ref[block] = part
            pass_on(block).start()

    if layer == 0:
        more = scratch[7 + 9 :]
        opening = Opening(count, inputs[:7], outputs[9:], [*more[:3], weights, *more[3:]])
        ring.meet(True, opening.everyone())
        opening.start()
        opening.parameters()
        loads = load_out_weights(outputs[10], layer, wide_w, load_sem[0], False)
        keep = [
            pltpu.make_async_copy(buf, all_ref, out_sem[0].at[0]),
            pltpu.make_async_copy(weights, outputs[9].at[0], out_sem[0].at[1]),
        ]

        def first(s):
            @pl.when(s == ring.steps - 1)
            def _():
                opening.rest()
                for load in loads:
                    load.start()
                opening.arrived(0)
                keep[1].start()
                project((ring.chip,))

            @pl.when(s == ring.steps)
            def _():
                project(ring.pair(ring.steps - 1))

        def second(s):
            @pl.when(s == ring.steps - 2)
            def _():
                opening.forward(0)

            @pl.when(s == ring.steps - 1)
            def _():
                def one(index, carry):
                    project(ring.pair(index))
                    return carry

                lax.fori_loop(1, ring.steps - 1, one, 0)

        drain = ring.gather(opening.x_ref, buf, sems, None, first, second)
        keep[0].start()
        project((ring.at(ring.steps),))
        for load in loads:
            load.wait()
    else:
        loads = [pltpu.make_async_copy(w_ref.at[layer], weights, load_sem[0].at[2])]
        loads[0].start()
        loads += load_out_weights(w_out_ref, layer, wide_w, load_sem[0])
        ring.meet(True)

        def first(s):
            @pl.when(s == 1)
            def _():
                for load in loads:
                    load.wait()
                project((ring.chip,))

        drain = ring.gather(x_ref, buf, sems, None, first, lambda s: project(ring.pair(s)))
        keep = [pltpu.make_async_copy(buf, all_ref, out_sem[0].at[0])]
        keep[0].start()
        project((ring.at(ring.steps),))
    for block in range(count):
        pass_on(block).wait()
    ring.depart()
    turn_keys(own_ref, other_ref, turned_ref)

    def attend(blocks):
        width = len(blocks) * GROUP * LANES
        q = jnp.concatenate([q_ref[b].reshape(GROUP * LANES, LANES) for b in blocks], 0)
        begin, query = query_rows(begin_ref, blocks, core)
        end = chunks_of(blocks)

        def score(chunk, top):
            keys = chunk_keys(own_ref, other_ref, chunk)
            scores = jnp.where(allowed_keys(begin, query, chunk, core), dot(keys, q, NT), MASKED)
            score_ref[chunk, :, :width] = scores
            return jnp.maximum(top, jnp.max(scores, 0, keepdims=True))

        top = lax.fori_loop(0, end, score, jnp.full((1, width), MASKED, F32))

        def add(chunk, state):
            total, acc = state
            weights = jnp.exp(score_ref[chunk, :, :width] - top)
            total = total + jnp.sum(weights, 0, keepdims=True)
            return total, acc + dot(turned_ref[chunk], weights.astype(BF16))

        total, acc = lax.fori_loop(
            0, end, add, (jnp.zeros((1, width), F32), jnp.zeros((LANES, width), F32))
        )
        lse = top + jnp.log(total)
        att = acc / total
        rows = []
        for place, block in enumerate(blocks):
            here = slice(place * GROUP * LANES, (place + 1) * GROUP * LANES)
            lse_ref[block] = lse[:, here]
            heads = by_head(att[:, here])
            low = lanes_of(heads[0]) < HD
            rows.append(
                jnp.concatenate(
                    [jnp.where(low, turn(heads[0]), heads[1]), jnp.where(low, turn(heads[2]), 0.0)], 1
                ).astype(BF16)
            )
            att_ref[block] = rows[-1]
        out = dot(jnp.concatenate(rows, 0) if len(rows) > 1 else rows[0], wide_w[...]).astype(BF16)
        for block, part in cut(out, blocks):
            partial[block] = part

    attend((ring.at(ring.steps),))

    def between():
        if layer == 0:
            for later in range(1, LAYERS):
                opening.forward(later)
        attend(ring.pair(ring.steps - 1))

    def work(s, place):
        if place == 2:

            @pl.when(s < ring.steps - 2)
            def _():
                attend(ring.pair(ring.steps - 2 - s))

            @pl.when(s == ring.steps - 2)
            def _():
                attend((ring.chip,))

    added, finish = ring.scatter(partial, land, scatter_sem, work, between)
    ring.settle()
    middle = hidden_ref[...].astype(F32) + added
    middle_ref[...] = middle
    x = (normal(middle)[1] * gain_row(params_ref, 1, layer)).astype(BF16)
    x_out_ref[...] = x
    experts = share_ref.shape[0]
    logits = dot(params_ref[router_rows(experts, layer), :].astype(BF16), x, NT)
    expert = lax.broadcasted_iota(jnp.int32, logits.shape, 0)
    named = expert < 0
    for choice in range(routes_ref.shape[1]):
        named = named | (expert == routes_ref[layer, choice : choice + 1, :])
    scores = jnp.where(named, logits, MASKED)
    weighted = jnp.where(named, jnp.exp(scores - jnp.max(scores, 0, keepdims=True)), 0.0)
    share_ref[...] = weighted / jnp.sum(weighted, 0, keepdims=True)
    drain()
    finish()
    for copy in keep:
        copy.wait()
    if layer == 0:
        for later in range(1, LAYERS):
            opening.arrived(later)
        opening.drain()


def gather_attend_scatter(count, layer, inputs, rows, width, columns, extra=()):
    block = cells((count, rows, LANES), BF16)
    everyone = pltpu.VMEM((count, rows, width), BF16)
    wide = 2 * LANES
    more_outputs, more_scratch = extra if extra else ([], [])
    return ring_call(
        functools.partial(attend_kernel, count, layer),
        ("attend", layer),
        inputs,
        [
            (cells((count, GROUP, rows, LANES), BF16), SOON),
            (block, SOON),
            (block, SOON),
            (cells((count, rows, width), BF16), ANYWHERE),
            (cells((count, rows, wide), BF16), OUT),
            (cells((count, 1, GROUP * rows), F32), OUT),
            (cells((rows, width), F32), OUT),
            (cells((rows, width), BF16), OUT),
            (cells((2 * count, rows), F32), OUT),
        ]
        + more_outputs,
        [
            everyone,
            pltpu.VMEM((width, columns), BF16),
            pltpu.VMEM((wide, width), BF16),
            pltpu.VMEM((count // SPAN, LANES, SPAN * wide), BF16),
            pltpu.VMEM((count // SPAN, SPAN * wide, 2 * GROUP * LANES), F32),
            everyone,
            land_scratch(count, rows, width),
        ]
        + gather_sems(count)
        + dmas((count,), (count,))
        + scatter_sems(count)
        + dmas((2,), (3,))
        + more_scratch,
        60,
    )


def open_attend_scatter(count, columns, tokens, projections, out_w, small, table, begin, routes):
    rows, width = tokens.shape
    layers, shard, _ = out_w.shape
    devices = 2 * count
    outputs = [
        (cells((layers, width, columns), BF16), ANYWHERE),
        (cells((2,) + out_w.shape, BF16), ANYWHERE),
        (cells((count,) + table.shape, F32), OUT),
        (cells((small.shape[0], width), F32), OUT),
    ]
    scratch = [
        pltpu.VMEM((rows, width), BF16),
        pltpu.VMEM((count, layers, shard, columns), BF16),
        pltpu.VMEM((devices,) + small.shape, BF16),
    ] + dmas(
        (3 + layers,), (2, count, layers), (2, count, layers), (2, devices), (2, count), (2,)
    )
    inputs = [(a, EARLY) for a in (tokens, *projections)] + [(a, ANYWHERE) for a in (out_w, small, table)]
    inputs += [(begin, EARLY), (routes, LATE)]
    return gather_attend_scatter(count, 0, inputs, rows, width, columns, (outputs, scratch))


def load_experts(refs, layer, bufs, sem):
    copies = [
        pltpu.make_async_copy(ref.at[layer, 0], buf.at[0], sem.at[place])
        for place, (ref, buf) in enumerate(zip(refs, bufs))
    ]
    for copy in copies:
        copy.start()
    return copies


def lend_experts(refs, layer, bufs, sems):
    copies = [
        remote(ref.at[layer, 0], buf.at[1], sems[0].at[place], sems[1].at[place], partner_of("fsdp"))
        for place, (ref, buf) in enumerate(zip(refs, bufs))
    ]
    for copy in copies:
        copy.start()
    return copies


def expert_of(e):
    me = lax.axis_index("fsdp")
    return me if e == 0 else me + 1 - 2 * lax.rem(me, 2)


def share_of(share_ref, e, blocks):
    columns = [as_column(share_ref[b, pl.ds(expert_of(e), 1), :]) for b in blocks]
    return jnp.concatenate(columns, 0) if len(columns) > 1 else columns[0]


def after_loads(loads, run):
    def first(s):
        @pl.when(s == 1)
        def _():
            for load in loads:
                load.wait()

        run(s)

    return first


def mix_kernel(count, layer, traffic, *refs):
    last = layer + 1 == LAYERS
    inputs, outputs, scratch = split(refs, 7 + last, 5 + last)
    x_ref, side_ref, middle_ref, params_ref = inputs[:4]
    mixed_ref, hidden_ref, next_ref, all_ref, share_ref = outputs[:5]
    buf, partial, land, acc, gates, ups, downs = scratch[:7]
    sems, scatter_sem, load_sem, lend_sem, out_sem = split(scratch[7:], 5, 2, 1, 2)
    ring = Ring(count, traffic)
    loads = load_experts(inputs[4:7], layer, (gates, ups, downs), load_sem[0])
    ring.meet(True)
    lent = lend_experts(inputs[4:7], layer, (gates, ups, downs), lend_sem)

    def ready():
        for copy in lent:
            copy.wait()

    def compute(e, blocks):
        x = stack(buf, blocks)
        act_gate, act_up = dot(x, gates[e]), dot(x, ups[e])
        hidden = jax.nn.silu(act_gate) * act_up * share_of(share_ref, e, blocks)
        part = dot(hidden.astype(BF16), downs[e])
        if e == 0:
            acc[: x.shape[0]] = part
        else:
            total = (acc[: x.shape[0]] + part).astype(BF16)
            for block, rows in cut(total, blocks):
                partial[block] = rows

    first, second = ring.meanwhile(compute, ready)
    drain = ring.gather(x_ref, buf, sems, (side_ref, share_ref), after_loads(loads, first), second)
    keep = pltpu.make_async_copy(buf, all_ref, out_sem[0].at[0])
    keep.start()
    for e in range(2):
        compute(e, (ring.at(ring.steps),))
    mixed, finish = ring.scatter(partial, land, scatter_sem)
    ring.settle()
    mixed_ref[...] = mixed
    hidden = middle_ref[...] + mixed
    hidden_ref[...] = hidden
    if layer + 1 < LAYERS:
        next_ref[...] = (normal(hidden)[1] * gain_row(params_ref, 0, layer + 1)).astype(BF16)
    else:
        next_ref[...] = hidden.astype(BF16)
        balance = jnp.sum(mixed * inputs[7][...].astype(F32), -1, keepdims=True)
        outputs[5][...] = jnp.broadcast_to(as_line(balance), outputs[5].shape)
    drain()
    finish()
    keep.wait()


def expert_scratch(weights):
    return [pltpu.VMEM((2,) + w.shape[2:], BF16) for w in weights]


def land_scratch(count, rows, width):
    return pltpu.VMEM((2, 2, count // 2, rows // 2, width), BF16)


def gather_mix_scatter(count, layer, x, share, middle, params, weights, cotangent):
    rows, width = x.shape
    everyone = pltpu.VMEM((count, rows, width), BF16)
    own = cells((rows, width), F32)
    return ring_call(
        functools.partial(mix_kernel, count, layer),
        ("mix", layer),
        [(x, ANYWHERE), (share, ANYWHERE), (middle, LATE), (params, LATE)]
        + [(w, ANYWHERE) for w in weights]
        + ([(cotangent, LATE)] if layer + 1 == LAYERS else []),
        [
            (own, OUT),
            (own, OUT),
            (cells((rows, width), BF16), OUT),
            (cells((count, rows, width), BF16), ANYWHERE),
            (cells((count,) + share.shape, F32), OUT),
        ]
        + ([(cells((8, rows), F32), OUT)] if layer + 1 == LAYERS else []),
        [everyone, everyone, land_scratch(count, rows, width), pltpu.VMEM((2 * rows, width), F32)]
        + expert_scratch(weights)
        + gather_sems(count, True)
        + scatter_sems(count)
        + dmas((3,), (3,), (3,), (1,)),
        60,
    )


def mix_back_kernel(count, layer, traffic, *refs):
    inputs, outputs, scratch = split(refs, 10, 5)
    d_ref, side_ref, m_ref, share_ref, params_ref, grad_ref, middle_ref = inputs[:7]
    mid_ref, branch_ref, gain_ref, sum_ref, g_router_ref = outputs
    buf, partial, land, acc, gates, ups, downs = scratch[:7]
    tokens, acts, hiddens, balance_ref, totals, got = scratch[7:13]
    sems, scatter_sem, load_sem, pair_sem, lend_sem, out_sem = split(scratch[13:], 5, 2, 1, 2, 2)
    ring = Ring(count, traffic)
    loads = load_experts(inputs[7:], layer, (gates, ups, downs), load_sem[0])
    loads.append(pltpu.make_async_copy(m_ref, tokens, load_sem[0].at[3]))
    loads[-1].start()
    ring.meet(True)
    lent = lend_experts(inputs[7:], layer, (gates, ups, downs), lend_sem)

    def ready():
        for copy in lent:
            copy.wait()

    ff = gates.shape[2]
    width = buf.shape[2]
    g_router_ref[...] = jnp.zeros_like(g_router_ref)
    routers = 2 * LAYERS + layer * 2 * count

    def compute(e, blocks):
        d, x = stack(buf, blocks), stack(tokens, blocks)
        share = share_of(share_ref, e, blocks)
        balance = [as_column(balance_ref[b, 0:1, :]) for b in blocks]
        balance = jnp.concatenate(balance, 0) if len(balance) > 1 else balance[0]
        act_gate, act_up = dot(x, gates[e]), dot(x, ups[e])
        sig = jax.nn.sigmoid(act_gate)
        swish = act_gate * sig
        hidden = swish * act_up
        raw = dot(d, downs[e], NT)
        d_logit = share * (jnp.sum(hidden * raw, -1, keepdims=True) - balance)
        d_hidden = raw * share
        d_gate = (d_hidden * act_up * sig * (1.0 + act_gate * (1.0 - sig))).astype(BF16)
        d_up = (d_hidden * swish).astype(BF16)
        weighted = (hidden * share).astype(BF16)
        part = dot(d_gate, gates[e], NT) + dot(d_up, ups[e], NT)
        part = part + d_logit * params_ref[pl.ds(routers + expert_of(e), 1), :]
        g_router_ref[e : e + 1, :] += jnp.sum(d_logit * x.astype(F32), 0, keepdims=True)
        for place, block in enumerate(blocks):
            here = slice(place * LANES, (place + 1) * LANES)
            acts[e, block, :, :ff] = d_gate[here]
            acts[e, block, :, ff:] = d_up[here]
            hiddens[e, block] = weighted[here]
        if e == 0:
            acc[: x.shape[0]] = part
        else:
            total = (acc[: x.shape[0]] + part).astype(BF16)
            for block, rows in cut(total, blocks):
                partial[block] = rows

    first, second = ring.meanwhile(compute, ready)
    drain = ring.gather(d_ref, buf, sems, (side_ref, balance_ref), after_loads(loads, first), second)
    for e in range(2):
        compute(e, (ring.at(ring.steps),))

    partner = partner_of("fsdp")
    strip = 2 * LANES
    strips = width // (2 * strip)
    groups = width // ff

    def regions(half):
        regions = [(group * width + half * (width // 2), width // 2) for group in range(2)]
        return regions + [(2 * width + group * ff + half * (ff // 2), ff // 2) for group in range(groups)]

    def swap(half):
        return [
            remote(
                totals.at[1, pl.ds(first, length)], got.at[pl.ds(first, length)],
                pair_sem[0].at[half, index], pair_sem[1].at[half, index], partner,
            )
            for index, (first, length) in enumerate(regions(half))
        ]

    def store(half):
        return [
            pltpu.make_async_copy(
                totals.at[0, pl.ds(first, length)], sum_ref.at[pl.ds(first, length)], out_sem[0].at[half, index]
            )
            for index, (first, length) in enumerate(regions(half))
        ]

    def work(s, place):
        e = 1 - s // 2
        half = lax.rem(s, 2)

        def put(first, value):
            rows = pl.ds(pl.multiple_of(first, strip), strip)

            @pl.when(s < 2)
            def _():
                totals[1, rows] = value.astype(BF16)

            @pl.when(s >= 2)
            def _():
                totals[0, rows] = (value + got[rows].astype(F32)).astype(BF16)

        if place == 0:
            for h in range(2):

                @pl.when(s == 2 + h)
                def _():
                    for copy in swap(h):
                        copy.wait_recv()

        if place < strips:
            first = (half * strips + place) * strip
            columns = pl.ds(pl.multiple_of(first, strip), strip)
            value = dot(flat(tokens[:, :, columns]), flat(acts[e]), TN)
            for group in range(2):
                put(group * width + first, value[:, group * ff : (group + 1) * ff])
        if place == 3:
            columns = pl.ds(pl.multiple_of(half * strip, strip), strip)
            value = dot(flat(hiddens[e, :, :, columns]), flat(buf[...]), TN)
            for group in range(groups):
                put(2 * width + group * ff + half * strip, value[:, group * ff : (group + 1) * ff])
            for h in range(2):

                @pl.when(s == h)
                def _():
                    for copy in swap(h):
                        copy.start()

                @pl.when(s == 2 + h)
                def _():
                    for copy in store(h):
                        copy.start()

    d_x, finish = ring.scatter(partial, land, scatter_sem, work)
    ring.settle()
    d_values, gain_ref[...] = normal_back(d_x, middle_ref[...], gain_row(params_ref, 1, layer))
    grad = grad_ref[...].astype(F32) + d_values
    mid_ref[...] = grad
    branch_ref[...] = grad.astype(BF16)
    drain()
    finish()
    for half in range(2):
        for copy in swap(half):
            copy.wait_send()
        for copy in store(half):
            copy.wait()


def gather_mix_back_scatter(count, layer, d, side, m_all, share, params, grad, middle, weights, rides):
    rows, width = d.shape
    ff = weights[0].shape[3]
    everyone = pltpu.VMEM((count, rows, width), BF16)
    groups = width // ff
    own = cells((rows, width), F32)
    return ring_call(
        functools.partial(mix_back_kernel, count, layer),
        ("mix_back", layer),
        [(d, ANYWHERE), (side, ANYWHERE), (m_all, ANYWHERE), (share, EARLY), (params, EARLY), (grad, LATE), (middle, LATE)]
        + [(w, ANYWHERE) for w in weights],
        [
            (own, OUT),
            (cells((rows, width), BF16), OUT),
            (cells((1, width), F32), OUT),
            (cells((3 * width, ff), BF16), ANYWHERE),
            (cells((2, width), F32), OUT),
        ],
        [everyone, everyone, land_scratch(count, rows, width), pltpu.VMEM((2 * rows, width), F32)]
        + expert_scratch(weights)
        + [
            everyone,
            pltpu.VMEM((2, count, rows, 2 * ff), BF16),
            pltpu.VMEM((2, count, rows, ff), BF16),
            pltpu.VMEM((count,) + side.shape, F32),
            pltpu.VMEM((2, 3 * width, ff), BF16),
            pltpu.VMEM((3 * width, ff), BF16),
        ]
        + gather_sems(count, True)
        + scatter_sems(count)
        + dmas((4,), (2, 2 + groups), (2, 2 + groups), (3,), (3,), (2, 2 + groups)),
        60,
        rides,
    )


def load_out_weights(w_ref, layer, wide_ref, sem, start=True):
    shard = w_ref.shape[2]
    copies = [
        pltpu.make_async_copy(w_ref.at[core, layer], wide_ref.at[pl.ds(core * shard, shard)], sem.at[core])
        for core in range(2)
    ]
    for copy in copies if start else []:
        copy.start()
    used = 2 * shard
    wide_ref[used:] = jnp.zeros((wide_ref.shape[0] - used, wide_ref.shape[1]), BF16)
    return copies


def attend_back_kernel(count, layer, traffic, *refs):
    inputs, outputs, scratch = split(refs, 17, 5)
    d_ref, w_out_ref, w_ref, x_ref, att_ref, q_ref, own_ref, other_ref, begin_ref, lse_ref, table_ref = inputs[:11]
    params_ref, mid_ref, hidden_ref, mixed_ref, router_ref, gain_two_ref = inputs[11:]
    g_out_ref, grad_ref, d_mix_ref, side_ref, g_ref = outputs
    buf, wide_w, g_acc, out_mail, out_got, turned_ref, d_own, d_other, mail, got, dq_ref = scratch[:11]
    partial, land, rows_ref, tokens, weights, last_ref = scratch[11:17]
    sems, scatter_sem, pair_sem, load_sem = split(scratch[17:], 3, 2, 2)
    ring = Ring(count, traffic)
    shard = g_out_ref.shape[0]
    loads = load_out_weights(w_out_ref, layer, wide_w, load_sem[0])
    later = [
        pltpu.make_async_copy(x_ref, tokens, load_sem[0].at[2]),
        pltpu.make_async_copy(w_ref.at[layer], weights, load_sem[0].at[3]),
    ]
    for load in later:
        load.start()
    ring.meet(True)
    core = lax.rem(lax.axis_index("fsdp"), 2)
    width = GROUP * LANES

    def spread(wide):
        front, back = wide[:, :LANES], wide[:, LANES:]
        low = lanes_of(front) < HD
        return [jnp.where(low, 0.0, part) for part in (turn(front), front, turn(back))]

    def compute(block):
        d = buf[block]
        wide = dot(d, wide_w[...], NT).astype(BF16)
        g_acc[...] += dot(att_ref[block], d, TN)
        slopes, deltas = [], []
        for piece, a in zip(spread(wide.astype(F32)), spread(att_ref[block].astype(F32))):
            slopes.append(piece)
            deltas.append(jnp.sum((piece * a).T, 0, keepdims=True))
        datt = jnp.concatenate(slopes, 0).astype(BF16)
        delta = jnp.concatenate(deltas, 1)
        q = q_ref[block].reshape(width, LANES)
        both = jnp.concatenate([q, datt], 0)
        begin, query = query_rows(begin_ref, (block,), core)
        lse = lse_ref[block]

        def one(chunk, acc):
            keys = chunk_keys(own_ref, other_ref, chunk)
            scores = jnp.where(allowed_keys(begin, query, chunk, core), dot(keys, q, NT), MASKED)
            weight = jnp.exp(scores - lse)
            slope = (weight * (dot(keys, datt, NT) - delta)).astype(BF16)
            d_keys = dot(jnp.concatenate([slope, weight.astype(BF16)], 1), both)
            half = SPAN * LANES
            chips = pl.ds(chunk * SPAN, SPAN)
            d_own[chips] += d_keys[:half].reshape(SPAN, LANES, LANES)
            d_other[chips] += d_keys[half:].reshape(SPAN, LANES, LANES)
            return acc + dot(turned_ref[chunk], slope)

        acc = lax.fori_loop(0, chunks_of((block,)), one, jnp.zeros((LANES, width), F32)) * (HD**-0.5)
        heads = by_head(acc)
        low = lanes_of(heads[0]) < HD
        cosine, sine = angles(table_ref[block])
        front = spin(jnp.where(low, heads[0], turn(heads[1])), cosine, -sine)
        back = spin(jnp.where(low, heads[2], 0.0), cosine, -sine)
        dq_ref[block] = jnp.concatenate([front, back], 1).astype(BF16)

    def first(s):
        @pl.when(s == 1)
        def _():
            for load in loads:
                load.wait()
            turn_keys(own_ref, other_ref, turned_ref)
            g_acc[...] = jnp.zeros_like(g_acc)
            d_own[...] = jnp.zeros_like(d_own)
            d_other[...] = jnp.zeros_like(d_other)

        compute(ring.at(1 - s))

    def second(s):
        compute(ring.at(s))

    drain = ring.gather(d_ref, buf, sems, None, first, second)
    compute(ring.at(ring.steps))
    partner = partner_of("fsdp")
    mail[...] = d_other[...].astype(BF16)
    out_mail[...] = g_acc[pl.ds(pl.multiple_of((1 - core) * shard, 8), shard), :].astype(BF16)
    swaps = [
        remote(mail, got, pair_sem[0].at[0], pair_sem[1].at[0], partner),
        remote(out_mail, out_got, pair_sem[0].at[1], pair_sem[1].at[1], partner),
    ]
    for swap in swaps:
        swap.start()
    for load in later:
        load.wait()
    drain()
    swaps[0].wait()

    def join(blocks):
        rows = []
        for b in blocks:
            pair = d_own[b] + got[b].astype(F32)
            cosine, sine = angles(table_ref[b])
            keys = spin(pair, cosine, -sine)
            low = lanes_of(pair) < HD
            middle = jnp.where(low, dq_ref[b, :, LANES:].astype(F32), turn(keys))
            last = jnp.where(low, turn(pair), 0.0)
            rows.append(
                jnp.concatenate([dq_ref[b, :, :LANES], middle.astype(BF16), last.astype(BF16)], 1)
            )
            rows_ref[b] = rows[-1]
        total = dot(jnp.concatenate(rows, 0), weights[...], NT).astype(BF16)
        for block, part in cut(total, blocks):
            partial[block] = part

    join((ring.at(ring.steps), ring.chip))
    strip = g_ref.shape[0] // ring.steps
    tile = 2 * LANES

    def between():
        def one(index, carry):
            join(ring.pair(ring.steps - 1 - index))
            return carry

        lax.fori_loop(0, ring.steps - 1, one, 0)

    def work(s, place):
        if place == 0:
            rows = pl.ds(pl.multiple_of(s * strip, LANES), strip)
            value = dot(flat(tokens[:, :, rows]), flat(rows_ref[...]), TN)
            g_ref[rows, :tile] = value[:, :tile].astype(BF16)
            last_ref[rows] = value[:, tile:]

    d_x, finish = ring.scatter(partial, land, scatter_sem, work, between)
    swaps[1].wait()
    own = g_acc[pl.ds(pl.multiple_of(core * shard, 8), shard), :]
    g_out_ref[...] = (own + out_got[...].astype(F32)).astype(BF16)
    ring.settle()
    d_values, gain_one = normal_back(d_x, hidden_ref[...].astype(F32), gain_row(params_ref, 0, layer))
    grad = mid_ref[...] + d_values
    grad_ref[...] = grad
    d_mix = grad.astype(BF16)
    d_mix_ref[...] = d_mix
    balance = jnp.sum(mixed_ref[...] * d_mix.astype(F32), -1, keepdims=True)
    side_ref[...] = jnp.broadcast_to(as_line(balance), side_ref.shape)
    routers = router_ref[...]
    lines = [
        jnp.where(core == 0, routers[0:1], routers[1:2]),
        jnp.where(core == 0, routers[1:2], routers[0:1]),
        gain_one,
        gain_two_ref[...],
    ]
    features = g_ref.shape[0]
    tall = jnp.concatenate(
        [jnp.zeros((HD, features), F32)] + lines + [jnp.zeros((HD - len(lines), features), F32)], 0
    )
    g_ref[:, tile:] = (last_ref[...] + tall.T).astype(BF16)
    finish()


def gather_attend_back_scatter(
    count, layer, d, w_out, w, x_all, att, q, own, other, begin, lse, tables, late, rides=()
):
    _, rows, width = x_all.shape
    shard = w_out.shape[2]
    columns = w.shape[2]
    everyone = pltpu.VMEM((count, rows, width), BF16)
    early = [att, q, own, other, begin, lse, tables]
    pairs = cells((count, rows, LANES), BF16)
    return ring_call(
        functools.partial(attend_back_kernel, count, layer),
        ("attend_back", layer),
        [(a, ANYWHERE) for a in (d, w_out, w, x_all)] + [(a, EARLY) for a in early] + [(a, LATE) for a in late],
        [
            (cells((shard, width), BF16), OUT),
            (cells((rows, width), F32), OUT),
            (cells((rows, width), BF16), OUT),
            (cells((8, rows), F32), OUT),
            (cells(w.shape[1:], BF16), OUT),
        ],
        [
            everyone,
            pltpu.VMEM((2 * LANES, width), BF16),
            pltpu.VMEM((2 * LANES, width), F32),
            pltpu.VMEM((shard, width), BF16),
            pltpu.VMEM((shard, width), BF16),
            pltpu.VMEM((count // SPAN, LANES, SPAN * 2 * LANES), BF16),
            pltpu.VMEM(pairs.shape, F32),
            pltpu.VMEM(pairs.shape, F32),
            pltpu.VMEM(pairs.shape, BF16),
            pltpu.VMEM(pairs.shape, BF16),
            pltpu.VMEM((count, rows, 2 * LANES), BF16),
            everyone,
            land_scratch(count, rows, width),
            pltpu.VMEM((count, rows, columns), BF16),
            everyone,
            pltpu.VMEM(w.shape[1:], BF16),
            pltpu.VMEM((width, LANES), F32),
        ]
        + gather_sems(count)
        + scatter_sems(count)
        + dmas((2,), (2,), (4,)),
        60,
        rides,
    )


def finish_kernel(count, replicas, *refs):
    inputs, outputs, scratch = split(refs, 3, 2)
    g_ref, early_ref, early_peer_ref = inputs
    mine, peer = outputs
    early, land, total = scratch[:3]
    pair_send, pair_recv, part_send, part_recv, rep_send, rep_recv = scratch[3:]
    me = lax.axis_index("fsdp")
    chip, core = me // 2, lax.rem(me, 2)
    partner = partner_of("fsdp")

    def chip_at(offset):
        return lax.rem(chip + offset + count, count)

    def device(offset):
        return {"fsdp": chip_at(offset) * 2 + core}

    across = [partner_of("rep")] if replicas == 2 else []
    meet([device(offset) for offset in range(1, count)] + [partner] + across)
    swaps = [remote(g_ref.at[:, 1 - core], land.at[0], pair_send.at[0], pair_recv.at[0], partner)]
    swaps[0].start()
    for block in range(count):
        for half in range(2):
            both = early_ref[block, half].astype(F32)
            if replicas == 2:
                both = both + early_peer_ref[block, half].astype(F32)
            early[half, block] = both.astype(BF16)
    if replicas != 2:
        peer[...] = jnp.zeros_like(peer)
    swaps.append(remote(early.at[1 - core], land.at[1], pair_send.at[1], pair_recv.at[1], partner))
    swaps[1].start()
    for swap in swaps:
        swap.wait()
    for block in range(count):
        total[block, 0] = (g_ref[block, core].astype(F32) + land[0, block].astype(F32)).astype(BF16)
        total[block, 1] = (early[core, block].astype(F32) + land[1, block].astype(F32)).astype(BF16)
    sends = [
        remote(
            total.at[chip_at(offset)], mine.at[chip],
            part_send.at[offset], part_recv.at[offset], device(offset),
        )
        for offset in range(1, count)
    ]
    for send in sends:
        send.start()
    mine[chip] = total[chip]

    def to_peer(offset):
        slot = chip_at(-offset)
        return remote(mine.at[slot, 0], peer.at[slot], rep_send.at[offset], rep_recv.at[offset], across[0])

    for offset in range(count):
        if offset > 0:
            slot = mine.at[chip_at(-offset)]
            remote(slot, slot, part_send.at[offset], part_recv.at[offset], partner).wait_recv()
        if replicas == 2:
            to_peer(offset).start()
    if replicas == 2:
        for offset in range(count):
            to_peer(offset).wait()

    for send in sends:
        send.wait_send()


def finish_heads(count, replicas, g, early, early_peer):
    _, _, rows, columns = g.shape
    part = (count, LAYERS, rows, columns)
    dma = pltpu.SemaphoreType.DMA
    return pl.pallas_call(
        functools.partial(finish_kernel, count, replicas),
        out_shape=(cells(part, BF16), cells((count, rows, columns), BF16)),
        in_specs=[HERE] * 3,
        out_specs=[HERE] * 2,
        scratch_shapes=[
            pltpu.VMEM((2, count, rows, columns), BF16),
            pltpu.VMEM((2, count, rows, columns), BF16),
            pltpu.VMEM(part, BF16),
            dma((2,)), dma((2,)), dma((count,)), dma((count,)), dma((count,)), dma((count,)),
        ],
        compiler_params=pltpu.CompilerParams(
            collective_id=identity(("finish",)), has_side_effects=True, vmem_limit_bytes=60 << 20
        ),
        cost_estimate=FREE,
        name="finish_heads",
    )(g, early, early_peer)


def close_kernel(layers, count, *refs):
    n_experts = 0 if len(refs) == 2 * layers + 13 else 10 * layers
    inputs, heads_in, rows_in, experts_in, outputs = split(refs, 2 * layers, 2, 2, n_experts)
    mine, peer = heads_in
    out_ref, q_out, k_out, v_out, router_out, gain_one_out, gain_two_out = outputs[:7]
    for source, target in zip(rows_in, outputs[7:9]):
        target[...] = source[...]

    @pl.when(pl.program_id(0) == 0)
    def _():
        for layer in range(layers):
            own, got = inputs[2 * layer : 2 * layer + 2]
            out_ref[layer] = own[...].astype(F32) + got[...].astype(F32)

            def tiles(block):
                value = mine[block, layer].astype(F32)
                if layer == 0:
                    value = value + peer[block].astype(F32)
                return [value[:, i * LANES : (i + 1) * LANES] for i in range(3)]

            shard = mine.shape[2]
            gains = jnp.zeros((shard, LANES), F32)
            routers = jnp.zeros((shard, LANES), F32)
            for half in range(count // 2):
                a, b = tiles(2 * half), tiles(2 * half + 1)
                low = lanes_of(a[0]) < HD
                for chip, tile in ((2 * half, a[2]), (2 * half + 1, b[2])):
                    gains = gains + tile
                    moved = pltpu.roll(tile, (2 * chip - HD) % LANES, 1)
                    lane = lanes_of(moved)
                    routers = jnp.where((lane >= 2 * chip) & (lane < 2 * chip + 2), moved, routers)
                q_out[layer, :, 3 * half * LANES : 3 * (half + 1) * LANES] = jnp.concatenate(
                    [a[0], jnp.where(low, a[1], turn(b[0])), jnp.where(low, turn(b[0]), turn(b[1]))], 1
                )
                here = slice(half * LANES, (half + 1) * LANES)
                k_out[layer, :, here] = jnp.where(low, turn(a[1]), b[1])
                v_out[layer, :, here] = jnp.where(low, a[2], turn(b[2]))

            router_out[layer] = routers[:, : 2 * count]
            tall = jnp.concatenate([gains, jnp.zeros((LANES - shard, LANES), F32)], 0).T
            gain_one_out[layer : layer + 1, :] = tall[HD + 2 : HD + 3, :shard]
            gain_two_out[layer : layer + 1, :] = tall[HD + 3 : HD + 4, :shard]

    if experts_in:
        expert_refs = outputs[9:]
        for layer in range(layers):
            pairs = experts_in[layer * 10 : (layer + 1) * 10]
            sums = [pairs[i][...].astype(F32) + pairs[i + 5][...].astype(F32) for i in range(5)]
            expert_refs[0][layer, 0] = sums[0]
            expert_refs[1][layer, 0] = sums[1]
            expert_refs[2][layer, 0] = jnp.concatenate(sums[2:], 1)


def close(count, outs, mine, peer, rows_out, experts):
    layers = len(outs)
    shard, width = outs[0][0].shape
    steps = 4

    def whole(shape):
        return pl.BlockSpec(shape, lambda i: (0,) * len(shape))

    arrays = [array for pair in outs for array in pair] + [mine, peer]
    specs = [whole(a.shape) for a in arrays]
    shapes = [
        (layers, shard, width),
        (layers, shard, count * GROUP * HD),
        (layers, shard, count * HD),
        (layers, shard, count * HD),
        (layers, shard, 2 * count),
        (layers, shard),
        (layers, shard),
    ]
    out_specs = [whole(shape) for shape in shapes]
    shapes = [cells(shape, F32) for shape in shapes] + [cells(a.shape, a.dtype) for a in rows_out]
    parts = [
        pl.BlockSpec((a.shape[0] // (steps if experts else 1), a.shape[1]), lambda i: (i, 0)) for a in rows_out
    ]
    arrays += rows_out
    specs += parts
    out_specs += parts
    if experts:
        rows, ff = experts[0][0].shape
        tall, short = width // steps, ff // steps
        groups = (rows - 2 * width) // ff

        def at(first, length):
            return pl.BlockSpec((length, ff), lambda i: (first // length + i, 0))

        parts = [at(0, tall), at(width, tall)] + [at(2 * width + g * ff, short) for g in range(groups)]
        arrays += [array for pair in experts for array in pair for _ in parts]
        specs += parts * (2 * layers)
        shapes += [cells((layers, 1, width, ff), F32)] * 2 + [cells((layers, 1, ff, width), F32)]
        tile = pl.BlockSpec((layers, 1, tall, ff), lambda i: (0, 0, i, 0))
        out_specs += [tile, tile, pl.BlockSpec((layers, 1, short, width), lambda i: (0, 0, i, 0))]
    return pl.pallas_call(
        functools.partial(close_kernel, layers, count),
        grid=(steps if experts else 1,),
        out_shape=tuple(shapes),
        in_specs=specs,
        out_specs=out_specs,
        compiler_params=pltpu.CompilerParams(vmem_limit_bytes=60 << 20),
        cost_estimate=FREE,
        name="close",
    )(*arrays)


def on_device(
    tokens,
    cotangent,
    positions,
    segments,
    routes,
    attn_gain,
    w_query,
    w_key,
    w_value,
    w_out,
    ffn_gain,
    router,
    w_gate,
    w_up,
    w_down,
):
    rows, width = tokens.shape
    devices = lax.axis_size("fsdp")
    replicas = lax.axis_size("rep")
    count = devices // 2
    me = lax.axis_index("fsdp")
    chip, core = me // 2, lax.rem(me, 2)
    shard = w_query.shape[1]
    experts = devices
    columns = 3 * LANES
    used = (GROUP + 2) * HD

    small = jnp.concatenate(
        [attn_gain, ffn_gain, router.transpose(0, 2, 1).reshape(LAYERS * experts, shard)], 0
    )
    small = jnp.pad(small, ((0, 48 - small.shape[0]), (0, LANES - shard)))
    rate = jnp.exp(-jnp.log(10000.0) * jnp.arange(HD // 2, dtype=F32) / (HD // 2))
    angle = rate[:, None] * positions.astype(F32)[None, :]
    table = jnp.concatenate([jnp.cos(angle), jnp.sin(angle)], 0)
    experts_w = [w_gate, w_up, w_down]

    flat_segments = segments.reshape(1, -1)
    kinds = jnp.arange(8, dtype=jnp.int32)[:, None]
    starts = jnp.sum((flat_segments < kinds).astype(jnp.int32), 1, keepdims=True)
    begin = jnp.sum(jnp.where(flat_segments == kinds, starts, 0), 0).reshape(count, 2, rows)
    begin = lax.dynamic_index_in_dim(begin, core, 1, True)

    chosen = routes.transpose(0, 2, 1)
    hidden = tokens
    saved = []
    for layer in range(LAYERS):
        if layer == 0:
            *results, heads_w, outs_w, tables, params = open_attend_scatter(
                count, columns, tokens, [w_query, w_key, w_value], w_out, small, table, begin, chosen
            )
        else:
            results = gather_attend_scatter(
                count,
                layer,
                [
                    (x_attn, ANYWHERE), (heads_w, ANYWHERE), (outs_w, ANYWHERE), (tables, EARLY),
                    (begin, EARLY), (hidden, LATE), (params, LATE), (chosen, LATE),
                ],
                rows,
                width,
                columns,
            )
        query, kv, kv_other, x_all, att, lse, middle, x_moe, share = results
        mixed, after, x_attn, m_all, share_all, *side = gather_mix_scatter(
            count, layer, x_moe, share, middle, params, experts_w, cotangent
        )
        saved.append((hidden, x_all, query, kv, kv_other, att, lse, middle, mixed, m_all, share_all))
        hidden = after
    activations = x_attn

    def across(array):
        return lax.ppermute(array, "rep", [(0, 1), (1, 0)]) if replicas == 2 else array

    grad = d_mix = cotangent
    (side,) = side
    expert_sums = [None] * LAYERS
    out_sums = [None] * LAYERS
    for layer in reversed(range(LAYERS)):
        hidden, x_all, query, kv, kv_other, att, lse, middle, mixed, m_all, share_all = saved[layer]
        rides = [out_sums[layer + 1], early] if layer + 1 < LAYERS and replicas == 2 else []
        grad_mid, d_branch, gain_two, expert_sum, g_router, *rode = gather_mix_back_scatter(
            count, layer, d_mix, side, m_all, share_all, params, grad, middle, experts_w, rides
        )
        if layer + 1 < LAYERS:
            d_branch, expert_sums[layer + 1] = lax.optimization_barrier(
                (d_branch, expert_sums[layer + 1])
            )
        expert_sums[layer] = (expert_sum, across(expert_sum))
        out_sum, grad, d_mix, side, heads = gather_attend_back_scatter(
            count, layer, d_branch, outs_w, heads_w, x_all, att, query, kv, kv_other, begin, lse, tables,
            [params, grad_mid, hidden, saved[max(layer - 1, 0)][8], g_router, gain_two],
        )
        out_sums[layer] = out_sum
        heads = heads.reshape(count, 2, shard, columns)
        early = heads if layer > 0 else early
    arrived, peer = finish_heads(count, replicas, heads, early, rode[1] if rode else early)
    if replicas == 2:
        outs = list(zip(out_sums, [across(out_sums[0]), rode[0]]))
        *results, g_gate, g_up, g_down = close(
            count, outs, arrived, peer, [activations, grad], expert_sums
        )
    else:
        outs = [(own, jnp.zeros_like(own)) for own in out_sums]
        results = close(count, outs, arrived, peer, [activations, grad], [])
        sums = (*results[:7], jnp.stack([own for own, _ in expert_sums]))
        *summed, flat_sums = [lax.psum(array.astype(BF16), "rep").astype(F32) for array in sums]
        results = summed + list(results[7:])
        ff = w_gate.shape[3]
        g_gate, g_up = flat_sums[:, None, :width], flat_sums[:, None, width : 2 * width]
        g_down = flat_sums[:, 2 * width :].reshape(LAYERS, width // ff, ff, ff)
        g_down = g_down.transpose(0, 2, 1, 3).reshape(LAYERS, 1, ff, width)
    g_out, g_query, g_key, g_value, g_router, gain_one, gain_two, activations, grad = results
    return (
        activations,
        grad,
        gain_one,
        g_query,
        g_key,
        g_value,
        g_out,
        gain_two,
        g_router,
        g_gate,
        g_up,
        g_down,
    )


def solution(mesh):
    placed = (
        P(("rep", "fsdp"), None),
        P(("rep", "fsdp"), None),
        P(("rep", "fsdp")),
        P("rep", None),
        P(None, ("rep", "fsdp"), None),
        P(None, "fsdp"),
        P(None, "fsdp", None),
        P(None, "fsdp", None),
        P(None, "fsdp", None),
        P(None, "fsdp", None),
        P(None, "fsdp"),
        P(None, "fsdp", None),
        P(None, "fsdp", None, None),
        P(None, "fsdp", None, None),
        P(None, "fsdp", None, None),
    )
    return jax.shard_map(
        on_device,
        mesh=mesh,
        in_specs=placed,
        out_specs=(
            P(("rep", "fsdp"), None),
            P(("rep", "fsdp"), None),
            P(None, "fsdp"),
            P(None, "fsdp", None),
            P(None, "fsdp", None),
            P(None, "fsdp", None),
            P(None, "fsdp", None),
            P(None, "fsdp"),
            P(None, "fsdp", None),
            P(None, "fsdp", None, None),
            P(None, "fsdp", None, None),
            P(None, "fsdp", None, None),
        ),
        check_vma=False,
    )
```

```python
import functools

import jax
import jax.numpy as jnp
from jax import lax
from jax.experimental import pallas as pl
from jax.experimental.pallas import tpu as pltpu
from jax.sharding import PartitionSpec as P

HEADS = 24
KV_HEADS = 8
HD = 64
LAYERS = 2
GROUP = HEADS // KV_HEADS
LANES = 128
SPAN = 2
EPS = 1e-06
MASKED = -1e30
MESH = pl.DeviceIdType.MESH
F32 = jnp.float32
BF16 = jnp.bfloat16


def ring_place(chip, count):
    return lax.select(lax.rem(chip, 2) == 0, chip // 2, count - 1 - chip // 2)


def ring_chip(place, count):
    return lax.select(place < count // 2, 2 * place, 2 * (count - 1 - place) + 1)


def ring_setup(count):
    me = lax.axis_index("fsdp")
    chip, core = me // 2, lax.rem(me, 2)
    place = ring_place(chip, count)

    def at(offset):
        return ring_chip(lax.rem(place + offset + 2 * count, count), count)

    near = [{"fsdp": at(1) * 2 + core}, {"fsdp": at(-1) * 2 + core}]
    return chip, at, near


def partner_of(axis):
    if axis == "rep":
        return {"rep": 1 - lax.axis_index("rep")}
    me = lax.axis_index("fsdp")
    return {"fsdp": me + 1 - 2 * lax.rem(me, 2)}


def meet(others):
    barrier = pltpu.get_barrier_semaphore()
    for other in others:
        pl.semaphore_signal(barrier, inc=1, device_id=other, device_id_type=MESH)
    pl.semaphore_wait(barrier, len(others))


def remote(src, dst, send_sem, recv_sem, device):
    return pltpu.make_async_remote_copy(
        src_ref=src,
        dst_ref=dst,
        send_sem=send_sem,
        recv_sem=recv_sem,
        device_id=device,
        device_id_type=MESH,
    )


def ring_hops(count):
    half = count // 2
    return {(0, 0): half, (1, 1): half, (0, 1): half - 1, (1, 0): half - 1}


IDENTITIES = {}


def identity(key):
    return IDENTITIES.setdefault(key, len(IDENTITIES))


class Ring:
    def __init__(self, count, traffic):
        self.count = count
        self.riders, self.early, self.late, self.soon = traffic
        self.steps = count // 2
        self.chip, self.at, self.near = ring_setup(count)

    def meet(self, partner=False, everyone=None, across=False):
        others = everyone or self.near + ([partner_of("fsdp")] if partner else [])
        meet(others + ([partner_of("rep")] if self.riders or across else []))
        for rider in self.riders:
            rider.start()
        for copy in self.early:
            copy.wait()

    def settle(self):
        for copy in self.late:
            copy.wait()

    def depart(self):
        for copy in self.soon:
            copy.start()

    def gather(self, x_ref, buf, sems, side=None, first=None, second=None):
        own_sem, send_sem, recv_sem = sems[:3]
        half_rows = x_ref.shape[0] // 2
        steps = self.steps
        own = [pltpu.make_async_copy(x_ref, buf.at[self.chip], own_sem.at[0])]
        if side is not None:
            side_ref, side_buf = side
            side_send, side_recv = sems[3:]
            own.append(pltpu.make_async_copy(side_ref, side_buf.at[self.chip], own_sem.at[1]))
        for copy in own:
            copy.start()

        def piece(key, step, block, source=None):
            direction, part = key
            rows = pl.ds(part * half_rows, half_rows)
            target = buf.at[block, rows]
            return remote(
                target if source is None else source.at[rows],
                target,
                send_sem.at[direction, part, step],
                recv_sem.at[direction, part, step],
                self.near[direction],
            )

        def side_piece(direction, step, block, source=None):
            target = side_buf.at[block]
            return remote(
                target if source is None else source,
                target,
                side_send.at[direction, step],
                side_recv.at[direction, step],
                self.near[direction],
            )

        def toward(key, places):
            return self.at(-places if key[0] == 0 else places)

        early, late = [(0, 0), (1, 1)], [(0, 1), (1, 0)]
        if side is not None:
            for direction in range(2):
                side_piece(direction, 0, self.chip, side_ref).start()
        for key in early + late:
            piece(key, 0, self.chip, x_ref).start()

        def take(keys, s, last):
            for key in keys:
                block = toward(key, s)
                piece(key, s - 1, block).wait_recv()

                @pl.when(s < last)
                def _():
                    piece(key, s, block).start()

        def take_side(s):
            if side is not None:
                for direction in range(2):

                    @pl.when(s <= steps - direction)
                    def _():
                        block = toward((direction, 0), s)
                        side_piece(direction, s - 1, block).wait_recv()

                        @pl.when(s < steps - direction)
                        def _():
                            side_piece(direction, s, block).start()

        def step(s, carry):
            take_side(s)
            take(early, s, steps)
            first(s)
            take(late, s, steps - 1)
            second(s)
            return carry

        for copy in own:
            copy.wait()
        lax.fori_loop(1, steps, step, 0)
        first(steps)
        take_side(steps)
        take(early, steps, steps)

        def drain():
            for s in range(steps):
                for key in early + (late if s < steps - 1 else []):
                    piece(key, s, toward(key, s)).wait_send()
                if side is not None:
                    for direction in range(2):
                        if s < steps - direction:
                            side_piece(direction, s, toward((direction, 0), s)).wait_send()

        return drain

    def pair(self, s):
        return self.at(s), self.at(-s)

    def meanwhile(self, compute, ready):
        def first(s):
            @pl.when(s == 1)
            def _():
                compute(0, (self.chip,))

            @pl.when(s > 1)
            def _():
                compute(1, self.pair(s - 1))

        def second(s):
            @pl.when(s == 1)
            def _():
                ready()
                compute(1, (self.chip,))

            compute(0, self.pair(s))

        return first, second

    def scatter(self, partial, land, sems, work=None, between=None):
        send_sem, recv_sem = sems
        half_rows = partial.shape[1] // 2
        steps = self.steps
        hops = ring_hops(self.count)

        def ahead(key, s):
            places = hops[key] - s
            return self.at(places if key[0] == 0 else -places)

        def piece(key, s, source):
            direction, part = key
            return remote(
                source,
                land.at[direction, part, s],
                send_sem.at[direction, part, s],
                recv_sem.at[direction, part, s],
                self.near[direction],
            )

        def rows_of(key):
            return pl.ds(key[1] * half_rows, half_rows)

        for place, key in enumerate(hops):
            if place == 2 and between is not None:
                between()
            piece(key, 0, partial.at[ahead(key, 0), rows_of(key)]).start()

        def step(s, carry):
            for place, key in enumerate(hops):
                if work is not None:
                    work(s - 1, place)

                @pl.when(s < hops[key])
                def _():
                    slot = land.at[key[0], key[1], s - 1]
                    piece(key, s - 1, slot).wait_recv()
                    mine = partial[ahead(key, s), rows_of(key)]
                    slot[...] = (slot[...].astype(F32) + mine.astype(F32)).astype(BF16)
                    piece(key, s, slot).start()

            return carry

        lax.fori_loop(1, steps + 1, step, 0)
        for key in hops:
            slot = land.at[key[0], key[1], hops[key] - 1]
            piece(key, hops[key] - 1, slot).wait_recv()
        halves = []
        for part in range(2):
            rows = pl.ds(part * half_rows, half_rows)
            total = partial[self.chip, rows].astype(F32)
            for direction in range(2):
                total = total + land[direction, part, hops[direction, part] - 1].astype(F32)
            halves.append(total)
        summed = jnp.concatenate(halves, 0)

        def drain():
            for key in hops:
                for s in range(hops[key]):
                    piece(key, s, land.at[key[0], key[1], s]).wait_send()

        return summed, drain


def dmas(*shapes):
    return [pltpu.SemaphoreType.DMA(shape) for shape in shapes]


def gather_sems(count, sided=False):
    steps = count // 2
    shapes = [(2,), (2, 2, steps), (2, 2, steps)]
    return dmas(*(shapes + ([(2, steps), (2, steps)] if sided else [])))


def scatter_sems(count):
    return dmas((2, 2, count // 2), (2, 2, count // 2))


ANYWHERE = pl.BlockSpec(memory_space=pltpu.HBM)
HERE = pl.BlockSpec(memory_space=pltpu.VMEM)
EARLY, LATE = "early", "late"
OUT, SOON = "out", "soon"


FREE = pl.CostEstimate(flops=0, bytes_accessed=0, transcendentals=0)


def ring_call(body, key, inputs, outputs, scratch, megabytes, rides=()):
    n_in, n_out, n_rides = len(inputs), len(outputs), len(rides)
    in_kinds = [kind for _, kind in inputs]
    out_kinds = [kind for _, kind in outputs]
    copied = [a for a, kind in inputs if kind in (EARLY, LATE)]
    returned = [a for a, kind in outputs if kind in (OUT, SOON)]
    moves = len(copied) + len(returned)

    def kernel(*refs):
        ins, ride_in, outs, ride_out, rest = split(refs, n_in, n_rides, n_out, n_rides)
        rest, own, rest_sems = rest[: len(scratch)], rest[len(scratch) : len(scratch) + moves], rest[len(scratch) + moves :]
        move_sem, rest_sems = rest_sems[0], rest_sems[1:]
        riders = []
        if n_rides:
            send_sem, recv_sem = rest_sems
            riders = [
                remote(ride_in[i], ride_out[i], send_sem.at[i], recv_sem.at[i], partner_of("rep"))
                for i in range(n_rides)
            ]
        used = 0
        early, late, leaving, soon = [], [], [], []
        ins, outs = list(ins), list(outs)
        for i, kind in enumerate(in_kinds):
            if kind in (EARLY, LATE):
                copy = pltpu.make_async_copy(ins[i], own[used], move_sem.at[used])
                copy.start()
                (early if kind == EARLY else late).append(copy)
                ins[i] = own[used]
                used += 1
        for i, kind in enumerate(out_kinds):
            if kind in (OUT, SOON):
                copy = pltpu.make_async_copy(own[used], outs[i], move_sem.at[used])
                (leaving if kind == OUT else soon).append(copy)
                outs[i] = own[used]
                used += 1
        body((riders, early, late, soon), *ins, *outs, *rest)
        for copy in leaving:
            copy.start()
        for rider in riders:
            rider.wait()
        for copy in leaving + soon:
            copy.wait()

    def spec(kind):
        return ANYWHERE if isinstance(kind, str) else kind

    return pl.pallas_call(
        kernel,
        out_shape=tuple(shape for shape, _ in outputs) + tuple(cells(a.shape, a.dtype) for a in rides),
        in_specs=[spec(kind) for kind in in_kinds] + [ANYWHERE] * n_rides,
        out_specs=[spec(kind) for kind in out_kinds] + [ANYWHERE] * n_rides,
        scratch_shapes=list(scratch)
        + [pltpu.VMEM(a.shape, a.dtype) for a in copied + returned]
        + dmas((max(moves, 1),))
        + (dmas((n_rides,), (n_rides,)) if n_rides else []),
        compiler_params=pltpu.CompilerParams(
            collective_id=identity(key),
            has_side_effects=True,
            vmem_limit_bytes=megabytes << 20,
        ),
        cost_estimate=FREE,
        name=key[0],
    )(*[array for array, _ in inputs], *rides)


def split(refs, *sizes):
    parts, place = [], 0
    for size in sizes:
        parts.append(refs[place : place + size])
        place += size
    return parts + [refs[place:]]


def cells(shape, dtype):
    return jax.ShapeDtypeStruct(shape, dtype)


def dot(left, right, contract=((1,), (0,))):
    return lax.dot_general(left, right, (contract, ((), ())), preferred_element_type=F32)


NT = ((1,), (1,))
TN = ((0,), (0,))


def lanes_of(field):
    return lax.broadcasted_iota(jnp.int32, field.shape, 1)


def turn(field):
    return pltpu.roll(field, HD, 1)


def spin(field, cosine, sine):
    swapped = jnp.where(
        lax.rem(lanes_of(field), HD) < HD // 2,
        -pltpu.roll(field, LANES - HD // 2, 1),
        pltpu.roll(field, HD // 2, 1),
    )
    return field * cosine + swapped * sine


def project_rows(rows, cosine, sine):
    first = spin(rows[:, :LANES], cosine, sine)
    second = spin(rows[:, LANES : 2 * LANES], cosine, sine)
    third = rows[:, 2 * LANES :]
    low = lanes_of(first) < HD
    heads = []
    for field in (first, turn(first), second):
        rounded = jnp.where(low, field, 0.0).astype(BF16).astype(F32)
        heads.append((rounded * (HD**-0.5)).astype(BF16))
    return heads, jnp.where(low, turn(second), turn(third)).astype(BF16)


def angles(table):
    rows = jnp.concatenate([table, table], 0).T
    early = lax.rem(lanes_of(rows), HD) < HD // 2
    cosine = jnp.where(early, rows, pltpu.roll(rows, HD // 2, 1))
    sine = jnp.where(early, pltpu.roll(rows, LANES - HD // 2, 1), rows)
    return cosine, sine


def normal(values):
    inverse = lax.rsqrt(jnp.mean(values * values, -1, keepdims=True) + EPS)
    return inverse, values * inverse


def normal_back(d_x, values, gain):
    inverse, normed = normal(values)
    d_norm = d_x * gain
    d_values = inverse * (d_norm - normed * jnp.mean(d_norm * normed, -1, keepdims=True))
    return d_values, jnp.sum(d_x * normed, 0, keepdims=True)


def diagonal():
    shape = (LANES, LANES)
    return lax.broadcasted_iota(jnp.int32, shape, 0) == lax.broadcasted_iota(jnp.int32, shape, 1)


def as_column(line):
    return jnp.sum(jnp.where(diagonal(), jnp.broadcast_to(line, (LANES, LANES)), 0.0), 1, keepdims=True)


def as_line(column):
    return jnp.sum(jnp.where(diagonal(), jnp.broadcast_to(column, (LANES, LANES)), 0.0), 0, keepdims=True)


def flat(value):
    return value.reshape(value.shape[0] * value.shape[1], value.shape[2])


def stack(ref, blocks):
    parts = [ref[b] for b in blocks]
    return parts[0] if len(parts) == 1 else jnp.concatenate(parts, 0)


def cut(value, blocks):
    return [(b, value[i * LANES : (i + 1) * LANES]) for i, b in enumerate(blocks)]


def gain_row(params_ref, kind, layer):
    row = kind * LAYERS + layer
    return params_ref[row : row + 1, :]


def router_rows(experts, layer):
    first = 2 * LAYERS + layer * experts
    return slice(first, first + experts)


def allowed_keys(begin, query, chunk, core):
    half = SPAN * LANES
    shape = (2 * half, begin.shape[1])
    place = lax.broadcasted_iota(jnp.int32, (2 * half, 1), 0)
    inner = lax.rem(place, half)
    whose = jnp.where(place < half, core, 1 - core)
    key = chunk * 2 * half + inner // LANES * (2 * LANES) + whose * LANES + lax.rem(inner, LANES)
    key = jnp.broadcast_to(key, shape)
    return (key >= begin) & (key <= query)


def query_rows(begin_ref, blocks, core):
    lane = lax.broadcasted_iota(jnp.int32, (1, LANES), 1)
    begin, query = [], []
    for block in blocks:
        begin += [begin_ref[block]] * GROUP
        query += [(2 * block + core) * LANES + lane] * GROUP
    return jnp.concatenate(begin, 1), jnp.concatenate(query, 1)


def chunk_keys(own_ref, other_ref, chunk):
    chips = pl.ds(chunk * SPAN, SPAN)
    return jnp.concatenate([flat(own_ref[chips]), flat(other_ref[chips])], 0)


def turn_keys(own_ref, other_ref, turned_ref):
    def one(chunk, carry):
        turned_ref[chunk] = chunk_keys(own_ref, other_ref, chunk).astype(F32).T.astype(BF16)
        return carry

    lax.fori_loop(0, turned_ref.shape[0], one, 0)


def by_head(field):
    return [field[:, h * LANES : (h + 1) * LANES].T for h in range(GROUP)]


def chunks_of(blocks):
    last = blocks[0] if len(blocks) == 1 else jnp.maximum(*blocks)
    return last // SPAN + 1


class Opening:
    def __init__(self, count, inputs, outputs, scratch):
        self.tokens_ref, *self.projections, self.out_w_ref, self.small_ref, self.table_ref = inputs
        self.heads_ref, self.outs_ref, self.tables_ref, self.params_ref = outputs
        (self.x_ref, self.slab_ref, self.smalls, self.weights, self.own_sem, self.slab_sem, self.pass_sem, self.small_sem,
         self.table_sem, self.out_sem) = scratch
        self.count = count
        self.devices = 2 * count
        self.me = lax.axis_index("fsdp")
        self.chip, self.core = self.me // 2, lax.rem(self.me, 2)
        self.partner = partner_of("fsdp")

    def device(self, offset):
        return {"fsdp": lax.rem(self.me + offset, self.devices)}

    def chip_at(self, offset):
        return lax.rem(self.chip + offset + self.count, self.count)

    def everyone(self):
        return [self.device(offset) for offset in range(1, self.devices)]

    def home(self, layer, origin):
        shard = self.slab_ref.shape[2]
        rows = pl.ds(pl.multiple_of(origin * shard, shard), shard)
        return self.weights.at[rows] if layer == 0 else self.heads_ref.at[layer, rows]

    def across(self, layer, offset, source=None, target=None):
        slot = self.home(layer, self.me) if source is None else source
        target = slot if target is None else target
        there = {"fsdp": self.chip_at(offset) * 2 + self.core}
        return remote(slot, target, self.slab_sem.at[0, offset, layer], self.slab_sem.at[1, offset, layer], there)

    def beside(self, layer, offset, slot, source=None):
        return remote(
            slot if source is None else source, slot,
            self.pass_sem.at[0, offset, layer], self.pass_sem.at[1, offset, layer], self.partner,
        )

    def small_to(self, offset, slot, source=None):
        return remote(
            slot if source is None else source, slot,
            self.small_sem.at[0, offset], self.small_sem.at[1, offset], self.device(offset),
        )

    def table_to(self, offset, slot, source=None):
        there = {"fsdp": self.chip_at(offset) * 2 + self.core}
        return remote(
            slot if source is None else source, slot,
            self.table_sem.at[0, offset], self.table_sem.at[1, offset], there,
        )

    def out_to(self, slot, source):
        return remote(source, slot, self.out_sem.at[0], self.out_sem.at[1], self.partner)

    def divide(self):
        for layer in range(LAYERS):
            query, key, value = [ref[layer].astype(F32) for ref in self.projections]
            for half in range(self.count // 2):
                first = 3 * half * LANES
                t = [query[:, first + i * LANES : first + (i + 1) * LANES] for i in range(3)]
                k, v = [a[:, half * LANES : (half + 1) * LANES] for a in (key, value)]
                low = lanes_of(k) < HD
                even = [t[0], jnp.where(low, t[1], turn(k)), jnp.where(low, v, 0.0)]
                odd = [
                    jnp.where(low, turn(t[1]), turn(t[2])),
                    jnp.where(low, turn(t[2]), k),
                    jnp.where(low, turn(v), 0.0),
                ]
                for place, tiles in enumerate((even, odd)):
                    self.slab_ref[2 * half + place, layer] = jnp.concatenate(tiles, 1).astype(BF16)

    def start(self):
        me, chip = self.me, self.chip
        self.divide()
        self.copies = [
            pltpu.make_async_copy(self.small_ref, self.smalls.at[me], self.own_sem.at[0]),
            pltpu.make_async_copy(self.table_ref, self.tables_ref.at[chip], self.own_sem.at[1]),
            pltpu.make_async_copy(self.out_w_ref, self.outs_ref.at[self.core], self.own_sem.at[2]),
        ] + [
            pltpu.make_async_copy(self.slab_ref.at[chip, layer], self.home(layer, me), self.own_sem.at[3 + layer])
            for layer in range(LAYERS)
        ]
        self.sends = [
            self.small_to(offset, self.smalls.at[me], self.small_ref) for offset in range(1, self.devices)
        ]
        for offset in range(1, self.count):
            self.sends.append(self.table_to(offset, self.tables_ref.at[chip], self.table_ref))
        for layer in range(LAYERS):
            for offset in range(1, self.count):
                slab = self.slab_ref.at[self.chip_at(offset), layer]
                self.sends.append(self.across(layer, offset, slab, self.home(layer, me)))
            self.sends.append(self.beside(layer, 0, self.home(layer, me), self.slab_ref.at[chip, layer]))
        self.sends.append(self.out_to(self.outs_ref.at[self.core], self.out_w_ref))
        for copy in self.copies + self.sends:
            copy.start()

    def parameters(self):
        for offset in range(1, self.devices):
            origin = lax.rem(self.me - offset + self.devices, self.devices)
            self.small_to(offset, self.smalls.at[origin]).wait_recv()
        self.copies[0].wait()
        shard = self.slab_ref.shape[2]
        width = self.params_ref.shape[1]
        shape = (LANES, width)
        feature = lax.broadcasted_iota(jnp.int32, shape, 1)
        spread = (lax.rem(feature, shard) == lax.broadcasted_iota(jnp.int32, shape, 0)).astype(F32).astype(BF16)
        owner = lax.broadcasted_iota(jnp.int32, self.params_ref.shape, 1) // shard
        self.params_ref[...] = jnp.zeros_like(self.params_ref)

        def one(device, carry):
            rows = dot(self.smalls[device], spread)
            self.params_ref[...] += jnp.where(owner == device, rows, 0.0)
            return carry

        lax.fori_loop(0, self.devices, one, 0)
        normed = normal(self.tokens_ref[...].astype(F32))[1]
        self.x_ref[...] = (normed * gain_row(self.params_ref, 0, 0)).astype(BF16)

    def forward(self, layer):
        for offset in range(1, self.count):
            slot = self.home(layer, self.chip_at(-offset) * 2 + self.core)
            self.across(layer, offset, slot).wait_recv()
            self.beside(layer, offset, slot).start()

    def arrived(self, layer):
        self.copies[3 + layer].wait()
        for offset in range(self.count):
            slot = self.home(layer, self.chip_at(-offset) * 2 + 1 - self.core)
            self.beside(layer, offset, slot).wait_recv()

    def rest(self):
        for offset in range(1, self.count):
            self.table_to(offset, self.tables_ref.at[self.chip_at(-offset)]).wait_recv()
        for copy in self.copies[1:3]:
            copy.wait()
        other = self.outs_ref.at[1 - self.core]
        self.out_to(other, other).wait_recv()

    def drain(self):
        for send in self.sends:
            send.wait_send()
        for layer in range(LAYERS):
            for offset in range(1, self.count):
                slot = self.home(layer, self.chip_at(-offset) * 2 + self.core)
                self.beside(layer, offset, slot).wait_send()


def attend_part(ring, count, layer, inputs, outputs, scratch, midway):
    if layer == 0:
        begin_ref, routes_ref = inputs[7:]
        hidden_ref, table_ref, params_ref = inputs[0], outputs[11], outputs[12]
    else:
        x_ref, w_ref, w_out_ref, table_ref, begin_ref, hidden_ref, params_ref, routes_ref = inputs
    q_ref, own_ref, other_ref, all_ref, att_ref, lse_ref, middle_ref, x_out_ref, share_ref = outputs[:9]
    buf, weights, wide_w, turned_ref, score_ref, partial, land = scratch[:7]
    sems, pair_sems, scatter_sem, out_sem, load_sem, more = split(scratch[7:], 3, 2, 2, 1, 1)[:5] + [scratch[16:]]
    partner = partner_of("fsdp")
    core = lax.rem(lax.axis_index("fsdp"), 2)

    def pass_on(block):
        return remote(
            own_ref.at[block], other_ref.at[block], pair_sems[0].at[block], pair_sems[1].at[block], partner
        )

    def project(blocks):
        rows = dot(stack(buf, blocks), weights[...])
        tables = [angles(table_ref[b]) for b in blocks]
        cosine = jnp.concatenate([t[0] for t in tables], 0)
        sine = jnp.concatenate([t[1] for t in tables], 0)
        heads, pair = project_rows(rows, cosine, sine)
        for index, head in enumerate(heads):
            for block, part in cut(head, blocks):
                q_ref[block, index] = part
        for block, part in cut(pair, blocks):
            own_ref[block] = part
            pass_on(block).start()

    if layer == 0:
        opening = Opening(count, inputs[:7], outputs[9:], [*more[:3], weights, *more[3:]])
        ring.meet(True, opening.everyone())
        opening.start()
        opening.parameters()
        loads = load_out_weights(outputs[10], layer, wide_w, load_sem[0], False)
        keep = [
            pltpu.make_async_copy(buf, all_ref, out_sem[0].at[0]),
            pltpu.make_async_copy(weights, outputs[9].at[0], out_sem[0].at[1]),
        ]

        def first(s):
            @pl.when(s == ring.steps - 1)
            def _():
                opening.rest()
                for load in loads:
                    load.start()
                opening.arrived(0)
                keep[1].start()
                project((ring.chip,))

            @pl.when(s == ring.steps)
            def _():
                project(ring.pair(ring.steps - 1))

        def second(s):
            @pl.when(s == ring.steps - 2)
            def _():
                opening.forward(0)

            @pl.when(s == ring.steps - 1)
            def _():
                def one(index, carry):
                    project(ring.pair(index))
                    return carry

                lax.fori_loop(1, ring.steps - 1, one, 0)

        drain = ring.gather(opening.x_ref, buf, sems, None, first, second)
        keep[0].start()
        project((ring.at(ring.steps),))
        for load in loads:
            load.wait()
    else:
        loads = [pltpu.make_async_copy(w_ref.at[layer], weights, load_sem[0].at[2])]
        loads[0].start()
        loads += load_out_weights(w_out_ref, layer, wide_w, load_sem[0])
        ring.meet(True)

        def first(s):
            @pl.when(s == 1)
            def _():
                for load in loads:
                    load.wait()
                project((ring.chip,))

        drain = ring.gather(x_ref, buf, sems, None, first, lambda s: project(ring.pair(s)))
        keep = [pltpu.make_async_copy(buf, all_ref, out_sem[0].at[0])]
        keep[0].start()
        project((ring.at(ring.steps),))
    for block in range(count):
        pass_on(block).wait()
    ring.depart()
    midway()
    turn_keys(own_ref, other_ref, turned_ref)

    def attend(blocks):
        width = len(blocks) * GROUP * LANES
        q = jnp.concatenate([q_ref[b].reshape(GROUP * LANES, LANES) for b in blocks], 0)
        begin, query = query_rows(begin_ref, blocks, core)
        end = chunks_of(blocks)

        def score(chunk, top):
            keys = chunk_keys(own_ref, other_ref, chunk)
            scores = jnp.where(allowed_keys(begin, query, chunk, core), dot(keys, q, NT), MASKED)
            score_ref[chunk, :, :width] = scores
            return jnp.maximum(top, jnp.max(scores, 0, keepdims=True))

        top = lax.fori_loop(0, end, score, jnp.full((1, width), MASKED, F32))

        def add(chunk, state):
            total, acc = state
            weights = jnp.exp(score_ref[chunk, :, :width] - top)
            total = total + jnp.sum(weights, 0, keepdims=True)
            return total, acc + dot(turned_ref[chunk], weights.astype(BF16))

        total, acc = lax.fori_loop(
            0, end, add, (jnp.zeros((1, width), F32), jnp.zeros((LANES, width), F32))
        )
        lse = top + jnp.log(total)
        att = acc / total
        rows = []
        for place, block in enumerate(blocks):
            here = slice(place * GROUP * LANES, (place + 1) * GROUP * LANES)
            lse_ref[block] = lse[:, here]
            heads = by_head(att[:, here])
            low = lanes_of(heads[0]) < HD
            rows.append(
                jnp.concatenate(
                    [jnp.where(low, turn(heads[0]), heads[1]), jnp.where(low, turn(heads[2]), 0.0)], 1
                ).astype(BF16)
            )
            att_ref[block] = rows[-1]
        out = dot(jnp.concatenate(rows, 0) if len(rows) > 1 else rows[0], wide_w[...]).astype(BF16)
        for block, part in cut(out, blocks):
            partial[block] = part

    attend((ring.at(ring.steps),))

    def between():
        if layer == 0:
            for later in range(1, LAYERS):
                opening.forward(later)
        attend(ring.pair(ring.steps - 1))

    def work(s, place):
        if place == 2:

            @pl.when(s < ring.steps - 2)
            def _():
                attend(ring.pair(ring.steps - 2 - s))

            @pl.when(s == ring.steps - 2)
            def _():
                attend((ring.chip,))

    added, finish = ring.scatter(partial, land, scatter_sem, work, between)
    ring.settle()
    middle = hidden_ref[...].astype(F32) + added
    middle_ref[...] = middle
    x = (normal(middle)[1] * gain_row(params_ref, 1, layer)).astype(BF16)
    x_out_ref[...] = x
    experts = share_ref.shape[0]
    logits = dot(params_ref[router_rows(experts, layer), :].astype(BF16), x, NT)
    expert = lax.broadcasted_iota(jnp.int32, logits.shape, 0)
    named = expert < 0
    for choice in range(routes_ref.shape[1]):
        named = named | (expert == routes_ref[layer, choice : choice + 1, :])
    scores = jnp.where(named, logits, MASKED)
    weighted = jnp.where(named, jnp.exp(scores - jnp.max(scores, 0, keepdims=True)), 0.0)
    share_ref[...] = weighted / jnp.sum(weighted, 0, keepdims=True)

    def end():
        drain()
        finish()
        for copy in keep:
            copy.wait()
        if layer == 0:
            for later in range(1, LAYERS):
                opening.arrived(later)
            opening.drain()

    return end


def attend_shapes(count, rows, width, columns, extra):
    block = cells((count, rows, LANES), BF16)
    everyone = pltpu.VMEM((count, rows, width), BF16)
    wide = 2 * LANES
    outputs = [
        (cells((count, GROUP, rows, LANES), BF16), SOON),
        (block, SOON),
        (block, SOON),
        (cells((count, rows, width), BF16), ANYWHERE),
        (cells((count, rows, wide), BF16), OUT),
        (cells((count, 1, GROUP * rows), F32), OUT),
        (cells((rows, width), F32), OUT),
        (cells((rows, width), BF16), OUT),
        (cells((2 * count, rows), F32), OUT),
    ]
    scratch = [
        everyone,
        pltpu.VMEM((width, columns), BF16),
        pltpu.VMEM((wide, width), BF16),
        pltpu.VMEM((count // SPAN, LANES, SPAN * wide), BF16),
        pltpu.VMEM((count // SPAN, SPAN * wide, 2 * GROUP * LANES), F32),
        everyone,
        land_scratch(count, rows, width),
    ]
    scratch += gather_sems(count) + dmas((count,), (count,)) + scatter_sems(count) + dmas((2,), (3,))
    return outputs + extra[0], scratch + extra[1]


def opening_shapes(count, tokens, columns, out_w, small, table):
    rows, width = tokens.shape
    layers, shard, _ = out_w.shape
    devices = 2 * count
    outputs = [
        (cells((layers, width, columns), BF16), ANYWHERE),
        (cells((2,) + out_w.shape, BF16), ANYWHERE),
        (cells((count,) + table.shape, F32), OUT),
        (cells((small.shape[0], width), F32), OUT),
    ]
    scratch = [
        pltpu.VMEM((rows, width), BF16),
        pltpu.VMEM((count, layers, shard, columns), BF16),
        pltpu.VMEM((devices,) + small.shape, BF16),
    ] + dmas((3 + layers,), (2, count, layers), (2, count, layers), (2, devices), (2, count), (2,))
    return outputs, scratch


def load_experts(refs, layer, bufs, sem):
    copies = [
        pltpu.make_async_copy(ref.at[layer, 0], buf.at[0], sem.at[place])
        for place, (ref, buf) in enumerate(zip(refs, bufs))
    ]
    for copy in copies:
        copy.start()
    return copies


def lend_experts(refs, layer, bufs, sems):
    copies = [
        remote(ref.at[layer, 0], buf.at[1], sems[0].at[place], sems[1].at[place], partner_of("fsdp"))
        for place, (ref, buf) in enumerate(zip(refs, bufs))
    ]
    for copy in copies:
        copy.start()
    return copies


def expert_of(e):
    me = lax.axis_index("fsdp")
    return me if e == 0 else me + 1 - 2 * lax.rem(me, 2)


def share_of(share_ref, e, blocks):
    columns = [as_column(share_ref[b, pl.ds(expert_of(e), 1), :]) for b in blocks]
    return jnp.concatenate(columns, 0) if len(columns) > 1 else columns[0]


def after_loads(loads, run):
    def first(s):
        @pl.when(s == 1)
        def _():
            for load in loads:
                load.wait()

        run(s)

    return first


def mix_part(ring, count, layer, given, cotangent, outputs, scratch, loads, lent):
    x_ref, side_ref, middle_ref, params_ref = given
    mixed_ref, hidden_ref, next_ref, all_ref, share_ref = outputs[:5]
    buf, partial, land, acc, gates, ups, downs = scratch[:7]
    sems, scatter_sem, out_sem = split(scratch[7:], 5, 2)

    def ready():
        for copy in lent:
            copy.wait()

    def compute(e, blocks):
        x = stack(buf, blocks)
        act_gate, act_up = dot(x, gates[e]), dot(x, ups[e])
        hidden = jax.nn.silu(act_gate) * act_up * share_of(share_ref, e, blocks)
        part = dot(hidden.astype(BF16), downs[e])
        if e == 0:
            acc[: x.shape[0]] = part
        else:
            total = (acc[: x.shape[0]] + part).astype(BF16)
            for block, rows in cut(total, blocks):
                partial[block] = rows

    first, second = ring.meanwhile(compute, ready)
    drain = ring.gather(x_ref, buf, sems, (side_ref, share_ref), after_loads(loads, first), second)
    keep = pltpu.make_async_copy(buf, all_ref, out_sem[0].at[0])
    keep.start()
    for e in range(2):
        compute(e, (ring.at(ring.steps),))
    mixed, finish = ring.scatter(partial, land, scatter_sem)
    mixed_ref[...] = mixed
    hidden = middle_ref[...] + mixed
    hidden_ref[...] = hidden
    if layer + 1 < LAYERS:
        next_ref[...] = (normal(hidden)[1] * gain_row(params_ref, 0, layer + 1)).astype(BF16)
    else:
        next_ref[...] = hidden.astype(BF16)
        balance = jnp.sum(mixed * cotangent[0][...].astype(F32), -1, keepdims=True)
        outputs[5][...] = jnp.broadcast_to(as_line(balance), outputs[5].shape)

    def end():
        drain()
        finish()
        keep.wait()

    return end


def expert_scratch(weights):
    return [pltpu.VMEM((2,) + w.shape[2:], BF16) for w in weights]


def land_scratch(count, rows, width):
    return pltpu.VMEM((2, 2, count // 2, rows // 2, width), BF16)


def mix_shapes(count, layer, rows, width, weights):
    everyone = pltpu.VMEM((count, rows, width), BF16)
    own = cells((rows, width), F32)
    outputs = [
        (own, OUT),
        (own, OUT),
        (cells((rows, width), BF16), OUT),
        (cells((count, rows, width), BF16), ANYWHERE),
        (cells((count, 2 * count, rows), F32), OUT),
    ]
    if layer + 1 == LAYERS:
        outputs.append((cells((8, rows), F32), OUT))
    scratch = [everyone, everyone, land_scratch(count, rows, width), pltpu.VMEM((2 * rows, width), F32)]
    scratch += expert_scratch(weights) + gather_sems(count, True) + scatter_sems(count) + dmas((1,))
    return outputs, scratch


def forward_kernel(count, layer, sizes, traffic, *refs):
    last = layer + 1 == LAYERS
    attend_in, weights, cotangent, attend_out, mix_out, scratch = split(
        refs, sizes[0], 3, int(last), sizes[1], sizes[2]
    )
    attend_scratch, mix_scratch, sems = split(scratch, sizes[3], sizes[4])
    bufs = mix_scratch[4:7]
    ring = Ring(count, traffic)
    loads = load_experts(weights, layer, bufs, sems[0])
    lent = []
    attend_end = attend_part(
        ring, count, layer, attend_in, attend_out, attend_scratch,
        lambda: lent.extend(lend_experts(weights, layer, bufs, sems[1:])),
    )
    params_ref = attend_out[12] if layer == 0 else attend_in[6]
    given = (attend_out[7], attend_out[8], attend_out[6], params_ref)
    mix_end = mix_part(ring, count, layer, given, cotangent, mix_out, mix_scratch, loads, lent)
    attend_end()
    mix_end()


def forward(count, layer, inputs, rows, width, columns, weights, cotangent, extra=([], [])):
    last = layer + 1 == LAYERS
    attend_out, attend_scratch = attend_shapes(count, rows, width, columns, extra)
    mix_out, mix_scratch = mix_shapes(count, layer, rows, width, weights)
    sizes = [len(part) for part in (inputs, attend_out, mix_out, attend_scratch, mix_scratch)]
    return ring_call(
        functools.partial(forward_kernel, count, layer, sizes),
        ("forward", layer),
        inputs + [(w, ANYWHERE) for w in weights] + ([(cotangent, LATE)] if last else []),
        attend_out + mix_out,
        attend_scratch + mix_scratch + dmas((3,), (3,), (3,)),
        60,
    )


def mix_back_kernel(count, layer, replicas, traffic, *refs):
    crossing = replicas == 2
    inputs, outputs, scratch = split(refs, 10, 6 + crossing)
    d_ref, side_ref, m_ref, share_ref, params_ref, grad_ref, middle_ref = inputs[:7]
    mid_ref, branch_ref, gain_ref, part_ref, sum_ref, g_router_ref = outputs[:6]
    buf, partial, land, acc, gates, ups, downs = scratch[:7]
    tokens, acts, hiddens, balance_ref, totals, got = scratch[7:13]
    sems, scatter_sem, load_sem, pair_sem, lend_sem, cross_sem, out_sem = split(scratch[13:], 5, 2, 1, 2, 2, 2)
    ring = Ring(count, traffic)
    loads = load_experts(inputs[7:], layer, (gates, ups, downs), load_sem[0])
    loads.append(pltpu.make_async_copy(m_ref, tokens, load_sem[0].at[3]))
    loads[-1].start()
    ring.meet(True, None, crossing)
    lent = lend_experts(inputs[7:], layer, (gates, ups, downs), lend_sem)

    def ready():
        for copy in lent:
            copy.wait()

    ff = gates.shape[2]
    width = buf.shape[2]
    g_router_ref[...] = jnp.zeros_like(g_router_ref)
    routers = 2 * LAYERS + layer * 2 * count

    def compute(e, blocks):
        d, x = stack(buf, blocks), stack(tokens, blocks)
        share = share_of(share_ref, e, blocks)
        balance = [as_column(balance_ref[b, 0:1, :]) for b in blocks]
        balance = jnp.concatenate(balance, 0) if len(balance) > 1 else balance[0]
        act_gate, act_up = dot(x, gates[e]), dot(x, ups[e])
        sig = jax.nn.sigmoid(act_gate)
        swish = act_gate * sig
        hidden = swish * act_up
        raw = dot(d, downs[e], NT)
        d_logit = share * (jnp.sum(hidden * raw, -1, keepdims=True) - balance)
        d_hidden = raw * share
        d_gate = (d_hidden * act_up * sig * (1.0 + act_gate * (1.0 - sig))).astype(BF16)
        d_up = (d_hidden * swish).astype(BF16)
        weighted = (hidden * share).astype(BF16)
        part = dot(d_gate, gates[e], NT) + dot(d_up, ups[e], NT)
        part = part + d_logit * params_ref[pl.ds(routers + expert_of(e), 1), :]
        g_router_ref[e : e + 1, :] += jnp.sum(d_logit * x.astype(F32), 0, keepdims=True)
        for place, block in enumerate(blocks):
            here = slice(place * LANES, (place + 1) * LANES)
            acts[e, block, :, :ff] = d_gate[here]
            acts[e, block, :, ff:] = d_up[here]
            hiddens[e, block] = weighted[here]
        if e == 0:
            acc[: x.shape[0]] = part
        else:
            total = (acc[: x.shape[0]] + part).astype(BF16)
            for block, rows in cut(total, blocks):
                partial[block] = rows

    first, second = ring.meanwhile(compute, ready)
    drain = ring.gather(d_ref, buf, sems, (side_ref, balance_ref), after_loads(loads, first), second)
    for e in range(2):
        compute(e, (ring.at(ring.steps),))

    partner = partner_of("fsdp")
    strip = 2 * LANES
    strips = width // (2 * strip)
    groups = width // ff

    def regions(half):
        regions = [(group * width + half * (width // 2), width // 2) for group in range(2)]
        return regions + [(2 * width + group * ff + half * (ff // 2), ff // 2) for group in range(groups)]

    def swap(half):
        return [
            remote(
                totals.at[1, pl.ds(first, length)], got.at[pl.ds(first, length)],
                pair_sem[0].at[half, index], pair_sem[1].at[half, index], partner,
            )
            for index, (first, length) in enumerate(regions(half))
        ]

    apart = width // 2

    def store(half):
        return [
            pltpu.make_async_copy(
                totals.at[0, pl.ds(first, length)],
                sum_ref.at[pl.ds(first - apart, length)] if first else part_ref,
                out_sem[0].at[half, index],
            )
            for index, (first, length) in enumerate(regions(half))
        ]

    crossings = []
    if crossing:
        crossings.append(
            remote(
                totals.at[0, pl.ds(0, apart)], outputs[6],
                cross_sem[0].at[0], cross_sem[1].at[0], partner_of("rep"),
            )
        )

    def work(s, place):
        e = 1 - s // 2
        half = lax.rem(s, 2)

        def put(first, value):
            rows = pl.ds(pl.multiple_of(first, strip), strip)

            @pl.when(s < 2)
            def _():
                totals[1, rows] = value.astype(BF16)

            @pl.when(s >= 2)
            def _():
                totals[0, rows] = (value + got[rows].astype(F32)).astype(BF16)

        if place == 0:
            for h in range(2):

                @pl.when(s == 2 + h)
                def _():
                    for copy in swap(h):
                        copy.wait_recv()

        if place < strips:
            first = (half * strips + place) * strip
            columns = pl.ds(pl.multiple_of(first, strip), strip)
            value = dot(flat(tokens[:, :, columns]), flat(acts[e]), TN)
            for group in range(2):
                put(group * width + first, value[:, group * ff : (group + 1) * ff])
        if place == 3:
            columns = pl.ds(pl.multiple_of(half * strip, strip), strip)
            value = dot(flat(hiddens[e, :, :, columns]), flat(buf[...]), TN)
            for group in range(groups):
                put(2 * width + group * ff + half * strip, value[:, group * ff : (group + 1) * ff])
            for h in range(2):

                @pl.when(s == h)
                def _():
                    for copy in swap(h):
                        copy.start()

                @pl.when(s == 2 + h)
                def _():
                    for copy in store(h) + (crossings if h == 0 else []):
                        copy.start()

    d_x, finish = ring.scatter(partial, land, scatter_sem, work)
    ring.settle()
    d_values, gain_ref[...] = normal_back(d_x, middle_ref[...], gain_row(params_ref, 1, layer))
    grad = grad_ref[...].astype(F32) + d_values
    mid_ref[...] = grad
    branch_ref[...] = grad.astype(BF16)
    drain()
    finish()
    for copy in crossings:
        copy.wait()
    for half in range(2):
        for copy in swap(half):
            copy.wait_send()
        for copy in store(half):
            copy.wait()


def gather_mix_back_scatter(count, layer, replicas, d, side, m_all, share, params, grad, middle, weights, rides):
    rows, width = d.shape
    ff = weights[0].shape[3]
    everyone = pltpu.VMEM((count, rows, width), BF16)
    groups = width // ff
    own = cells((rows, width), F32)
    return ring_call(
        functools.partial(mix_back_kernel, count, layer, replicas),
        ("mix_back", layer),
        [(d, ANYWHERE), (side, ANYWHERE), (m_all, ANYWHERE), (share, EARLY), (params, EARLY), (grad, LATE), (middle, LATE)]
        + [(w, ANYWHERE) for w in weights],
        [
            (own, OUT),
            (cells((rows, width), BF16), OUT),
            (cells((1, width), F32), OUT),
            (cells((width // 2, ff), BF16), ANYWHERE),
            (cells((3 * width - width // 2, ff), BF16), ANYWHERE),
            (cells((2, width), F32), OUT),
        ]
        + ([(cells((width // 2, ff), BF16), ANYWHERE)] if replicas == 2 else []),
        [everyone, everyone, land_scratch(count, rows, width), pltpu.VMEM((2 * rows, width), F32)]
        + expert_scratch(weights)
        + [
            everyone,
            pltpu.VMEM((2, count, rows, 2 * ff), BF16),
            pltpu.VMEM((2, count, rows, ff), BF16),
            pltpu.VMEM((count,) + side.shape, F32),
            pltpu.VMEM((2, 3 * width, ff), BF16),
            pltpu.VMEM((3 * width, ff), BF16),
        ]
        + gather_sems(count, True)
        + scatter_sems(count)
        + dmas((4,), (2, 2 + groups), (2, 2 + groups), (3,), (3,), (1,), (1,), (2, 2 + groups)),
        60,
        rides,
    )


def load_out_weights(w_ref, layer, wide_ref, sem, start=True):
    shard = w_ref.shape[2]
    copies = [
        pltpu.make_async_copy(w_ref.at[core, layer], wide_ref.at[pl.ds(core * shard, shard)], sem.at[core])
        for core in range(2)
    ]
    for copy in copies if start else []:
        copy.start()
    used = 2 * shard
    wide_ref[used:] = jnp.zeros((wide_ref.shape[0] - used, wide_ref.shape[1]), BF16)
    return copies


def attend_back_kernel(count, layer, traffic, *refs):
    inputs, outputs, scratch = split(refs, 17, 5)
    d_ref, w_out_ref, w_ref, x_ref, att_ref, q_ref, own_ref, other_ref, begin_ref, lse_ref, table_ref = inputs[:11]
    params_ref, mid_ref, hidden_ref, mixed_ref, router_ref, gain_two_ref = inputs[11:]
    g_out_ref, grad_ref, d_mix_ref, side_ref, g_ref = outputs
    buf, wide_w, g_acc, out_mail, out_got, turned_ref, d_own, d_other, mail, got, dq_ref = scratch[:11]
    partial, land, rows_ref, tokens, weights, last_ref = scratch[11:17]
    sems, scatter_sem, pair_sem, load_sem = split(scratch[17:], 3, 2, 2)
    ring = Ring(count, traffic)
    shard = g_out_ref.shape[0]
    loads = load_out_weights(w_out_ref, layer, wide_w, load_sem[0])
    later = [
        pltpu.make_async_copy(x_ref, tokens, load_sem[0].at[2]),
        pltpu.make_async_copy(w_ref.at[layer], weights, load_sem[0].at[3]),
    ]
    for load in later:
        load.start()
    ring.meet(True)
    core = lax.rem(lax.axis_index("fsdp"), 2)
    width = GROUP * LANES

    def spread(wide):
        front, back = wide[:, :LANES], wide[:, LANES:]
        low = lanes_of(front) < HD
        return [jnp.where(low, 0.0, part) for part in (turn(front), front, turn(back))]

    def compute(block):
        d = buf[block]
        wide = dot(d, wide_w[...], NT).astype(BF16)
        g_acc[...] += dot(att_ref[block], d, TN)
        slopes, deltas = [], []
        for piece, a in zip(spread(wide.astype(F32)), spread(att_ref[block].astype(F32))):
            slopes.append(piece)
            deltas.append(jnp.sum((piece * a).T, 0, keepdims=True))
        datt = jnp.concatenate(slopes, 0).astype(BF16)
        delta = jnp.concatenate(deltas, 1)
        q = q_ref[block].reshape(width, LANES)
        both = jnp.concatenate([q, datt], 0)
        begin, query = query_rows(begin_ref, (block,), core)
        lse = lse_ref[block]

        def one(chunk, acc):
            keys = chunk_keys(own_ref, other_ref, chunk)
            scores = jnp.where(allowed_keys(begin, query, chunk, core), dot(keys, q, NT), MASKED)
            weight = jnp.exp(scores - lse)
            slope = (weight * (dot(keys, datt, NT) - delta)).astype(BF16)
            d_keys = dot(jnp.concatenate([slope, weight.astype(BF16)], 1), both)
            half = SPAN * LANES
            chips = pl.ds(chunk * SPAN, SPAN)
            d_own[chips] += d_keys[:half].reshape(SPAN, LANES, LANES)
            d_other[chips] += d_keys[half:].reshape(SPAN, LANES, LANES)
            return acc + dot(turned_ref[chunk], slope)

        acc = lax.fori_loop(0, chunks_of((block,)), one, jnp.zeros((LANES, width), F32)) * (HD**-0.5)
        heads = by_head(acc)
        low = lanes_of(heads[0]) < HD
        cosine, sine = angles(table_ref[block])
        front = spin(jnp.where(low, heads[0], turn(heads[1])), cosine, -sine)
        back = spin(jnp.where(low, heads[2], 0.0), cosine, -sine)
        dq_ref[block] = jnp.concatenate([front, back], 1).astype(BF16)

    def first(s):
        @pl.when(s == 1)
        def _():
            for load in loads:
                load.wait()
            turn_keys(own_ref, other_ref, turned_ref)
            g_acc[...] = jnp.zeros_like(g_acc)
            d_own[...] = jnp.zeros_like(d_own)
            d_other[...] = jnp.zeros_like(d_other)

        compute(ring.at(1 - s))

    def second(s):
        compute(ring.at(s))

    drain = ring.gather(d_ref, buf, sems, None, first, second)
    compute(ring.at(ring.steps))
    partner = partner_of("fsdp")
    mail[...] = d_other[...].astype(BF16)
    out_mail[...] = g_acc[pl.ds(pl.multiple_of((1 - core) * shard, 8), shard), :].astype(BF16)
    swaps = [
        remote(mail, got, pair_sem[0].at[0], pair_sem[1].at[0], partner),
        remote(out_mail, out_got, pair_sem[0].at[1], pair_sem[1].at[1], partner),
    ]
    for swap in swaps:
        swap.start()
    for load in later:
        load.wait()
    drain()
    swaps[0].wait()

    def join(blocks):
        rows = []
        for b in blocks:
            pair = d_own[b] + got[b].astype(F32)
            cosine, sine = angles(table_ref[b])
            keys = spin(pair, cosine, -sine)
            low = lanes_of(pair) < HD
            middle = jnp.where(low, dq_ref[b, :, LANES:].astype(F32), turn(keys))
            last = jnp.where(low, turn(pair), 0.0)
            rows.append(
                jnp.concatenate([dq_ref[b, :, :LANES], middle.astype(BF16), last.astype(BF16)], 1)
            )
            rows_ref[b] = rows[-1]
        total = dot(jnp.concatenate(rows, 0), weights[...], NT).astype(BF16)
        for block, part in cut(total, blocks):
            partial[block] = part

    join((ring.at(ring.steps), ring.chip))
    strip = g_ref.shape[0] // ring.steps
    tile = 2 * LANES

    def between():
        def one(index, carry):
            join(ring.pair(ring.steps - 1 - index))
            return carry

        lax.fori_loop(0, ring.steps - 1, one, 0)

    def work(s, place):
        if place == 0:
            rows = pl.ds(pl.multiple_of(s * strip, LANES), strip)
            value = dot(flat(tokens[:, :, rows]), flat(rows_ref[...]), TN)
            g_ref[rows, :tile] = value[:, :tile].astype(BF16)
            last_ref[rows] = value[:, tile:]

    d_x, finish = ring.scatter(partial, land, scatter_sem, work, between)
    swaps[1].wait()
    own = g_acc[pl.ds(pl.multiple_of(core * shard, 8), shard), :]
    g_out_ref[...] = (own + out_got[...].astype(F32)).astype(BF16)
    ring.settle()
    d_values, gain_one = normal_back(d_x, hidden_ref[...].astype(F32), gain_row(params_ref, 0, layer))
    grad = mid_ref[...] + d_values
    grad_ref[...] = grad
    d_mix = grad.astype(BF16)
    d_mix_ref[...] = d_mix
    balance = jnp.sum(mixed_ref[...] * d_mix.astype(F32), -1, keepdims=True)
    side_ref[...] = jnp.broadcast_to(as_line(balance), side_ref.shape)
    routers = router_ref[...]
    lines = [
        jnp.where(core == 0, routers[0:1], routers[1:2]),
        jnp.where(core == 0, routers[1:2], routers[0:1]),
        gain_one,
        gain_two_ref[...],
    ]
    features = g_ref.shape[0]
    tall = jnp.concatenate(
        [jnp.zeros((HD, features), F32)] + lines + [jnp.zeros((HD - len(lines), features), F32)], 0
    )
    g_ref[:, tile:] = (last_ref[...] + tall.T).astype(BF16)
    finish()


def gather_attend_back_scatter(
    count, layer, d, w_out, w, x_all, att, q, own, other, begin, lse, tables, late, rides=()
):
    _, rows, width = x_all.shape
    shard = w_out.shape[2]
    columns = w.shape[2]
    everyone = pltpu.VMEM((count, rows, width), BF16)
    early = [att, q, own, other, begin, lse, tables]
    pairs = cells((count, rows, LANES), BF16)
    return ring_call(
        functools.partial(attend_back_kernel, count, layer),
        ("attend_back", layer),
        [(a, ANYWHERE) for a in (d, w_out, w, x_all)] + [(a, EARLY) for a in early] + [(a, LATE) for a in late],
        [
            (cells((shard, width), BF16), OUT),
            (cells((rows, width), F32), OUT),
            (cells((rows, width), BF16), OUT),
            (cells((8, rows), F32), OUT),
            (cells(w.shape[1:], BF16), OUT),
        ],
        [
            everyone,
            pltpu.VMEM((2 * LANES, width), BF16),
            pltpu.VMEM((2 * LANES, width), F32),
            pltpu.VMEM((shard, width), BF16),
            pltpu.VMEM((shard, width), BF16),
            pltpu.VMEM((count // SPAN, LANES, SPAN * 2 * LANES), BF16),
            pltpu.VMEM(pairs.shape, F32),
            pltpu.VMEM(pairs.shape, F32),
            pltpu.VMEM(pairs.shape, BF16),
            pltpu.VMEM(pairs.shape, BF16),
            pltpu.VMEM((count, rows, 2 * LANES), BF16),
            everyone,
            land_scratch(count, rows, width),
            pltpu.VMEM((count, rows, columns), BF16),
            everyone,
            pltpu.VMEM(w.shape[1:], BF16),
            pltpu.VMEM((width, LANES), F32),
        ]
        + gather_sems(count)
        + scatter_sems(count)
        + dmas((2,), (2,), (4,)),
        60,
        rides,
    )


def finish_kernel(count, replicas, *refs):
    inputs, outputs, scratch = split(refs, 3, 2)
    mine, peer = outputs
    g_ref, early_ref, early_peer_ref, early, land, total = scratch[:6]
    pair_send, pair_recv, part_send, part_recv, rep_send, rep_recv, load_sem = scratch[6:]
    loads = [
        pltpu.make_async_copy(source, target, load_sem.at[i])
        for i, (source, target) in enumerate(zip(inputs, scratch))
    ]
    for load in loads:
        load.start()
    me = lax.axis_index("fsdp")
    chip, core = me // 2, lax.rem(me, 2)
    partner = partner_of("fsdp")

    def chip_at(offset):
        return lax.rem(chip + offset + count, count)

    def device(offset):
        return {"fsdp": chip_at(offset) * 2 + core}

    across = [partner_of("rep")] if replicas == 2 else []
    meet([device(offset) for offset in range(1, count)] + [partner] + across)
    swaps = [remote(inputs[0].at[:, 1 - core], land.at[0], pair_send.at[0], pair_recv.at[0], partner)]
    swaps[0].start()
    for load in loads:
        load.wait()
    for block in range(count):
        both = early_ref[block, 1 - core].astype(F32)
        if replicas == 2:
            both = both + early_peer_ref[block, 1 - core].astype(F32)
        early[block] = both.astype(BF16)
    swaps.append(remote(early, land.at[1], pair_send.at[1], pair_recv.at[1], partner))
    swaps[1].start()
    if replicas != 2:
        peer[...] = jnp.zeros_like(peer)
    sends = []
    for layer in range(2):
        swaps[layer].wait()
        for block in range(count):
            own = (g_ref, early_ref)[layer][block, core].astype(F32)
            if layer == 1 and replicas == 2:
                own = own + early_peer_ref[block, core].astype(F32)
            total[layer, block] = (own + land[layer, block].astype(F32)).astype(BF16)
        for offset in range(1, count):
            sends.append(
                remote(
                    total.at[layer, chip_at(offset)], mine.at[layer, chip],
                    part_send.at[layer, offset], part_recv.at[layer, offset], device(offset),
                )
            )
            sends[-1].start()
        mine[layer, chip] = total[layer, chip]

    def to_peer(offset):
        slot = chip_at(-offset)
        return remote(mine.at[0, slot], peer.at[slot], rep_send.at[offset], rep_recv.at[offset], across[0])

    for layer in range(2):
        for offset in range(count):
            if offset > 0:
                slot = mine.at[layer, chip_at(-offset)]
                remote(slot, slot, part_send.at[layer, offset], part_recv.at[layer, offset], partner).wait_recv()
            if layer == 0 and replicas == 2:
                to_peer(offset).start()
    if replicas == 2:
        for offset in range(count):
            to_peer(offset).wait()

    for send in sends:
        send.wait_send()


def finish_heads(count, replicas, g, early, early_peer):
    _, _, rows, columns = g.shape
    part = (LAYERS, count, rows, columns)
    dma = pltpu.SemaphoreType.DMA
    return pl.pallas_call(
        functools.partial(finish_kernel, count, replicas),
        out_shape=(cells(part, BF16), cells((count, rows, columns), BF16)),
        in_specs=[ANYWHERE] * 3,
        out_specs=[HERE] * 2,
        scratch_shapes=[
            pltpu.VMEM(g.shape, BF16),
            pltpu.VMEM(g.shape, BF16),
            pltpu.VMEM(g.shape, BF16),
            pltpu.VMEM((count, rows, columns), BF16),
            pltpu.VMEM(part, BF16),
            pltpu.VMEM(part, BF16),
            dma((2,)), dma((2,)), dma((2, count)), dma((2, count)), dma((count,)), dma((count,)), dma((3,)),
        ],
        compiler_params=pltpu.CompilerParams(
            collective_id=identity(("finish",)), has_side_effects=True, vmem_limit_bytes=60 << 20
        ),
        cost_estimate=FREE,
        name="finish_heads",
    )(g, early, early_peer)


def close_kernel(layers, count, *refs):
    n_experts = 0 if len(refs) == 2 * layers + 13 else 12 * layers
    inputs, heads_in, rows_in, experts_in, outputs = split(refs, 2 * layers, 2, 2, n_experts)
    mine, peer = heads_in
    out_ref, q_out, k_out, v_out, router_out, gain_one_out, gain_two_out = outputs[:7]
    for source, target in zip(rows_in, outputs[7:9]):
        target[...] = source[...]

    @pl.when(pl.program_id(0) == 0)
    def _():
        for layer in range(layers):
            own, got = inputs[2 * layer : 2 * layer + 2]
            out_ref[layer] = own[...].astype(F32) + got[...].astype(F32)

            def tiles(block):
                value = mine[layer, block].astype(F32)
                if layer == 0:
                    value = value + peer[block].astype(F32)
                return [value[:, i * LANES : (i + 1) * LANES] for i in range(3)]

            shard = mine.shape[2]
            gains = jnp.zeros((shard, LANES), F32)
            routers = jnp.zeros((shard, LANES), F32)
            for half in range(count // 2):
                a, b = tiles(2 * half), tiles(2 * half + 1)
                low = lanes_of(a[0]) < HD
                for chip, tile in ((2 * half, a[2]), (2 * half + 1, b[2])):
                    gains = gains + tile
                    moved = pltpu.roll(tile, (2 * chip - HD) % LANES, 1)
                    lane = lanes_of(moved)
                    routers = jnp.where((lane >= 2 * chip) & (lane < 2 * chip + 2), moved, routers)
                q_out[layer, :, 3 * half * LANES : 3 * (half + 1) * LANES] = jnp.concatenate(
                    [a[0], jnp.where(low, a[1], turn(b[0])), jnp.where(low, turn(b[0]), turn(b[1]))], 1
                )
                here = slice(half * LANES, (half + 1) * LANES)
                k_out[layer, :, here] = jnp.where(low, turn(a[1]), b[1])
                v_out[layer, :, here] = jnp.where(low, a[2], turn(b[2]))

            router_out[layer] = routers[:, : 2 * count]
            tall = jnp.concatenate([gains, jnp.zeros((LANES - shard, LANES), F32)], 0).T
            gain_one_out[layer : layer + 1, :] = tall[HD + 2 : HD + 3, :shard]
            gain_two_out[layer : layer + 1, :] = tall[HD + 3 : HD + 4, :shard]

    if experts_in:
        expert_refs = outputs[9:]
        for layer in range(layers):
            pairs = experts_in[layer * 12 : (layer + 1) * 12]
            sums = [pairs[i][...].astype(F32) + pairs[i + 6][...].astype(F32) for i in range(6)]
            early = pl.program_id(0) < pl.num_programs(0) // 2
            expert_refs[0][layer, 0] = jnp.where(early, sums[0], sums[1])
            expert_refs[1][layer, 0] = sums[2]
            expert_refs[2][layer, 0] = jnp.concatenate(sums[3:], 1)


def close(count, outs, mine, peer, rows_out, experts):
    layers = len(outs)
    shard, width = outs[0][0].shape
    steps = 4

    def whole(shape):
        return pl.BlockSpec(shape, lambda i: (0,) * len(shape))

    arrays = [array for pair in outs for array in pair] + [mine, peer]
    specs = [whole(a.shape) for a in arrays]
    shapes = [
        (layers, shard, width),
        (layers, shard, count * GROUP * HD),
        (layers, shard, count * HD),
        (layers, shard, count * HD),
        (layers, shard, 2 * count),
        (layers, shard),
        (layers, shard),
    ]
    out_specs = [whole(shape) for shape in shapes]
    shapes = [cells(shape, F32) for shape in shapes] + [cells(a.shape, a.dtype) for a in rows_out]
    parts = [
        pl.BlockSpec((a.shape[0] // (steps if experts else 1), a.shape[1]), lambda i: (i, 0)) for a in rows_out
    ]
    arrays += rows_out
    specs += parts
    out_specs += parts
    if experts:
        (_, _), (rest, _) = experts[0]
        rows, ff = rest.shape
        tall, short = width // steps, ff // steps
        apart = width // 2
        groups = (rows + apart - 2 * width) // ff

        def at(first, length):
            return pl.BlockSpec((length, ff), lambda i: ((first - apart) // length + i, 0))

        parts = [
            pl.BlockSpec((tall, ff), lambda i: (jnp.minimum(i, steps // 2 - 1), 0)),
            pl.BlockSpec((tall, ff), lambda i: (jnp.maximum(i - steps // 2, 0), 0)),
            at(width, tall),
        ] + [at(2 * width + g * ff, short) for g in range(groups)]
        for front, back in experts:
            for own, other in zip(front, back):
                arrays += [own] + [other] * (len(parts) - 1)
        specs += parts * (2 * layers)
        shapes += [cells((layers, 1, width, ff), F32)] * 2 + [cells((layers, 1, ff, width), F32)]
        tile = pl.BlockSpec((layers, 1, tall, ff), lambda i: (0, 0, i, 0))
        out_specs += [tile, tile, pl.BlockSpec((layers, 1, short, width), lambda i: (0, 0, i, 0))]
    return pl.pallas_call(
        functools.partial(close_kernel, layers, count),
        grid=(steps if experts else 1,),
        out_shape=tuple(shapes),
        in_specs=specs,
        out_specs=out_specs,
        compiler_params=pltpu.CompilerParams(vmem_limit_bytes=60 << 20),
        cost_estimate=FREE,
        name="close",
    )(*arrays)


def on_device(
    tokens,
    cotangent,
    positions,
    segments,
    routes,
    attn_gain,
    w_query,
    w_key,
    w_value,
    w_out,
    ffn_gain,
    router,
    w_gate,
    w_up,
    w_down,
):
    rows, width = tokens.shape
    devices = lax.axis_size("fsdp")
    replicas = lax.axis_size("rep")
    count = devices // 2
    me = lax.axis_index("fsdp")
    chip, core = me // 2, lax.rem(me, 2)
    shard = w_query.shape[1]
    experts = devices
    columns = 3 * LANES
    used = (GROUP + 2) * HD

    small = jnp.concatenate(
        [attn_gain, ffn_gain, router.transpose(0, 2, 1).reshape(LAYERS * experts, shard)], 0
    )
    small = jnp.pad(small, ((0, 48 - small.shape[0]), (0, LANES - shard)))
    rate = jnp.exp(-jnp.log(10000.0) * jnp.arange(HD // 2, dtype=F32) / (HD // 2))
    angle = rate[:, None] * positions.astype(F32)[None, :]
    table = jnp.concatenate([jnp.cos(angle), jnp.sin(angle)], 0)
    experts_w = [w_gate, w_up, w_down]

    flat_segments = segments.reshape(1, -1)
    kinds = jnp.arange(8, dtype=jnp.int32)[:, None]
    starts = jnp.sum((flat_segments < kinds).astype(jnp.int32), 1, keepdims=True)
    begin = jnp.sum(jnp.where(flat_segments == kinds, starts, 0), 0).reshape(count, 2, rows)
    begin = lax.dynamic_index_in_dim(begin, core, 1, True)

    chosen = routes.transpose(0, 2, 1)
    hidden = tokens
    saved = []
    for layer in range(LAYERS):
        if layer == 0:
            projections = [w_query, w_key, w_value]
            inputs = [(a, EARLY) for a in (tokens, *projections)]
            inputs += [(a, ANYWHERE) for a in (w_out, small, table)] + [(begin, EARLY), (chosen, LATE)]
            extra = opening_shapes(count, tokens, columns, w_out, small, table)
        else:
            inputs = [(a, ANYWHERE) for a in (x_attn, heads_w, outs_w)] + [(tables, EARLY), (begin, EARLY)]
            inputs += [(hidden, LATE), (params, LATE), (chosen, LATE)]
            extra = [], []
        results = forward(count, layer, inputs, rows, width, columns, experts_w, cotangent, extra)
        query, kv, kv_other, x_all, att, lse, middle, _, _ = results[:9]
        if layer == 0:
            heads_w, outs_w, tables, params = results[9:13]
        mixed, after, x_attn, m_all, share_all, *side = results[9 + len(extra[0]) :]
        saved.append((hidden, x_all, query, kv, kv_other, att, lse, middle, mixed, m_all, share_all))
        hidden = after
    activations = x_attn

    def across(array):
        return lax.ppermute(array, "rep", [(0, 1), (1, 0)]) if replicas == 2 else array

    grad = d_mix = cotangent
    (side,) = side
    expert_sums = [None] * LAYERS
    out_sums = [None] * LAYERS
    for layer in reversed(range(LAYERS)):
        hidden, x_all, query, kv, kv_other, att, lse, middle, mixed, m_all, share_all = saved[layer]
        rides = [out_sums[layer + 1], early] if layer + 1 < LAYERS and replicas == 2 else []
        grad_mid, d_branch, gain_two, front, expert_sum, g_router, *rode = gather_mix_back_scatter(
            count, layer, replicas, d_mix, side, m_all, share_all, params, grad, middle, experts_w, rides
        )
        if layer + 1 < LAYERS:
            d_branch, expert_sums[layer + 1] = lax.optimization_barrier(
                (d_branch, expert_sums[layer + 1])
            )
        peer_front = rode.pop(0) if replicas == 2 else front
        expert_sums[layer] = ((front, peer_front), (expert_sum, across(expert_sum)))
        out_sum, grad, d_mix, side, heads = gather_attend_back_scatter(
            count, layer, d_branch, outs_w, heads_w, x_all, att, query, kv, kv_other, begin, lse, tables,
            [params, grad_mid, hidden, saved[max(layer - 1, 0)][8], g_router, gain_two],
        )
        out_sums[layer] = out_sum
        heads = heads.reshape(count, 2, shard, columns)
        early = heads if layer > 0 else early
    arrived, peer = finish_heads(count, replicas, heads, early, rode[1] if rode else early)
    if replicas == 2:
        outs = list(zip(out_sums, [across(out_sums[0]), rode[0]]))
        *results, g_gate, g_up, g_down = close(
            count, outs, arrived, peer, [activations, grad], expert_sums
        )
    else:
        outs = [(own, jnp.zeros_like(own)) for own in out_sums]
        results = close(count, outs, arrived, peer, [activations, grad], [])
        sums = (*results[:7], jnp.stack([jnp.concatenate([a, b]) for (a, _), (b, _) in expert_sums]))
        *summed, flat_sums = [lax.psum(array.astype(BF16), "rep").astype(F32) for array in sums]
        results = summed + list(results[7:])
        ff = w_gate.shape[3]
        g_gate, g_up = flat_sums[:, None, :width], flat_sums[:, None, width : 2 * width]
        g_down = flat_sums[:, 2 * width :].reshape(LAYERS, width // ff, ff, ff)
        g_down = g_down.transpose(0, 2, 1, 3).reshape(LAYERS, 1, ff, width)
    g_out, g_query, g_key, g_value, g_router, gain_one, gain_two, activations, grad = results
    return (
        activations,
        grad,
        gain_one,
        g_query,
        g_key,
        g_value,
        g_out,
        gain_two,
        g_router,
        g_gate,
        g_up,
        g_down,
    )


def solution(mesh):
    placed = (
        P(("rep", "fsdp"), None),
        P(("rep", "fsdp"), None),
        P(("rep", "fsdp")),
        P("rep", None),
        P(None, ("rep", "fsdp"), None),
        P(None, "fsdp"),
        P(None, "fsdp", None),
        P(None, "fsdp", None),
        P(None, "fsdp", None),
        P(None, "fsdp", None),
        P(None, "fsdp"),
        P(None, "fsdp", None),
        P(None, "fsdp", None, None),
        P(None, "fsdp", None, None),
        P(None, "fsdp", None, None),
    )
    return jax.shard_map(
        on_device,
        mesh=mesh,
        in_specs=placed,
        out_specs=(
            P(("rep", "fsdp"), None),
            P(("rep", "fsdp"), None),
            P(None, "fsdp"),
            P(None, "fsdp", None),
            P(None, "fsdp", None),
            P(None, "fsdp", None),
            P(None, "fsdp", None),
            P(None, "fsdp"),
            P(None, "fsdp", None),
            P(None, "fsdp", None, None),
            P(None, "fsdp", None, None),
            P(None, "fsdp", None, None),
        ),
        check_vma=False,
    )
```

```python
import functools

import jax
import jax.numpy as jnp
from jax import lax
from jax.experimental import pallas as pl
from jax.experimental.pallas import tpu as pltpu
from jax.sharding import PartitionSpec as P

HEADS = 24
KV_HEADS = 8
HD = 64
LAYERS = 2
GROUP = HEADS // KV_HEADS
LANES = 128
SPAN = 2
EPS = 1e-06
MASKED = -1e30
MESH = pl.DeviceIdType.MESH
F32 = jnp.float32
BF16 = jnp.bfloat16


def ring_place(chip, count):
    return lax.select(lax.rem(chip, 2) == 0, chip // 2, count - 1 - chip // 2)


def ring_chip(place, count):
    return lax.select(place < count // 2, 2 * place, 2 * (count - 1 - place) + 1)


def ring_setup(count):
    me = lax.axis_index("fsdp")
    chip, core = me // 2, lax.rem(me, 2)
    place = ring_place(chip, count)

    def at(offset):
        return ring_chip(lax.rem(place + offset + 2 * count, count), count)

    near = [{"fsdp": at(1) * 2 + core}, {"fsdp": at(-1) * 2 + core}]
    return chip, at, near


def partner_of(axis):
    if axis == "rep":
        return {"rep": 1 - lax.axis_index("rep")}
    me = lax.axis_index("fsdp")
    return {"fsdp": me + 1 - 2 * lax.rem(me, 2)}


def meet(others):
    barrier = pltpu.get_barrier_semaphore()
    for other in others:
        pl.semaphore_signal(barrier, inc=1, device_id=other, device_id_type=MESH)
    pl.semaphore_wait(barrier, len(others))


def remote(src, dst, send_sem, recv_sem, device):
    return pltpu.make_async_remote_copy(
        src_ref=src,
        dst_ref=dst,
        send_sem=send_sem,
        recv_sem=recv_sem,
        device_id=device,
        device_id_type=MESH,
    )


def ring_hops(count):
    half = count // 2
    return {(0, 0): half, (1, 1): half, (0, 1): half - 1, (1, 0): half - 1}


IDENTITIES = {}


def identity(key):
    return IDENTITIES.setdefault(key, len(IDENTITIES))


class Ring:
    def __init__(self, count, traffic):
        self.count = count
        self.riders, self.early, self.late, self.soon = traffic
        self.steps = count // 2
        self.chip, self.at, self.near = ring_setup(count)

    def meet(self, partner=False, everyone=None, across=False):
        others = everyone or self.near + ([partner_of("fsdp")] if partner else [])
        meet(others + ([partner_of("rep")] if self.riders or across else []))
        for rider in self.riders:
            rider.start()
        for copy in self.early:
            copy.wait()

    def settle(self):
        for copy in self.late:
            copy.wait()

    def depart(self):
        for copy in self.soon:
            copy.start()

    def gather(self, x_ref, buf, sems, side=None, first=None, second=None):
        own_sem, send_sem, recv_sem = sems[:3]
        half_rows = x_ref.shape[0] // 2
        steps = self.steps
        own = [pltpu.make_async_copy(x_ref, buf.at[self.chip], own_sem.at[0])]
        if side is not None:
            side_ref, side_buf = side
            side_send, side_recv = sems[3:]
            own.append(pltpu.make_async_copy(side_ref, side_buf.at[self.chip], own_sem.at[1]))
        for copy in own:
            copy.start()

        def piece(key, step, block, source=None):
            direction, part = key
            rows = pl.ds(part * half_rows, half_rows)
            target = buf.at[block, rows]
            return remote(
                target if source is None else source.at[rows],
                target,
                send_sem.at[direction, part, step],
                recv_sem.at[direction, part, step],
                self.near[direction],
            )

        def side_piece(direction, step, block, source=None):
            target = side_buf.at[block]
            return remote(
                target if source is None else source,
                target,
                side_send.at[direction, step],
                side_recv.at[direction, step],
                self.near[direction],
            )

        def toward(key, places):
            return self.at(-places if key[0] == 0 else places)

        early, late = [(0, 0), (1, 1)], [(0, 1), (1, 0)]
        if side is not None:
            for direction in range(2):
                side_piece(direction, 0, self.chip, side_ref).start()
        for key in early + late:
            piece(key, 0, self.chip, x_ref).start()

        def take(keys, s, last):
            for key in keys:
                block = toward(key, s)
                piece(key, s - 1, block).wait_recv()

                @pl.when(s < last)
                def _():
                    piece(key, s, block).start()

        def take_side(s):
            if side is not None:
                for direction in range(2):

                    @pl.when(s <= steps - direction)
                    def _():
                        block = toward((direction, 0), s)
                        side_piece(direction, s - 1, block).wait_recv()

                        @pl.when(s < steps - direction)
                        def _():
                            side_piece(direction, s, block).start()

        def step(s, carry):
            take_side(s)
            take(early, s, steps)
            first(s)
            take(late, s, steps - 1)
            second(s)
            return carry

        for copy in own:
            copy.wait()
        lax.fori_loop(1, steps, step, 0)
        first(steps)
        take_side(steps)
        take(early, steps, steps)

        def drain():
            for s in range(steps):
                for key in early + (late if s < steps - 1 else []):
                    piece(key, s, toward(key, s)).wait_send()
                if side is not None:
                    for direction in range(2):
                        if s < steps - direction:
                            side_piece(direction, s, toward((direction, 0), s)).wait_send()

        return drain

    def pair(self, s):
        return self.at(s), self.at(-s)

    def meanwhile(self, compute, ready):
        def first(s):
            @pl.when(s == 1)
            def _():
                compute(0, (self.chip,))

            @pl.when(s > 1)
            def _():
                compute(1, self.pair(s - 1))

        def second(s):
            @pl.when(s == 1)
            def _():
                ready()
                compute(1, (self.chip,))

            compute(0, self.pair(s))

        return first, second

    def scatter(self, partial, land, sems, work=None, between=None):
        send_sem, recv_sem = sems
        half_rows = partial.shape[1] // 2
        steps = self.steps
        hops = ring_hops(self.count)

        def ahead(key, s):
            places = hops[key] - s
            return self.at(places if key[0] == 0 else -places)

        def piece(key, s, source):
            direction, part = key
            return remote(
                source,
                land.at[direction, part, s],
                send_sem.at[direction, part, s],
                recv_sem.at[direction, part, s],
                self.near[direction],
            )

        def rows_of(key):
            return pl.ds(key[1] * half_rows, half_rows)

        for place, key in enumerate(hops):
            if place == 2 and between is not None:
                between()
            piece(key, 0, partial.at[ahead(key, 0), rows_of(key)]).start()

        def step(s, carry):
            for place, key in enumerate(hops):
                if work is not None:
                    work(s - 1, place)

                @pl.when(s < hops[key])
                def _():
                    slot = land.at[key[0], key[1], s - 1]
                    piece(key, s - 1, slot).wait_recv()
                    mine = partial[ahead(key, s), rows_of(key)]
                    slot[...] = (slot[...].astype(F32) + mine.astype(F32)).astype(BF16)
                    piece(key, s, slot).start()

            return carry

        lax.fori_loop(1, steps + 1, step, 0)
        for key in hops:
            slot = land.at[key[0], key[1], hops[key] - 1]
            piece(key, hops[key] - 1, slot).wait_recv()
        halves = []
        for part in range(2):
            rows = pl.ds(part * half_rows, half_rows)
            total = partial[self.chip, rows].astype(F32)
            for direction in range(2):
                total = total + land[direction, part, hops[direction, part] - 1].astype(F32)
            halves.append(total)
        summed = jnp.concatenate(halves, 0)

        def drain():
            for key in hops:
                for s in range(hops[key]):
                    piece(key, s, land.at[key[0], key[1], s]).wait_send()

        return summed, drain


def dmas(*shapes):
    return [pltpu.SemaphoreType.DMA(shape) for shape in shapes]


def gather_sems(count, sided=False):
    steps = count // 2
    shapes = [(2,), (2, 2, steps), (2, 2, steps)]
    return dmas(*(shapes + ([(2, steps), (2, steps)] if sided else [])))


def scatter_sems(count):
    return dmas((2, 2, count // 2), (2, 2, count // 2))


ANYWHERE = pl.BlockSpec(memory_space=pltpu.HBM)
HERE = pl.BlockSpec(memory_space=pltpu.VMEM)
EARLY, LATE = "early", "late"
OUT, SOON = "out", "soon"


FREE = pl.CostEstimate(flops=0, bytes_accessed=0, transcendentals=0)


def ring_call(body, key, inputs, outputs, scratch, megabytes, rides=()):
    n_in, n_out, n_rides = len(inputs), len(outputs), len(rides)
    in_kinds = [kind for _, kind in inputs]
    out_kinds = [kind for _, kind in outputs]
    copied = [a for a, kind in inputs if kind in (EARLY, LATE)]
    returned = [a for a, kind in outputs if kind in (OUT, SOON)]
    moves = len(copied) + len(returned)

    def kernel(*refs):
        ins, ride_in, outs, ride_out, rest = split(refs, n_in, n_rides, n_out, n_rides)
        rest, own, rest_sems = rest[: len(scratch)], rest[len(scratch) : len(scratch) + moves], rest[len(scratch) + moves :]
        move_sem, rest_sems = rest_sems[0], rest_sems[1:]
        riders = []
        if n_rides:
            send_sem, recv_sem = rest_sems
            riders = [
                remote(ride_in[i], ride_out[i], send_sem.at[i], recv_sem.at[i], partner_of("rep"))
                for i in range(n_rides)
            ]
        used = 0
        early, late, leaving, soon = [], [], [], []
        ins, outs = list(ins), list(outs)
        for i, kind in enumerate(in_kinds):
            if kind in (EARLY, LATE):
                copy = pltpu.make_async_copy(ins[i], own[used], move_sem.at[used])
                copy.start()
                (early if kind == EARLY else late).append(copy)
                ins[i] = own[used]
                used += 1
        for i, kind in enumerate(out_kinds):
            if kind in (OUT, SOON):
                copy = pltpu.make_async_copy(own[used], outs[i], move_sem.at[used])
                (leaving if kind == OUT else soon).append(copy)
                outs[i] = own[used]
                used += 1
        body((riders, early, late, soon), *ins, *outs, *rest)
        for copy in leaving:
            copy.start()
        for rider in riders:
            rider.wait()
        for copy in leaving + soon:
            copy.wait()

    def spec(kind):
        return ANYWHERE if isinstance(kind, str) else kind

    return pl.pallas_call(
        kernel,
        out_shape=tuple(shape for shape, _ in outputs) + tuple(cells(a.shape, a.dtype) for a in rides),
        in_specs=[spec(kind) for kind in in_kinds] + [ANYWHERE] * n_rides,
        out_specs=[spec(kind) for kind in out_kinds] + [ANYWHERE] * n_rides,
        scratch_shapes=list(scratch)
        + [pltpu.VMEM(a.shape, a.dtype) for a in copied + returned]
        + dmas((max(moves, 1),))
        + (dmas((n_rides,), (n_rides,)) if n_rides else []),
        compiler_params=pltpu.CompilerParams(
            collective_id=identity(key),
            has_side_effects=True,
            vmem_limit_bytes=megabytes << 20,
        ),
        cost_estimate=FREE,
        name=key[0],
    )(*[array for array, _ in inputs], *rides)


def split(refs, *sizes):
    parts, place = [], 0
    for size in sizes:
        parts.append(refs[place : place + size])
        place += size
    return parts + [refs[place:]]


def cells(shape, dtype):
    return jax.ShapeDtypeStruct(shape, dtype)


def dot(left, right, contract=((1,), (0,))):
    return lax.dot_general(left, right, (contract, ((), ())), preferred_element_type=F32)


NT = ((1,), (1,))
TN = ((0,), (0,))


def lanes_of(field):
    return lax.broadcasted_iota(jnp.int32, field.shape, 1)


def turn(field):
    return pltpu.roll(field, HD, 1)


def spin(field, cosine, sine):
    swapped = jnp.where(
        lax.rem(lanes_of(field), HD) < HD // 2,
        -pltpu.roll(field, LANES - HD // 2, 1),
        pltpu.roll(field, HD // 2, 1),
    )
    return field * cosine + swapped * sine


def project_rows(rows, cosine, sine):
    first = spin(rows[:, :LANES], cosine, sine)
    second = spin(rows[:, LANES : 2 * LANES], cosine, sine)
    third = rows[:, 2 * LANES :]
    low = lanes_of(first) < HD
    heads = []
    for field in (first, turn(first), second):
        rounded = jnp.where(low, field, 0.0).astype(BF16).astype(F32)
        heads.append((rounded * (HD**-0.5)).astype(BF16))
    return heads, jnp.where(low, turn(second), turn(third)).astype(BF16)


def angles(table):
    rows = jnp.concatenate([table, table], 0).T
    early = lax.rem(lanes_of(rows), HD) < HD // 2
    cosine = jnp.where(early, rows, pltpu.roll(rows, HD // 2, 1))
    sine = jnp.where(early, pltpu.roll(rows, LANES - HD // 2, 1), rows)
    return cosine, sine


def normal(values):
    inverse = lax.rsqrt(jnp.mean(values * values, -1, keepdims=True) + EPS)
    return inverse, values * inverse


def normal_back(d_x, values, gain):
    inverse, normed = normal(values)
    d_norm = d_x * gain
    d_values = inverse * (d_norm - normed * jnp.mean(d_norm * normed, -1, keepdims=True))
    return d_values, jnp.sum(d_x * normed, 0, keepdims=True)


def diagonal():
    shape = (LANES, LANES)
    return lax.broadcasted_iota(jnp.int32, shape, 0) == lax.broadcasted_iota(jnp.int32, shape, 1)


def as_column(line):
    return jnp.sum(jnp.where(diagonal(), jnp.broadcast_to(line, (LANES, LANES)), 0.0), 1, keepdims=True)


def as_line(column):
    return jnp.sum(jnp.where(diagonal(), jnp.broadcast_to(column, (LANES, LANES)), 0.0), 0, keepdims=True)


def flat(value):
    return value.reshape(value.shape[0] * value.shape[1], value.shape[2])


def stack(ref, blocks):
    parts = [ref[b] for b in blocks]
    return parts[0] if len(parts) == 1 else jnp.concatenate(parts, 0)


def cut(value, blocks):
    return [(b, value[i * LANES : (i + 1) * LANES]) for i, b in enumerate(blocks)]


def gain_row(params_ref, kind, layer):
    row = kind * LAYERS + layer
    return params_ref[row : row + 1, :]


def router_rows(experts, layer):
    first = 2 * LAYERS + layer * experts
    return slice(first, first + experts)


def allowed_keys(begin, query, chunk, core):
    half = SPAN * LANES
    shape = (2 * half, begin.shape[1])
    place = lax.broadcasted_iota(jnp.int32, (2 * half, 1), 0)
    inner = lax.rem(place, half)
    whose = jnp.where(place < half, core, 1 - core)
    key = chunk * 2 * half + inner // LANES * (2 * LANES) + whose * LANES + lax.rem(inner, LANES)
    key = jnp.broadcast_to(key, shape)
    return (key >= begin) & (key <= query)


def query_rows(begin_ref, blocks, core):
    lane = lax.broadcasted_iota(jnp.int32, (1, LANES), 1)
    begin, query = [], []
    for block in blocks:
        begin += [begin_ref[block]] * GROUP
        query += [(2 * block + core) * LANES + lane] * GROUP
    return jnp.concatenate(begin, 1), jnp.concatenate(query, 1)


def chunk_keys(own_ref, other_ref, chunk):
    chips = pl.ds(chunk * SPAN, SPAN)
    return jnp.concatenate([flat(own_ref[chips]), flat(other_ref[chips])], 0)


def turn_keys(own_ref, other_ref, turned_ref):
    def one(chunk, carry):
        turned_ref[chunk] = chunk_keys(own_ref, other_ref, chunk).astype(F32).T.astype(BF16)
        return carry

    lax.fori_loop(0, turned_ref.shape[0], one, 0)


def by_head(field):
    return [field[:, h * LANES : (h + 1) * LANES].T for h in range(GROUP)]


def chunks_of(blocks):
    last = blocks[0] if len(blocks) == 1 else jnp.maximum(*blocks)
    return last // SPAN + 1


class Opening:
    def __init__(self, count, inputs, outputs, scratch):
        self.tokens_ref, *self.projections, self.out_w_ref, self.small_ref, self.table_ref = inputs
        self.heads_ref, self.outs_ref, self.tables_ref, self.params_ref = outputs
        (self.x_ref, self.slab_ref, self.smalls, self.weights, self.own_sem, self.slab_sem, self.pass_sem, self.small_sem,
         self.table_sem, self.out_sem) = scratch
        self.count = count
        self.devices = 2 * count
        self.me = lax.axis_index("fsdp")
        self.chip, self.core = self.me // 2, lax.rem(self.me, 2)
        self.partner = partner_of("fsdp")

    def device(self, offset):
        return {"fsdp": lax.rem(self.me + offset, self.devices)}

    def chip_at(self, offset):
        return lax.rem(self.chip + offset + self.count, self.count)

    def everyone(self):
        return [self.device(offset) for offset in range(1, self.devices)]

    def home(self, layer, origin):
        shard = self.slab_ref.shape[2]
        rows = pl.ds(pl.multiple_of(origin * shard, shard), shard)
        return self.weights.at[rows] if layer == 0 else self.heads_ref.at[layer, rows]

    def across(self, layer, offset, source=None, target=None):
        slot = self.home(layer, self.me) if source is None else source
        target = slot if target is None else target
        there = {"fsdp": self.chip_at(offset) * 2 + self.core}
        return remote(slot, target, self.slab_sem.at[0, offset, layer], self.slab_sem.at[1, offset, layer], there)

    def beside(self, layer, offset, slot, source=None):
        return remote(
            slot if source is None else source, slot,
            self.pass_sem.at[0, offset, layer], self.pass_sem.at[1, offset, layer], self.partner,
        )

    def small_to(self, offset, slot, source=None):
        return remote(
            slot if source is None else source, slot,
            self.small_sem.at[0, offset], self.small_sem.at[1, offset], self.device(offset),
        )

    def table_to(self, offset, slot, source=None):
        there = {"fsdp": self.chip_at(offset) * 2 + self.core}
        return remote(
            slot if source is None else source, slot,
            self.table_sem.at[0, offset], self.table_sem.at[1, offset], there,
        )

    def out_to(self, slot, source):
        return remote(source, slot, self.out_sem.at[0], self.out_sem.at[1], self.partner)

    def divide(self):
        for layer in range(LAYERS):
            query, key, value = [ref[layer].astype(F32) for ref in self.projections]
            for half in range(self.count // 2):
                first = 3 * half * LANES
                t = [query[:, first + i * LANES : first + (i + 1) * LANES] for i in range(3)]
                k, v = [a[:, half * LANES : (half + 1) * LANES] for a in (key, value)]
                low = lanes_of(k) < HD
                even = [t[0], jnp.where(low, t[1], turn(k)), jnp.where(low, v, 0.0)]
                odd = [
                    jnp.where(low, turn(t[1]), turn(t[2])),
                    jnp.where(low, turn(t[2]), k),
                    jnp.where(low, turn(v), 0.0),
                ]
                for place, tiles in enumerate((even, odd)):
                    self.slab_ref[2 * half + place, layer] = jnp.concatenate(tiles, 1).astype(BF16)

    def start(self):
        me, chip = self.me, self.chip
        self.divide()
        self.copies = [
            pltpu.make_async_copy(self.small_ref, self.smalls.at[me], self.own_sem.at[0]),
            pltpu.make_async_copy(self.table_ref, self.tables_ref.at[chip], self.own_sem.at[1]),
            pltpu.make_async_copy(self.out_w_ref, self.outs_ref.at[self.core], self.own_sem.at[2]),
        ] + [
            pltpu.make_async_copy(self.slab_ref.at[chip, layer], self.home(layer, me), self.own_sem.at[3 + layer])
            for layer in range(LAYERS)
        ]
        self.sends = [
            self.small_to(offset, self.smalls.at[me], self.small_ref) for offset in range(1, self.devices)
        ]
        for offset in range(1, self.count):
            self.sends.append(self.table_to(offset, self.tables_ref.at[chip], self.table_ref))
        for layer in range(LAYERS):
            for offset in range(1, self.count):
                slab = self.slab_ref.at[self.chip_at(offset), layer]
                self.sends.append(self.across(layer, offset, slab, self.home(layer, me)))
            self.sends.append(self.beside(layer, 0, self.home(layer, me), self.slab_ref.at[chip, layer]))
        self.sends.append(self.out_to(self.outs_ref.at[self.core], self.out_w_ref))
        for copy in self.copies + self.sends:
            copy.start()

    def parameters(self):
        for offset in range(1, self.devices):
            origin = lax.rem(self.me - offset + self.devices, self.devices)
            self.small_to(offset, self.smalls.at[origin]).wait_recv()
        self.copies[0].wait()
        shard = self.slab_ref.shape[2]
        width = self.params_ref.shape[1]
        shape = (LANES, width)
        feature = lax.broadcasted_iota(jnp.int32, shape, 1)
        spread = (lax.rem(feature, shard) == lax.broadcasted_iota(jnp.int32, shape, 0)).astype(F32).astype(BF16)
        owner = lax.broadcasted_iota(jnp.int32, self.params_ref.shape, 1) // shard
        self.params_ref[...] = jnp.zeros_like(self.params_ref)

        def one(device, carry):
            rows = dot(self.smalls[device], spread)
            self.params_ref[...] += jnp.where(owner == device, rows, 0.0)
            return carry

        lax.fori_loop(0, self.devices, one, 0)
        normed = normal(self.tokens_ref[...].astype(F32))[1]
        self.x_ref[...] = (normed * gain_row(self.params_ref, 0, 0)).astype(BF16)

    def forward(self, layer):
        for offset in range(1, self.count):
            slot = self.home(layer, self.chip_at(-offset) * 2 + self.core)
            self.across(layer, offset, slot).wait_recv()
            self.beside(layer, offset, slot).start()

    def arrived(self, layer):
        self.copies[3 + layer].wait()
        for offset in range(self.count):
            slot = self.home(layer, self.chip_at(-offset) * 2 + 1 - self.core)
            self.beside(layer, offset, slot).wait_recv()

    def rest(self):
        for offset in range(1, self.count):
            self.table_to(offset, self.tables_ref.at[self.chip_at(-offset)]).wait_recv()
        for copy in self.copies[1:3]:
            copy.wait()
        other = self.outs_ref.at[1 - self.core]
        self.out_to(other, other).wait_recv()

    def drain(self):
        for send in self.sends:
            send.wait_send()
        for layer in range(LAYERS):
            for offset in range(1, self.count):
                slot = self.home(layer, self.chip_at(-offset) * 2 + self.core)
                self.beside(layer, offset, slot).wait_send()


def attend_part(ring, count, layer, inputs, outputs, scratch, midway):
    if layer == 0:
        begin_ref, routes_ref = inputs[7:]
        hidden_ref, table_ref, params_ref = inputs[0], outputs[11], outputs[12]
    else:
        x_ref, w_ref, w_out_ref, table_ref, begin_ref, hidden_ref, params_ref, routes_ref = inputs
    q_ref, own_ref, other_ref, all_ref, att_ref, lse_ref, middle_ref, x_out_ref, share_ref = outputs[:9]
    buf, weights, wide_w, turned_ref, score_ref, partial, land = scratch[:7]
    sems, pair_sems, scatter_sem, out_sem, load_sem, more = split(scratch[7:], 3, 2, 2, 1, 1)[:5] + [scratch[16:]]
    partner = partner_of("fsdp")
    core = lax.rem(lax.axis_index("fsdp"), 2)

    def pass_on(block):
        return remote(
            own_ref.at[block], other_ref.at[block], pair_sems[0].at[block], pair_sems[1].at[block], partner
        )

    def project(blocks):
        rows = dot(stack(buf, blocks), weights[...])
        tables = [angles(table_ref[b]) for b in blocks]
        cosine = jnp.concatenate([t[0] for t in tables], 0)
        sine = jnp.concatenate([t[1] for t in tables], 0)
        heads, pair = project_rows(rows, cosine, sine)
        for index, head in enumerate(heads):
            for block, part in cut(head, blocks):
                q_ref[block, index] = part
        for block, part in cut(pair, blocks):
            own_ref[block] = part
            pass_on(block).start()

    if layer == 0:
        opening = Opening(count, inputs[:7], outputs[9:], [*more[:3], weights, *more[3:]])
        ring.meet(True, opening.everyone())
        opening.start()
        opening.parameters()
        loads = load_out_weights(outputs[10], layer, wide_w, load_sem[0], False)
        keep = [
            pltpu.make_async_copy(buf, all_ref, out_sem[0].at[0]),
            pltpu.make_async_copy(weights, outputs[9].at[0], out_sem[0].at[1]),
        ]

        def first(s):
            @pl.when(s == ring.steps - 1)
            def _():
                opening.rest()
                for load in loads:
                    load.start()
                opening.arrived(0)
                keep[1].start()
                project((ring.chip,))

            @pl.when(s == ring.steps)
            def _():
                project(ring.pair(ring.steps - 1))

        def second(s):
            @pl.when(s == ring.steps - 2)
            def _():
                opening.forward(0)

            @pl.when(s == ring.steps - 1)
            def _():
                def one(index, carry):
                    project(ring.pair(index))
                    return carry

                lax.fori_loop(1, ring.steps - 1, one, 0)

        drain = ring.gather(opening.x_ref, buf, sems, None, first, second)
        keep[0].start()
        project((ring.at(ring.steps),))
        for load in loads:
            load.wait()
    else:
        loads = [pltpu.make_async_copy(w_ref.at[layer], weights, load_sem[0].at[2])]
        loads[0].start()
        loads += load_out_weights(w_out_ref, layer, wide_w, load_sem[0])
        ring.meet(True)

        def first(s):
            @pl.when(s == 1)
            def _():
                for load in loads:
                    load.wait()
                project((ring.chip,))

        drain = ring.gather(x_ref, buf, sems, None, first, lambda s: project(ring.pair(s)))
        keep = [pltpu.make_async_copy(buf, all_ref, out_sem[0].at[0])]
        keep[0].start()
        project((ring.at(ring.steps),))
    for block in range(count):
        pass_on(block).wait()
    ring.depart()
    midway()
    turn_keys(own_ref, other_ref, turned_ref)

    def attend(blocks):
        width = len(blocks) * GROUP * LANES
        q = jnp.concatenate([q_ref[b].reshape(GROUP * LANES, LANES) for b in blocks], 0)
        begin, query = query_rows(begin_ref, blocks, core)
        end = chunks_of(blocks)

        def score(chunk, top):
            keys = chunk_keys(own_ref, other_ref, chunk)
            scores = jnp.where(allowed_keys(begin, query, chunk, core), dot(keys, q, NT), MASKED)
            score_ref[chunk, :, :width] = scores
            return jnp.maximum(top, jnp.max(scores, 0, keepdims=True))

        top = lax.fori_loop(0, end, score, jnp.full((1, width), MASKED, F32))

        def add(chunk, state):
            total, acc = state
            weights = jnp.exp(score_ref[chunk, :, :width] - top)
            total = total + jnp.sum(weights, 0, keepdims=True)
            return total, acc + dot(turned_ref[chunk], weights.astype(BF16))

        total, acc = lax.fori_loop(
            0, end, add, (jnp.zeros((1, width), F32), jnp.zeros((LANES, width), F32))
        )
        lse = top + jnp.log(total)
        att = acc / total
        rows = []
        for place, block in enumerate(blocks):
            here = slice(place * GROUP * LANES, (place + 1) * GROUP * LANES)
            lse_ref[block] = lse[:, here]
            heads = by_head(att[:, here])
            low = lanes_of(heads[0]) < HD
            rows.append(
                jnp.concatenate(
                    [jnp.where(low, turn(heads[0]), heads[1]), jnp.where(low, turn(heads[2]), 0.0)], 1
                ).astype(BF16)
            )
            att_ref[block] = rows[-1]
        out = dot(jnp.concatenate(rows, 0) if len(rows) > 1 else rows[0], wide_w[...]).astype(BF16)
        for block, part in cut(out, blocks):
            partial[block] = part

    attend((ring.at(ring.steps),))

    def between():
        if layer == 0:
            for later in range(1, LAYERS):
                opening.forward(later)
        attend(ring.pair(ring.steps - 1))

    def work(s, place):
        if place == 2:

            @pl.when(s < ring.steps - 2)
            def _():
                attend(ring.pair(ring.steps - 2 - s))

            @pl.when(s == ring.steps - 2)
            def _():
                attend((ring.chip,))

    added, finish = ring.scatter(partial, land, scatter_sem, work, between)
    ring.settle()
    middle = hidden_ref[...].astype(F32) + added
    middle_ref[...] = middle
    x = (normal(middle)[1] * gain_row(params_ref, 1, layer)).astype(BF16)
    x_out_ref[...] = x
    experts = share_ref.shape[0]
    logits = dot(params_ref[router_rows(experts, layer), :].astype(BF16), x, NT)
    expert = lax.broadcasted_iota(jnp.int32, logits.shape, 0)
    named = expert < 0
    for choice in range(routes_ref.shape[1]):
        named = named | (expert == routes_ref[layer, choice : choice + 1, :])
    scores = jnp.where(named, logits, MASKED)
    weighted = jnp.where(named, jnp.exp(scores - jnp.max(scores, 0, keepdims=True)), 0.0)
    share_ref[...] = weighted / jnp.sum(weighted, 0, keepdims=True)

    def end():
        drain()
        finish()
        for copy in keep:
            copy.wait()
        if layer == 0:
            for later in range(1, LAYERS):
                opening.arrived(later)
            opening.drain()

    return end


def attend_shapes(count, rows, width, columns, extra):
    block = cells((count, rows, LANES), BF16)
    everyone = pltpu.VMEM((count, rows, width), BF16)
    wide = 2 * LANES
    outputs = [
        (cells((count, GROUP, rows, LANES), BF16), SOON),
        (block, SOON),
        (block, SOON),
        (cells((count, rows, width), BF16), ANYWHERE),
        (cells((count, rows, wide), BF16), OUT),
        (cells((count, 1, GROUP * rows), F32), OUT),
        (cells((rows, width), F32), OUT),
        (cells((rows, width), BF16), OUT),
        (cells((2 * count, rows), F32), OUT),
    ]
    scratch = [
        everyone,
        pltpu.VMEM((width, columns), BF16),
        pltpu.VMEM((wide, width), BF16),
        pltpu.VMEM((count // SPAN, LANES, SPAN * wide), BF16),
        pltpu.VMEM((count // SPAN, SPAN * wide, 2 * GROUP * LANES), F32),
        everyone,
        land_scratch(count, rows, width),
    ]
    scratch += gather_sems(count) + dmas((count,), (count,)) + scatter_sems(count) + dmas((2,), (3,))
    return outputs + extra[0], scratch + extra[1]


def opening_shapes(count, tokens, columns, out_w, small, table):
    rows, width = tokens.shape
    layers, shard, _ = out_w.shape
    devices = 2 * count
    outputs = [
        (cells((layers, width, columns), BF16), ANYWHERE),
        (cells((2,) + out_w.shape, BF16), ANYWHERE),
        (cells((count,) + table.shape, F32), OUT),
        (cells((small.shape[0], width), F32), OUT),
    ]
    scratch = [
        pltpu.VMEM((rows, width), BF16),
        pltpu.VMEM((count, layers, shard, columns), BF16),
        pltpu.VMEM((devices,) + small.shape, BF16),
    ] + dmas((3 + layers,), (2, count, layers), (2, count, layers), (2, devices), (2, count), (2,))
    return outputs, scratch


def load_experts(refs, layer, bufs, sem):
    copies = [
        pltpu.make_async_copy(ref.at[layer, 0], buf.at[0], sem.at[place])
        for place, (ref, buf) in enumerate(zip(refs, bufs))
    ]
    for copy in copies:
        copy.start()
    return copies


def lend_experts(refs, layer, bufs, sems):
    copies = [
        remote(ref.at[layer, 0], buf.at[1], sems[0].at[place], sems[1].at[place], partner_of("fsdp"))
        for place, (ref, buf) in enumerate(zip(refs, bufs))
    ]
    for copy in copies:
        copy.start()
    return copies


def expert_of(e):
    me = lax.axis_index("fsdp")
    return me if e == 0 else me + 1 - 2 * lax.rem(me, 2)


def share_of(share_ref, e, blocks):
    columns = [as_column(share_ref[b, pl.ds(expert_of(e), 1), :]) for b in blocks]
    return jnp.concatenate(columns, 0) if len(columns) > 1 else columns[0]


def after_loads(loads, run):
    def first(s):
        @pl.when(s == 1)
        def _():
            for load in loads:
                load.wait()

        run(s)

    return first


def mix_part(ring, count, layer, given, cotangent, outputs, scratch, loads, lent):
    x_ref, side_ref, middle_ref, params_ref = given
    mixed_ref, hidden_ref, next_ref, all_ref, share_ref = outputs[:5]
    buf, partial, land, acc, gates, ups, downs = scratch[:7]
    sems, scatter_sem, out_sem = split(scratch[7:], 5, 2)

    def ready():
        for copy in lent:
            copy.wait()

    def compute(e, blocks):
        x = stack(buf, blocks)
        act_gate, act_up = dot(x, gates[e]), dot(x, ups[e])
        hidden = jax.nn.silu(act_gate) * act_up * share_of(share_ref, e, blocks)
        part = dot(hidden.astype(BF16), downs[e])
        if e == 0:
            acc[: x.shape[0]] = part
        else:
            total = (acc[: x.shape[0]] + part).astype(BF16)
            for block, rows in cut(total, blocks):
                partial[block] = rows

    first, second = ring.meanwhile(compute, ready)
    drain = ring.gather(x_ref, buf, sems, (side_ref, share_ref), after_loads(loads, first), second)
    keep = pltpu.make_async_copy(buf, all_ref, out_sem[0].at[0])
    keep.start()
    for e in range(2):
        compute(e, (ring.at(ring.steps),))
    mixed, finish = ring.scatter(partial, land, scatter_sem)
    mixed_ref[...] = mixed
    hidden = middle_ref[...] + mixed
    hidden_ref[...] = hidden
    if layer + 1 < LAYERS:
        next_ref[...] = (normal(hidden)[1] * gain_row(params_ref, 0, layer + 1)).astype(BF16)
    else:
        next_ref[...] = hidden.astype(BF16)
        balance = jnp.sum(mixed * cotangent[0][...].astype(F32), -1, keepdims=True)
        outputs[5][...] = jnp.broadcast_to(as_line(balance), outputs[5].shape)

    def end():
        drain()
        finish()
        keep.wait()

    return end


def expert_scratch(weights):
    return [pltpu.VMEM((2,) + w.shape[2:], BF16) for w in weights]


def land_scratch(count, rows, width):
    return pltpu.VMEM((2, 2, count // 2, rows // 2, width), BF16)


def mix_shapes(count, layer, rows, width, weights):
    everyone = pltpu.VMEM((count, rows, width), BF16)
    own = cells((rows, width), F32)
    outputs = [
        (own, OUT),
        (own, OUT),
        (cells((rows, width), BF16), OUT),
        (cells((count, rows, width), BF16), ANYWHERE),
        (cells((count, 2 * count, rows), F32), OUT),
    ]
    if layer + 1 == LAYERS:
        outputs.append((cells((8, rows), F32), OUT))
    scratch = [everyone, everyone, land_scratch(count, rows, width), pltpu.VMEM((2 * rows, width), F32)]
    scratch += expert_scratch(weights) + gather_sems(count, True) + scatter_sems(count) + dmas((1,))
    return outputs, scratch


def forward_kernel(count, layer, sizes, traffic, *refs):
    last = layer + 1 == LAYERS
    attend_in, weights, cotangent, attend_out, mix_out, scratch = split(
        refs, sizes[0], 3, int(last), sizes[1], sizes[2]
    )
    attend_scratch, mix_scratch, sems = split(scratch, sizes[3], sizes[4])
    bufs = mix_scratch[4:7]
    ring = Ring(count, traffic)
    loads = load_experts(weights, layer, bufs, sems[0])
    lent = []
    attend_end = attend_part(
        ring, count, layer, attend_in, attend_out, attend_scratch,
        lambda: lent.extend(lend_experts(weights, layer, bufs, sems[1:])),
    )
    params_ref = attend_out[12] if layer == 0 else attend_in[6]
    given = (attend_out[7], attend_out[8], attend_out[6], params_ref)
    mix_end = mix_part(ring, count, layer, given, cotangent, mix_out, mix_scratch, loads, lent)
    attend_end()
    mix_end()


def forward(count, layer, inputs, rows, width, columns, weights, cotangent, extra=([], [])):
    last = layer + 1 == LAYERS
    attend_out, attend_scratch = attend_shapes(count, rows, width, columns, extra)
    mix_out, mix_scratch = mix_shapes(count, layer, rows, width, weights)
    sizes = [len(part) for part in (inputs, attend_out, mix_out, attend_scratch, mix_scratch)]
    return ring_call(
        functools.partial(forward_kernel, count, layer, sizes),
        ("forward", layer),
        inputs + [(w, ANYWHERE) for w in weights] + ([(cotangent, LATE)] if last else []),
        attend_out + mix_out,
        attend_scratch + mix_scratch + dmas((3,), (3,), (3,)),
        60,
    )


def crosses_early(layer, replicas):
    return replicas == 2 and layer == 0


def mix_back_kernel(count, layer, replicas, traffic, *refs):
    crossing = crosses_early(layer, replicas)
    inputs, outputs, scratch = split(refs, 10, 6 + crossing)
    d_ref, side_ref, m_ref, share_ref, params_ref, grad_ref, middle_ref = inputs[:7]
    mid_ref, branch_ref, gain_ref, part_ref, sum_ref, g_router_ref = outputs[:6]
    buf, partial, land, acc, gates, ups, downs = scratch[:7]
    tokens, acts, hiddens, balance_ref, totals, got = scratch[7:13]
    sems, scatter_sem, load_sem, pair_sem, lend_sem, cross_sem, out_sem = split(scratch[13:], 5, 2, 1, 2, 2, 2)
    ring = Ring(count, traffic)
    loads = load_experts(inputs[7:], layer, (gates, ups, downs), load_sem[0])
    loads.append(pltpu.make_async_copy(m_ref, tokens, load_sem[0].at[3]))
    loads[-1].start()
    ring.meet(True, None, crossing)
    lent = lend_experts(inputs[7:], layer, (gates, ups, downs), lend_sem)

    def ready():
        for copy in lent:
            copy.wait()

    ff = gates.shape[2]
    width = buf.shape[2]
    g_router_ref[...] = jnp.zeros_like(g_router_ref)
    routers = 2 * LAYERS + layer * 2 * count

    def compute(e, blocks):
        d, x = stack(buf, blocks), stack(tokens, blocks)
        share = share_of(share_ref, e, blocks)
        balance = [as_column(balance_ref[b, 0:1, :]) for b in blocks]
        balance = jnp.concatenate(balance, 0) if len(balance) > 1 else balance[0]
        act_gate, act_up = dot(x, gates[e]), dot(x, ups[e])
        sig = jax.nn.sigmoid(act_gate)
        swish = act_gate * sig
        hidden = swish * act_up
        raw = dot(d, downs[e], NT)
        d_logit = share * (jnp.sum(hidden * raw, -1, keepdims=True) - balance)
        d_hidden = raw * share
        d_gate = (d_hidden * act_up * sig * (1.0 + act_gate * (1.0 - sig))).astype(BF16)
        d_up = (d_hidden * swish).astype(BF16)
        weighted = (hidden * share).astype(BF16)
        part = dot(d_gate, gates[e], NT) + dot(d_up, ups[e], NT)
        part = part + d_logit * params_ref[pl.ds(routers + expert_of(e), 1), :]
        g_router_ref[e : e + 1, :] += jnp.sum(d_logit * x.astype(F32), 0, keepdims=True)
        for place, block in enumerate(blocks):
            here = slice(place * LANES, (place + 1) * LANES)
            acts[e, block, :, :ff] = d_gate[here]
            acts[e, block, :, ff:] = d_up[here]
            hiddens[e, block] = weighted[here]
        if e == 0:
            acc[: x.shape[0]] = part
        else:
            total = (acc[: x.shape[0]] + part).astype(BF16)
            for block, rows in cut(total, blocks):
                partial[block] = rows

    first, second = ring.meanwhile(compute, ready)
    drain = ring.gather(d_ref, buf, sems, (side_ref, balance_ref), after_loads(loads, first), second)
    for e in range(2):
        compute(e, (ring.at(ring.steps),))

    partner = partner_of("fsdp")
    strip = 2 * LANES
    strips = width // (2 * strip)
    groups = width // ff

    def regions(half):
        regions = [(group * width + half * (width // 2), width // 2) for group in range(2)]
        return regions + [(2 * width + group * ff + half * (ff // 2), ff // 2) for group in range(groups)]

    def swap(half):
        return [
            remote(
                totals.at[1, pl.ds(first, length)], got.at[pl.ds(first, length)],
                pair_sem[0].at[half, index], pair_sem[1].at[half, index], partner,
            )
            for index, (first, length) in enumerate(regions(half))
        ]

    apart = width // 4

    def store(half):
        parts = []
        for first, length in regions(half):
            if first == 0:
                parts.append((pl.ds(0, apart), part_ref))
                parts.append((pl.ds(apart, length - apart), sum_ref.at[pl.ds(0, length - apart)]))
            else:
                parts.append((pl.ds(first, length), sum_ref.at[pl.ds(first - apart, length)]))
        return [
            pltpu.make_async_copy(totals.at[0, rows], target, out_sem[0].at[half, index])
            for index, (rows, target) in enumerate(parts)
        ]

    crossings = []
    if crossing:
        crossings.append(
            remote(
                totals.at[0, pl.ds(0, apart)], outputs[6],
                cross_sem[0].at[0], cross_sem[1].at[0], partner_of("rep"),
            )
        )

    def work(s, place):
        e = 1 - s // 2
        half = lax.rem(s, 2)

        def put(first, value):
            rows = pl.ds(pl.multiple_of(first, strip), strip)

            @pl.when(s < 2)
            def _():
                totals[1, rows] = value.astype(BF16)

            @pl.when(s >= 2)
            def _():
                totals[0, rows] = (value + got[rows].astype(F32)).astype(BF16)

        if place == 0:
            for h in range(2):

                @pl.when(s == 2 + h)
                def _():
                    for copy in swap(h):
                        copy.wait_recv()

        if place == 2:

            @pl.when(s == 2)
            def _():
                for copy in crossings:
                    copy.start()

        if place < strips:
            first = (half * strips + place) * strip
            columns = pl.ds(pl.multiple_of(first, strip), strip)
            value = dot(flat(tokens[:, :, columns]), flat(acts[e]), TN)
            for group in range(2):
                put(group * width + first, value[:, group * ff : (group + 1) * ff])
        if place == 3:
            columns = pl.ds(pl.multiple_of(half * strip, strip), strip)
            value = dot(flat(hiddens[e, :, :, columns]), flat(buf[...]), TN)
            for group in range(groups):
                put(2 * width + group * ff + half * strip, value[:, group * ff : (group + 1) * ff])
            for h in range(2):

                @pl.when(s == h)
                def _():
                    for copy in swap(h):
                        copy.start()

                @pl.when(s == 2 + h)
                def _():
                    for copy in store(h):
                        copy.start()

    d_x, finish = ring.scatter(partial, land, scatter_sem, work)
    ring.settle()
    d_values, gain_ref[...] = normal_back(d_x, middle_ref[...], gain_row(params_ref, 1, layer))
    grad = grad_ref[...].astype(F32) + d_values
    mid_ref[...] = grad
    branch_ref[...] = grad.astype(BF16)
    drain()
    finish()
    for copy in crossings:
        copy.wait()
    for half in range(2):
        for copy in swap(half):
            copy.wait_send()
        for copy in store(half):
            copy.wait()


def gather_mix_back_scatter(count, layer, replicas, d, side, m_all, share, params, grad, middle, weights, rides):
    rows, width = d.shape
    ff = weights[0].shape[3]
    everyone = pltpu.VMEM((count, rows, width), BF16)
    groups = width // ff
    own = cells((rows, width), F32)
    return ring_call(
        functools.partial(mix_back_kernel, count, layer, replicas),
        ("mix_back", layer),
        [(d, ANYWHERE), (side, ANYWHERE), (m_all, ANYWHERE), (share, EARLY), (params, EARLY), (grad, LATE), (middle, LATE)]
        + [(w, ANYWHERE) for w in weights],
        [
            (own, OUT),
            (cells((rows, width), BF16), OUT),
            (cells((1, width), F32), OUT),
            (cells((width // 4, ff), BF16), ANYWHERE),
            (cells((3 * width - width // 4, ff), BF16), ANYWHERE),
            (cells((2, width), F32), OUT),
        ]
        + ([(cells((width // 4, ff), BF16), ANYWHERE)] if crosses_early(layer, replicas) else []),
        [everyone, everyone, land_scratch(count, rows, width), pltpu.VMEM((2 * rows, width), F32)]
        + expert_scratch(weights)
        + [
            everyone,
            pltpu.VMEM((2, count, rows, 2 * ff), BF16),
            pltpu.VMEM((2, count, rows, ff), BF16),
            pltpu.VMEM((count,) + side.shape, F32),
            pltpu.VMEM((2, 3 * width, ff), BF16),
            pltpu.VMEM((3 * width, ff), BF16),
        ]
        + gather_sems(count, True)
        + scatter_sems(count)
        + dmas((4,), (2, 2 + groups), (2, 2 + groups), (3,), (3,), (1,), (1,), (2, 3 + groups)),
        60,
        rides,
    )


def load_out_weights(w_ref, layer, wide_ref, sem, start=True):
    shard = w_ref.shape[2]
    copies = [
        pltpu.make_async_copy(w_ref.at[core, layer], wide_ref.at[pl.ds(core * shard, shard)], sem.at[core])
        for core in range(2)
    ]
    for copy in copies if start else []:
        copy.start()
    used = 2 * shard
    wide_ref[used:] = jnp.zeros((wide_ref.shape[0] - used, wide_ref.shape[1]), BF16)
    return copies


def attend_back_kernel(count, layer, traffic, *refs):
    inputs, outputs, scratch = split(refs, 17, 5)
    d_ref, w_out_ref, w_ref, x_ref, att_ref, q_ref, own_ref, other_ref, begin_ref, lse_ref, table_ref = inputs[:11]
    params_ref, mid_ref, hidden_ref, mixed_ref, router_ref, gain_two_ref = inputs[11:]
    g_out_ref, grad_ref, d_mix_ref, side_ref, g_ref = outputs
    buf, wide_w, g_acc, out_mail, out_got, turned_ref, d_own, d_other, mail, got, dq_ref = scratch[:11]
    partial, land, rows_ref, tokens, weights, last_ref = scratch[11:17]
    sems, scatter_sem, pair_sem, load_sem = split(scratch[17:], 3, 2, 2)
    ring = Ring(count, traffic)
    shard = g_out_ref.shape[0]
    loads = load_out_weights(w_out_ref, layer, wide_w, load_sem[0])
    later = [
        pltpu.make_async_copy(x_ref, tokens, load_sem[0].at[2]),
        pltpu.make_async_copy(w_ref.at[layer], weights, load_sem[0].at[3]),
    ]
    for load in later:
        load.start()
    ring.meet(True)
    core = lax.rem(lax.axis_index("fsdp"), 2)
    width = GROUP * LANES

    def spread(wide):
        front, back = wide[:, :LANES], wide[:, LANES:]
        low = lanes_of(front) < HD
        return [jnp.where(low, 0.0, part) for part in (turn(front), front, turn(back))]

    def compute(block):
        d = buf[block]
        wide = dot(d, wide_w[...], NT).astype(BF16)
        g_acc[...] += dot(att_ref[block], d, TN)
        slopes, deltas = [], []
        for piece, a in zip(spread(wide.astype(F32)), spread(att_ref[block].astype(F32))):
            slopes.append(piece)
            deltas.append(jnp.sum((piece * a).T, 0, keepdims=True))
        datt = jnp.concatenate(slopes, 0).astype(BF16)
        delta = jnp.concatenate(deltas, 1)
        q = q_ref[block].reshape(width, LANES)
        both = jnp.concatenate([q, datt], 0)
        begin, query = query_rows(begin_ref, (block,), core)
        lse = lse_ref[block]

        def one(chunk, acc):
            keys = chunk_keys(own_ref, other_ref, chunk)
            scores = jnp.where(allowed_keys(begin, query, chunk, core), dot(keys, q, NT), MASKED)
            weight = jnp.exp(scores - lse)
            slope = (weight * (dot(keys, datt, NT) - delta)).astype(BF16)
            d_keys = dot(jnp.concatenate([slope, weight.astype(BF16)], 1), both)
            half = SPAN * LANES
            chips = pl.ds(chunk * SPAN, SPAN)
            d_own[chips] += d_keys[:half].reshape(SPAN, LANES, LANES)
            d_other[chips] += d_keys[half:].reshape(SPAN, LANES, LANES)
            return acc + dot(turned_ref[chunk], slope)

        acc = lax.fori_loop(0, chunks_of((block,)), one, jnp.zeros((LANES, width), F32)) * (HD**-0.5)
        heads = by_head(acc)
        low = lanes_of(heads[0]) < HD
        cosine, sine = angles(table_ref[block])
        front = spin(jnp.where(low, heads[0], turn(heads[1])), cosine, -sine)
        back = spin(jnp.where(low, heads[2], 0.0), cosine, -sine)
        dq_ref[block] = jnp.concatenate([front, back], 1).astype(BF16)

    def first(s):
        @pl.when(s == 1)
        def _():
            for load in loads:
                load.wait()
            turn_keys(own_ref, other_ref, turned_ref)
            g_acc[...] = jnp.zeros_like(g_acc)
            d_own[...] = jnp.zeros_like(d_own)
            d_other[...] = jnp.zeros_like(d_other)

        compute(ring.at(1 - s))

    def second(s):
        compute(ring.at(s))

    drain = ring.gather(d_ref, buf, sems, None, first, second)
    compute(ring.at(ring.steps))
    partner = partner_of("fsdp")
    mail[...] = d_other[...].astype(BF16)
    out_mail[...] = g_acc[pl.ds(pl.multiple_of((1 - core) * shard, 8), shard), :].astype(BF16)
    swaps = [
        remote(mail, got, pair_sem[0].at[0], pair_sem[1].at[0], partner),
        remote(out_mail, out_got, pair_sem[0].at[1], pair_sem[1].at[1], partner),
    ]
    for swap in swaps:
        swap.start()
    for load in later:
        load.wait()
    drain()
    swaps[0].wait()

    def join(blocks):
        rows = []
        for b in blocks:
            pair = d_own[b] + got[b].astype(F32)
            cosine, sine = angles(table_ref[b])
            keys = spin(pair, cosine, -sine)
            low = lanes_of(pair) < HD
            middle = jnp.where(low, dq_ref[b, :, LANES:].astype(F32), turn(keys))
            last = jnp.where(low, turn(pair), 0.0)
            rows.append(
                jnp.concatenate([dq_ref[b, :, :LANES], middle.astype(BF16), last.astype(BF16)], 1)
            )
            rows_ref[b] = rows[-1]
        total = dot(jnp.concatenate(rows, 0), weights[...], NT).astype(BF16)
        for block, part in cut(total, blocks):
            partial[block] = part

    join((ring.at(ring.steps), ring.chip))
    strip = g_ref.shape[0] // ring.steps
    tile = 2 * LANES

    def between():
        def one(index, carry):
            join(ring.pair(ring.steps - 1 - index))
            return carry

        lax.fori_loop(0, ring.steps - 1, one, 0)

    def work(s, place):
        if place == 0:
            rows = pl.ds(pl.multiple_of(s * strip, LANES), strip)
            value = dot(flat(tokens[:, :, rows]), flat(rows_ref[...]), TN)
            g_ref[rows, :tile] = value[:, :tile].astype(BF16)
            last_ref[rows] = value[:, tile:]

    d_x, finish = ring.scatter(partial, land, scatter_sem, work, between)
    swaps[1].wait()
    own = g_acc[pl.ds(pl.multiple_of(core * shard, 8), shard), :]
    g_out_ref[...] = (own + out_got[...].astype(F32)).astype(BF16)
    ring.settle()
    d_values, gain_one = normal_back(d_x, hidden_ref[...].astype(F32), gain_row(params_ref, 0, layer))
    grad = mid_ref[...] + d_values
    grad_ref[...] = grad
    d_mix = grad.astype(BF16)
    d_mix_ref[...] = d_mix
    balance = jnp.sum(mixed_ref[...] * d_mix.astype(F32), -1, keepdims=True)
    side_ref[...] = jnp.broadcast_to(as_line(balance), side_ref.shape)
    routers = router_ref[...]
    lines = [
        jnp.where(core == 0, routers[0:1], routers[1:2]),
        jnp.where(core == 0, routers[1:2], routers[0:1]),
        gain_one,
        gain_two_ref[...],
    ]
    features = g_ref.shape[0]
    tall = jnp.concatenate(
        [jnp.zeros((HD, features), F32)] + lines + [jnp.zeros((HD - len(lines), features), F32)], 0
    )
    g_ref[:, tile:] = (last_ref[...] + tall.T).astype(BF16)
    finish()


def gather_attend_back_scatter(
    count, layer, d, w_out, w, x_all, att, q, own, other, begin, lse, tables, late, rides=()
):
    _, rows, width = x_all.shape
    shard = w_out.shape[2]
    columns = w.shape[2]
    everyone = pltpu.VMEM((count, rows, width), BF16)
    early = [att, q, own, other, begin, lse, tables]
    pairs = cells((count, rows, LANES), BF16)
    return ring_call(
        functools.partial(attend_back_kernel, count, layer),
        ("attend_back", layer),
        [(a, ANYWHERE) for a in (d, w_out, w, x_all)] + [(a, EARLY) for a in early] + [(a, LATE) for a in late],
        [
            (cells((shard, width), BF16), OUT),
            (cells((rows, width), F32), OUT),
            (cells((rows, width), BF16), OUT),
            (cells((8, rows), F32), OUT),
            (cells(w.shape[1:], BF16), OUT),
        ],
        [
            everyone,
            pltpu.VMEM((2 * LANES, width), BF16),
            pltpu.VMEM((2 * LANES, width), F32),
            pltpu.VMEM((shard, width), BF16),
            pltpu.VMEM((shard, width), BF16),
            pltpu.VMEM((count // SPAN, LANES, SPAN * 2 * LANES), BF16),
            pltpu.VMEM(pairs.shape, F32),
            pltpu.VMEM(pairs.shape, F32),
            pltpu.VMEM(pairs.shape, BF16),
            pltpu.VMEM(pairs.shape, BF16),
            pltpu.VMEM((count, rows, 2 * LANES), BF16),
            everyone,
            land_scratch(count, rows, width),
            pltpu.VMEM((count, rows, columns), BF16),
            everyone,
            pltpu.VMEM(w.shape[1:], BF16),
            pltpu.VMEM((width, LANES), F32),
        ]
        + gather_sems(count)
        + scatter_sems(count)
        + dmas((2,), (2,), (4,)),
        60,
        rides,
    )


def finish_kernel(count, replicas, *refs):
    inputs, outputs, scratch = split(refs, 3, 2)
    mine, peer = outputs
    g_ref, early_ref, early_peer_ref, early, land, total = scratch[:6]
    pair_send, pair_recv, part_send, part_recv, rep_send, rep_recv, load_sem = scratch[6:]
    loads = [
        pltpu.make_async_copy(source, target, load_sem.at[i])
        for i, (source, target) in enumerate(zip(inputs, scratch))
    ]
    for load in loads:
        load.start()
    me = lax.axis_index("fsdp")
    chip, core = me // 2, lax.rem(me, 2)
    partner = partner_of("fsdp")

    def chip_at(offset):
        return lax.rem(chip + offset + count, count)

    def device(offset):
        return {"fsdp": chip_at(offset) * 2 + core}

    across = [partner_of("rep")] if replicas == 2 else []
    meet([device(offset) for offset in range(1, count)] + [partner] + across)
    swaps = [remote(inputs[0].at[:, 1 - core], land.at[0], pair_send.at[0], pair_recv.at[0], partner)]
    swaps[0].start()
    for load in loads:
        load.wait()
    for block in range(count):
        both = early_ref[block, 1 - core].astype(F32)
        if replicas == 2:
            both = both + early_peer_ref[block, 1 - core].astype(F32)
        early[block] = both.astype(BF16)
    swaps.append(remote(early, land.at[1], pair_send.at[1], pair_recv.at[1], partner))
    swaps[1].start()
    if replicas != 2:
        peer[...] = jnp.zeros_like(peer)
    sends = []
    for layer in range(2):
        swaps[layer].wait()
        for block in range(count):
            own = (g_ref, early_ref)[layer][block, core].astype(F32)
            if layer == 1 and replicas == 2:
                own = own + early_peer_ref[block, core].astype(F32)
            total[layer, block] = (own + land[layer, block].astype(F32)).astype(BF16)
        for offset in range(1, count):
            sends.append(
                remote(
                    total.at[layer, chip_at(offset)], mine.at[layer, chip],
                    part_send.at[layer, offset], part_recv.at[layer, offset], device(offset),
                )
            )
            sends[-1].start()
        mine[layer, chip] = total[layer, chip]

    def to_peer(offset):
        slot = chip_at(-offset)
        return remote(mine.at[0, slot], peer.at[slot], rep_send.at[offset], rep_recv.at[offset], across[0])

    for layer in range(2):
        for offset in range(count):
            if offset > 0:
                slot = mine.at[layer, chip_at(-offset)]
                remote(slot, slot, part_send.at[layer, offset], part_recv.at[layer, offset], partner).wait_recv()
            if layer == 0 and replicas == 2:
                to_peer(offset).start()
    if replicas == 2:
        for offset in range(count):
            to_peer(offset).wait()

    for send in sends:
        send.wait_send()


def finish_heads(count, replicas, g, early, early_peer):
    _, _, rows, columns = g.shape
    part = (LAYERS, count, rows, columns)
    dma = pltpu.SemaphoreType.DMA
    return pl.pallas_call(
        functools.partial(finish_kernel, count, replicas),
        out_shape=(cells(part, BF16), cells((count, rows, columns), BF16)),
        in_specs=[ANYWHERE] * 3,
        out_specs=[HERE] * 2,
        scratch_shapes=[
            pltpu.VMEM(g.shape, BF16),
            pltpu.VMEM(g.shape, BF16),
            pltpu.VMEM(g.shape, BF16),
            pltpu.VMEM((count, rows, columns), BF16),
            pltpu.VMEM(part, BF16),
            pltpu.VMEM(part, BF16),
            dma((2,)), dma((2,)), dma((2, count)), dma((2, count)), dma((count,)), dma((count,)), dma((3,)),
        ],
        compiler_params=pltpu.CompilerParams(
            collective_id=identity(("finish",)), has_side_effects=True, vmem_limit_bytes=60 << 20
        ),
        cost_estimate=FREE,
        name="finish_heads",
    )(g, early, early_peer)


def close_kernel(layers, count, *refs):
    n_experts = 0 if len(refs) == 2 * layers + 13 else 12 * layers
    inputs, heads_in, rows_in, experts_in, outputs = split(refs, 2 * layers, 2, 2, n_experts)
    mine, peer = heads_in
    out_ref, q_out, k_out, v_out, router_out, gain_one_out, gain_two_out = outputs[:7]
    for source, target in zip(rows_in, outputs[7:9]):
        target[...] = source[...]

    @pl.when(pl.program_id(0) == 0)
    def _():
        for layer in range(layers):
            own, got = inputs[2 * layer : 2 * layer + 2]
            out_ref[layer] = own[...].astype(F32) + got[...].astype(F32)

            def tiles(block):
                value = mine[layer, block].astype(F32)
                if layer == 0:
                    value = value + peer[block].astype(F32)
                return [value[:, i * LANES : (i + 1) * LANES] for i in range(3)]

            shard = mine.shape[2]
            gains = jnp.zeros((shard, LANES), F32)
            routers = jnp.zeros((shard, LANES), F32)
            for half in range(count // 2):
                a, b = tiles(2 * half), tiles(2 * half + 1)
                low = lanes_of(a[0]) < HD
                for chip, tile in ((2 * half, a[2]), (2 * half + 1, b[2])):
                    gains = gains + tile
                    moved = pltpu.roll(tile, (2 * chip - HD) % LANES, 1)
                    lane = lanes_of(moved)
                    routers = jnp.where((lane >= 2 * chip) & (lane < 2 * chip + 2), moved, routers)
                q_out[layer, :, 3 * half * LANES : 3 * (half + 1) * LANES] = jnp.concatenate(
                    [a[0], jnp.where(low, a[1], turn(b[0])), jnp.where(low, turn(b[0]), turn(b[1]))], 1
                )
                here = slice(half * LANES, (half + 1) * LANES)
                k_out[layer, :, here] = jnp.where(low, turn(a[1]), b[1])
                v_out[layer, :, here] = jnp.where(low, a[2], turn(b[2]))

            router_out[layer] = routers[:, : 2 * count]
            tall = jnp.concatenate([gains, jnp.zeros((LANES - shard, LANES), F32)], 0).T
            gain_one_out[layer : layer + 1, :] = tall[HD + 2 : HD + 3, :shard]
            gain_two_out[layer : layer + 1, :] = tall[HD + 3 : HD + 4, :shard]

    if experts_in:
        expert_refs = outputs[9:]
        for layer in range(layers):
            pairs = experts_in[layer * 12 : (layer + 1) * 12]
            sums = [pairs[i][...].astype(F32) + pairs[i + 6][...].astype(F32) for i in range(6)]
            early = pl.program_id(0) == 0
            expert_refs[0][layer, 0] = jnp.where(early, sums[0], sums[1])
            expert_refs[1][layer, 0] = sums[2]
            expert_refs[2][layer, 0] = jnp.concatenate(sums[3:], 1)


def close(count, outs, mine, peer, rows_out, experts):
    layers = len(outs)
    shard, width = outs[0][0].shape
    steps = 4

    def whole(shape):
        return pl.BlockSpec(shape, lambda i: (0,) * len(shape))

    arrays = [array for pair in outs for array in pair] + [mine, peer]
    specs = [whole(a.shape) for a in arrays]
    shapes = [
        (layers, shard, width),
        (layers, shard, count * GROUP * HD),
        (layers, shard, count * HD),
        (layers, shard, count * HD),
        (layers, shard, 2 * count),
        (layers, shard),
        (layers, shard),
    ]
    out_specs = [whole(shape) for shape in shapes]
    shapes = [cells(shape, F32) for shape in shapes] + [cells(a.shape, a.dtype) for a in rows_out]
    parts = [
        pl.BlockSpec((a.shape[0] // (steps if experts else 1), a.shape[1]), lambda i: (i, 0)) for a in rows_out
    ]
    arrays += rows_out
    specs += parts
    out_specs += parts
    if experts:
        (_, _), (rest, _) = experts[0]
        rows, ff = rest.shape
        tall, short = width // steps, ff // steps
        apart = width // steps
        groups = (rows + apart - 2 * width) // ff

        def at(first, length):
            return pl.BlockSpec((length, ff), lambda i: ((first - apart) // length + i, 0))

        parts = [
            pl.BlockSpec((tall, ff), lambda i: (0, 0)),
            pl.BlockSpec((tall, ff), lambda i: (jnp.maximum(i - 1, 0), 0)),
            at(width, tall),
        ] + [at(2 * width + g * ff, short) for g in range(groups)]
        for front, back in experts:
            for own, other in zip(front, back):
                arrays += [own] + [other] * (len(parts) - 1)
        specs += parts * (2 * layers)
        shapes += [cells((layers, 1, width, ff), F32)] * 2 + [cells((layers, 1, ff, width), F32)]
        tile = pl.BlockSpec((layers, 1, tall, ff), lambda i: (0, 0, i, 0))
        out_specs += [tile, tile, pl.BlockSpec((layers, 1, short, width), lambda i: (0, 0, i, 0))]
    return pl.pallas_call(
        functools.partial(close_kernel, layers, count),
        grid=(steps if experts else 1,),
        out_shape=tuple(shapes),
        in_specs=specs,
        out_specs=out_specs,
        compiler_params=pltpu.CompilerParams(vmem_limit_bytes=60 << 20),
        cost_estimate=FREE,
        name="close",
    )(*arrays)


def on_device(
    tokens,
    cotangent,
    positions,
    segments,
    routes,
    attn_gain,
    w_query,
    w_key,
    w_value,
    w_out,
    ffn_gain,
    router,
    w_gate,
    w_up,
    w_down,
):
    rows, width = tokens.shape
    devices = lax.axis_size("fsdp")
    replicas = lax.axis_size("rep")
    count = devices // 2
    me = lax.axis_index("fsdp")
    chip, core = me // 2, lax.rem(me, 2)
    shard = w_query.shape[1]
    experts = devices
    columns = 3 * LANES
    used = (GROUP + 2) * HD

    small = jnp.concatenate(
        [attn_gain, ffn_gain, router.transpose(0, 2, 1).reshape(LAYERS * experts, shard)], 0
    )
    small = jnp.pad(small, ((0, 48 - small.shape[0]), (0, LANES - shard)))
    rate = jnp.exp(-jnp.log(10000.0) * jnp.arange(HD // 2, dtype=F32) / (HD // 2))
    angle = rate[:, None] * positions.astype(F32)[None, :]
    table = jnp.concatenate([jnp.cos(angle), jnp.sin(angle)], 0)
    experts_w = [w_gate, w_up, w_down]

    flat_segments = segments.reshape(1, -1)
    kinds = jnp.arange(8, dtype=jnp.int32)[:, None]
    starts = jnp.sum((flat_segments < kinds).astype(jnp.int32), 1, keepdims=True)
    begin = jnp.sum(jnp.where(flat_segments == kinds, starts, 0), 0).reshape(count, 2, rows)
    begin = lax.dynamic_index_in_dim(begin, core, 1, True)

    chosen = routes.transpose(0, 2, 1)
    hidden = tokens
    saved = []
    for layer in range(LAYERS):
        if layer == 0:
            projections = [w_query, w_key, w_value]
            inputs = [(a, EARLY) for a in (tokens, *projections)]
            inputs += [(a, ANYWHERE) for a in (w_out, small, table)] + [(begin, EARLY), (chosen, LATE)]
            extra = opening_shapes(count, tokens, columns, w_out, small, table)
        else:
            inputs = [(a, ANYWHERE) for a in (x_attn, heads_w, outs_w)] + [(tables, EARLY), (begin, EARLY)]
            inputs += [(hidden, LATE), (params, LATE), (chosen, LATE)]
            extra = [], []
        results = forward(count, layer, inputs, rows, width, columns, experts_w, cotangent, extra)
        query, kv, kv_other, x_all, att, lse, middle, _, _ = results[:9]
        if layer == 0:
            heads_w, outs_w, tables, params = results[9:13]
        mixed, after, x_attn, m_all, share_all, *side = results[9 + len(extra[0]) :]
        saved.append((hidden, x_all, query, kv, kv_other, att, lse, middle, mixed, m_all, share_all))
        hidden = after
    activations = x_attn

    def across(array):
        return lax.ppermute(array, "rep", [(0, 1), (1, 0)]) if replicas == 2 else array

    grad = d_mix = cotangent
    (side,) = side
    expert_sums = [None] * LAYERS
    fronts = [None] * LAYERS
    out_sums = [None] * LAYERS
    for layer in reversed(range(LAYERS)):
        hidden, x_all, query, kv, kv_other, att, lse, middle, mixed, m_all, share_all = saved[layer]
        rides = [out_sums[layer + 1], early, fronts[layer + 1][0]] if layer + 1 < LAYERS and replicas == 2 else []
        grad_mid, d_branch, gain_two, front, expert_sum, g_router, *rode = gather_mix_back_scatter(
            count, layer, replicas, d_mix, side, m_all, share_all, params, grad, middle, experts_w, rides
        )
        if layer + 1 < LAYERS:
            d_branch, expert_sums[layer + 1] = lax.optimization_barrier(
                (d_branch, expert_sums[layer + 1])
            )
        fronts[layer] = (front, rode.pop(0) if crosses_early(layer, replicas) else front)
        if rides:
            fronts[layer + 1] = (fronts[layer + 1][0], rode[2])
        expert_sums[layer] = (expert_sum, across(expert_sum))
        out_sum, grad, d_mix, side, heads = gather_attend_back_scatter(
            count, layer, d_branch, outs_w, heads_w, x_all, att, query, kv, kv_other, begin, lse, tables,
            [params, grad_mid, hidden, saved[max(layer - 1, 0)][8], g_router, gain_two],
        )
        out_sums[layer] = out_sum
        heads = heads.reshape(count, 2, shard, columns)
        early = heads if layer > 0 else early
    arrived, peer = finish_heads(count, replicas, heads, early, rode[1] if rode else early)
    if replicas == 2:
        outs = list(zip(out_sums, [across(out_sums[0]), rode[0]]))
        *results, g_gate, g_up, g_down = close(
            count, outs, arrived, peer, [activations, grad], list(zip(fronts, expert_sums))
        )
    else:
        outs = [(own, jnp.zeros_like(own)) for own in out_sums]
        results = close(count, outs, arrived, peer, [activations, grad], [])
        sums = (*results[:7], jnp.stack([jnp.concatenate([a, b]) for (a, _), (b, _) in zip(fronts, expert_sums)]))
        *summed, flat_sums = [lax.psum(array.astype(BF16), "rep").astype(F32) for array in sums]
        results = summed + list(results[7:])
        ff = w_gate.shape[3]
        g_gate, g_up = flat_sums[:, None, :width], flat_sums[:, None, width : 2 * width]
        g_down = flat_sums[:, 2 * width :].reshape(LAYERS, width // ff, ff, ff)
        g_down = g_down.transpose(0, 2, 1, 3).reshape(LAYERS, 1, ff, width)
    g_out, g_query, g_key, g_value, g_router, gain_one, gain_two, activations, grad = results
    return (
        activations,
        grad,
        gain_one,
        g_query,
        g_key,
        g_value,
        g_out,
        gain_two,
        g_router,
        g_gate,
        g_up,
        g_down,
    )


def solution(mesh):
    placed = (
        P(("rep", "fsdp"), None),
        P(("rep", "fsdp"), None),
        P(("rep", "fsdp")),
        P("rep", None),
        P(None, ("rep", "fsdp"), None),
        P(None, "fsdp"),
        P(None, "fsdp", None),
        P(None, "fsdp", None),
        P(None, "fsdp", None),
        P(None, "fsdp", None),
        P(None, "fsdp"),
        P(None, "fsdp", None),
        P(None, "fsdp", None, None),
        P(None, "fsdp", None, None),
        P(None, "fsdp", None, None),
    )
    return jax.shard_map(
        on_device,
        mesh=mesh,
        in_specs=placed,
        out_specs=(
            P(("rep", "fsdp"), None),
            P(("rep", "fsdp"), None),
            P(None, "fsdp"),
            P(None, "fsdp", None),
            P(None, "fsdp", None),
            P(None, "fsdp", None),
            P(None, "fsdp", None),
            P(None, "fsdp"),
            P(None, "fsdp", None),
            P(None, "fsdp", None, None),
            P(None, "fsdp", None, None),
            P(None, "fsdp", None, None),
        ),
        check_vma=False,
    )
```

```python
import functools

import jax
import jax.numpy as jnp
from jax import lax
from jax.experimental import pallas as pl
from jax.experimental.pallas import tpu as pltpu
from jax.sharding import PartitionSpec as P

HEADS = 24
KV_HEADS = 8
HD = 64
LAYERS = 2
GROUP = HEADS // KV_HEADS
LANES = 128
SPAN = 2
EPS = 1e-06
MASKED = -1e30
MESH = pl.DeviceIdType.MESH
F32 = jnp.float32
BF16 = jnp.bfloat16


def ring_place(chip, count):
    return lax.select(lax.rem(chip, 2) == 0, chip // 2, count - 1 - chip // 2)


def ring_chip(place, count):
    return lax.select(place < count // 2, 2 * place, 2 * (count - 1 - place) + 1)


def ring_setup(count):
    me = lax.axis_index("fsdp")
    chip, core = me // 2, lax.rem(me, 2)
    place = ring_place(chip, count)

    def at(offset):
        return ring_chip(lax.rem(place + offset + 2 * count, count), count)

    near = [{"fsdp": at(1) * 2 + core}, {"fsdp": at(-1) * 2 + core}]
    return chip, at, near


def partner_of(axis):
    if axis == "rep":
        return {"rep": 1 - lax.axis_index("rep")}
    me = lax.axis_index("fsdp")
    return {"fsdp": me + 1 - 2 * lax.rem(me, 2)}


def meet(others):
    barrier = pltpu.get_barrier_semaphore()
    for other in others:
        pl.semaphore_signal(barrier, inc=1, device_id=other, device_id_type=MESH)
    pl.semaphore_wait(barrier, len(others))


def remote(src, dst, send_sem, recv_sem, device):
    return pltpu.make_async_remote_copy(
        src_ref=src,
        dst_ref=dst,
        send_sem=send_sem,
        recv_sem=recv_sem,
        device_id=device,
        device_id_type=MESH,
    )


def ring_hops(count):
    half = count // 2
    return {(0, 0): half, (1, 1): half, (0, 1): half - 1, (1, 0): half - 1}


IDENTITIES = {}


def identity(key):
    return IDENTITIES.setdefault(key, len(IDENTITIES))


class Ring:
    def __init__(self, count, traffic):
        self.count = count
        self.riders, self.early, self.late, self.soon = traffic
        self.steps = count // 2
        self.chip, self.at, self.near = ring_setup(count)

    def meet(self, partner=False, everyone=None, across=False):
        others = everyone or self.near + ([partner_of("fsdp")] if partner else [])
        meet(others + ([partner_of("rep")] if self.riders or across else []))
        for rider in self.riders:
            rider.start()
        for copy in self.early:
            copy.wait()

    def settle(self):
        for copy in self.late:
            copy.wait()

    def depart(self):
        for copy in self.soon:
            copy.start()

    def gather(self, x_ref, buf, sems, side=None, first=None, second=None):
        own_sem, send_sem, recv_sem = sems[:3]
        half_rows = x_ref.shape[0] // 2
        steps = self.steps
        own = [pltpu.make_async_copy(x_ref, buf.at[self.chip], own_sem.at[0])]
        if side is not None:
            side_ref, side_buf = side
            side_send, side_recv = sems[3:]
            own.append(pltpu.make_async_copy(side_ref, side_buf.at[self.chip], own_sem.at[1]))
        for copy in own:
            copy.start()

        def piece(key, step, block, source=None):
            direction, part = key
            rows = pl.ds(part * half_rows, half_rows)
            target = buf.at[block, rows]
            return remote(
                target if source is None else source.at[rows],
                target,
                send_sem.at[direction, part, step],
                recv_sem.at[direction, part, step],
                self.near[direction],
            )

        def side_piece(direction, step, block, source=None):
            target = side_buf.at[block]
            return remote(
                target if source is None else source,
                target,
                side_send.at[direction, step],
                side_recv.at[direction, step],
                self.near[direction],
            )

        def toward(key, places):
            return self.at(-places if key[0] == 0 else places)

        early, late = [(0, 0), (1, 1)], [(0, 1), (1, 0)]
        if side is not None:
            for direction in range(2):
                side_piece(direction, 0, self.chip, side_ref).start()
        for key in early + late:
            piece(key, 0, self.chip, x_ref).start()

        def take(keys, s, last):
            for key in keys:
                block = toward(key, s)
                piece(key, s - 1, block).wait_recv()

                @pl.when(s < last)
                def _():
                    piece(key, s, block).start()

        def take_side(s):
            if side is not None:
                for direction in range(2):

                    @pl.when(s <= steps - direction)
                    def _():
                        block = toward((direction, 0), s)
                        side_piece(direction, s - 1, block).wait_recv()

                        @pl.when(s < steps - direction)
                        def _():
                            side_piece(direction, s, block).start()

        def step(s, carry):
            take_side(s)
            take(early, s, steps)
            first(s)
            take(late, s, steps - 1)
            second(s)
            return carry

        for copy in own:
            copy.wait()
        lax.fori_loop(1, steps, step, 0)
        first(steps)
        take_side(steps)
        take(early, steps, steps)

        def drain():
            for s in range(steps):
                for key in early + (late if s < steps - 1 else []):
                    piece(key, s, toward(key, s)).wait_send()
                if side is not None:
                    for direction in range(2):
                        if s < steps - direction:
                            side_piece(direction, s, toward((direction, 0), s)).wait_send()

        return drain

    def pair(self, s):
        return self.at(s), self.at(-s)

    def meanwhile(self, compute, ready):
        def first(s):
            @pl.when(s == 1)
            def _():
                compute(0, (self.chip,))

            @pl.when(s > 1)
            def _():
                compute(1, self.pair(s - 1))

        def second(s):
            @pl.when(s == 1)
            def _():
                ready()
                compute(1, (self.chip,))

            compute(0, self.pair(s))

        return first, second

    def scatter(self, partial, land, sems, work=None, between=None):
        send_sem, recv_sem = sems
        half_rows = partial.shape[1] // 2
        steps = self.steps
        hops = ring_hops(self.count)

        def ahead(key, s):
            places = hops[key] - s
            return self.at(places if key[0] == 0 else -places)

        def piece(key, s, source):
            direction, part = key
            return remote(
                source,
                land.at[direction, part, s],
                send_sem.at[direction, part, s],
                recv_sem.at[direction, part, s],
                self.near[direction],
            )

        def rows_of(key):
            return pl.ds(key[1] * half_rows, half_rows)

        for place, key in enumerate(hops):
            if place == 2 and between is not None:
                between()
            piece(key, 0, partial.at[ahead(key, 0), rows_of(key)]).start()

        def step(s, carry):
            for place, key in enumerate(hops):
                if work is not None:
                    work(s - 1, place)

                @pl.when(s < hops[key])
                def _():
                    slot = land.at[key[0], key[1], s - 1]
                    piece(key, s - 1, slot).wait_recv()
                    mine = partial[ahead(key, s), rows_of(key)]
                    slot[...] = (slot[...].astype(F32) + mine.astype(F32)).astype(BF16)
                    piece(key, s, slot).start()

            return carry

        lax.fori_loop(1, steps + 1, step, 0)
        for key in hops:
            slot = land.at[key[0], key[1], hops[key] - 1]
            piece(key, hops[key] - 1, slot).wait_recv()
        halves = []
        for part in range(2):
            rows = pl.ds(part * half_rows, half_rows)
            total = partial[self.chip, rows].astype(F32)
            for direction in range(2):
                total = total + land[direction, part, hops[direction, part] - 1].astype(F32)
            halves.append(total)
        summed = jnp.concatenate(halves, 0)

        def drain():
            for key in hops:
                for s in range(hops[key]):
                    piece(key, s, land.at[key[0], key[1], s]).wait_send()

        return summed, drain


def dmas(*shapes):
    return [pltpu.SemaphoreType.DMA(shape) for shape in shapes]


def gather_sems(count, sided=False):
    steps = count // 2
    shapes = [(2,), (2, 2, steps), (2, 2, steps)]
    return dmas(*(shapes + ([(2, steps), (2, steps)] if sided else [])))


def scatter_sems(count):
    return dmas((2, 2, count // 2), (2, 2, count // 2))


ANYWHERE = pl.BlockSpec(memory_space=pltpu.HBM)
HERE = pl.BlockSpec(memory_space=pltpu.VMEM)
EARLY, LATE = "early", "late"
OUT, SOON = "out", "soon"


FREE = pl.CostEstimate(flops=0, bytes_accessed=0, transcendentals=0)


def ring_call(body, key, inputs, outputs, scratch, megabytes, rides=()):
    n_in, n_out, n_rides = len(inputs), len(outputs), len(rides)
    in_kinds = [kind for _, kind in inputs]
    out_kinds = [kind for _, kind in outputs]
    copied = [a for a, kind in inputs if kind in (EARLY, LATE)]
    returned = [a for a, kind in outputs if kind in (OUT, SOON)]
    moves = len(copied) + len(returned)

    def kernel(*refs):
        ins, ride_in, outs, ride_out, rest = split(refs, n_in, n_rides, n_out, n_rides)
        rest, own, rest_sems = rest[: len(scratch)], rest[len(scratch) : len(scratch) + moves], rest[len(scratch) + moves :]
        move_sem, rest_sems = rest_sems[0], rest_sems[1:]
        riders = []
        if n_rides:
            send_sem, recv_sem = rest_sems
            riders = [
                remote(ride_in[i], ride_out[i], send_sem.at[i], recv_sem.at[i], partner_of("rep"))
                for i in range(n_rides)
            ]
        used = 0
        early, late, leaving, soon = [], [], [], []
        ins, outs = list(ins), list(outs)
        for i, kind in enumerate(in_kinds):
            if kind in (EARLY, LATE):
                copy = pltpu.make_async_copy(ins[i], own[used], move_sem.at[used])
                copy.start()
                (early if kind == EARLY else late).append(copy)
                ins[i] = own[used]
                used += 1
        for i, kind in enumerate(out_kinds):
            if kind in (OUT, SOON):
                copy = pltpu.make_async_copy(own[used], outs[i], move_sem.at[used])
                (leaving if kind == OUT else soon).append(copy)
                outs[i] = own[used]
                used += 1
        body((riders, early, late, soon), *ins, *outs, *rest)
        for copy in leaving:
            copy.start()
        for rider in riders:
            rider.wait()
        for copy in leaving + soon:
            copy.wait()

    def spec(kind):
        return ANYWHERE if isinstance(kind, str) else kind

    return pl.pallas_call(
        kernel,
        out_shape=tuple(shape for shape, _ in outputs) + tuple(cells(a.shape, a.dtype) for a in rides),
        in_specs=[spec(kind) for kind in in_kinds] + [ANYWHERE] * n_rides,
        out_specs=[spec(kind) for kind in out_kinds] + [ANYWHERE] * n_rides,
        scratch_shapes=list(scratch)
        + [pltpu.VMEM(a.shape, a.dtype) for a in copied + returned]
        + dmas((max(moves, 1),))
        + (dmas((n_rides,), (n_rides,)) if n_rides else []),
        compiler_params=pltpu.CompilerParams(
            collective_id=identity(key),
            has_side_effects=True,
            vmem_limit_bytes=megabytes << 20,
        ),
        cost_estimate=FREE,
        name=key[0],
    )(*[array for array, _ in inputs], *rides)


def split(refs, *sizes):
    parts, place = [], 0
    for size in sizes:
        parts.append(refs[place : place + size])
        place += size
    return parts + [refs[place:]]


def cells(shape, dtype):
    return jax.ShapeDtypeStruct(shape, dtype)


def dot(left, right, contract=((1,), (0,))):
    return lax.dot_general(left, right, (contract, ((), ())), preferred_element_type=F32)


NT = ((1,), (1,))
TN = ((0,), (0,))


def lanes_of(field):
    return lax.broadcasted_iota(jnp.int32, field.shape, 1)


def turn(field):
    return pltpu.roll(field, HD, 1)


def spin(field, cosine, sine):
    swapped = jnp.where(
        lax.rem(lanes_of(field), HD) < HD // 2,
        -pltpu.roll(field, LANES - HD // 2, 1),
        pltpu.roll(field, HD // 2, 1),
    )
    return field * cosine + swapped * sine


def project_rows(rows, cosine, sine):
    first = spin(rows[:, :LANES], cosine, sine)
    second = spin(rows[:, LANES : 2 * LANES], cosine, sine)
    third = rows[:, 2 * LANES :]
    low = lanes_of(first) < HD
    heads = []
    for field in (first, turn(first), second):
        rounded = jnp.where(low, field, 0.0).astype(BF16).astype(F32)
        heads.append((rounded * (HD**-0.5)).astype(BF16))
    return heads, jnp.where(low, turn(second), turn(third)).astype(BF16)


def angles(table):
    rows = jnp.concatenate([table, table], 0).T
    early = lax.rem(lanes_of(rows), HD) < HD // 2
    cosine = jnp.where(early, rows, pltpu.roll(rows, HD // 2, 1))
    sine = jnp.where(early, pltpu.roll(rows, LANES - HD // 2, 1), rows)
    return cosine, sine


def normal(values):
    inverse = lax.rsqrt(jnp.mean(values * values, -1, keepdims=True) + EPS)
    return inverse, values * inverse


def normal_back(d_x, values, gain):
    inverse, normed = normal(values)
    d_norm = d_x * gain
    d_values = inverse * (d_norm - normed * jnp.mean(d_norm * normed, -1, keepdims=True))
    return d_values, jnp.sum(d_x * normed, 0, keepdims=True)


def diagonal():
    shape = (LANES, LANES)
    return lax.broadcasted_iota(jnp.int32, shape, 0) == lax.broadcasted_iota(jnp.int32, shape, 1)


def as_column(line):
    return jnp.sum(jnp.where(diagonal(), jnp.broadcast_to(line, (LANES, LANES)), 0.0), 1, keepdims=True)


def as_line(column):
    return jnp.sum(jnp.where(diagonal(), jnp.broadcast_to(column, (LANES, LANES)), 0.0), 0, keepdims=True)


def flat(value):
    return value.reshape(value.shape[0] * value.shape[1], value.shape[2])


def stack(ref, blocks):
    parts = [ref[b] for b in blocks]
    return parts[0] if len(parts) == 1 else jnp.concatenate(parts, 0)


def cut(value, blocks):
    return [(b, value[i * LANES : (i + 1) * LANES]) for i, b in enumerate(blocks)]


def gain_row(params_ref, kind, layer):
    row = kind * LAYERS + layer
    return params_ref[row : row + 1, :]


def router_rows(experts, layer):
    first = 2 * LAYERS + layer * experts
    return slice(first, first + experts)


def allowed_keys(begin, query, chunk, core):
    half = SPAN * LANES
    shape = (2 * half, begin.shape[1])
    place = lax.broadcasted_iota(jnp.int32, (2 * half, 1), 0)
    inner = lax.rem(place, half)
    whose = jnp.where(place < half, core, 1 - core)
    key = chunk * 2 * half + inner // LANES * (2 * LANES) + whose * LANES + lax.rem(inner, LANES)
    key = jnp.broadcast_to(key, shape)
    return (key >= begin) & (key <= query)


def query_rows(begin_ref, blocks, core):
    lane = lax.broadcasted_iota(jnp.int32, (1, LANES), 1)
    begin, query = [], []
    for block in blocks:
        begin += [begin_ref[block]] * GROUP
        query += [(2 * block + core) * LANES + lane] * GROUP
    return jnp.concatenate(begin, 1), jnp.concatenate(query, 1)


def chunk_keys(own_ref, other_ref, chunk):
    chips = pl.ds(chunk * SPAN, SPAN)
    return jnp.concatenate([flat(own_ref[chips]), flat(other_ref[chips])], 0)


def turn_keys(own_ref, other_ref, turned_ref):
    def one(chunk, carry):
        turned_ref[chunk] = chunk_keys(own_ref, other_ref, chunk).astype(F32).T.astype(BF16)
        return carry

    lax.fori_loop(0, turned_ref.shape[0], one, 0)


def by_head(field):
    return [field[:, h * LANES : (h + 1) * LANES].T for h in range(GROUP)]


def chunks_of(blocks):
    last = blocks[0] if len(blocks) == 1 else jnp.maximum(*blocks)
    return last // SPAN + 1


class Opening:
    def __init__(self, count, inputs, outputs, scratch):
        self.tokens_ref, *self.projections, self.out_w_ref, self.small_ref, self.table_ref = inputs
        self.heads_ref, self.outs_ref, self.tables_ref, self.params_ref = outputs
        (self.x_ref, self.slab_ref, self.smalls, self.weights, self.own_sem, self.slab_sem, self.pass_sem, self.small_sem,
         self.table_sem, self.out_sem) = scratch
        self.count = count
        self.devices = 2 * count
        self.me = lax.axis_index("fsdp")
        self.chip, self.core = self.me // 2, lax.rem(self.me, 2)
        self.partner = partner_of("fsdp")

    def device(self, offset):
        return {"fsdp": lax.rem(self.me + offset, self.devices)}

    def chip_at(self, offset):
        return lax.rem(self.chip + offset + self.count, self.count)

    def everyone(self):
        return [self.device(offset) for offset in range(1, self.devices)]

    def home(self, layer, origin):
        shard = self.slab_ref.shape[2]
        rows = pl.ds(pl.multiple_of(origin * shard, shard), shard)
        return self.weights.at[rows] if layer == 0 else self.heads_ref.at[layer, rows]

    def across(self, layer, offset, source=None, target=None):
        slot = self.home(layer, self.me) if source is None else source
        target = slot if target is None else target
        there = {"fsdp": self.chip_at(offset) * 2 + self.core}
        return remote(slot, target, self.slab_sem.at[0, offset, layer], self.slab_sem.at[1, offset, layer], there)

    def beside(self, layer, offset, slot, source=None):
        return remote(
            slot if source is None else source, slot,
            self.pass_sem.at[0, offset, layer], self.pass_sem.at[1, offset, layer], self.partner,
        )

    def small_to(self, offset, slot, source=None):
        return remote(
            slot if source is None else source, slot,
            self.small_sem.at[0, offset], self.small_sem.at[1, offset], self.device(offset),
        )

    def table_to(self, offset, slot, source=None):
        there = {"fsdp": self.chip_at(offset) * 2 + self.core}
        return remote(
            slot if source is None else source, slot,
            self.table_sem.at[0, offset], self.table_sem.at[1, offset], there,
        )

    def out_to(self, slot, source):
        return remote(source, slot, self.out_sem.at[0], self.out_sem.at[1], self.partner)

    def divide(self):
        for layer in range(LAYERS):
            query, key, value = [ref[layer].astype(F32) for ref in self.projections]
            for half in range(self.count // 2):
                first = 3 * half * LANES
                t = [query[:, first + i * LANES : first + (i + 1) * LANES] for i in range(3)]
                k, v = [a[:, half * LANES : (half + 1) * LANES] for a in (key, value)]
                low = lanes_of(k) < HD
                even = [t[0], jnp.where(low, t[1], turn(k)), jnp.where(low, v, 0.0)]
                odd = [
                    jnp.where(low, turn(t[1]), turn(t[2])),
                    jnp.where(low, turn(t[2]), k),
                    jnp.where(low, turn(v), 0.0),
                ]
                for place, tiles in enumerate((even, odd)):
                    self.slab_ref[2 * half + place, layer] = jnp.concatenate(tiles, 1).astype(BF16)

    def start(self):
        me, chip = self.me, self.chip
        self.divide()
        self.copies = [
            pltpu.make_async_copy(self.small_ref, self.smalls.at[me], self.own_sem.at[0]),
            pltpu.make_async_copy(self.table_ref, self.tables_ref.at[chip], self.own_sem.at[1]),
            pltpu.make_async_copy(self.out_w_ref, self.outs_ref.at[self.core], self.own_sem.at[2]),
        ] + [
            pltpu.make_async_copy(self.slab_ref.at[chip, layer], self.home(layer, me), self.own_sem.at[3 + layer])
            for layer in range(LAYERS)
        ]
        self.sends = [
            self.small_to(offset, self.smalls.at[me], self.small_ref) for offset in range(1, self.devices)
        ]
        for offset in range(1, self.count):
            self.sends.append(self.table_to(offset, self.tables_ref.at[chip], self.table_ref))
        for layer in range(LAYERS):
            for offset in range(1, self.count):
                slab = self.slab_ref.at[self.chip_at(offset), layer]
                self.sends.append(self.across(layer, offset, slab, self.home(layer, me)))
            self.sends.append(self.beside(layer, 0, self.home(layer, me), self.slab_ref.at[chip, layer]))
        self.sends.append(self.out_to(self.outs_ref.at[self.core], self.out_w_ref))
        for copy in self.copies + self.sends:
            copy.start()

    def parameters(self):
        for offset in range(1, self.devices):
            origin = lax.rem(self.me - offset + self.devices, self.devices)
            self.small_to(offset, self.smalls.at[origin]).wait_recv()
        self.copies[0].wait()
        shard = self.slab_ref.shape[2]
        width = self.params_ref.shape[1]
        shape = (LANES, width)
        feature = lax.broadcasted_iota(jnp.int32, shape, 1)
        spread = (lax.rem(feature, shard) == lax.broadcasted_iota(jnp.int32, shape, 0)).astype(F32).astype(BF16)
        owner = lax.broadcasted_iota(jnp.int32, self.params_ref.shape, 1) // shard
        self.params_ref[...] = jnp.zeros_like(self.params_ref)

        def one(device, carry):
            rows = dot(self.smalls[device], spread)
            self.params_ref[...] += jnp.where(owner == device, rows, 0.0)
            return carry

        lax.fori_loop(0, self.devices, one, 0)
        normed = normal(self.tokens_ref[...].astype(F32))[1]
        self.x_ref[...] = (normed * gain_row(self.params_ref, 0, 0)).astype(BF16)

    def forward(self, layer):
        for offset in range(1, self.count):
            slot = self.home(layer, self.chip_at(-offset) * 2 + self.core)
            self.across(layer, offset, slot).wait_recv()
            self.beside(layer, offset, slot).start()

    def arrived(self, layer):
        self.copies[3 + layer].wait()
        for offset in range(self.count):
            slot = self.home(layer, self.chip_at(-offset) * 2 + 1 - self.core)
            self.beside(layer, offset, slot).wait_recv()

    def rest(self):
        for offset in range(1, self.count):
            self.table_to(offset, self.tables_ref.at[self.chip_at(-offset)]).wait_recv()
        for copy in self.copies[1:3]:
            copy.wait()
        other = self.outs_ref.at[1 - self.core]
        self.out_to(other, other).wait_recv()

    def drain(self):
        for send in self.sends:
            send.wait_send()
        for layer in range(LAYERS):
            for offset in range(1, self.count):
                slot = self.home(layer, self.chip_at(-offset) * 2 + self.core)
                self.beside(layer, offset, slot).wait_send()


def attend_part(ring, count, layer, inputs, outputs, scratch, midway):
    if layer == 0:
        begin_ref, routes_ref = inputs[7:]
        hidden_ref, table_ref, params_ref = inputs[0], outputs[11], outputs[12]
    else:
        x_ref, w_ref, w_out_ref, table_ref, begin_ref, hidden_ref, params_ref, routes_ref = inputs
    q_ref, own_ref, other_ref, all_ref, att_ref, lse_ref, middle_ref, x_out_ref, share_ref = outputs[:9]
    buf, weights, wide_w, turned_ref, score_ref, partial, land = scratch[:7]
    sems, pair_sems, scatter_sem, out_sem, load_sem, more = split(scratch[7:], 3, 2, 2, 1, 1)[:5] + [scratch[16:]]
    partner = partner_of("fsdp")
    core = lax.rem(lax.axis_index("fsdp"), 2)

    def pass_on(block):
        return remote(
            own_ref.at[block], other_ref.at[block], pair_sems[0].at[block], pair_sems[1].at[block], partner
        )

    def project(blocks):
        rows = dot(stack(buf, blocks), weights[...])
        tables = [angles(table_ref[b]) for b in blocks]
        cosine = jnp.concatenate([t[0] for t in tables], 0)
        sine = jnp.concatenate([t[1] for t in tables], 0)
        heads, pair = project_rows(rows, cosine, sine)
        for index, head in enumerate(heads):
            for block, part in cut(head, blocks):
                q_ref[block, index] = part
        for block, part in cut(pair, blocks):
            own_ref[block] = part
            pass_on(block).start()

    if layer == 0:
        opening = Opening(count, inputs[:7], outputs[9:], [*more[:3], weights, *more[3:]])
        ring.meet(True, opening.everyone())
        opening.start()
        opening.parameters()
        loads = load_out_weights(outputs[10], layer, wide_w, load_sem[0], False)
        keep = [
            pltpu.make_async_copy(buf, all_ref, out_sem[0].at[0]),
            pltpu.make_async_copy(weights, outputs[9].at[0], out_sem[0].at[1]),
        ]

        def first(s):
            @pl.when(s == ring.steps - 1)
            def _():
                opening.rest()
                for load in loads:
                    load.start()
                opening.arrived(0)
                keep[1].start()
                project((ring.chip,))

            @pl.when(s == ring.steps)
            def _():
                project(ring.pair(ring.steps - 1))

        def second(s):
            @pl.when(s == ring.steps - 2)
            def _():
                opening.forward(0)

            @pl.when(s == ring.steps - 1)
            def _():
                def one(index, carry):
                    project(ring.pair(index))
                    return carry

                lax.fori_loop(1, ring.steps - 1, one, 0)

        drain = ring.gather(opening.x_ref, buf, sems, None, first, second)
        keep[0].start()
        project((ring.at(ring.steps),))
        for load in loads:
            load.wait()
    else:
        loads = [pltpu.make_async_copy(w_ref.at[layer], weights, load_sem[0].at[2])]
        loads[0].start()
        loads += load_out_weights(w_out_ref, layer, wide_w, load_sem[0])
        ring.meet(True)

        def first(s):
            @pl.when(s == 1)
            def _():
                for load in loads:
                    load.wait()
                project((ring.chip,))

        drain = ring.gather(x_ref, buf, sems, None, first, lambda s: project(ring.pair(s)))
        keep = [pltpu.make_async_copy(buf, all_ref, out_sem[0].at[0])]
        keep[0].start()
        project((ring.at(ring.steps),))
    for block in range(count):
        pass_on(block).wait()
    ring.depart()
    midway()
    turn_keys(own_ref, other_ref, turned_ref)

    def attend(blocks):
        width = len(blocks) * GROUP * LANES
        q = jnp.concatenate([q_ref[b].reshape(GROUP * LANES, LANES) for b in blocks], 0)
        begin, query = query_rows(begin_ref, blocks, core)
        end = chunks_of(blocks)

        def score(chunk, top):
            keys = chunk_keys(own_ref, other_ref, chunk)
            scores = jnp.where(allowed_keys(begin, query, chunk, core), dot(keys, q, NT), MASKED)
            score_ref[chunk, :, :width] = scores
            return jnp.maximum(top, jnp.max(scores, 0, keepdims=True))

        top = lax.fori_loop(0, end, score, jnp.full((1, width), MASKED, F32))

        def add(chunk, state):
            total, acc = state
            weights = jnp.exp(score_ref[chunk, :, :width] - top)
            total = total + jnp.sum(weights, 0, keepdims=True)
            return total, acc + dot(turned_ref[chunk], weights.astype(BF16))

        total, acc = lax.fori_loop(
            0, end, add, (jnp.zeros((1, width), F32), jnp.zeros((LANES, width), F32))
        )
        lse = top + jnp.log(total)
        att = acc / total
        rows = []
        for place, block in enumerate(blocks):
            here = slice(place * GROUP * LANES, (place + 1) * GROUP * LANES)
            lse_ref[block] = lse[:, here]
            heads = by_head(att[:, here])
            low = lanes_of(heads[0]) < HD
            rows.append(
                jnp.concatenate(
                    [jnp.where(low, turn(heads[0]), heads[1]), jnp.where(low, turn(heads[2]), 0.0)], 1
                ).astype(BF16)
            )
            att_ref[block] = rows[-1]
        out = dot(jnp.concatenate(rows, 0) if len(rows) > 1 else rows[0], wide_w[...]).astype(BF16)
        for block, part in cut(out, blocks):
            partial[block] = part

    attend((ring.at(ring.steps),))

    def between():
        if layer == 0:
            for later in range(1, LAYERS):
                opening.forward(later)
        attend(ring.pair(ring.steps - 1))

    def work(s, place):
        if place == 2:

            @pl.when(s < ring.steps - 2)
            def _():
                attend(ring.pair(ring.steps - 2 - s))

            @pl.when(s == ring.steps - 2)
            def _():
                attend((ring.chip,))

    added, finish = ring.scatter(partial, land, scatter_sem, work, between)
    ring.settle()
    middle = hidden_ref[...].astype(F32) + added
    middle_ref[...] = middle
    x = (normal(middle)[1] * gain_row(params_ref, 1, layer)).astype(BF16)
    x_out_ref[...] = x
    experts = share_ref.shape[0]
    logits = dot(params_ref[router_rows(experts, layer), :].astype(BF16), x, NT)
    expert = lax.broadcasted_iota(jnp.int32, logits.shape, 0)
    named = expert < 0
    for choice in range(routes_ref.shape[1]):
        named = named | (expert == routes_ref[layer, choice : choice + 1, :])
    scores = jnp.where(named, logits, MASKED)
    weighted = jnp.where(named, jnp.exp(scores - jnp.max(scores, 0, keepdims=True)), 0.0)
    share_ref[...] = weighted / jnp.sum(weighted, 0, keepdims=True)

    def end():
        drain()
        finish()
        for copy in keep:
            copy.wait()
        if layer == 0:
            for later in range(1, LAYERS):
                opening.arrived(later)
            opening.drain()

    return end


def attend_shapes(count, rows, width, columns, extra):
    block = cells((count, rows, LANES), BF16)
    everyone = pltpu.VMEM((count, rows, width), BF16)
    wide = 2 * LANES
    outputs = [
        (cells((count, GROUP, rows, LANES), BF16), SOON),
        (block, SOON),
        (block, SOON),
        (cells((count, rows, width), BF16), ANYWHERE),
        (cells((count, rows, wide), BF16), OUT),
        (cells((count, 1, GROUP * rows), F32), OUT),
        (cells((rows, width), F32), OUT),
        (cells((rows, width), BF16), OUT),
        (cells((2 * count, rows), F32), OUT),
    ]
    scratch = [
        everyone,
        pltpu.VMEM((width, columns), BF16),
        pltpu.VMEM((wide, width), BF16),
        pltpu.VMEM((count // SPAN, LANES, SPAN * wide), BF16),
        pltpu.VMEM((count // SPAN, SPAN * wide, 2 * GROUP * LANES), F32),
        everyone,
        land_scratch(count, rows, width),
    ]
    scratch += gather_sems(count) + dmas((count,), (count,)) + scatter_sems(count) + dmas((2,), (3,))
    return outputs + extra[0], scratch + extra[1]


def opening_shapes(count, tokens, columns, out_w, small, table):
    rows, width = tokens.shape
    layers, shard, _ = out_w.shape
    devices = 2 * count
    outputs = [
        (cells((layers, width, columns), BF16), ANYWHERE),
        (cells((2,) + out_w.shape, BF16), ANYWHERE),
        (cells((count,) + table.shape, F32), OUT),
        (cells((small.shape[0], width), F32), OUT),
    ]
    scratch = [
        pltpu.VMEM((rows, width), BF16),
        pltpu.VMEM((count, layers, shard, columns), BF16),
        pltpu.VMEM((devices,) + small.shape, BF16),
    ] + dmas((3 + layers,), (2, count, layers), (2, count, layers), (2, devices), (2, count), (2,))
    return outputs, scratch


def load_experts(refs, layer, bufs, sem):
    copies = [
        pltpu.make_async_copy(ref.at[layer, 0], buf.at[0], sem.at[place])
        for place, (ref, buf) in enumerate(zip(refs, bufs))
    ]
    for copy in copies:
        copy.start()
    return copies


def lend_experts(refs, layer, bufs, sems):
    copies = [
        remote(ref.at[layer, 0], buf.at[1], sems[0].at[place], sems[1].at[place], partner_of("fsdp"))
        for place, (ref, buf) in enumerate(zip(refs, bufs))
    ]
    for copy in copies:
        copy.start()
    return copies


def expert_of(e):
    me = lax.axis_index("fsdp")
    return me if e == 0 else me + 1 - 2 * lax.rem(me, 2)


def share_of(share_ref, e, blocks):
    columns = [as_column(share_ref[b, pl.ds(expert_of(e), 1), :]) for b in blocks]
    return jnp.concatenate(columns, 0) if len(columns) > 1 else columns[0]


def after_loads(loads, run):
    def first(s):
        @pl.when(s == 1)
        def _():
            for load in loads:
                load.wait()

        run(s)

    return first


def mix_part(ring, count, layer, given, cotangent, outputs, scratch, loads, lent):
    x_ref, side_ref, middle_ref, params_ref = given
    mixed_ref, hidden_ref, next_ref, all_ref, share_ref = outputs[:5]
    buf, partial, land, acc, gates, ups, downs = scratch[:7]
    sems, scatter_sem, out_sem = split(scratch[7:], 5, 2)

    def ready():
        for copy in lent:
            copy.wait()

    def compute(e, blocks):
        x = stack(buf, blocks)
        act_gate, act_up = dot(x, gates[e]), dot(x, ups[e])
        hidden = jax.nn.silu(act_gate) * act_up * share_of(share_ref, e, blocks)
        part = dot(hidden.astype(BF16), downs[e])
        if e == 0:
            acc[: x.shape[0]] = part
        else:
            total = (acc[: x.shape[0]] + part).astype(BF16)
            for block, rows in cut(total, blocks):
                partial[block] = rows

    first, second = ring.meanwhile(compute, ready)
    drain = ring.gather(x_ref, buf, sems, (side_ref, share_ref), after_loads(loads, first), second)
    keep = pltpu.make_async_copy(buf, all_ref, out_sem[0].at[0])
    keep.start()
    for e in range(2):
        compute(e, (ring.at(ring.steps),))
    mixed, finish = ring.scatter(partial, land, scatter_sem)
    mixed_ref[...] = mixed
    hidden = middle_ref[...] + mixed
    hidden_ref[...] = hidden
    if layer + 1 < LAYERS:
        next_ref[...] = (normal(hidden)[1] * gain_row(params_ref, 0, layer + 1)).astype(BF16)
    else:
        next_ref[...] = hidden.astype(BF16)
        balance = jnp.sum(mixed * cotangent[0][...].astype(F32), -1, keepdims=True)
        outputs[5][...] = jnp.broadcast_to(as_line(balance), outputs[5].shape)

    def end():
        drain()
        finish()
        keep.wait()

    return end


def expert_scratch(weights):
    return [pltpu.VMEM((2,) + w.shape[2:], BF16) for w in weights]


def land_scratch(count, rows, width):
    return pltpu.VMEM((2, 2, count // 2, rows // 2, width), BF16)


def mix_shapes(count, layer, rows, width, weights):
    everyone = pltpu.VMEM((count, rows, width), BF16)
    own = cells((rows, width), F32)
    outputs = [
        (own, OUT),
        (own, OUT),
        (cells((rows, width), BF16), OUT),
        (cells((count, rows, width), BF16), ANYWHERE),
        (cells((count, 2 * count, rows), F32), OUT),
    ]
    if layer + 1 == LAYERS:
        outputs.append((cells((8, rows), F32), OUT))
    scratch = [everyone, everyone, land_scratch(count, rows, width), pltpu.VMEM((2 * rows, width), F32)]
    scratch += expert_scratch(weights) + gather_sems(count, True) + scatter_sems(count) + dmas((1,))
    return outputs, scratch


def forward_kernel(count, layer, sizes, traffic, *refs):
    last = layer + 1 == LAYERS
    attend_in, weights, cotangent, attend_out, mix_out, scratch = split(
        refs, sizes[0], 3, int(last), sizes[1], sizes[2]
    )
    attend_scratch, mix_scratch, sems = split(scratch, sizes[3], sizes[4])
    bufs = mix_scratch[4:7]
    ring = Ring(count, traffic)
    loads = load_experts(weights, layer, bufs, sems[0])
    lent = []
    attend_end = attend_part(
        ring, count, layer, attend_in, attend_out, attend_scratch,
        lambda: lent.extend(lend_experts(weights, layer, bufs, sems[1:])),
    )
    params_ref = attend_out[12] if layer == 0 else attend_in[6]
    given = (attend_out[7], attend_out[8], attend_out[6], params_ref)
    mix_end = mix_part(ring, count, layer, given, cotangent, mix_out, mix_scratch, loads, lent)
    attend_end()
    mix_end()


def forward(count, layer, inputs, rows, width, columns, weights, cotangent, extra=([], [])):
    last = layer + 1 == LAYERS
    attend_out, attend_scratch = attend_shapes(count, rows, width, columns, extra)
    mix_out, mix_scratch = mix_shapes(count, layer, rows, width, weights)
    sizes = [len(part) for part in (inputs, attend_out, mix_out, attend_scratch, mix_scratch)]
    return ring_call(
        functools.partial(forward_kernel, count, layer, sizes),
        ("forward", layer),
        inputs + [(w, ANYWHERE) for w in weights] + ([(cotangent, LATE)] if last else []),
        attend_out + mix_out,
        attend_scratch + mix_scratch + dmas((3,), (3,), (3,)),
        60,
    )


def crosses_early(layer, replicas):
    return replicas == 2 and layer == 0


def mix_back_kernel(count, layer, replicas, traffic, *refs):
    crossing = crosses_early(layer, replicas)
    inputs, outputs, scratch = split(refs, 10, 6 + crossing)
    d_ref, side_ref, m_ref, share_ref, params_ref, grad_ref, middle_ref = inputs[:7]
    mid_ref, branch_ref, gain_ref, part_ref, sum_ref, g_router_ref = outputs[:6]
    buf, partial, land, acc, gates, ups, downs = scratch[:7]
    tokens, acts, hiddens, balance_ref, totals, got = scratch[7:13]
    sems, scatter_sem, load_sem, pair_sem, lend_sem, cross_sem, out_sem = split(scratch[13:], 5, 2, 1, 2, 2, 2)
    ring = Ring(count, traffic)
    loads = load_experts(inputs[7:], layer, (gates, ups, downs), load_sem[0])
    loads.append(pltpu.make_async_copy(m_ref, tokens, load_sem[0].at[3]))
    loads[-1].start()
    ring.meet(True, None, crossing)
    lent = lend_experts(inputs[7:], layer, (gates, ups, downs), lend_sem)

    def ready():
        for copy in lent:
            copy.wait()

    ff = gates.shape[2]
    width = buf.shape[2]
    g_router_ref[...] = jnp.zeros_like(g_router_ref)
    routers = 2 * LAYERS + layer * 2 * count

    def compute(e, blocks):
        d, x = stack(buf, blocks), stack(tokens, blocks)
        share = share_of(share_ref, e, blocks)
        balance = [as_column(balance_ref[b, 0:1, :]) for b in blocks]
        balance = jnp.concatenate(balance, 0) if len(balance) > 1 else balance[0]
        act_gate, act_up = dot(x, gates[e]), dot(x, ups[e])
        sig = jax.nn.sigmoid(act_gate)
        swish = act_gate * sig
        hidden = swish * act_up
        raw = dot(d, downs[e], NT)
        d_logit = share * (jnp.sum(hidden * raw, -1, keepdims=True) - balance)
        d_hidden = raw * share
        d_gate = (d_hidden * act_up * sig * (1.0 + act_gate * (1.0 - sig))).astype(BF16)
        d_up = (d_hidden * swish).astype(BF16)
        weighted = (hidden * share).astype(BF16)
        part = dot(d_gate, gates[e], NT) + dot(d_up, ups[e], NT)
        part = part + d_logit * params_ref[pl.ds(routers + expert_of(e), 1), :]
        g_router_ref[e : e + 1, :] += jnp.sum(d_logit * x.astype(F32), 0, keepdims=True)
        for place, block in enumerate(blocks):
            here = slice(place * LANES, (place + 1) * LANES)
            acts[e, block, :, :ff] = d_gate[here]
            acts[e, block, :, ff:] = d_up[here]
            hiddens[e, block] = weighted[here]
        if e == 0:
            acc[: x.shape[0]] = part
        else:
            total = (acc[: x.shape[0]] + part).astype(BF16)
            for block, rows in cut(total, blocks):
                partial[block] = rows

    first, second = ring.meanwhile(compute, ready)
    drain = ring.gather(d_ref, buf, sems, (side_ref, balance_ref), after_loads(loads, first), second)
    for e in range(2):
        compute(e, (ring.at(ring.steps),))

    partner = partner_of("fsdp")
    strip = 2 * LANES
    strips = width // (2 * strip)
    groups = width // ff

    def regions(half):
        regions = [(group * width + half * (width // 2), width // 2) for group in range(2)]
        return regions + [(2 * width + group * ff + half * (ff // 2), ff // 2) for group in range(groups)]

    def swap(half):
        return [
            remote(
                totals.at[1, pl.ds(first, length)], got.at[pl.ds(first, length)],
                pair_sem[0].at[half, index], pair_sem[1].at[half, index], partner,
            )
            for index, (first, length) in enumerate(regions(half))
        ]

    apart = width // 4

    def store(half):
        parts = []
        for first, length in regions(half):
            if first == 0:
                parts.append((pl.ds(0, apart), part_ref))
                parts.append((pl.ds(apart, length - apart), sum_ref.at[pl.ds(0, length - apart)]))
            else:
                parts.append((pl.ds(first, length), sum_ref.at[pl.ds(first - apart, length)]))
        return [
            pltpu.make_async_copy(totals.at[0, rows], target, out_sem[0].at[half, index])
            for index, (rows, target) in enumerate(parts)
        ]

    crossings = []
    if crossing:
        crossings.append(
            remote(
                totals.at[0, pl.ds(0, apart)], outputs[6],
                cross_sem[0].at[0], cross_sem[1].at[0], partner_of("rep"),
            )
        )

    def work(s, place):
        e = 1 - s // 2
        half = lax.rem(s, 2)

        def put(first, value):
            rows = pl.ds(pl.multiple_of(first, strip), strip)

            @pl.when(s < 2)
            def _():
                totals[1, rows] = value.astype(BF16)

            @pl.when(s >= 2)
            def _():
                totals[0, rows] = (value + got[rows].astype(F32)).astype(BF16)

        if place == 0:
            for h in range(2):

                @pl.when(s == 2 + h)
                def _():
                    for copy in swap(h):
                        copy.wait_recv()

        if place == 2:

            @pl.when(s == 2)
            def _():
                for copy in crossings:
                    copy.start()

        if place < strips:
            first = (half * strips + place) * strip
            columns = pl.ds(pl.multiple_of(first, strip), strip)
            value = dot(flat(tokens[:, :, columns]), flat(acts[e]), TN)
            for group in range(2):
                put(group * width + first, value[:, group * ff : (group + 1) * ff])
        if place == 3:
            columns = pl.ds(pl.multiple_of(half * strip, strip), strip)
            value = dot(flat(hiddens[e, :, :, columns]), flat(buf[...]), TN)
            for group in range(groups):
                put(2 * width + group * ff + half * strip, value[:, group * ff : (group + 1) * ff])
            for h in range(2):

                @pl.when(s == h)
                def _():
                    for copy in swap(h):
                        copy.start()

                @pl.when(s == 2 + h)
                def _():
                    for copy in store(h):
                        copy.start()

    d_x, finish = ring.scatter(partial, land, scatter_sem, work)
    ring.settle()
    d_values, gain_ref[...] = normal_back(d_x, middle_ref[...], gain_row(params_ref, 1, layer))
    grad = grad_ref[...].astype(F32) + d_values
    mid_ref[...] = grad
    branch_ref[...] = grad.astype(BF16)
    drain()
    finish()
    for copy in crossings:
        copy.wait()
    for half in range(2):
        for copy in swap(half):
            copy.wait_send()
        for copy in store(half):
            copy.wait()


def gather_mix_back_scatter(count, layer, replicas, d, side, m_all, share, params, grad, middle, weights, rides):
    rows, width = d.shape
    ff = weights[0].shape[3]
    everyone = pltpu.VMEM((count, rows, width), BF16)
    groups = width // ff
    own = cells((rows, width), F32)
    return ring_call(
        functools.partial(mix_back_kernel, count, layer, replicas),
        ("mix_back", layer),
        [(d, ANYWHERE), (side, ANYWHERE), (m_all, ANYWHERE), (share, EARLY), (params, EARLY), (grad, LATE), (middle, LATE)]
        + [(w, ANYWHERE) for w in weights],
        [
            (own, OUT),
            (cells((rows, width), BF16), OUT),
            (cells((1, width), F32), OUT),
            (cells((width // 4, ff), BF16), ANYWHERE),
            (cells((3 * width - width // 4, ff), BF16), ANYWHERE),
            (cells((2, width), F32), OUT),
        ]
        + ([(cells((width // 4, ff), BF16), ANYWHERE)] if crosses_early(layer, replicas) else []),
        [everyone, everyone, land_scratch(count, rows, width), pltpu.VMEM((2 * rows, width), F32)]
        + expert_scratch(weights)
        + [
            everyone,
            pltpu.VMEM((2, count, rows, 2 * ff), BF16),
            pltpu.VMEM((2, count, rows, ff), BF16),
            pltpu.VMEM((count,) + side.shape, F32),
            pltpu.VMEM((2, 3 * width, ff), BF16),
            pltpu.VMEM((3 * width, ff), BF16),
        ]
        + gather_sems(count, True)
        + scatter_sems(count)
        + dmas((4,), (2, 2 + groups), (2, 2 + groups), (3,), (3,), (1,), (1,), (2, 3 + groups)),
        60,
        rides,
    )


def load_out_weights(w_ref, layer, wide_ref, sem, start=True):
    shard = w_ref.shape[2]
    copies = [
        pltpu.make_async_copy(w_ref.at[core, layer], wide_ref.at[pl.ds(core * shard, shard)], sem.at[core])
        for core in range(2)
    ]
    for copy in copies if start else []:
        copy.start()
    used = 2 * shard
    wide_ref[used:] = jnp.zeros((wide_ref.shape[0] - used, wide_ref.shape[1]), BF16)
    return copies


def attend_back_kernel(count, layer, traffic, *refs):
    inputs, outputs, scratch = split(refs, 17, 5)
    d_ref, w_out_ref, w_ref, x_ref, att_ref, q_ref, own_ref, other_ref, begin_ref, lse_ref, table_ref = inputs[:11]
    params_ref, mid_ref, hidden_ref, mixed_ref, router_ref, gain_two_ref = inputs[11:]
    g_out_ref, grad_ref, d_mix_ref, side_ref, g_ref = outputs
    buf, wide_w, g_acc, out_mail, out_got, turned_ref, d_own, d_other, mail, got, dq_ref = scratch[:11]
    partial, land, rows_ref, tokens, weights, last_ref = scratch[11:17]
    sems, scatter_sem, pair_sem, load_sem = split(scratch[17:], 3, 2, 2)
    ring = Ring(count, traffic)
    shard = g_out_ref.shape[0]
    loads = load_out_weights(w_out_ref, layer, wide_w, load_sem[0])
    later = [
        pltpu.make_async_copy(x_ref, tokens, load_sem[0].at[2]),
        pltpu.make_async_copy(w_ref.at[layer], weights, load_sem[0].at[3]),
    ]
    for load in later:
        load.start()
    ring.meet(True)
    core = lax.rem(lax.axis_index("fsdp"), 2)
    width = GROUP * LANES

    def spread(wide):
        front, back = wide[:, :LANES], wide[:, LANES:]
        low = lanes_of(front) < HD
        return [jnp.where(low, 0.0, part) for part in (turn(front), front, turn(back))]

    def compute(block):
        d = buf[block]
        wide = dot(d, wide_w[...], NT).astype(BF16)
        g_acc[...] += dot(att_ref[block], d, TN)
        slopes, deltas = [], []
        for piece, a in zip(spread(wide.astype(F32)), spread(att_ref[block].astype(F32))):
            slopes.append(piece)
            deltas.append(jnp.sum((piece * a).T, 0, keepdims=True))
        datt = jnp.concatenate(slopes, 0).astype(BF16)
        delta = jnp.concatenate(deltas, 1)
        q = q_ref[block].reshape(width, LANES)
        both = jnp.concatenate([q, datt], 0)
        begin, query = query_rows(begin_ref, (block,), core)
        lse = lse_ref[block]

        def one(chunk, acc):
            keys = chunk_keys(own_ref, other_ref, chunk)
            scores = jnp.where(allowed_keys(begin, query, chunk, core), dot(keys, q, NT), MASKED)
            weight = jnp.exp(scores - lse)
            slope = (weight * (dot(keys, datt, NT) - delta)).astype(BF16)
            d_keys = dot(jnp.concatenate([slope, weight.astype(BF16)], 1), both)
            half = SPAN * LANES
            chips = pl.ds(chunk * SPAN, SPAN)
            d_own[chips] += d_keys[:half].reshape(SPAN, LANES, LANES)
            d_other[chips] += d_keys[half:].reshape(SPAN, LANES, LANES)
            return acc + dot(turned_ref[chunk], slope)

        acc = lax.fori_loop(0, chunks_of((block,)), one, jnp.zeros((LANES, width), F32)) * (HD**-0.5)
        heads = by_head(acc)
        low = lanes_of(heads[0]) < HD
        cosine, sine = angles(table_ref[block])
        front = spin(jnp.where(low, heads[0], turn(heads[1])), cosine, -sine)
        back = spin(jnp.where(low, heads[2], 0.0), cosine, -sine)
        dq_ref[block] = jnp.concatenate([front, back], 1).astype(BF16)

    def first(s):
        @pl.when(s == 1)
        def _():
            for load in loads:
                load.wait()
            turn_keys(own_ref, other_ref, turned_ref)
            g_acc[...] = jnp.zeros_like(g_acc)
            d_own[...] = jnp.zeros_like(d_own)
            d_other[...] = jnp.zeros_like(d_other)

        compute(ring.at(1 - s))

    def second(s):
        compute(ring.at(s))

    drain = ring.gather(d_ref, buf, sems, None, first, second)
    compute(ring.at(ring.steps))
    partner = partner_of("fsdp")
    mail[...] = d_other[...].astype(BF16)
    out_mail[...] = g_acc[pl.ds(pl.multiple_of((1 - core) * shard, 8), shard), :].astype(BF16)
    swaps = [
        remote(mail, got, pair_sem[0].at[0], pair_sem[1].at[0], partner),
        remote(out_mail, out_got, pair_sem[0].at[1], pair_sem[1].at[1], partner),
    ]
    for swap in swaps:
        swap.start()
    for load in later:
        load.wait()
    drain()
    swaps[0].wait()

    def join(blocks):
        rows = []
        for b in blocks:
            pair = d_own[b] + got[b].astype(F32)
            cosine, sine = angles(table_ref[b])
            keys = spin(pair, cosine, -sine)
            low = lanes_of(pair) < HD
            middle = jnp.where(low, dq_ref[b, :, LANES:].astype(F32), turn(keys))
            last = jnp.where(low, turn(pair), 0.0)
            rows.append(
                jnp.concatenate([dq_ref[b, :, :LANES], middle.astype(BF16), last.astype(BF16)], 1)
            )
            rows_ref[b] = rows[-1]
        total = dot(jnp.concatenate(rows, 0), weights[...], NT).astype(BF16)
        for block, part in cut(total, blocks):
            partial[block] = part

    join((ring.at(ring.steps), ring.chip))
    strip = g_ref.shape[0] // ring.steps
    tile = 2 * LANES

    def between():
        def one(index, carry):
            join(ring.pair(ring.steps - 1 - index))
            return carry

        lax.fori_loop(0, ring.steps - 1, one, 0)

    def work(s, place):
        if place == 0:
            rows = pl.ds(pl.multiple_of(s * strip, LANES), strip)
            value = dot(flat(tokens[:, :, rows]), flat(rows_ref[...]), TN)
            g_ref[rows, :tile] = value[:, :tile].astype(BF16)
            last_ref[rows] = value[:, tile:]

    d_x, finish = ring.scatter(partial, land, scatter_sem, work, between)
    swaps[1].wait()
    own = g_acc[pl.ds(pl.multiple_of(core * shard, 8), shard), :]
    g_out_ref[...] = (own + out_got[...].astype(F32)).astype(BF16)
    ring.settle()
    d_values, gain_one = normal_back(d_x, hidden_ref[...].astype(F32), gain_row(params_ref, 0, layer))
    grad = mid_ref[...] + d_values
    grad_ref[...] = grad
    d_mix = grad.astype(BF16)
    d_mix_ref[...] = d_mix
    balance = jnp.sum(mixed_ref[...] * d_mix.astype(F32), -1, keepdims=True)
    side_ref[...] = jnp.broadcast_to(as_line(balance), side_ref.shape)
    routers = router_ref[...]
    lines = [
        jnp.where(core == 0, routers[0:1], routers[1:2]),
        jnp.where(core == 0, routers[1:2], routers[0:1]),
        gain_one,
        gain_two_ref[...],
    ]
    features = g_ref.shape[0]
    tall = jnp.concatenate(
        [jnp.zeros((HD, features), F32)] + lines + [jnp.zeros((HD - len(lines), features), F32)], 0
    )
    g_ref[:, tile:] = (last_ref[...] + tall.T).astype(BF16)
    finish()


def gather_attend_back_scatter(
    count, layer, d, w_out, w, x_all, att, q, own, other, begin, lse, tables, late, rides=()
):
    _, rows, width = x_all.shape
    shard = w_out.shape[2]
    columns = w.shape[2]
    everyone = pltpu.VMEM((count, rows, width), BF16)
    early = [att, q, own, other, begin, lse, tables]
    pairs = cells((count, rows, LANES), BF16)
    return ring_call(
        functools.partial(attend_back_kernel, count, layer),
        ("attend_back", layer),
        [(a, ANYWHERE) for a in (d, w_out, w, x_all)] + [(a, EARLY) for a in early] + [(a, LATE) for a in late],
        [
            (cells((shard, width), BF16), OUT),
            (cells((rows, width), F32), OUT),
            (cells((rows, width), BF16), OUT),
            (cells((8, rows), F32), OUT),
            (cells(w.shape[1:], BF16), OUT),
        ],
        [
            everyone,
            pltpu.VMEM((2 * LANES, width), BF16),
            pltpu.VMEM((2 * LANES, width), F32),
            pltpu.VMEM((shard, width), BF16),
            pltpu.VMEM((shard, width), BF16),
            pltpu.VMEM((count // SPAN, LANES, SPAN * 2 * LANES), BF16),
            pltpu.VMEM(pairs.shape, F32),
            pltpu.VMEM(pairs.shape, F32),
            pltpu.VMEM(pairs.shape, BF16),
            pltpu.VMEM(pairs.shape, BF16),
            pltpu.VMEM((count, rows, 2 * LANES), BF16),
            everyone,
            land_scratch(count, rows, width),
            pltpu.VMEM((count, rows, columns), BF16),
            everyone,
            pltpu.VMEM(w.shape[1:], BF16),
            pltpu.VMEM((width, LANES), F32),
        ]
        + gather_sems(count)
        + scatter_sems(count)
        + dmas((2,), (2,), (4,)),
        60,
        rides,
    )


def finish_kernel(count, replicas, *refs):
    inputs, outputs, scratch = split(refs, 3, 2)
    mine, peer = outputs
    g_ref, early_ref, early_peer_ref, early, land, total = scratch[:6]
    pair_send, pair_recv, part_send, part_recv, rep_send, rep_recv, load_sem = scratch[6:]
    loads = [
        pltpu.make_async_copy(source, target, load_sem.at[i])
        for i, (source, target) in enumerate(zip(inputs, scratch))
    ]
    for load in loads:
        load.start()
    me = lax.axis_index("fsdp")
    chip, core = me // 2, lax.rem(me, 2)
    partner = partner_of("fsdp")

    def chip_at(offset):
        return lax.rem(chip + offset + count, count)

    def device(offset):
        return {"fsdp": chip_at(offset) * 2 + core}

    across = [partner_of("rep")] if replicas == 2 else []
    meet([device(offset) for offset in range(1, count)] + [partner] + across)
    swaps = [remote(inputs[0].at[:, 1 - core], land.at[0], pair_send.at[0], pair_recv.at[0], partner)]
    swaps[0].start()
    for load in loads:
        load.wait()
    for block in range(count):
        both = early_ref[block, 1 - core].astype(F32)
        if replicas == 2:
            both = both + early_peer_ref[block, 1 - core].astype(F32)
        early[block] = both.astype(BF16)
    swaps.append(remote(early, land.at[1], pair_send.at[1], pair_recv.at[1], partner))
    swaps[1].start()
    if replicas != 2:
        peer[...] = jnp.zeros_like(peer)
    sends = []
    for layer in range(2):
        swaps[layer].wait()
        for block in range(count):
            own = (g_ref, early_ref)[layer][block, core].astype(F32)
            if layer == 1 and replicas == 2:
                own = own + early_peer_ref[block, core].astype(F32)
            total[layer, block] = (own + land[layer, block].astype(F32)).astype(BF16)
        for offset in range(1, count):
            sends.append(
                remote(
                    total.at[layer, chip_at(offset)], mine.at[layer, chip],
                    part_send.at[layer, offset], part_recv.at[layer, offset], device(offset),
                )
            )
            sends[-1].start()
        mine[layer, chip] = total[layer, chip]

    def to_peer(offset):
        slot = chip_at(-offset)
        return remote(mine.at[0, slot], peer.at[slot], rep_send.at[offset], rep_recv.at[offset], across[0])

    for layer in range(2):
        for offset in range(count):
            if offset > 0:
                slot = mine.at[layer, chip_at(-offset)]
                remote(slot, slot, part_send.at[layer, offset], part_recv.at[layer, offset], partner).wait_recv()
            if layer == 0 and replicas == 2:
                to_peer(offset).start()
    if replicas == 2:
        for offset in range(count):
            to_peer(offset).wait()

    for send in sends:
        send.wait_send()


def finish_heads(count, replicas, g, early, early_peer):
    _, _, rows, columns = g.shape
    part = (LAYERS, count, rows, columns)
    dma = pltpu.SemaphoreType.DMA
    return pl.pallas_call(
        functools.partial(finish_kernel, count, replicas),
        out_shape=(cells(part, BF16), cells((count, rows, columns), BF16)),
        in_specs=[ANYWHERE] * 3,
        out_specs=[HERE] * 2,
        scratch_shapes=[
            pltpu.VMEM(g.shape, BF16),
            pltpu.VMEM(g.shape, BF16),
            pltpu.VMEM(g.shape, BF16),
            pltpu.VMEM((count, rows, columns), BF16),
            pltpu.VMEM(part, BF16),
            pltpu.VMEM(part, BF16),
            dma((2,)), dma((2,)), dma((2, count)), dma((2, count)), dma((count,)), dma((count,)), dma((3,)),
        ],
        compiler_params=pltpu.CompilerParams(
            collective_id=identity(("finish",)), has_side_effects=True, vmem_limit_bytes=60 << 20
        ),
        cost_estimate=FREE,
        name="finish_heads",
    )(g, early, early_peer)


def close_kernel(layers, count, *refs):
    n_experts = 0 if len(refs) == 2 * layers + 13 else 12 * layers
    inputs, heads_in, rows_in, experts_in, outputs = split(refs, 2 * layers, 2, 2, n_experts)
    mine, peer = heads_in
    out_ref, q_out, k_out, v_out, router_out, gain_one_out, gain_two_out = outputs[:7]
    for source, target in zip(rows_in, outputs[7:9]):
        target[...] = source[...]

    @pl.when(pl.program_id(0) == 0)
    def _():
        for layer in range(layers):
            own, got = inputs[2 * layer : 2 * layer + 2]
            out_ref[layer] = own[...].astype(F32) + got[...].astype(F32)

            def tiles(block):
                value = mine[layer, block].astype(F32)
                if layer == 0:
                    value = value + peer[block].astype(F32)
                return [value[:, i * LANES : (i + 1) * LANES] for i in range(3)]

            shard = mine.shape[2]
            gains = jnp.zeros((shard, LANES), F32)
            routers = jnp.zeros((shard, LANES), F32)
            for half in range(count // 2):
                a, b = tiles(2 * half), tiles(2 * half + 1)
                low = lanes_of(a[0]) < HD
                for chip, tile in ((2 * half, a[2]), (2 * half + 1, b[2])):
                    gains = gains + tile
                    moved = pltpu.roll(tile, (2 * chip - HD) % LANES, 1)
                    lane = lanes_of(moved)
                    routers = jnp.where((lane >= 2 * chip) & (lane < 2 * chip + 2), moved, routers)
                q_out[layer, :, 3 * half * LANES : 3 * (half + 1) * LANES] = jnp.concatenate(
                    [a[0], jnp.where(low, a[1], turn(b[0])), jnp.where(low, turn(b[0]), turn(b[1]))], 1
                )
                here = slice(half * LANES, (half + 1) * LANES)
                k_out[layer, :, here] = jnp.where(low, turn(a[1]), b[1])
                v_out[layer, :, here] = jnp.where(low, a[2], turn(b[2]))

            router_out[layer] = routers[:, : 2 * count]
            tall = jnp.concatenate([gains, jnp.zeros((LANES - shard, LANES), F32)], 0).T
            gain_one_out[layer : layer + 1, :] = tall[HD + 2 : HD + 3, :shard]
            gain_two_out[layer : layer + 1, :] = tall[HD + 3 : HD + 4, :shard]

    if experts_in:
        expert_refs = outputs[9:]
        for layer in range(layers):
            pairs = experts_in[layer * 12 : (layer + 1) * 12]
            sums = [pairs[i][...].astype(F32) + pairs[i + 6][...].astype(F32) for i in range(6)]
            early = pl.program_id(0) < pl.num_programs(0) // 4
            expert_refs[0][layer, 0] = jnp.where(early, sums[0], sums[1])
            expert_refs[1][layer, 0] = sums[2]
            expert_refs[2][layer, 0] = jnp.concatenate(sums[3:], 1)


def close(count, outs, mine, peer, rows_out, experts):
    layers = len(outs)
    shard, width = outs[0][0].shape
    steps = 8

    def whole(shape):
        return pl.BlockSpec(shape, lambda i: (0,) * len(shape))

    arrays = [array for pair in outs for array in pair] + [mine, peer]
    specs = [whole(a.shape) for a in arrays]
    shapes = [
        (layers, shard, width),
        (layers, shard, count * GROUP * HD),
        (layers, shard, count * HD),
        (layers, shard, count * HD),
        (layers, shard, 2 * count),
        (layers, shard),
        (layers, shard),
    ]
    out_specs = [whole(shape) for shape in shapes]
    shapes = [cells(shape, F32) for shape in shapes] + [cells(a.shape, a.dtype) for a in rows_out]
    parts = [
        pl.BlockSpec((a.shape[0] // (steps if experts else 1), a.shape[1]), lambda i: (i, 0)) for a in rows_out
    ]
    arrays += rows_out
    specs += parts
    out_specs += parts
    if experts:
        (_, _), (rest, _) = experts[0]
        rows, ff = rest.shape
        tall, short = width // steps, ff // steps
        apart = width // 4
        groups = (rows + apart - 2 * width) // ff

        def at(first, length):
            return pl.BlockSpec((length, ff), lambda i: ((first - apart) // length + i, 0))

        parts = [
            pl.BlockSpec((tall, ff), lambda i: (jnp.minimum(i, apart // tall - 1), 0)),
            pl.BlockSpec((tall, ff), lambda i: (jnp.maximum(i - apart // tall, 0), 0)),
            at(width, tall),
        ] + [at(2 * width + g * ff, short) for g in range(groups)]
        for front, back in experts:
            for own, other in zip(front, back):
                arrays += [own] + [other] * (len(parts) - 1)
        specs += parts * (2 * layers)
        shapes += [cells((layers, 1, width, ff), F32)] * 2 + [cells((layers, 1, ff, width), F32)]
        tile = pl.BlockSpec((layers, 1, tall, ff), lambda i: (0, 0, i, 0))
        out_specs += [tile, tile, pl.BlockSpec((layers, 1, short, width), lambda i: (0, 0, i, 0))]
    return pl.pallas_call(
        functools.partial(close_kernel, layers, count),
        grid=(steps if experts else 1,),
        out_shape=tuple(shapes),
        in_specs=specs,
        out_specs=out_specs,
        compiler_params=pltpu.CompilerParams(vmem_limit_bytes=60 << 20),
        cost_estimate=FREE,
        name="close",
    )(*arrays)


def on_device(
    tokens,
    cotangent,
    positions,
    segments,
    routes,
    attn_gain,
    w_query,
    w_key,
    w_value,
    w_out,
    ffn_gain,
    router,
    w_gate,
    w_up,
    w_down,
):
    rows, width = tokens.shape
    devices = lax.axis_size("fsdp")
    replicas = lax.axis_size("rep")
    count = devices // 2
    me = lax.axis_index("fsdp")
    chip, core = me // 2, lax.rem(me, 2)
    shard = w_query.shape[1]
    experts = devices
    columns = 3 * LANES
    used = (GROUP + 2) * HD

    small = jnp.concatenate(
        [attn_gain, ffn_gain, router.transpose(0, 2, 1).reshape(LAYERS * experts, shard)], 0
    )
    small = jnp.pad(small, ((0, 48 - small.shape[0]), (0, LANES - shard)))
    rate = jnp.exp(-jnp.log(10000.0) * jnp.arange(HD // 2, dtype=F32) / (HD // 2))
    angle = rate[:, None] * positions.astype(F32)[None, :]
    table = jnp.concatenate([jnp.cos(angle), jnp.sin(angle)], 0)
    experts_w = [w_gate, w_up, w_down]

    flat_segments = segments.reshape(1, -1)
    kinds = jnp.arange(8, dtype=jnp.int32)[:, None]
    starts = jnp.sum((flat_segments < kinds).astype(jnp.int32), 1, keepdims=True)
    begin = jnp.sum(jnp.where(flat_segments == kinds, starts, 0), 0).reshape(count, 2, rows)
    begin = lax.dynamic_index_in_dim(begin, core, 1, True)

    chosen = routes.transpose(0, 2, 1)
    hidden = tokens
    saved = []
    for layer in range(LAYERS):
        if layer == 0:
            projections = [w_query, w_key, w_value]
            inputs = [(a, EARLY) for a in (tokens, *projections)]
            inputs += [(a, ANYWHERE) for a in (w_out, small, table)] + [(begin, EARLY), (chosen, LATE)]
            extra = opening_shapes(count, tokens, columns, w_out, small, table)
        else:
            inputs = [(a, ANYWHERE) for a in (x_attn, heads_w, outs_w)] + [(tables, EARLY), (begin, EARLY)]
            inputs += [(hidden, LATE), (params, LATE), (chosen, LATE)]
            extra = [], []
        results = forward(count, layer, inputs, rows, width, columns, experts_w, cotangent, extra)
        query, kv, kv_other, x_all, att, lse, middle, _, _ = results[:9]
        if layer == 0:
            heads_w, outs_w, tables, params = results[9:13]
        mixed, after, x_attn, m_all, share_all, *side = results[9 + len(extra[0]) :]
        saved.append((hidden, x_all, query, kv, kv_other, att, lse, middle, mixed, m_all, share_all))
        hidden = after
    activations = x_attn

    def across(array):
        return lax.ppermute(array, "rep", [(0, 1), (1, 0)]) if replicas == 2 else array

    grad = d_mix = cotangent
    (side,) = side
    expert_sums = [None] * LAYERS
    fronts = [None] * LAYERS
    out_sums = [None] * LAYERS
    for layer in reversed(range(LAYERS)):
        hidden, x_all, query, kv, kv_other, att, lse, middle, mixed, m_all, share_all = saved[layer]
        rides = [out_sums[layer + 1], early, fronts[layer + 1][0]] if layer + 1 < LAYERS and replicas == 2 else []
        grad_mid, d_branch, gain_two, front, expert_sum, g_router, *rode = gather_mix_back_scatter(
            count, layer, replicas, d_mix, side, m_all, share_all, params, grad, middle, experts_w, rides
        )
        if layer + 1 < LAYERS:
            d_branch, expert_sums[layer + 1] = lax.optimization_barrier(
                (d_branch, expert_sums[layer + 1])
            )
        fronts[layer] = (front, rode.pop(0) if crosses_early(layer, replicas) else front)
        if rides:
            fronts[layer + 1] = (fronts[layer + 1][0], rode[2])
        expert_sums[layer] = (expert_sum, across(expert_sum))
        out_sum, grad, d_mix, side, heads = gather_attend_back_scatter(
            count, layer, d_branch, outs_w, heads_w, x_all, att, query, kv, kv_other, begin, lse, tables,
            [params, grad_mid, hidden, saved[max(layer - 1, 0)][8], g_router, gain_two],
        )
        out_sums[layer] = out_sum
        heads = heads.reshape(count, 2, shard, columns)
        early = heads if layer > 0 else early
    arrived, peer = finish_heads(count, replicas, heads, early, rode[1] if rode else early)
    if replicas == 2:
        outs = list(zip(out_sums, [across(out_sums[0]), rode[0]]))
        *results, g_gate, g_up, g_down = close(
            count, outs, arrived, peer, [activations, grad], list(zip(fronts, expert_sums))
        )
    else:
        outs = [(own, jnp.zeros_like(own)) for own in out_sums]
        results = close(count, outs, arrived, peer, [activations, grad], [])
        sums = (*results[:7], jnp.stack([jnp.concatenate([a, b]) for (a, _), (b, _) in zip(fronts, expert_sums)]))
        *summed, flat_sums = [lax.psum(array.astype(BF16), "rep").astype(F32) for array in sums]
        results = summed + list(results[7:])
        ff = w_gate.shape[3]
        g_gate, g_up = flat_sums[:, None, :width], flat_sums[:, None, width : 2 * width]
        g_down = flat_sums[:, 2 * width :].reshape(LAYERS, width // ff, ff, ff)
        g_down = g_down.transpose(0, 2, 1, 3).reshape(LAYERS, 1, ff, width)
    g_out, g_query, g_key, g_value, g_router, gain_one, gain_two, activations, grad = results
    return (
        activations,
        grad,
        gain_one,
        g_query,
        g_key,
        g_value,
        g_out,
        gain_two,
        g_router,
        g_gate,
        g_up,
        g_down,
    )


def solution(mesh):
    placed = (
        P(("rep", "fsdp"), None),
        P(("rep", "fsdp"), None),
        P(("rep", "fsdp")),
        P("rep", None),
        P(None, ("rep", "fsdp"), None),
        P(None, "fsdp"),
        P(None, "fsdp", None),
        P(None, "fsdp", None),
        P(None, "fsdp", None),
        P(None, "fsdp", None),
        P(None, "fsdp"),
        P(None, "fsdp", None),
        P(None, "fsdp", None, None),
        P(None, "fsdp", None, None),
        P(None, "fsdp", None, None),
    )
    return jax.shard_map(
        on_device,
        mesh=mesh,
        in_specs=placed,
        out_specs=(
            P(("rep", "fsdp"), None),
            P(("rep", "fsdp"), None),
            P(None, "fsdp"),
            P(None, "fsdp", None),
            P(None, "fsdp", None),
            P(None, "fsdp", None),
            P(None, "fsdp", None),
            P(None, "fsdp"),
            P(None, "fsdp", None),
            P(None, "fsdp", None, None),
            P(None, "fsdp", None, None),
            P(None, "fsdp", None, None),
        ),
        check_vma=False,
    )
```
